32 devices in a mesh: ctx: 16 (over z, y, core), fsdp: 2 (over x).
Axes of the slice: x: 2, y: 2, z: 4, core: 2. Of those that a mesh axis runs over, the one named last changes fastest.
Arguments:
- resid: bfloat16 [2, 4096, 767], P('fsdp', 'ctx'), may hold values from -6 to 6
- lengths: int32 [2], P('fsdp'), may hold values from 1024 to 4096, as said below
- gain_one: bfloat16 [768], P('fsdp'), may hold values from 0.099609375 to 1.8984375
- w_qkv: bfloat16 [768, 2304], P('fsdp'), may hold values from -0.21875 to 0.21875
- w_out: bfloat16 [768, 767], P('fsdp'), may hold values from -3.5 to 3.5
- gain_two: bfloat16 [768], P('fsdp'), may hold values from 0.099609375 to 1.8984375
- w_up: bfloat16 [768, 3072], P(None, 'fsdp'), may hold values from -0.21875 to 0.21875
- w_down: bfloat16 [3072, 767], P('fsdp'), may hold values from -0.109375 to 0.109375
- cotangent: bfloat16 [2, 4096, 767], P('fsdp', 'ctx'), may hold values from -6 to 6
Outputs:
- output: bfloat16 [2, 4096, 767], P('fsdp', 'ctx')
- grad_input: float32 [2, 4096, 767], P('fsdp', 'ctx')
- grad_gain_one: float32 [768], P('fsdp')
- grad_qkv: float32 [768, 2304], P('fsdp')
- grad_out: float32 [768, 767], P('fsdp')
- grad_gain_two: float32 [768], P('fsdp')
- grad_up: float32 [768, 3072], P(None, 'fsdp')
- grad_down: float32 [3072, 767], P('fsdp')
The draws below stay inside these ranges and needn't reach their ends.
Inputs may be any that keep to these rules, and one draw needn't show every extreme that they name: `lengths`: live slots of each sequence, counted from its first slot; one sequence has all 4096 live and one has 1024.
All inputs are finite; a program needn't handle non-finite values.
Results may differ from the reference program's by a relative error of at most 0.024.
Values may be sent and summed in bfloat16 or wider, within the bound.
A program may use at most 128 MiB of HBM per device.

```python
import jax
import jax.numpy as jnp
from jax import lax

D = 768
HEADS = 12
HDIM = 64
FF = 3072
DC = 767
LEN = 4096
SEQS = 2


def draw_lengths(key, part):
    key_draw = jax.random.fold_in(key, 11)
    key_top = jax.random.fold_in(key, 12)
    key_low = jax.random.fold_in(key, 13)
    counts_drawn = jax.random.randint(key_draw, (SEQS,), LEN // 4, LEN + 1, dtype=jnp.int32)
    top_at = jax.random.randint(key_top, (), 0, SEQS, dtype=jnp.int32)
    low_at = (top_at + 1 + jax.random.randint(key_low, (), 0, SEQS - 1, dtype=jnp.int32)) % SEQS
    positions = jnp.arange(SEQS, dtype=jnp.int32)
    counts_drawn = jnp.where(positions == top_at, LEN, counts_drawn)
    counts_drawn = jnp.where(positions == low_at, LEN // 4, counts_drawn)
    return counts_drawn.astype(jnp.int32)


def levels(rng, dims, split, least, top_value):
    def one(axis_at, blocks):
        heights = jax.random.uniform(jax.random.fold_in(jax.random.fold_in(rng, 6), axis_at), (blocks,), jnp.float32, least / len(split), top_value / len(split))
        return jnp.repeat(jnp.exp(heights), dims[axis_at] // blocks).reshape((-1,) + (1,) * (len(dims) - axis_at - 1))

    loudness = one(*split[0])
    for cut in split[1:]:
        loudness = loudness * one(*cut)
    return loudness


def bell_draw(key, dims, spread, bound, split=(), kind=jnp.bfloat16):
    entries = jax.random.normal(key, dims, jnp.float32) * spread
    if len(split) > 0:
        entries = levels(key, dims, split, -0.22, 0.18) * entries
    return jnp.clip(entries, min=-bound, max=bound).astype(kind)


def setup_inputs(seed: int = 0) -> dict:
    arg_keys = jax.random.split(jax.random.key(seed), 10)
    return {
        "resid": bell_draw(arg_keys[0], (SEQS, LEN, DC), 1.0, 6.0, ((0, 2), (1, 16))),
        "lengths": draw_lengths(jax.random.fold_in(arg_keys[9], 71), 0),
        "gain_one": jnp.clip(1.0 + 0.18 * jax.random.normal(arg_keys[2], (D,), jnp.float32), 0.099609375, 1.8984375).astype(jnp.bfloat16),
        "w_qkv": bell_draw(arg_keys[3], (D, 3 * D), D ** -0.5, 0.21875, ((0, 2),)),
        "w_out": bell_draw(arg_keys[4], (D, DC), (max(1, D * 16 // LEN)) ** -0.5, 3.5, ((0, 2),)),
        "gain_two": jnp.clip(1.0 + 0.18 * jax.random.normal(arg_keys[5], (D,), jnp.float32), 0.099609375, 1.8984375).astype(jnp.bfloat16),
        "w_up": bell_draw(arg_keys[6], (D, FF), D ** -0.5, 0.21875, ((1, 2),)),
        "w_down": bell_draw(arg_keys[7], (FF, DC), FF ** -0.5, 0.109375, ((0, 2),)),
        "cotangent": bell_draw(arg_keys[8], (SEQS, LEN, DC), 1.0, 6.0, ((0, 2), (1, 16))),
    }


@jax.custom_vjp
def low(v):
    return lax.optimization_barrier(v.astype(jnp.bfloat16)).astype(jnp.float32)

@jax.custom_vjp
def low_back(v):
    return v

def low_keep(v):
    return (low(v), None)

def low_pass(kept, grad):
    return (grad,)

def back_keep(v):
    return (v, None)

def back_low(kept, grad):
    return (low(grad),)
low.defvjp(low_keep, low_pass)
low_back.defvjp(back_keep, back_low)
epsilon = 1e-05
masked = -1e+30

def crms(residual, gain):
    extended = jnp.concatenate([residual, -lax.optimization_barrier(jnp.sum(residual, axis=-1, keepdims=True))], axis=-1)
    inverse = lax.rsqrt(lax.optimization_barrier(jnp.mean(extended * extended, axis=-1, keepdims=True)) + epsilon)
    return extended * inverse * gain

def gelu_tanh(values):
    return jax.nn.gelu(values, approximate=True)

def attend_sequence(queries, key_rows, value_rows, length):
    factor = HDIM ** (-0.5)
    block_rows = min(512, LEN)
    key_pos = jnp.arange(LEN, dtype=jnp.int32)

    def one_block(block_start):
        block_queries = lax.dynamic_slice_in_dim(queries, block_start, block_rows, 0)
        query_pos = block_start + jnp.arange(block_rows, dtype=jnp.int32)
        scores = low_back(jnp.einsum('qhd,khd->hqk', block_queries, key_rows, precision=lax.Precision.HIGHEST) * factor)
        allowed = (key_pos[None, :] <= query_pos[:, None]) & (key_pos[None, :] < length)
        scores = jnp.where(allowed[None], scores, masked)
        shifted = scores - lax.optimization_barrier(jnp.max(scores, axis=-1, keepdims=True))
        expons = jnp.exp(shifted)
        softmax_w = expons / lax.optimization_barrier(jnp.sum(expons, axis=-1, keepdims=True))
        return jnp.einsum('hqk,khd->qhd', low(softmax_w), value_rows, precision=lax.Precision.HIGHEST)
    starts = jnp.arange(0, LEN, block_rows, dtype=jnp.int32)
    blocks = lax.map(jax.checkpoint(one_block), starts)
    return blocks.reshape(LEN, HEADS, HDIM)

def layer(residual, params, length):
    gain_one, w_qkv, w_out, gain_two, w_up, w_down = params
    hidden_one = low(crms(residual, gain_one))
    projected = low_back(low(jnp.dot(hidden_one, w_qkv, precision=lax.Precision.HIGHEST)))
    queries = projected[:, :D].reshape(LEN, HEADS, HDIM)
    key_rows = projected[:, D:2 * D].reshape(LEN, HEADS, HDIM)
    value_rows = projected[:, 2 * D:].reshape(LEN, HEADS, HDIM)
    attended = low_back(low(attend_sequence(queries, key_rows, value_rows, length).reshape(LEN, D)))
    branch = low_back(jnp.dot(attended, w_out, precision=lax.Precision.HIGHEST))
    middle = residual + branch
    hidden_two = low(crms(middle, gain_two))
    pre_act = low_back(jnp.dot(hidden_two, w_up, precision=lax.Precision.HIGHEST))
    activated = low(gelu_tanh(pre_act))
    return middle + low_back(jnp.dot(activated, w_down, precision=lax.Precision.HIGHEST))

def reference(resid, lengths, gain_one, w_qkv, w_out, gain_two, w_up, w_down, cotangent):
    params = (gain_one.astype(jnp.float32), w_qkv.astype(jnp.float32), w_out.astype(jnp.float32), gain_two.astype(jnp.float32), w_up.astype(jnp.float32), w_down.astype(jnp.float32))

    def forward(residual, weights_all):

        def per_sequence(sequence):
            return layer(sequence[0], weights_all, sequence[1])
        return lax.map(jax.checkpoint(per_sequence), (residual, lengths))
    final, pullback = jax.vjp(forward, resid.astype(jnp.float32), params)
    live = (jnp.arange(LEN, dtype=jnp.int32)[None, :] < lengths[:, None]).astype(jnp.float32)
    grad_input, grad_params = pullback(cotangent.astype(jnp.float32) * live[:, :, None])
    return (final.astype(jnp.bfloat16), grad_input, grad_params[0], grad_params[1], grad_params[2], grad_params[3], grad_params[4], grad_params[5])
```

```python
import functools

import jax
import jax.numpy as jnp
from jax import lax
from jax.experimental import pallas as pl
from jax.experimental.pallas import tpu as pltpu
from jax.sharding import PartitionSpec as P

F32 = jnp.float32
BF16 = jnp.bfloat16
MESH = pl.DeviceIdType.MESH
NT = (((1,), (1,)), ((), ()))
TN = (((0,), (0,)), ((), ()))
EPS = 1e-05
MASKED = -1e30
LOG2E = 1.4426950408889634
SCALE = 0.125
GROUPS = 4
GH = 3
HD = 64
SUB = 1024
VLIM = 60 * 1024 * 1024

VM = pl.BlockSpec(memory_space=pltpu.VMEM)
SM = pl.BlockSpec(memory_space=pltpu.SMEM)
ANY = pl.BlockSpec(memory_space=pl.ANY)
DMA = pltpu.SemaphoreType.DMA


def dot(a, b):
    return jnp.dot(a, b, preferred_element_type=F32)


def dg(a, b, dims):
    return lax.dot_general(a, b, dims, preferred_element_type=F32)


def rcopy(src, dst, send, recv, dev):
    return pltpu.make_async_remote_copy(
        src_ref=src, dst_ref=dst, send_sem=send, recv_sem=recv, device_id=dev, device_id_type=MESH
    )


class Place:
    def __init__(self, n):
        self.n = n
        self.m = n // GROUPS
        self.chips = self.m // 2
        c = lax.axis_index("ctx")
        self.x = lax.axis_index("fsdp")
        self.a = c // self.m
        self.b = c % self.m
        self.chip = self.b // 2
        self.k = self.b % 2

    def xpeer(self):
        return {"fsdp": 1 - self.x}

    def sibling(self):
        return {"ctx": self.a * self.m + self.chip * 2 + 1 - self.k}

    def on_chip(self, chip):
        return {"ctx": self.a * self.m + chip * 2 + self.k}

    def on_line(self, a):
        return {"ctx": a * self.m + self.b}


def greet(p, xpeer=False, sibling=False, chips=False, line=False):
    bar = pltpu.get_barrier_semaphore()
    count = 0
    if xpeer:
        pl.semaphore_signal(bar, inc=1, device_id=p.xpeer(), device_id_type=MESH)
        count += 1
    if sibling:
        pl.semaphore_signal(bar, inc=1, device_id=p.sibling(), device_id_type=MESH)
        count += 1
    if chips:
        for d in range(1, p.chips):
            pl.semaphore_signal(
                bar, inc=1, device_id=p.on_chip((p.chip + d) % p.chips), device_id_type=MESH
            )
            count += 1
    if line:
        for d in range(1, GROUPS):
            pl.semaphore_signal(
                bar, inc=1, device_id=p.on_line((p.a + d) % GROUPS), device_id_type=MESH
            )
            count += 1
    return lambda: pl.semaphore_wait(bar, count)


def ext_of(v):
    last = lax.broadcasted_iota(jnp.int32, v.shape, 1) == v.shape[1] - 1
    return jnp.where(last, -jnp.sum(v, axis=1, keepdims=True), v)


def inv_rms(u):
    return lax.rsqrt(jnp.mean(u * u, axis=1, keepdims=True) + EPS)


def crms_back(u, inv, gain, dy):
    dx = dy * gain
    du = inv * (dx - u * (inv * inv * jnp.mean(dx * u, axis=1, keepdims=True)))
    width = u.shape[1]
    last = lax.broadcasted_iota(jnp.int32, u.shape, 1) == width - 1
    return jnp.where(last, 0.0, du - du[:, width - 1 :])


def low_half(shape):
    return lax.broadcasted_iota(jnp.int32, shape, len(shape) - 1) < HD


def pack_tail(t):
    half = t.shape[0] // 2
    top, bottom = t[:half], t[half:]
    return jnp.where(low_half(top.shape), pltpu.roll(bottom, HD, 1), top)


def unpack_tail(t):
    low = low_half(t.shape)
    zero = jnp.zeros_like(t)
    return jnp.where(low, zero, t), jnp.where(low, zero, pltpu.roll(t, HD, 1))


def project_kernel(n, rp, gains, wg, wo, h1, q3, kv, wa, woa, gfull, ss, rs, ls, hs, hr, ks, kr, fs):
    p = Place(n)
    rows, width = rp.shape
    half = width // 2
    ready = greet(p, xpeer=True, sibling=True, chips=True, line=True)
    own = pltpu.make_async_copy(
        wg.at[p.a], wa.at[pl.ds(pl.multiple_of(p.x * half, half), half)], ls.at[0]
    )
    own.start()
    zero_rows = jnp.zeros((HD, width), BF16)
    for g in range(GROUPS):
        woa[pl.ds(g * 256 + 128, HD), :] = zero_rows
    local = []
    for i in range(2):
        g = p.x * 2 + i
        for j, (src, size, dst) in enumerate(((0, 128, 0), (128, 64, 192))):
            c = pltpu.make_async_copy(
                wo.at[pl.ds(i * 192 + src, size)],
                woa.at[pl.ds(pl.multiple_of(g * 256 + dst, 64), size)],
                ls.at[1 + 2 * i + j],
            )
            c.start()
            local.append(c)
    gfull[p.x] = gains[...]
    u = ext_of(rp[...].astype(F32))
    normed = u * inv_rms(u)
    ready()
    xg = rcopy(gains, gfull.at[p.x], ss.at[0], rs.at[0], p.xpeer())
    xg.start()
    xw = rcopy(
        wg.at[p.a],
        wa.at[pl.ds(pl.multiple_of(p.x * half, half), half)],
        ss.at[1],
        rs.at[1],
        p.xpeer(),
    )
    xw.start()
    xg.wait()
    gain = jnp.concatenate([gfull[0, 0:1, :], gfull[1, 0:1, :]], axis=1)
    h1[p.a] = (normed * gain).astype(BF16)

    def line_copy(block, dst, sem):
        return rcopy(h1.at[block], h1.at[block], hs.at[sem], hr.at[block], p.on_line(dst))

    def kv_rows(block, b):
        return kv.at[pl.ds(pl.multiple_of((block * p.m + b) * rows, rows), rows)]

    def kv_copy(block, b, dev, send):
        r = kv_rows(block, b)
        return rcopy(r, r, send, kr.at[block, b], dev)

    @pl.when(p.a < GROUPS - 1)
    def _():
        line_copy(p.a, p.a + 1, 0).start()

    @pl.when(p.a > 0)
    def _():
        line_copy(p.a, p.a - 1, 1).start()

    xo = []
    for i in range(2):
        g = p.x * 2 + i
        for j, (src, size, dst) in enumerate(((0, 128, 0), (128, 64, 192))):
            c = rcopy(
                wo.at[pl.ds(i * 192 + src, size)],
                woa.at[pl.ds(pl.multiple_of(g * 256 + dst, 64), size)],
                ss.at[2 + 2 * i + j],
                rs.at[2 + 2 * i + j],
                p.xpeer(),
            )
            c.start()
            xo.append(c)
    own.wait()
    xw.wait()

    def produce(block):
        y = dot(h1[block], wa[...]).astype(BF16)
        low = low_half((rows, 128))
        zero = jnp.zeros((rows, 128), BF16)
        at = pl.ds(pl.multiple_of(block * rows, rows), rows)
        q3[0, at, :] = jnp.where(low, y[:, :128], zero)
        q3[1, at, :] = jnp.where(low, zero, y[:, :128])
        q3[2, at, :] = y[:, 128:256]
        kv[pl.ds(pl.multiple_of((block * p.m + p.b) * rows, rows), rows), :] = y[:, 256:]
        for d in range(1, p.chips):
            kv_copy(block, p.b, p.on_chip((p.chip + d) % p.chips), ks.at[block, d]).start()
        kv_copy(block, p.b, p.sibling(), ks.at[block, 0]).start()

    def pass_on(block):
        for d in range(1, p.chips):
            b = ((p.chip + d) % p.chips) * 2 + p.k
            kv_copy(block, b, p.sibling(), fs.at[block, d]).wait_recv()
            kv_copy(block, b, p.sibling(), fs.at[block, d]).start()

    produce(p.a)
    for s in range(1, GROUPS):

        @pl.when(p.a - s >= 0)
        def _():
            line_copy(p.a - s, p.a, 0).wait_recv()

            @pl.when(p.a < GROUPS - 1)
            def _():
                line_copy(p.a - s, p.a + 1, 2 * s).start()

        @pl.when(p.a + s < GROUPS)
        def _():
            line_copy(p.a + s, p.a, 0).wait_recv()

            @pl.when(p.a > 0)
            def _():
                line_copy(p.a + s, p.a - 1, 2 * s + 1).start()

        @pl.when(p.a - s >= 0)
        def _():
            produce(p.a - s)

        @pl.when(p.a + s < GROUPS)
        def _():
            produce(p.a + s)

        @pl.when(p.a - s + 1 >= 0)
        def _():
            pass_on(p.a - s + 1)

        if s > 1:

            @pl.when(p.a + s - 1 < GROUPS)
            def _():
                pass_on(p.a + s - 1)

    @pl.when(p.a - GROUPS + 1 >= 0)
    def _():
        pass_on(p.a - GROUPS + 1)

    @pl.when(p.a + GROUPS - 1 < GROUPS)
    def _():
        pass_on(p.a + GROUPS - 1)

    for block in range(GROUPS):
        kv_copy(block, p.b, p.sibling(), ks.at[block, 0]).wait_send()
        sib = p.chip * 2 + 1 - p.k
        kv_copy(block, sib, p.sibling(), ks.at[block, 0]).wait_recv()
        for d in range(1, p.chips):
            kv_copy(block, p.b, p.sibling(), ks.at[block, d]).wait_send()
            b = ((p.chip + d) % p.chips) * 2
            kv_copy(block, b + p.k, p.sibling(), fs.at[block, d]).wait_send()
            kv_copy(block, b + 1 - p.k, p.sibling(), fs.at[block, d]).wait_recv()
    for s in range(GROUPS):

        @pl.when((p.a - s >= 0) & (p.a < GROUPS - 1))
        def _():
            line_copy(p.a - s, p.a + 1, 2 * s).wait_send()

        @pl.when((p.a + s < GROUPS) & (p.a > 0))
        def _():
            line_copy(p.a + s, p.a - 1, 2 * s + 1).wait_send()

    for c in xo:
        c.wait()
    for c in local:
        c.wait()


def project(n, rp, gains, wg, wo):
    rows, width = rp.shape
    m = n // GROUPS
    lanes = wg.shape[2]
    sds = jax.ShapeDtypeStruct
    return pl.pallas_call(
        functools.partial(project_kernel, n),
        name="project",
        out_shape=(
            sds((GROUPS, rows, width), BF16),
            sds((GH, GROUPS * rows, 128), BF16),
            sds((n * rows, 384), BF16),
            sds((width, lanes), BF16),
            sds((GROUPS * 256, width), BF16),
            sds((2,) + gains.shape, F32),
        ),
        in_specs=[VM, VM, ANY, VM],
        out_specs=[VM] * 6,
        scratch_shapes=[
            DMA((6,)),
            DMA((6,)),
            DMA((5,)),
            DMA((2 * GROUPS,)),
            DMA((GROUPS,)),
            DMA((GROUPS, m // 2)),
            DMA((GROUPS, m)),
            DMA((GROUPS, m // 2)),
        ],
        compiler_params=pltpu.CompilerParams(
            collective_id=0, has_side_effects=True, vmem_limit_bytes=VLIM
        ),
    )(rp, gains, wg, wo)


def key_steps(z, keys):
    subs = keys // min(SUB, keys)
    return [(z, s) for s in range(subs)] + [(c, s) for c in range(z) for s in range(subs)]


def causal(shape, sub, size, first_query):
    col = lax.broadcasted_iota(jnp.int32, shape, 1) + sub * size
    row = lax.broadcasted_iota(jnp.int32, shape, 0) + first_query
    return col <= row


def attend_kernel(meta, q3, kv, att, o3, l3):
    rows = q3.shape[1] // GROUPS
    keys = kv.shape[0] // GROUPS
    size = min(SUB, keys)
    first_query = meta[0] * rows
    dead = jnp.where(meta[1] > keys, 0.0, MASKED).astype(F32)

    def head(h, carry):
        kt = pl.multiple_of(128 * (h // 2), 128)
        vt = pl.multiple_of(128 * (2 - h // 2 - (h + 1) % 2 * 0), 128)
        vt = pl.multiple_of(jnp.where(h == 2, 128, 256), 128)
        for z in range(GROUPS):
            q = q3[h, pl.ds(z * rows, rows), :]
            top = total = acc = None
            for c, s in key_steps(z, keys):
                at = pl.ds(c * keys + s * size, size)
                scores = dg(q, kv[at, pl.ds(kt, 128)], NT) * (SCALE * LOG2E)
                if c == z:
                    scores = jnp.where(
                        causal(scores.shape, s, size, first_query), scores, MASKED
                    )
                bias = dead if c > 0 else 0.0
                if c == z and c > 0:
                    bias = dead
                here = jnp.max(scores, axis=1, keepdims=True) + bias
                newest = here if top is None else jnp.maximum(top, here)
                weights = jnp.exp2(scores - (newest - bias))
                sums = jnp.sum(weights, axis=1, keepdims=True)
                part = dot(weights.astype(BF16), kv[at, pl.ds(vt, 128)])
                if top is None:
                    total, acc = sums, part
                else:
                    shrink = jnp.exp2(top - newest)
                    total = total * shrink + sums
                    acc = acc * shrink + part
                top = newest
            o3[h, pl.ds(z * rows, rows), :] = acc / total
            l3[h, pl.ds(z * rows, rows), :] = jnp.broadcast_to(top + jnp.log2(total), (rows, 128))
        return carry

    lax.fori_loop(0, GH, head, 0)
    for z in range(GROUPS):
        at = pl.ds(z * rows, rows)
        both = jnp.where(low_half((rows, 128)), o3[0, at, :], o3[1, at, :])
        att[z, 0:rows, :] = both.astype(BF16)
        att[z, rows : rows + rows // 2, :] = pack_tail(o3[2, at, :]).astype(BF16)


def attend(meta, q3, kv):
    sds = jax.ShapeDtypeStruct
    rows = q3.shape[1] // GROUPS
    return pl.pallas_call(
        attend_kernel,
        name="attend",
        out_shape=(
            sds((GROUPS, rows * 3 // 2, 128), BF16),
            sds(q3.shape, F32),
            sds(q3.shape, F32),
        ),
        in_specs=[SM, VM, VM],
        out_specs=[VM] * 3,
        compiler_params=pltpu.CompilerParams(vmem_limit_bytes=VLIM),
    )(meta, q3, kv)


def gelu_both(a):
    c = 0.7978845608028654
    a2 = a * a
    t = jnp.tanh(c * a * (1.0 + 0.044715 * a2))
    half = 0.5 * (1.0 + t)
    slope = half + 0.5 * a * (1.0 - t * t) * (c * (1.0 + 0.134145 * a2))
    return a * half, slope


def mlp_kernel(
    n, att, rp, cp, gfull, woa, wu, wd,
    out, gmid, gm, dog, dg2,
    attg, attp, wide, hid, gmb, act, gpre, osum, osend, orecv, esend, erecv, dsend, gbb, mid,
    ss, rs, ls, as_, ar, ds_, dr,
):
    p = Place(n)
    rows, width = rp.shape
    ff = wu.shape[1]
    pk = rows * 3 // 2
    ready = greet(p, xpeer=True, line=True)
    gmb[0] = cp[...]
    ready()

    def xc(i, src, dst):
        return rcopy(src, dst, ss.at[i], rs.at[i], p.xpeer())

    def ac(i, to):
        return rcopy(att.at[to], attg.at[i], as_.at[to], ar.at[i], p.on_line(to))

    def dc(i, to):
        return rcopy(dsend.at[to], dog.at[i], ds_.at[to], dr.at[i], p.on_line(to))

    for d in range(1, GROUPS):
        to = (p.a + d) % GROUPS
        ac(p.a, to).start()
    attg[p.a] = att[p.a]
    x_gm = xc(0, cp, gmb.at[1])
    x_gm.start()
    for d in range(1, GROUPS):
        fr = (p.a + d) % GROUPS
        ac(fr, fr).wait_recv()
    other = 1 - p.x
    x_att = [xc(1 + i, attg.at[other * 2 + i], attp.at[i]) for i in range(2)]
    for g in range(GROUPS):
        wide[:, g * 256 : g * 256 + 128] = attg[g, 0:rows, :]
        top, bottom = unpack_tail(attg[g, rows:pk, :])
        wide[0 : rows // 2, g * 256 + 128 : g * 256 + 256] = top
        wide[rows // 2 : rows, g * 256 + 128 : g * 256 + 256] = bottom
    mid[...] = rp[...].astype(F32) + dot(wide[...], woa[...])
    u = ext_of(mid[...])
    gain = jnp.concatenate([gfull[0, 1:2, :], gfull[1, 1:2, :]], axis=1)
    hid[0] = (u * inv_rms(u) * gain).astype(BF16)
    x_hid = xc(3, hid.at[0], hid.at[1])
    x_hid.start()
    for c in x_att:
        c.start()
    x_gm.wait()
    x_hid.wait()
    tiles = ff // 256

    def up(t, carry):
        at = pl.ds(pl.multiple_of(t * 256, 256), 256)
        for i in range(2):
            pre = dot(hid[i], wu[:, at])
            a, slope = gelu_both(pre)
            act[i, :, at] = a.astype(BF16)
            gpre[i, :, at] = (slope * dg(gmb[i], wd[at, :], NT)).astype(BF16)
        return carry

    lax.fori_loop(0, tiles, up, 0)
    esend[...] = dg(gpre[1], wu[...], NT).astype(BF16)
    x_e = xc(4, esend, erecv)
    x_e.start()
    osend[...] = dot(act[1], wd[...]).astype(BF16)
    x_o = xc(5, osend, orecv)
    x_o.start()
    e_own = dg(gpre[0], wu[...], NT)
    osum[...] = dot(act[0], wd[...])

    def grads(t, carry):
        at = pl.ds(pl.multiple_of(t * 256, 256), 256)
        g = dg(hid[0], gpre[0, :, at], TN) + dg(hid[1], gpre[1, :, at], TN)
        per = width // 256
        r0 = pl.multiple_of((t // per) * width, width)
        c0 = pl.multiple_of((t % per) * 256, 256)
        gm[pl.ds(r0, width), pl.ds(c0, 256)] = g.astype(BF16)
        g = dg(act[0, :, at], gmb[0], TN) + dg(act[1, :, at], gmb[1], TN)
        gm[pl.ds(pl.multiple_of(ff + t * 256, 256), 256), :] = g.astype(BF16)
        return carry

    lax.fori_loop(0, tiles, grads, 0)
    x_e.wait()
    e = e_own + erecv[...].astype(F32)
    u = ext_of(mid[...])
    inv = inv_rms(u)
    dg2[...] = jnp.broadcast_to(jnp.sum(e * (u * inv), axis=0, keepdims=True), dg2.shape)
    gmid[...] = cp[...].astype(F32) + crms_back(u, inv, gain, e)
    gbb[0] = gmid[...].astype(BF16)
    x_gb = xc(6, gbb.at[0], gbb.at[1])
    x_gb.start()
    for g in range(GROUPS):
        da = dg(gbb[0], woa[g * 256 : (g + 1) * 256, :], NT).astype(BF16)
        dsend[g, 0:rows, :] = da[:, 0:128]
        dsend[g, rows:pk, :] = pack_tail(da[:, 128:256])
    for d in range(1, GROUPS):
        dc(p.a, (p.a + d) % GROUPS).start()
    dog[p.a] = dsend[p.a]
    x_o.wait()
    final = mid[...] + osum[...] + orecv[...].astype(F32)
    out[...] = final[:, : width - 1].astype(BF16)
    for c in x_att:
        c.wait()
    x_gb.wait()
    for i in range(2):
        own_tail = jnp.concatenate(unpack_tail(attg[p.x * 2 + i, rows:pk, :]), axis=0)
        peer_tail = jnp.concatenate(unpack_tail(attp[i, rows:pk, :]), axis=0)
        g = dg(attg[p.x * 2 + i, 0:rows, :], gbb[0], TN) + dg(attp[i, 0:rows, :], gbb[1], TN)
        base = 2 * ff + i * 192
        gm[base : base + 128, :] = g.astype(BF16)
        g = dg(own_tail, gbb[0], TN) + dg(peer_tail, gbb[1], TN)
        gm[base + 128 : base + 192, :] = g[HD:, :].astype(BF16)
    for d in range(1, GROUPS):
        to = (p.a + d) % GROUPS
        ac(p.a, to).wait_send()
        dc(p.a, to).wait_send()
        dc(to, to).wait_recv()


def mlp(n, att, rp, cp, gfull, woa, wu, wd):
    rows, width = rp.shape
    ff = wu.shape[1]
    pk = rows * 3 // 2
    sds = jax.ShapeDtypeStruct
    v = pltpu.VMEM
    return pl.pallas_call(
        functools.partial(mlp_kernel, n),
        name="mlp",
        out_shape=(
            sds((rows, width - 1), BF16),
            sds((rows, width), F32),
            sds((2 * ff + width // 2, width), BF16),
            sds((GROUPS, pk, 128), BF16),
            sds((8, width), F32),
        ),
        in_specs=[VM] * 7,
        out_specs=[VM] * 5,
        scratch_shapes=[
            v((GROUPS, pk, 128), BF16),
            v((2, pk, 128), BF16),
            v((rows, GROUPS * 256), BF16),
            v((2, rows, width), BF16),
            v((2, rows, width), BF16),
            v((2, rows, ff), BF16),
            v((2, rows, ff), BF16),
            v((rows, width), F32),
            v((rows, width), BF16),
            v((rows, width), BF16),
            v((rows, width), BF16),
            v((rows, width), BF16),
            v((GROUPS, pk, 128), BF16),
            v((2, rows, width), BF16),
            v((rows, width), F32),
            DMA((8,)),
            DMA((8,)),
            DMA((2,)),
            DMA((GROUPS,)),
            DMA((GROUPS,)),
            DMA((GROUPS,)),
            DMA((GROUPS,)),
        ],
        compiler_params=pltpu.CompilerParams(
            collective_id=1, has_side_effects=True, vmem_limit_bytes=VLIM
        ),
    )(att, rp, cp, gfull, woa, wu, wd)


def attend_back_kernel(meta, q3, kv, o3, l3, dog, dqp, dkvb, do3, dkv):
    rows = q3.shape[1] // GROUPS
    keys = kv.shape[0] // GROUPS
    size = min(SUB, keys)
    first_query = meta[0] * rows
    dead = jnp.where(meta[1] > keys, 0.0, -MASKED).astype(F32)
    low = low_half((rows, 128))
    for z in range(GROUPS):
        at = pl.ds(z * rows, rows)
        both = dog[z, 0:rows, :]
        zero = jnp.zeros_like(both)
        do3[0, at, :] = jnp.where(low, both, zero)
        do3[1, at, :] = jnp.where(low, zero, both)
        top, bottom = unpack_tail(dog[z, rows:, :])
        do3[2, pl.ds(z * rows, rows // 2), :] = top
        do3[2, pl.ds(z * rows + rows // 2, rows // 2), :] = bottom
    dkv[...] = jnp.zeros_like(dkv)

    def head(h, carry):
        kt = pl.multiple_of(128 * (h // 2), 128)
        vt = pl.multiple_of(jnp.where(h == 2, 128, 256), 128)
        for z in range(GROUPS):
            at_q = pl.ds(z * rows, rows)
            q = q3[h, at_q, :]
            do = do3[h, at_q, :]
            lse = l3[h, at_q, 0:1]
            delta = jnp.sum(o3[h, at_q, :] * do.astype(F32), axis=1, keepdims=True)
            dq = jnp.zeros((rows, 128), F32)
            for c, s in key_steps(z, keys):
                at = pl.ds(c * keys + s * size, size)
                k = kv[at, pl.ds(kt, 128)]
                scores = dg(q, k, NT) * (SCALE * LOG2E)
                if c == z:
                    scores = jnp.where(
                        causal(scores.shape, s, size, first_query), scores, MASKED
                    )
                weights = jnp.exp2(scores - (lse + dead if c > 0 else lse))
                gp = dg(do, kv[at, pl.ds(vt, 128)], NT)
                gs = (weights * (gp - delta)).astype(BF16)
                dq = dq + dot(gs, k)
                dkv[at, pl.ds(vt, 128)] += dg(weights.astype(BF16), do, TN)
                dkv[at, pl.ds(kt, 128)] += dg(gs, q, TN) * SCALE
            dq = dq * SCALE

            @pl.when(h == 0)
            def _():
                dqp[at_q, 0:128] = dq.astype(BF16)

            @pl.when(h == 1)
            def _():
                dqp[at_q, 0:128] = jnp.where(low, dqp[at_q, 0:128], dq.astype(BF16))

            @pl.when(h == 2)
            def _():
                dqp[at_q, 128:256] = jnp.where(low, dq, 0.0).astype(BF16)

        return carry

    lax.fori_loop(0, GH, head, 0)
    dkvb[...] = dkv[...].astype(BF16)


def attend_back(meta, q3, kv, o3, l3, dog):
    sds = jax.ShapeDtypeStruct
    return pl.pallas_call(
        attend_back_kernel,
        name="attend_back",
        out_shape=(sds((q3.shape[1], 256), BF16), sds(kv.shape, BF16)),
        in_specs=[SM] + [VM] * 5,
        out_specs=[VM] * 2,
        scratch_shapes=[pltpu.VMEM(q3.shape, BF16), pltpu.VMEM(kv.shape, F32)],
        compiler_params=pltpu.CompilerParams(vmem_limit_bytes=VLIM),
    )(meta, q3, kv, o3, l3, dog)


def finish_kernel(
    n, dqp, dkvb, wg, h1, rp, gmid, gfull, dg2,
    gin, gq, gains,
    wfull, rk, sy, ry, gps, gpr, gqb, qk, q1, qx, q2, qy, g0, gk, gx, gy, ga,
    xs, xr, ls, ks, kr, ys, yr, zs, zr, qs, qr, ns, nr, bs, br, cs, cr,
):
    p = Place(n)
    rows, width = rp.shape
    half = width // 2
    quarter = width // 4
    ready = greet(p, xpeer=True, sibling=True, chips=True, line=True)
    at_x = pl.ds(pl.multiple_of(p.x * half, half), half)
    local = [
        pltpu.make_async_copy(wg.at[g], wfull.at[g, at_x], ls.at[g]) for g in range(GROUPS)
    ]
    for c in local:
        c.start()
    ready()
    wx = [
        rcopy(wg.at[g], wfull.at[g, at_x], xs.at[g], xr.at[g], p.xpeer()) for g in range(GROUPS)
    ]

    def block(ref, z, b):
        return ref.at[pl.ds(pl.multiple_of((z * p.m + b) * rows, rows), rows)]

    def kc(z, chip):
        return rcopy(
            block(dkvb, z, chip * 2 + 1 - p.k), rk.at[z, chip], ks.at[z, chip], kr.at[z, chip],
            p.sibling(),
        )

    def yc(z, chip, slot):
        return rcopy(sy.at[z, chip], ry.at[z, slot], ys.at[z, chip], yr.at[z, slot], p.on_chip(chip))

    def zc(slot, to):
        return rcopy(gps.at[to], gpr.at[slot], zs.at[to], zr.at[slot], p.on_line(to))

    order = [(p.a + d) % GROUPS for d in range(1, GROUPS)] + [p.a]
    for z in order:
        for d in range(1, p.chips):
            kc(z, (p.chip + d) % p.chips).start()
        kc(z, p.chip).start()
    for c in wx:
        c.start()
    for z in order:
        for d in range(1, p.chips):
            chip = (p.chip + d) % p.chips
            kc(z, chip).wait()
            mine = dkvb[pl.ds(pl.multiple_of((z * p.m + chip * 2 + p.k) * rows, rows), rows), :]
            sy[z, chip] = (mine.astype(F32) + rk[z, chip].astype(F32)).astype(BF16)
            yc(z, chip, p.chip).start()
    for i, z in enumerate(order):
        kc(z, p.chip).wait()
        mine = dkvb[pl.ds(pl.multiple_of((z * p.m + p.b) * rows, rows), rows), :]
        total = mine.astype(F32) + rk[z, p.chip].astype(F32)
        for d in range(1, p.chips):
            chip = (p.chip + d) % p.chips
            yc(z, chip, chip).wait_recv()
            total = total + ry[z, chip].astype(F32)
        gps[z, :, 0:256] = dqp[pl.ds(pl.multiple_of(z * rows, rows), rows), :]
        gps[z, :, 256:640] = total.astype(BF16)
        if i < GROUPS - 1:
            zc(p.a, z).start()
    gpr[p.a] = gps[p.a]

    def rowdot(z, carry):
        for t in range(width // 256):
            at = pl.ds(t * 256, 256)
            gqb[at, :] += dg(h1[z, :, at], gps[z], TN)
        return carry

    gqb[...] = jnp.zeros_like(gqb)
    lax.fori_loop(0, GROUPS, rowdot, 0)

    def part(i, core):
        return pl.ds(pl.multiple_of(i * half + core * quarter, quarter), quarter)

    for i in range(2):
        qk[0, i] = gqb[part(i, 1 - p.k), :].astype(BF16)
    q_k = rcopy(qk.at[0], qk.at[1], qs.at[0], qr.at[0], p.sibling())
    q_k.start()
    q_k.wait()
    for i in range(2):
        q1[i] = gqb[part(i, p.k), :] + qk[1, i].astype(F32)
    qx[0] = q1[1 - p.x].astype(BF16)
    q_x = rcopy(qx.at[0], qx.at[1], qs.at[1], qr.at[1], p.xpeer())
    q_x.start()
    q_x.wait()
    q2[...] = q1[p.x] + qx[1].astype(F32)
    qy[p.chip] = q2[...].astype(BF16)

    def qc(chip, slot):
        return rcopy(qy.at[p.chip], qy.at[slot], ns.at[chip], nr.at[slot], p.on_chip(chip))

    for d in range(1, p.chips):
        qc((p.chip + d) % p.chips, p.chip).start()
    total = q2[...]
    for d in range(1, p.chips):
        chip = (p.chip + d) % p.chips
        qc(chip, chip).wait_recv()
        total = total + qy[chip].astype(F32)
    gq[p.a, p.k] = total.astype(BF16)

    def bc(slot, to):
        return rcopy(gq.at[slot, p.k], gq.at[slot, p.k], bs.at[to], br.at[slot], p.on_line(to))

    def sc(slot, core):
        return rcopy(gq.at[slot, core], gq.at[slot, core], cs.at[slot], cr.at[slot], p.sibling())

    for d in range(1, GROUPS):
        bc(p.a, (p.a + d) % GROUPS).start()
    sc(p.a, p.k).start()
    for c in local:
        c.wait()
    for c in wx:
        c.wait()
    h = dg(gpr[p.a], wfull[p.a], NT)
    for d in range(1, GROUPS):
        g = (p.a + d) % GROUPS
        zc(g, g).wait_recv()
        h = h + dg(gpr[g], wfull[g], NT)
    u = ext_of(rp[...].astype(F32))
    inv = inv_rms(u)
    gain = jnp.concatenate([gfull[0, 0:1, :], gfull[1, 0:1, :]], axis=1)
    result = gmid[...] + crms_back(u, inv, gain, h)
    gin[...] = result[:, : width - 1]
    first = jnp.sum(h * (u * inv), axis=0, keepdims=True)
    which = lax.broadcasted_iota(jnp.int32, (8, width), 0)
    g0[...] = jnp.where(which == 0, first, dg2[...])
    g_k = rcopy(g0, gk, qs.at[2], qr.at[2], p.sibling())
    g_k.start()
    g_k.wait()
    g0[...] += gk[...]
    g_x = rcopy(g0, gx, qs.at[3], qr.at[3], p.xpeer())
    g_x.start()
    g_x.wait()
    gy[p.chip] = g0[...] + gx[...]

    def gc(chip, slot):
        return rcopy(gy.at[p.chip], gy.at[slot], ys.at[GROUPS, chip], yr.at[GROUPS, slot], p.on_chip(chip))

    for d in range(1, p.chips):
        gc((p.chip + d) % p.chips, p.chip).start()
    for d in range(1, p.chips):
        chip = (p.chip + d) % p.chips
        gc(chip, chip).wait_recv()
    total = gy[0]
    for chip in range(1, p.chips):
        total = total + gy[chip]
    ga[p.a] = total

    def lc(slot, to):
        return rcopy(ga.at[p.a], ga.at[slot], zs.at[GROUPS + to], zr.at[GROUPS + slot], p.on_line(to))

    for d in range(1, GROUPS):
        lc(p.a, (p.a + d) % GROUPS).start()
    for d in range(1, GROUPS):
        g = (p.a + d) % GROUPS
        lc(g, g).wait_recv()
    total = ga[0]
    for g in range(1, GROUPS):
        total = total + ga[g]
    gains[...] = total
    for d in range(1, GROUPS):
        g = (p.a + d) % GROUPS
        bc(g, g).wait_recv()
        sc(g, p.k).start()
    for g in range(GROUPS):
        sc(g, 1 - p.k).wait_recv()
        sc(g, p.k).wait_send()
    for d in range(1, p.chips):
        chip = (p.chip + d) % p.chips
        qc(chip, p.chip).wait_send()
        gc(chip, p.chip).wait_send()
        for z in range(GROUPS):
            yc(z, chip, p.chip).wait_send()
    for d in range(1, GROUPS):
        to = (p.a + d) % GROUPS
        zc(p.a, to).wait_send()
        bc(p.a, to).wait_send()
        lc(p.a, to).wait_send()


def finish(n, dqp, dkvb, wg, h1, rp, gmid, gfull, dg2):
    rows, width = rp.shape
    half = width // 2
    quarter = width // 4
    lanes = wg.shape[2]
    chips = n // GROUPS // 2
    sds = jax.ShapeDtypeStruct
    v = pltpu.VMEM
    return pl.pallas_call(
        functools.partial(finish_kernel, n),
        name="finish",
        out_shape=(
            sds((rows, width - 1), F32),
            sds((GROUPS, 2, quarter, lanes), BF16),
            sds((8, width), F32),
        ),
        in_specs=[VM, VM, ANY] + [VM] * 5,
        out_specs=[VM] * 3,
        scratch_shapes=[
            v((GROUPS, width, lanes), BF16),
            v((GROUPS, chips, rows, 384), BF16),
            v((GROUPS, chips, rows, 384), BF16),
            v((GROUPS, chips, rows, 384), BF16),
            v((GROUPS, rows, lanes), BF16),
            v((GROUPS, rows, lanes), BF16),
            v((width, lanes), F32),
            v((2, 2, quarter, lanes), BF16),
            v((2, quarter, lanes), F32),
            v((2, quarter, lanes), BF16),
            v((quarter, lanes), F32),
            v((chips, quarter, lanes), BF16),
            v((8, width), F32),
            v((8, width), F32),
            v((8, width), F32),
            v((chips, 8, width), F32),
            v((GROUPS, 8, width), F32),
            DMA((GROUPS,)),
            DMA((GROUPS,)),
            DMA((GROUPS,)),
            DMA((GROUPS, chips)),
            DMA((GROUPS, chips)),
            DMA((GROUPS + 1, chips)),
            DMA((GROUPS + 1, chips)),
            DMA((2 * GROUPS,)),
            DMA((2 * GROUPS,)),
            DMA((4,)),
            DMA((4,)),
            DMA((chips,)),
            DMA((chips,)),
            DMA((GROUPS,)),
            DMA((GROUPS,)),
            DMA((GROUPS,)),
            DMA((GROUPS,)),
        ],
        compiler_params=pltpu.CompilerParams(
            collective_id=2, has_side_effects=True, vmem_limit_bytes=VLIM
        ),
    )(dqp, dkvb, wg, h1, rp, gmid, gfull, dg2)


def sum_kernel(n, gm, res, rk, run, left, right, ry, ks, kr, zs, zr, ys, yr, as_, ar, cs, cr):
    p = Place(n)
    half = gm.shape[0] // 2
    piece = half // GROUPS
    ready = greet(p, sibling=True, chips=True, line=True)
    ready()

    def gm_at(core, z):
        return pl.ds(pl.multiple_of(core * half + z * piece, 16), piece)

    def kc(z):
        return rcopy(gm.at[gm_at(1 - p.k, z)], rk.at[z], ks.at[z], kr.at[z], p.sibling())

    for z in range(GROUPS):
        kc(z).start()
    for z in range(GROUPS):
        kc(z).wait()
        run[z] = (gm[gm_at(p.k, z), :].astype(F32) + rk[z].astype(F32)).astype(BF16)

    def rightward(z):
        return rcopy(run.at[z], left.at[z], zs.at[0, z], zr.at[0, z], p.on_line(p.a + 1))

    def leftward(z):
        return rcopy(run.at[z], right.at[z], zs.at[1, z], zr.at[1, z], p.on_line(p.a - 1))

    for s in range(GROUPS - 1, 0, -1):
        @pl.when(p.a + s < GROUPS)
        def _():
            @pl.when(p.a > 0)
            def _():
                rightward(p.a + s).wait_recv()
                run[p.a + s] = (run[p.a + s].astype(F32) + left[p.a + s].astype(F32)).astype(BF16)

            rightward(p.a + s).start()

        @pl.when(p.a - s >= 0)
        def _():
            @pl.when(p.a < GROUPS - 1)
            def _():
                leftward(p.a - s).wait_recv()
                run[p.a - s] = (run[p.a - s].astype(F32) + right[p.a - s].astype(F32)).astype(BF16)

            leftward(p.a - s).start()

    @pl.when(p.a > 0)
    def _():
        rightward(p.a).wait_recv()
        run[p.a] = (run[p.a].astype(F32) + left[p.a].astype(F32)).astype(BF16)

    @pl.when(p.a < GROUPS - 1)
    def _():
        leftward(p.a).wait_recv()
        run[p.a] = (run[p.a].astype(F32) + right[p.a].astype(F32)).astype(BF16)

    def yc(chip, slot):
        return rcopy(run.at[p.a], ry.at[slot], ys.at[chip], yr.at[slot], p.on_chip(chip))

    for d in range(1, p.chips):
        yc((p.chip + d) % p.chips, p.chip).start()
    ry[p.chip] = run[p.a]
    for d in range(1, p.chips):
        chip = (p.chip + d) % p.chips
        yc(chip, chip).wait_recv()
    total = ry[0].astype(F32)
    for chip in range(1, p.chips):
        total = total + ry[chip].astype(F32)
    res[gm_at(p.k, p.a), :] = total.astype(BF16)

    def ac(z, dst, sem):
        r = res.at[gm_at(p.k, z)]
        return rcopy(r, r, as_.at[sem], ar.at[z], p.on_line(dst))

    def sc(z, core):
        r = res.at[gm_at(core, z)]
        return rcopy(r, r, cs.at[z], cr.at[z], p.sibling())

    @pl.when(p.a < GROUPS - 1)
    def _():
        ac(p.a, p.a + 1, 0).start()

    @pl.when(p.a > 0)
    def _():
        ac(p.a, p.a - 1, 1).start()

    sc(p.a, p.k).start()
    for s in range(1, GROUPS):

        @pl.when(p.a - s >= 0)
        def _():
            ac(p.a - s, p.a, 0).wait_recv()

            @pl.when(p.a < GROUPS - 1)
            def _():
                ac(p.a - s, p.a + 1, 2 * s).start()

            sc(p.a - s, p.k).start()

        @pl.when(p.a + s < GROUPS)
        def _():
            ac(p.a + s, p.a, 0).wait_recv()

            @pl.when(p.a > 0)
            def _():
                ac(p.a + s, p.a - 1, 2 * s + 1).start()

            sc(p.a + s, p.k).start()

    for z in range(GROUPS):
        sc(z, 1 - p.k).wait_recv()
        sc(z, p.k).wait_send()
    for s in range(GROUPS):

        @pl.when((p.a - s >= 0) & (p.a < GROUPS - 1))
        def _():
            ac(p.a - s, p.a + 1, 2 * s).wait_send()

        @pl.when((p.a + s < GROUPS) & (p.a > 0))
        def _():
            ac(p.a + s, p.a - 1, 2 * s + 1).wait_send()

        if s > 0:

            @pl.when(p.a + s < GROUPS)
            def _():
                rightward(p.a + s).wait_send()

            @pl.when(p.a - s >= 0)
            def _():
                leftward(p.a - s).wait_send()

    for d in range(1, p.chips):
        yc((p.chip + d) % p.chips, p.chip).wait_send()


def sum_over_ctx(n, gm):
    chips = n // GROUPS // 2
    piece = gm.shape[0] // 2 // GROUPS
    width = gm.shape[1]
    v = pltpu.VMEM
    return pl.pallas_call(
        functools.partial(sum_kernel, n),
        name="sum_over_ctx",
        out_shape=jax.ShapeDtypeStruct(gm.shape, BF16),
        in_specs=[VM],
        out_specs=VM,
        scratch_shapes=[
            v((GROUPS, piece, width), BF16),
            v((GROUPS, piece, width), BF16),
            v((GROUPS, piece, width), BF16),
            v((GROUPS, piece, width), BF16),
            v((chips, piece, width), BF16),
            DMA((GROUPS,)),
            DMA((GROUPS,)),
            DMA((2, GROUPS)),
            DMA((2, GROUPS)),
            DMA((chips,)),
            DMA((chips,)),
            DMA((2 * GROUPS,)),
            DMA((GROUPS,)),
            DMA((GROUPS,)),
            DMA((GROUPS,)),
        ],
        compiler_params=pltpu.CompilerParams(
            collective_id=3, has_side_effects=True, vmem_limit_bytes=VLIM
        ),
    )(gm)


def by_group(w):
    r = w.shape[0]
    w = w.reshape(r, 3, GROUPS, GH, HD).transpose(2, 0, 1, 3, 4)
    q, k, v = w[:, :, 0], w[:, :, 1], w[:, :, 2]
    zero = jnp.zeros_like(q[:, :, 0])
    return jnp.concatenate(
        [q[:, :, 0], q[:, :, 1], q[:, :, 2], zero, k[:, :, 0], k[:, :, 1], k[:, :, 2], v[:, :, 2],
         v[:, :, 0], v[:, :, 1]],
        axis=-1,
    )


def from_groups(g):
    r = g.shape[1]
    t = g.reshape(GROUPS, r, 10, HD).transpose(1, 0, 2, 3)
    q = t[:, :, 0:3]
    k = t[:, :, 4:7]
    v = jnp.stack([t[:, :, 8], t[:, :, 9], t[:, :, 7]], axis=2)
    return jnp.stack([q, k, v], axis=1).reshape(r, 3 * GROUPS * GH * HD)


def shards(n, resid, lengths, gain_one, w_qkv, w_out, gain_two, w_up, w_down, cotangent):
    _, rows, narrow = resid.shape
    width = narrow + 1
    ff = w_up.shape[1]
    c = lax.axis_index("ctx")
    pos = c * rows + jnp.arange(rows, dtype=jnp.int32)
    pad = ((0, 0), (0, 1))
    rp = jnp.pad(resid[0], pad)
    live = pos[:, None] < lengths[0]
    cp = jnp.pad(jnp.where(live, cotangent[0], jnp.zeros_like(cotangent[0])), pad)
    wo = jnp.pad(w_out, pad)
    wd = jnp.pad(w_down, pad)
    gains = jnp.pad(jnp.stack([gain_one, gain_two]).astype(F32), ((0, 6), (0, 0)))
    wg = by_group(w_qkv)
    meta = jnp.stack([c % (n // GROUPS), lengths[0]]).astype(jnp.int32)

    h1, q3, kv, _, woa, gfull = project(n, rp, gains, wg, wo)
    att, o3, l3 = attend(meta, q3, kv)
    out, gmid, gm, dog, dg2 = mlp(n, att, rp, cp, gfull, woa, w_up, wd)
    dqp, dkvb = attend_back(meta, q3, kv, o3, l3, dog)
    gin, gq, gsum = finish(n, dqp, dkvb, wg, h1, rp, gmid, gfull, dg2)
    res = sum_over_ctx(n, gm)

    half = width // 2
    grad_qkv = from_groups(gq.reshape(GROUPS, half, -1).astype(F32))
    mine = lax.dynamic_slice_in_dim(gsum, lax.axis_index("fsdp") * half, half, 1)
    up = jnp.concatenate([res[:width], res[width : 2 * width]], axis=1).astype(F32)
    down = res[ff : 2 * ff, :narrow].astype(F32)
    gout = res[2 * ff :, :narrow].astype(F32)
    return out[None], gin[None], mine[0], grad_qkv, gout, mine[1], up, down


def solution(mesh):
    n = mesh.shape["ctx"]
    return jax.shard_map(
        functools.partial(shards, n),
        mesh=mesh,
        in_specs=(
            P("fsdp", "ctx", None),
            P("fsdp"),
            P("fsdp"),
            P("fsdp", None),
            P("fsdp", None),
            P("fsdp"),
            P(None, "fsdp"),
            P("fsdp", None),
            P("fsdp", "ctx", None),
        ),
        out_specs=(
            P("fsdp", "ctx", None),
            P("fsdp", "ctx", None),
            P("fsdp"),
            P("fsdp", None),
            P("fsdp", None),
            P("fsdp"),
            P(None, "fsdp"),
            P("fsdp", None),
        ),
        check_vma=False,
    )
```

```python
import functools

import jax
import jax.numpy as jnp
from jax import lax
from jax.experimental import pallas as pl
from jax.experimental.pallas import tpu as pltpu
from jax.sharding import PartitionSpec as P

F32 = jnp.float32
BF16 = jnp.bfloat16
MESH = pl.DeviceIdType.MESH
NT = (((1,), (1,)), ((), ()))
TN = (((0,), (0,)), ((), ()))
EPS = 1e-05
MASKED = -1e30
LOG2E = 1.4426950408889634
SCALE = 0.125
GROUPS = 4
GH = 3
HD = 64
SUB = 1024
VLIM = 60 * 1024 * 1024

VM = pl.BlockSpec(memory_space=pltpu.VMEM)
SM = pl.BlockSpec(memory_space=pltpu.SMEM)
ANY = pl.BlockSpec(memory_space=pl.ANY)
DMA = pltpu.SemaphoreType.DMA


def dot(a, b):
    return jnp.dot(a, b, preferred_element_type=F32)


def dg(a, b, dims):
    return lax.dot_general(a, b, dims, preferred_element_type=F32)


def rcopy(src, dst, send, recv, dev):
    return pltpu.make_async_remote_copy(
        src_ref=src, dst_ref=dst, send_sem=send, recv_sem=recv, device_id=dev, device_id_type=MESH
    )


class Place:
    def __init__(self, n):
        self.n = n
        self.m = n // GROUPS
        self.chips = self.m // 2
        c = lax.axis_index("ctx")
        self.x = lax.axis_index("fsdp")
        self.a = c // self.m
        self.b = c % self.m
        self.chip = self.b // 2
        self.k = self.b % 2

    def xpeer(self):
        return {"fsdp": 1 - self.x}

    def sibling(self):
        return {"ctx": self.a * self.m + self.chip * 2 + 1 - self.k}

    def on_chip(self, chip):
        return {"ctx": self.a * self.m + chip * 2 + self.k}

    def on_line(self, a):
        return {"ctx": a * self.m + self.b}


def greet(p, xpeer=False, sibling=False, chips=False, line=False):
    bar = pltpu.get_barrier_semaphore()
    count = 0
    if xpeer:
        pl.semaphore_signal(bar, inc=1, device_id=p.xpeer(), device_id_type=MESH)
        count += 1
    if sibling:
        pl.semaphore_signal(bar, inc=1, device_id=p.sibling(), device_id_type=MESH)
        count += 1
    if chips:
        for d in range(1, p.chips):
            pl.semaphore_signal(
                bar, inc=1, device_id=p.on_chip((p.chip + d) % p.chips), device_id_type=MESH
            )
            count += 1
    if line:
        for d in range(1, GROUPS):
            pl.semaphore_signal(
                bar, inc=1, device_id=p.on_line((p.a + d) % GROUPS), device_id_type=MESH
            )
            count += 1
    return lambda: pl.semaphore_wait(bar, count)


def ext_of(v):
    last = lax.broadcasted_iota(jnp.int32, v.shape, 1) == v.shape[1] - 1
    return jnp.where(last, -jnp.sum(v, axis=1, keepdims=True), v)


def inv_rms(u):
    return lax.rsqrt(jnp.mean(u * u, axis=1, keepdims=True) + EPS)


def crms_back(u, inv, gain, dy):
    dx = dy * gain
    du = inv * (dx - u * (inv * inv * jnp.mean(dx * u, axis=1, keepdims=True)))
    width = u.shape[1]
    last = lax.broadcasted_iota(jnp.int32, u.shape, 1) == width - 1
    return jnp.where(last, 0.0, du - du[:, width - 1 :])


def low_half(shape):
    return lax.broadcasted_iota(jnp.int32, shape, len(shape) - 1) < HD


def pack_tail(t):
    half = t.shape[0] // 2
    top, bottom = t[:half], t[half:]
    return jnp.where(low_half(top.shape), pltpu.roll(bottom, HD, 1), top)


def unpack_tail(t):
    low = low_half(t.shape)
    zero = jnp.zeros_like(t)
    return jnp.where(low, zero, t), jnp.where(low, zero, pltpu.roll(t, HD, 1))


def project_kernel(n, rp, gains, wg, wo, h1, q3, kv, wa, woa, gfull, ss, rs, ls, hs, hr, ks, kr, fs):
    p = Place(n)
    rows, width = rp.shape
    half = width // 2
    ready = greet(p, xpeer=True, sibling=True, chips=True, line=True)
    own = pltpu.make_async_copy(
        wg.at[p.a], wa.at[pl.ds(pl.multiple_of(p.x * half, half), half)], ls.at[0]
    )
    own.start()
    zero_rows = jnp.zeros((HD, width), BF16)
    for g in range(GROUPS):
        woa[pl.ds(g * 256 + 128, HD), :] = zero_rows
    local = []
    for i in range(2):
        g = p.x * 2 + i
        for j, (src, size, dst) in enumerate(((0, 128, 0), (128, 64, 192))):
            c = pltpu.make_async_copy(
                wo.at[pl.ds(i * 192 + src, size)],
                woa.at[pl.ds(pl.multiple_of(g * 256 + dst, 64), size)],
                ls.at[1 + 2 * i + j],
            )
            c.start()
            local.append(c)
    gfull[p.x] = gains[...]
    u = ext_of(rp[...].astype(F32))
    normed = u * inv_rms(u)
    ready()
    xg = rcopy(gains, gfull.at[p.x], ss.at[0], rs.at[0], p.xpeer())
    xg.start()
    xw = rcopy(
        wg.at[p.a],
        wa.at[pl.ds(pl.multiple_of(p.x * half, half), half)],
        ss.at[1],
        rs.at[1],
        p.xpeer(),
    )
    xw.start()
    xg.wait()
    gain = jnp.concatenate([gfull[0, 0:1, :], gfull[1, 0:1, :]], axis=1)
    h1[p.a] = (normed * gain).astype(BF16)

    def line_copy(block, dst, sem):
        return rcopy(h1.at[block], h1.at[block], hs.at[sem], hr.at[block], p.on_line(dst))

    def kv_rows(block, b):
        return kv.at[pl.ds(pl.multiple_of((block * p.m + b) * rows, rows), rows)]

    def kv_copy(block, b, dev, send):
        r = kv_rows(block, b)
        return rcopy(r, r, send, kr.at[block, b], dev)

    @pl.when(p.a < GROUPS - 1)
    def _():
        line_copy(p.a, p.a + 1, 0).start()

    @pl.when(p.a > 0)
    def _():
        line_copy(p.a, p.a - 1, 1).start()

    xo = []
    for i in range(2):
        g = p.x * 2 + i
        for j, (src, size, dst) in enumerate(((0, 128, 0), (128, 64, 192))):
            c = rcopy(
                wo.at[pl.ds(i * 192 + src, size)],
                woa.at[pl.ds(pl.multiple_of(g * 256 + dst, 64), size)],
                ss.at[2 + 2 * i + j],
                rs.at[2 + 2 * i + j],
                p.xpeer(),
            )
            c.start()
            xo.append(c)
    own.wait()
    xw.wait()

    def produce(block):
        y = dot(h1[block], wa[...]).astype(BF16)
        low = low_half((rows, 128))
        zero = jnp.zeros((rows, 128), BF16)
        at = pl.ds(pl.multiple_of(block * rows, rows), rows)
        q3[0, at, :] = jnp.where(low, y[:, :128], zero)
        q3[1, at, :] = jnp.where(low, zero, y[:, :128])
        q3[2, at, :] = y[:, 128:256]
        kv[pl.ds(pl.multiple_of((block * p.m + p.b) * rows, rows), rows), :] = y[:, 256:]
        for d in range(1, p.chips):
            kv_copy(block, p.b, p.on_chip((p.chip + d) % p.chips), ks.at[block, d]).start()
        kv_copy(block, p.b, p.sibling(), ks.at[block, 0]).start()

    def pass_on(block):
        for d in range(1, p.chips):
            b = ((p.chip + d) % p.chips) * 2 + p.k
            kv_copy(block, b, p.sibling(), fs.at[block, d]).wait_recv()
            kv_copy(block, b, p.sibling(), fs.at[block, d]).start()

    produce(p.a)
    for s in range(1, GROUPS):

        @pl.when(p.a - s >= 0)
        def _():
            line_copy(p.a - s, p.a, 0).wait_recv()

            @pl.when(p.a < GROUPS - 1)
            def _():
                line_copy(p.a - s, p.a + 1, 2 * s).start()

        @pl.when(p.a + s < GROUPS)
        def _():
            line_copy(p.a + s, p.a, 0).wait_recv()

            @pl.when(p.a > 0)
            def _():
                line_copy(p.a + s, p.a - 1, 2 * s + 1).start()

        @pl.when(p.a - s >= 0)
        def _():
            produce(p.a - s)

        @pl.when(p.a + s < GROUPS)
        def _():
            produce(p.a + s)

        @pl.when(p.a - s + 1 >= 0)
        def _():
            pass_on(p.a - s + 1)

        if s > 1:

            @pl.when(p.a + s - 1 < GROUPS)
            def _():
                pass_on(p.a + s - 1)

    @pl.when(p.a - GROUPS + 1 >= 0)
    def _():
        pass_on(p.a - GROUPS + 1)

    @pl.when(p.a + GROUPS - 1 < GROUPS)
    def _():
        pass_on(p.a + GROUPS - 1)

    for block in range(GROUPS):
        kv_copy(block, p.b, p.sibling(), ks.at[block, 0]).wait_send()
        sib = p.chip * 2 + 1 - p.k
        kv_copy(block, sib, p.sibling(), ks.at[block, 0]).wait_recv()
        for d in range(1, p.chips):
            kv_copy(block, p.b, p.sibling(), ks.at[block, d]).wait_send()
            b = ((p.chip + d) % p.chips) * 2
            kv_copy(block, b + p.k, p.sibling(), fs.at[block, d]).wait_send()
            kv_copy(block, b + 1 - p.k, p.sibling(), fs.at[block, d]).wait_recv()
    for s in range(GROUPS):

        @pl.when((p.a - s >= 0) & (p.a < GROUPS - 1))
        def _():
            line_copy(p.a - s, p.a + 1, 2 * s).wait_send()

        @pl.when((p.a + s < GROUPS) & (p.a > 0))
        def _():
            line_copy(p.a + s, p.a - 1, 2 * s + 1).wait_send()

    for c in xo:
        c.wait()
    for c in local:
        c.wait()


def project(n, rp, gains, wg, wo):
    rows, width = rp.shape
    m = n // GROUPS
    lanes = wg.shape[2]
    sds = jax.ShapeDtypeStruct
    return pl.pallas_call(
        functools.partial(project_kernel, n),
        name="project",
        out_shape=(
            sds((GROUPS, rows, width), BF16),
            sds((GH, GROUPS * rows, 128), BF16),
            sds((n * rows, 384), BF16),
            sds((width, lanes), BF16),
            sds((GROUPS * 256, width), BF16),
            sds((2,) + gains.shape, F32),
        ),
        in_specs=[VM, VM, ANY, VM],
        out_specs=[VM] * 6,
        scratch_shapes=[
            DMA((6,)),
            DMA((6,)),
            DMA((5,)),
            DMA((2 * GROUPS,)),
            DMA((GROUPS,)),
            DMA((GROUPS, m // 2)),
            DMA((GROUPS, m)),
            DMA((GROUPS, m // 2)),
        ],
        compiler_params=pltpu.CompilerParams(
            collective_id=0, has_side_effects=True, vmem_limit_bytes=VLIM
        ),
    )(rp, gains, wg, wo)


def key_steps(z, keys):
    subs = keys // min(SUB, keys)
    return [(z, s) for s in range(subs)] + [(c, s) for c in range(z) for s in range(subs)]


def causal(shape, sub, size, first_query):
    col = lax.broadcasted_iota(jnp.int32, shape, 1) + sub * size
    row = lax.broadcasted_iota(jnp.int32, shape, 0) + first_query
    return col <= row


def attend_kernel(meta, q3, kv, att, o3, l3):
    rows = q3.shape[1] // GROUPS
    keys = kv.shape[0] // GROUPS
    size = min(SUB, keys)
    first_query = meta[0] * rows
    dead = jnp.where(meta[1] > keys, 0.0, MASKED).astype(F32)

    def head(h, carry):
        kt = pl.multiple_of(128 * (h // 2), 128)
        vt = pl.multiple_of(128 * (2 - h // 2 - (h + 1) % 2 * 0), 128)
        vt = pl.multiple_of(jnp.where(h == 2, 128, 256), 128)
        for z in range(GROUPS):
            q = q3[h, pl.ds(z * rows, rows), :]
            top = total = acc = None
            for c, s in key_steps(z, keys):
                at = pl.ds(c * keys + s * size, size)
                scores = dg(q, kv[at, pl.ds(kt, 128)], NT) * (SCALE * LOG2E)
                if c == z:
                    scores = jnp.where(
                        causal(scores.shape, s, size, first_query), scores, MASKED
                    )
                bias = dead if c > 0 else 0.0
                if c == z and c > 0:
                    bias = dead
                here = jnp.max(scores, axis=1, keepdims=True) + bias
                newest = here if top is None else jnp.maximum(top, here)
                weights = jnp.exp2(scores - (newest - bias))
                sums = jnp.sum(weights, axis=1, keepdims=True)
                part = dot(weights.astype(BF16), kv[at, pl.ds(vt, 128)])
                if top is None:
                    total, acc = sums, part
                else:
                    shrink = jnp.exp2(top - newest)
                    total = total * shrink + sums
                    acc = acc * shrink + part
                top = newest
            o3[h, pl.ds(z * rows, rows), :] = acc / total
            l3[h, pl.ds(z * rows, rows), :] = jnp.broadcast_to(top + jnp.log2(total), (rows, 128))
        return carry

    lax.fori_loop(0, GH, head, 0)
    for z in range(GROUPS):
        at = pl.ds(z * rows, rows)
        both = jnp.where(low_half((rows, 128)), o3[0, at, :], o3[1, at, :])
        att[z, 0:rows, :] = both.astype(BF16)
        att[z, rows : rows + rows // 2, :] = pack_tail(o3[2, at, :]).astype(BF16)


def attend(meta, q3, kv):
    sds = jax.ShapeDtypeStruct
    rows = q3.shape[1] // GROUPS
    return pl.pallas_call(
        attend_kernel,
        name="attend",
        out_shape=(
            sds((GROUPS, rows * 3 // 2, 128), BF16),
            sds(q3.shape, F32),
            sds(q3.shape, F32),
        ),
        in_specs=[SM, VM, VM],
        out_specs=[VM] * 3,
        compiler_params=pltpu.CompilerParams(vmem_limit_bytes=VLIM),
    )(meta, q3, kv)


def gelu_both(a):
    c = 0.7978845608028654
    a2 = a * a
    t = jnp.tanh(c * a * (1.0 + 0.044715 * a2))
    half = 0.5 * (1.0 + t)
    slope = half + 0.5 * a * (1.0 - t * t) * (c * (1.0 + 0.134145 * a2))
    return a * half, slope


def mlp_kernel(
    n, att, rp, cp, gfull, woa, wu, wd,
    out, gmid, red, go, dog, dg2,
    attg, attp, wide, hid, gmb, act, gpre, osum, osend, orecv, esend, erecv, dsend, gbb, mid,
    gm, gk, ys_, yr_,
    ss, rs, as_, ar, ds_, dr, ks, kr, qs, qr,
):
    p = Place(n)
    rows, width = rp.shape
    ff = wu.shape[1]
    pk = rows * 3 // 2
    piece = red.shape[1]
    part = GROUPS * piece
    ready = greet(p, xpeer=True, sibling=True, chips=True, line=True)
    gmb[0] = cp[...]
    ready()

    def xc(i, src, dst):
        return rcopy(src, dst, ss.at[i], rs.at[i], p.xpeer())

    def ac(i, to):
        return rcopy(att.at[to], attg.at[i], as_.at[to], ar.at[i], p.on_line(to))

    def dc(i, to):
        return rcopy(dsend.at[to], dog.at[i], ds_.at[to], dr.at[i], p.on_line(to))

    def kc(chip):
        at = pl.ds(pl.multiple_of(chip * part, part), part)
        return rcopy(gm.at[1 - p.k, at], gk.at[at], ks.at[chip], kr.at[chip], p.sibling())

    def yc(chip, slot, z):
        return rcopy(ys_.at[chip, z], yr_.at[slot, z], qs.at[chip, z], qr.at[slot, z], p.on_chip(chip))

    for d in range(1, GROUPS):
        to = (p.a + d) % GROUPS
        ac(p.a, to).start()
    attg[p.a] = att[p.a]
    x_gm = xc(0, cp, gmb.at[1])
    x_gm.start()
    for d in range(1, GROUPS):
        fr = (p.a + d) % GROUPS
        ac(fr, fr).wait_recv()
    other = 1 - p.x
    x_att = [xc(1 + i, attg.at[other * 2 + i], attp.at[i]) for i in range(2)]
    for g in range(GROUPS):
        wide[:, g * 256 : g * 256 + 128] = attg[g, 0:rows, :]
        top, bottom = unpack_tail(attg[g, rows:pk, :])
        wide[0 : rows // 2, g * 256 + 128 : g * 256 + 256] = top
        wide[rows // 2 : rows, g * 256 + 128 : g * 256 + 256] = bottom
    mid[...] = rp[...].astype(F32) + dot(wide[...], woa[...])
    u = ext_of(mid[...])
    gain = jnp.concatenate([gfull[0, 1:2, :], gfull[1, 1:2, :]], axis=1)
    hid[0] = (u * inv_rms(u) * gain).astype(BF16)
    x_hid = xc(3, hid.at[0], hid.at[1])
    x_hid.start()
    for c in x_att:
        c.start()
    tiles = ff // 256

    def up(i):
        def tile(t, carry):
            at = pl.ds(pl.multiple_of(t * 256, 256), 256)
            a, slope = gelu_both(dot(hid[i], wu[:, at]))
            act[i, :, at] = a.astype(BF16)
            gpre[i, :, at] = (slope * dg(gmb[i], wd[at, :], NT)).astype(BF16)
            return carry

        lax.fori_loop(0, tiles, tile, 0)

    up(0)
    x_gm.wait()
    x_hid.wait()
    up(1)
    esend[...] = dg(gpre[1], wu[...], NT).astype(BF16)
    x_e = xc(4, esend, erecv)
    x_e.start()

    def grad_up(t, carry):
        at = pl.ds(pl.multiple_of(t * 256, 256), 256)
        g = dg(hid[0], gpre[0, :, at], TN) + dg(hid[1], gpre[1, :, at], TN)
        per = width // 256
        r0 = pl.multiple_of((t // per) * width, width)
        c0 = pl.multiple_of((t % per) * 256, 256)
        gm[0, pl.ds(r0, width), pl.ds(c0, 256)] = g.astype(BF16)
        return carry

    def grad_down(t, carry):
        at = pl.ds(pl.multiple_of(t * 256, 256), 256)
        g = dg(act[0, :, at], gmb[0], TN) + dg(act[1, :, at], gmb[1], TN)
        gm[1, at, :] = g.astype(BF16)
        return carry

    @pl.when(p.k == 0)
    def _():
        lax.fori_loop(0, tiles, grad_down, 0)

    @pl.when(p.k == 1)
    def _():
        lax.fori_loop(0, tiles, grad_up, 0)

    for d in range(1, p.chips):
        kc((p.chip + d) % p.chips).start()
    kc(p.chip).start()

    @pl.when(p.k == 0)
    def _():
        lax.fori_loop(0, tiles, grad_up, 0)

    @pl.when(p.k == 1)
    def _():
        lax.fori_loop(0, tiles, grad_down, 0)

    for d in range(1, p.chips):
        chip = (p.chip + d) % p.chips
        kc(chip).wait()
        for z in range(GROUPS):
            at = pl.ds(pl.multiple_of(chip * part + z * piece, 16), piece)
            ys_[chip, z] = (gm[p.k, at, :].astype(F32) + gk[at, :].astype(F32)).astype(BF16)
            yc(chip, p.chip, z).start()
    osend[...] = dot(act[1], wd[...]).astype(BF16)
    e_own = dg(gpre[0], wu[...], NT)
    x_e.wait()
    x_o = xc(5, osend, orecv)
    x_o.start()
    e = e_own + erecv[...].astype(F32)
    u = ext_of(mid[...])
    inv = inv_rms(u)
    gmid[...] = cp[...].astype(F32) + crms_back(u, inv, gain, e)
    gbb[0] = gmid[...].astype(BF16)
    x_gb = xc(6, gbb.at[0], gbb.at[1])
    x_gb.start()
    for d in range(1, GROUPS + 1):
        to = (p.a + d) % GROUPS
        w = woa[pl.ds(pl.multiple_of(to * 256, 256), 256), :]
        da = dg(gbb[0], w, NT).astype(BF16)
        if d < GROUPS:
            dsend[to, 0:rows, :] = da[:, 0:128]
            dsend[to, rows:pk, :] = pack_tail(da[:, 128:256])
            dc(p.a, to).start()
        else:
            dog[to, 0:rows, :] = da[:, 0:128]
            dog[to, rows:pk, :] = pack_tail(da[:, 128:256])
    dg2[...] = jnp.broadcast_to(jnp.sum(e * (u * inv), axis=0, keepdims=True), dg2.shape)
    osum[...] = mid[...] + dot(act[0], wd[...])
    for c in x_att:
        c.wait()
    x_o.wait()
    final = osum[...] + orecv[...].astype(F32)
    out[...] = final[:, : width - 1].astype(BF16)
    x_gb.wait()
    for i in range(2):
        own_tail = jnp.concatenate(unpack_tail(attg[p.x * 2 + i, rows:pk, :]), axis=0)
        peer_tail = jnp.concatenate(unpack_tail(attp[i, rows:pk, :]), axis=0)
        g = dg(attg[p.x * 2 + i, 0:rows, :], gbb[0], TN) + dg(attp[i, 0:rows, :], gbb[1], TN)
        go[i * 192 : i * 192 + 128, :] = g.astype(BF16)
        g = dg(own_tail, gbb[0], TN) + dg(peer_tail, gbb[1], TN)
        go[i * 192 + 128 : i * 192 + 192, :] = g[HD:, :].astype(BF16)
    kc(p.chip).wait()
    for z in range(GROUPS):
        at = pl.ds(pl.multiple_of(p.chip * part + z * piece, 16), piece)
        total = gm[p.k, at, :].astype(F32) + gk[at, :].astype(F32)
        for d in range(1, p.chips):
            chip = (p.chip + d) % p.chips
            yc(chip, chip, z).wait_recv()
            total = total + yr_[chip, z].astype(F32)
        red[z] = total.astype(BF16)
    for d in range(1, GROUPS):
        to = (p.a + d) % GROUPS
        ac(p.a, to).wait_send()
        dc(p.a, to).wait_send()
        dc(to, to).wait_recv()
    for d in range(1, p.chips):
        for z in range(GROUPS):
            yc((p.chip + d) % p.chips, p.chip, z).wait_send()


def mlp(n, att, rp, cp, gfull, woa, wu, wd):
    rows, width = rp.shape
    ff = wu.shape[1]
    pk = rows * 3 // 2
    chips = n // GROUPS // 2
    piece = ff // GROUPS // chips
    sds = jax.ShapeDtypeStruct
    v = pltpu.VMEM
    return pl.pallas_call(
        functools.partial(mlp_kernel, n),
        name="mlp",
        out_shape=(
            sds((rows, width - 1), BF16),
            sds((rows, width), F32),
            sds((GROUPS, piece, width), BF16),
            sds((width // 2, width), BF16),
            sds((GROUPS, pk, 128), BF16),
            sds((8, width), F32),
        ),
        in_specs=[VM] * 7,
        out_specs=[VM] * 6,
        scratch_shapes=[
            v((GROUPS, pk, 128), BF16),
            v((2, pk, 128), BF16),
            v((rows, GROUPS * 256), BF16),
            v((2, rows, width), BF16),
            v((2, rows, width), BF16),
            v((2, rows, ff), BF16),
            v((2, rows, ff), BF16),
            v((rows, width), F32),
            v((rows, width), BF16),
            v((rows, width), BF16),
            v((rows, width), BF16),
            v((rows, width), BF16),
            v((GROUPS, pk, 128), BF16),
            v((2, rows, width), BF16),
            v((rows, width), F32),
            v((2, ff, width), BF16),
            v((ff, width), BF16),
            v((chips, GROUPS, piece, width), BF16),
            v((chips, GROUPS, piece, width), BF16),
            DMA((8,)),
            DMA((8,)),
            DMA((GROUPS,)),
            DMA((GROUPS,)),
            DMA((GROUPS,)),
            DMA((GROUPS,)),
            DMA((chips,)),
            DMA((chips,)),
            DMA((chips, GROUPS)),
            DMA((chips, GROUPS)),
        ],
        compiler_params=pltpu.CompilerParams(
            collective_id=1, has_side_effects=True, vmem_limit_bytes=VLIM
        ),
    )(att, rp, cp, gfull, woa, wu, wd)


def back_kernel(
    n, lens, q3, kv, o3, l3, dog, wg, h1, rp, gmid, gfull, dg2, red, go,
    gin, gq, gains, res, goo,
    do3, dq3, kvc, dkv, dkvb, rk, ry, wfull, gps, gpr, gqb, qk, qx, qy,
    g0, gk, gx, gy, ga, left, right, sumr, suml, ok, os_, oy, oz, ozr,
    xs, xr, ls, vs, ks, kr, ys, yr, zs, zr, ws, wr, qs, qr, ns, nr, bs, br, cs, cr,
    rs_, rr, ls_, lr, as_, ar, es, er, fs, fr, ts, tr, us, ur, is_, ir,
):
    p = Place(n)
    rows, width = rp.shape
    half = width // 2
    quarter = width // 4
    last = GROUPS - 1
    keys = dkv.shape[0]
    size = min(SUB, keys)
    subs = keys // size
    slots = kvc.shape[0]
    others = [(p.chip + d) % p.chips for d in range(1, p.chips)]
    line = [(p.a + d) % GROUPS for d in range(1, GROUPS)]
    ready = greet(p, xpeer=True, sibling=True, chips=True, line=True)
    at_x = pl.ds(pl.multiple_of(p.x * half, half), half)
    local = [
        pltpu.make_async_copy(wg.at[g], wfull.at[g, at_x], ls.at[g]) for g in range(GROUPS)
    ]

    def chunk_of(i):
        return (p.a + 1 + i) % GROUPS

    def fetch(i):
        c = chunk_of(i)
        src = kv.at[pl.ds(pl.multiple_of(c * keys, keys), keys)]
        return pltpu.make_async_copy(src, kvc.at[i % slots], vs.at[i % slots])

    fetch(0).start()
    for c in local:
        c.start()
    wx = [
        rcopy(wg.at[g], wfull.at[g, at_x], xs.at[g], xr.at[g], p.xpeer()) for g in range(GROUPS)
    ]

    def rightward(z, src):
        return rcopy(src, left.at[z], rs_.at[z], rr.at[z], p.on_line(p.a + 1))

    def leftward(z, src):
        return rcopy(src, right.at[z], ls_.at[z], lr.at[z], p.on_line(p.a - 1))

    def reduce_step(s):
        @pl.when((p.a >= 1) & (p.a <= s))
        def _():
            z = last + p.a - s
            rightward(z, sumr.at[z]).wait_recv()
            if s < last:
                sumr[z] = (red[z].astype(F32) + left[z].astype(F32)).astype(BF16)
                rightward(z, sumr.at[z]).start()

        b = last - p.a

        @pl.when((b >= 1) & (b <= s))
        def _():
            z = s - b
            leftward(z, suml.at[z]).wait_recv()
            if s < last:
                suml[z] = (red[z].astype(F32) + right[z].astype(F32)).astype(BF16)
                leftward(z, suml.at[z]).start()

    def line_share(z, dst, sem):
        r = res.at[p.k, p.chip, z]
        return rcopy(r, r, as_.at[sem], ar.at[z], p.on_line(dst))

    def chip_share(chip, z, dst):
        r = res.at[p.k, chip, z]
        return rcopy(r, r, es.at[dst, z], er.at[chip, z], p.on_chip(dst))

    def core_share(core, chip, z):
        r = res.at[core, chip, z]
        return rcopy(r, r, fs.at[chip, z], fr.at[chip, z], p.sibling())

    def spread(z):
        for c in others:
            chip_share(p.chip, z, c).start()
        core_share(p.k, p.chip, z).start()

    def gather_first():
        z = p.a
        res[p.k, p.chip, z] = red[z]

        @pl.when(p.a > 0)
        def _():
            cur = res[p.k, p.chip, z].astype(F32)
            res[p.k, p.chip, z] = (cur + left[z].astype(F32)).astype(BF16)

        @pl.when(p.a < last)
        def _():
            cur = res[p.k, p.chip, z].astype(F32)
            res[p.k, p.chip, z] = (cur + right[z].astype(F32)).astype(BF16)
            line_share(z, p.a + 1, 0).start()

        @pl.when(p.a > 0)
        def _():
            line_share(z, p.a - 1, 1).start()

        spread(z)

    def gather_step(s):
        @pl.when(p.a - s >= 0)
        def _():
            line_share(p.a - s, p.a, 0).wait_recv()

            @pl.when(p.a < last)
            def _():
                line_share(p.a - s, p.a + 1, 2 * s).start()

            spread(p.a - s)

        @pl.when(p.a + s <= last)
        def _():
            line_share(p.a + s, p.a, 0).wait_recv()

            @pl.when(p.a > 0)
            def _():
                line_share(p.a + s, p.a - 1, 2 * s + 1).start()

            spread(p.a + s)

    def pass_on(z):
        for c in others:
            chip_share(c, z, c).wait_recv()
            core_share(p.k, c, z).start()

    orow = go.shape[0] // 2
    opart = orow // GROUPS

    def out_core():
        at = pl.ds(pl.multiple_of((1 - p.k) * orow, orow), orow)
        return rcopy(go.at[at], ok, is_.at[0], ir.at[0], p.sibling())

    def out_chip(chip, slot):
        return rcopy(os_, oy.at[slot], ts.at[chip], tr.at[slot], p.on_chip(chip))

    def out_line(slot, to):
        return rcopy(oz.at[to], ozr.at[slot], us.at[to], ur.at[slot], p.on_line(to))

    def out_back(slot, to):
        r = goo.at[p.k, slot]
        return rcopy(r, r, us.at[GROUPS + to], ur.at[GROUPS + slot], p.on_line(to))

    def out_share(core, z):
        r = goo.at[core, z]
        return rcopy(r, r, is_.at[1 + z], ir.at[1 + z], p.sibling())

    def out_1():
        out_core().wait()
        at = pl.ds(pl.multiple_of(p.k * orow, orow), orow)
        os_[...] = (go[at, :].astype(F32) + ok[...].astype(F32)).astype(BF16)
        for c in others:
            out_chip(c, p.chip).start()

    def out_2():
        total = os_[...].astype(F32)
        for c in others:
            out_chip(c, c).wait_recv()
            total = total + oy[c].astype(F32)
        for z in range(GROUPS):
            oz[z] = total[z * opart : (z + 1) * opart].astype(BF16)
        for z in line:
            out_line(p.a, z).start()

    def out_3():
        total = oz[p.a].astype(F32)
        for z in line:
            out_line(z, z).wait_recv()
            total = total + ozr[z].astype(F32)
        goo[p.k, p.a] = total.astype(BF16)
        for z in line:
            out_back(p.a, z).start()
        out_share(p.k, p.a).start()

    def kc(i, chip):
        c = chunk_of(i)
        at = pl.ds(pl.multiple_of((chip * 2 + 1 - p.k) * rows, rows), rows)
        return rcopy(
            dkvb.at[at], rk.at[c, chip], ks.at[c, chip], kr.at[c, chip], p.sibling()
        )

    def yc(c, chip, slot):
        return rcopy(rk.at[c, chip], ry.at[c, slot], ys.at[c, chip], yr.at[c, slot], p.on_chip(chip))

    def zkv(slot, to):
        lanes = pl.ds(256, 384)
        return rcopy(
            gps.at[to, :, lanes], gpr.at[slot, :, lanes], zs.at[to], zr.at[slot], p.on_line(to)
        )

    def zq(slot, to):
        lanes = pl.ds(0, 256)
        return rcopy(
            gps.at[to, :, lanes], gpr.at[slot, :, lanes], ws.at[to], wr.at[slot], p.on_line(to)
        )

    def mine(chip):
        at = pl.ds(pl.multiple_of((chip * 2 + p.k) * rows, rows), rows)
        return dkvb[at, :].astype(F32)

    def kv_1(i):
        dkvb[...] = dkv[...].astype(BF16)
        for c in others:
            kc(i, c).start()
        kc(i, p.chip).start()

    def kv_2(i):
        c = chunk_of(i)
        for chip in others:
            kc(i, chip).wait()
            rk[c, chip] = (mine(chip) + rk[c, chip].astype(F32)).astype(BF16)
            yc(c, chip, p.chip).start()
        kc(i, p.chip).wait()
        rk[c, p.chip] = (mine(p.chip) + rk[c, p.chip].astype(F32)).astype(BF16)

    def kv_3(i, send):
        c = chunk_of(i)
        total = rk[c, p.chip].astype(F32)
        for chip in others:
            yc(c, chip, chip).wait_recv()
            total = total + ry[c, chip].astype(F32)
        gps[c, :, 256:640] = total.astype(BF16)
        if send:
            zkv(p.a, c).start()

    ready()
    out_core().start()

    @pl.when(p.a == 0)
    def _():
        for z in range(last, 0, -1):
            rightward(z, red.at[z]).start()

    @pl.when(p.a == last)
    def _():
        for z in range(last):
            leftward(z, red.at[z]).start()

    for c in wx:
        c.start()

    first_query = p.b * rows
    low = low_half((rows, 128))
    for z in range(GROUPS):
        at = pl.ds(z * rows, rows)
        both = dog[z, 0:rows, :]
        zero = jnp.zeros_like(both)
        do3[0, at, :] = jnp.where(low, both, zero)
        do3[1, at, :] = jnp.where(low, zero, both)
        top, bottom = unpack_tail(dog[z, rows:, :])
        do3[2, pl.ds(z * rows, rows // 2), :] = top
        do3[2, pl.ds(z * rows + rows // 2, rows // 2), :] = bottom
        for h in range(GH):
            delta = jnp.sum(o3[h, at, :] * do3[h, at, :].astype(F32), axis=1, keepdims=True)
            gqb[h * rows : (h + 1) * rows, z * 128 : (z + 1) * 128] = jnp.broadcast_to(delta, (rows, 128))
    dq3[...] = jnp.zeros_like(dq3)
    gone = jnp.where(lens[0] > keys, 0.0, -MASKED).astype(F32)

    def chunk(i, carry):
        c = chunk_of(i)
        fetch(i).wait()

        if slots > 1:

            @pl.when(i < last)
            def _():
                fetch(i + 1).start()

        dead = jnp.where(c > 0, gone, 0.0)

        def head(h, carry):
            kt = pl.multiple_of(128 * (h // 2), 128)
            vt = pl.multiple_of(jnp.where(h == 2, 128, 256), 128)

            def step(z, masked):
                at_q = pl.ds(pl.multiple_of(z * rows, rows), rows)
                q = q3[h, at_q, :]
                do = do3[h, at_q, :]
                lse = l3[h, at_q, 0:1] + dead
                delta = gqb[
                    pl.ds(pl.multiple_of(h * rows, rows), rows),
                    pl.ds(pl.multiple_of(z * 128, 128), 128),
                ][:, 0:1]
                for sub in range(subs):
                    at = pl.ds(sub * size, size)
                    k = kvc[i % slots, at, pl.ds(kt, 128)]
                    v = kvc[i % slots, at, pl.ds(vt, 128)]
                    scores = dg(q, k, NT) * (SCALE * LOG2E)
                    if masked:
                        scores = jnp.where(
                            causal(scores.shape, sub, size, first_query), scores, MASKED
                        )
                    weights = jnp.exp2(scores - lse)
                    gp = dg(do, v, NT)
                    gs = (weights * (gp - delta)).astype(BF16)
                    dq3[h, at_q, :] += dot(gs, k)
                    gv = dg(weights.astype(BF16), do, TN)
                    gk_ = dg(gs, q, TN) * SCALE
                    if masked:
                        dkv[at, pl.ds(kt, 128)] = jnp.where(h == 1, dkv[at, pl.ds(kt, 128)], 0.0) + gk_
                        dkv[at, pl.ds(vt, 128)] = jnp.where(h == 0, 0.0, dkv[at, pl.ds(vt, 128)]) + gv
                    else:
                        dkv[at, pl.ds(kt, 128)] += gk_
                        dkv[at, pl.ds(vt, 128)] += gv

            step(c, True)

            def rest(z, carry):
                step(z, False)
                return carry

            lax.fori_loop(c + 1, GROUPS, rest, 0)

            @pl.when(h == 0)
            def _():
                @pl.when(i >= 1)
                def _():
                    kv_2(i - 1)

            @pl.when(h == 1)
            def _():
                @pl.when(i >= 2)
                def _():
                    kv_3(i - 2, True)

                @pl.when(i == 2)
                def _():
                    reduce_step(2)

                @pl.when(i == 3)
                def _():
                    reduce_step(3)
                    gather_first()

            @pl.when(h == 2)
            def _():
                @pl.when(i == 0)
                def _():
                    out_1()

                @pl.when(i == 1)
                def _():
                    reduce_step(1)
                    out_2()

                @pl.when(i == 2)
                def _():
                    out_3()

            return carry

        lax.fori_loop(0, GH, head, 0)
        if slots == 1:

            @pl.when(i < last)
            def _():
                fetch(i + 1).start()

        kv_1(i)
        return carry

    lax.fori_loop(0, GROUPS, chunk, 0)
    kv_3(2, True)
    for d in range(1, GROUPS + 1):
        z = (p.a + d) % GROUPS
        at = pl.ds(pl.multiple_of(z * rows, rows), rows)
        gps[z, :, 0:128] = (jnp.where(low, dq3[0, at, :], dq3[1, at, :]) * SCALE).astype(BF16)
        gps[z, :, 128:256] = (jnp.where(low, dq3[2, at, :], 0.0) * SCALE).astype(BF16)
        if d < GROUPS:
            zq(p.a, z).start()
    kv_2(3)
    gather_step(1)
    kv_3(3, False)
    gpr[p.a] = gps[p.a]

    gqb[...] = jnp.zeros_like(gqb)

    def rowdot(z, carry):
        for t in range(width // 256):
            at = pl.ds(t * 256, 256)
            gqb[at, :] += dg(h1[z, :, at], gps[z], TN)
        return carry

    lax.fori_loop(0, GROUPS, rowdot, 0)

    def rows_of(i, core):
        return pl.ds(pl.multiple_of(i * half + core * quarter, quarter), quarter)

    for i in range(2):
        qk[0, i] = gqb[rows_of(i, 1 - p.k), :].astype(BF16)
    q_k = rcopy(qk.at[0], qk.at[1], qs.at[0], qr.at[0], p.sibling())
    q_k.start()
    for c in local:
        c.wait()
    q_k.wait()
    for i in range(2):
        gqb[rows_of(i, p.k), :] += qk[1, i].astype(F32)
    qx[0] = gqb[rows_of(1 - p.x, p.k), :].astype(BF16)
    q_x = rcopy(qx.at[0], qx.at[1], qs.at[1], qr.at[1], p.xpeer())
    q_x.start()
    gather_step(2)
    q_x.wait()
    gqb[rows_of(p.x, p.k), :] += qx[1].astype(F32)
    qy[p.chip] = gqb[rows_of(p.x, p.k), :].astype(BF16)

    def qc(chip, slot):
        return rcopy(qy.at[p.chip], qy.at[slot], ns.at[chip], nr.at[slot], p.on_chip(chip))

    for c in others:
        qc(c, p.chip).start()
    for c in wx:
        c.wait()
    h = dg(gpr[p.a], wfull[p.a], NT)
    for g in line:
        zkv(g, g).wait_recv()
        zq(g, g).wait_recv()
        h = h + dg(gpr[g], wfull[g], NT)
    total = gqb[rows_of(p.x, p.k), :]
    for c in others:
        qc(c, c).wait_recv()
        total = total + qy[c].astype(F32)
    gq[p.a, p.k] = total.astype(BF16)

    def bc(slot, to, sem):
        r = gq.at[slot, p.k]
        return rcopy(r, r, bs.at[sem], br.at[slot], p.on_line(to))

    def sc(slot, core):
        return rcopy(gq.at[slot, core], gq.at[slot, core], cs.at[slot], cr.at[slot], p.sibling())

    @pl.when(p.a < last)
    def _():
        bc(p.a, p.a + 1, 0).start()

    @pl.when(p.a > 0)
    def _():
        bc(p.a, p.a - 1, 1).start()

    sc(p.a, p.k).start()
    u = ext_of(rp[...].astype(F32))
    inv = inv_rms(u)
    gain = jnp.concatenate([gfull[0, 0:1, :], gfull[1, 0:1, :]], axis=1)
    result = gmid[...] + crms_back(u, inv, gain, h)
    gin[...] = result[:, : width - 1]
    first = jnp.sum(h * (u * inv), axis=0, keepdims=True)
    which = lax.broadcasted_iota(jnp.int32, (8, width), 0)
    g0[...] = jnp.where(which == 0, first, dg2[...])
    g_k = rcopy(g0, gk, qs.at[2], qr.at[2], p.sibling())
    g_k.start()
    gather_step(3)
    for z in range(GROUPS):
        pass_on(z)
    g_k.wait()
    g0[...] += gk[...]
    g_x = rcopy(g0, gx, qs.at[3], qr.at[3], p.xpeer())
    g_x.start()
    for s in range(1, GROUPS):

        @pl.when(p.a - s >= 0)
        def _():
            bc(p.a - s, p.a, 0).wait_recv()

            @pl.when(p.a < last)
            def _():
                bc(p.a - s, p.a + 1, 2 * s).start()

            sc(p.a - s, p.k).start()

        @pl.when(p.a + s <= last)
        def _():
            bc(p.a + s, p.a, 0).wait_recv()

            @pl.when(p.a > 0)
            def _():
                bc(p.a + s, p.a - 1, 2 * s + 1).start()

            sc(p.a + s, p.k).start()

        if s == 1:
            g_x.wait()
            gy[p.chip] = g0[...] + gx[...]

            def gc(chip, slot):
                return rcopy(
                    gy.at[p.chip], gy.at[slot], ys.at[GROUPS, chip], yr.at[GROUPS, slot],
                    p.on_chip(chip),
                )

            for c in others:
                gc(c, p.chip).start()
        if s == 2:
            for c in others:
                gc(c, c).wait_recv()
            total = gy[0]
            for c in range(1, p.chips):
                total = total + gy[c]
            ga[p.a] = total

            def lc(slot, to):
                return rcopy(
                    ga.at[p.a], ga.at[slot], zs.at[GROUPS + to], zr.at[GROUPS + slot], p.on_line(to)
                )

            for g in line:
                lc(p.a, g).start()
    for g in line:
        lc(g, g).wait_recv()
    total = ga[0]
    for g in range(1, GROUPS):
        total = total + ga[g]
    gains[...] = total
    for g in line:
        out_back(g, g).wait_recv()
        out_share(p.k, g).start()
    for g in range(GROUPS):
        sc(g, 1 - p.k).wait_recv()
        sc(g, p.k).wait_send()
        out_share(1 - p.k, g).wait_recv()
        out_share(p.k, g).wait_send()
        for c in range(p.chips):
            core_share(1 - p.k, c, g).wait_recv()
            core_share(p.k, c, g).wait_send()
        for c in others:
            chip_share(p.chip, g, c).wait_send()
            yc(g, c, p.chip).wait_send()
    for c in others:
        qc(c, p.chip).wait_send()
        gc(c, p.chip).wait_send()
        out_chip(c, p.chip).wait_send()
    for g in line:
        zkv(p.a, g).wait_send()
        zq(p.a, g).wait_send()
        lc(p.a, g).wait_send()
        out_line(p.a, g).wait_send()
        out_back(p.a, g).wait_send()
    for s in range(GROUPS):

        @pl.when((p.a - s >= 0) & (p.a < last))
        def _():
            bc(p.a - s, p.a + 1, 2 * s).wait_send()
            line_share(p.a - s, p.a + 1, 2 * s).wait_send()

        @pl.when((p.a + s <= last) & (p.a > 0))
        def _():
            bc(p.a + s, p.a - 1, 2 * s + 1).wait_send()
            line_share(p.a + s, p.a - 1, 2 * s + 1).wait_send()

        if s > 0:

            @pl.when(p.a + s <= last)
            def _():
                rightward(p.a + s, red.at[0]).wait_send()

            @pl.when(p.a - s >= 0)
            def _():
                leftward(p.a - s, red.at[0]).wait_send()


def back(n, lens, q3, kv, o3, l3, dog, wg, h1, rp, gmid, gfull, dg2, red, go):
    rows, width = rp.shape
    quarter = width // 4
    lanes = wg.shape[2]
    chips = n // GROUPS // 2
    keys = kv.shape[0] // GROUPS
    piece = red.shape[1]
    orow = go.shape[0] // 2
    sds = jax.ShapeDtypeStruct
    v = pltpu.VMEM
    sem = lambda *shape: [DMA(shape), DMA(shape)]
    return pl.pallas_call(
        functools.partial(back_kernel, n),
        name="back",
        out_shape=(
            sds((rows, width - 1), F32),
            sds((GROUPS, 2, quarter, lanes), BF16),
            sds((8, width), F32),
            sds((2, chips, GROUPS, piece, width), BF16),
            sds((2, GROUPS, orow // GROUPS, width), BF16),
        ),
        in_specs=[SM, VM, ANY, VM, VM, VM, ANY] + [VM] * 7,
        out_specs=[VM] * 5,
        scratch_shapes=[
            v(q3.shape, BF16),
            v(q3.shape, F32),
            v((2 if keys <= SUB else 1, keys, 384), BF16),
            v((keys, 384), F32),
            v((keys, 384), BF16),
            v((GROUPS, chips, rows, 384), BF16),
            v((GROUPS, chips, rows, 384), BF16),
            v((GROUPS, width, lanes), BF16),
            v((GROUPS, rows, lanes), BF16),
            v((GROUPS, rows, lanes), BF16),
            v((width, lanes), F32),
            v((2, 2, quarter, lanes), BF16),
            v((2, quarter, lanes), BF16),
            v((chips, quarter, lanes), BF16),
            v((8, width), F32),
            v((8, width), F32),
            v((8, width), F32),
            v((chips, 8, width), F32),
            v((GROUPS, 8, width), F32),
            v((GROUPS, piece, width), BF16),
            v((GROUPS, piece, width), BF16),
            v((GROUPS, piece, width), BF16),
            v((GROUPS, piece, width), BF16),
            v((orow, width), BF16),
            v((orow, width), BF16),
            v((chips, orow, width), BF16),
            v((GROUPS, orow // GROUPS, width), BF16),
            v((GROUPS, orow // GROUPS, width), BF16),
            *sem(GROUPS),
            DMA((GROUPS,)),
            DMA((2,)),
            *sem(GROUPS, chips),
            *sem(GROUPS + 1, chips),
            *sem(2 * GROUPS),
            *sem(GROUPS),
            *sem(4),
            *sem(chips),
            DMA((2 * GROUPS,)),
            DMA((GROUPS,)),
            *sem(GROUPS),
            *sem(GROUPS),
            *sem(GROUPS),
            DMA((2 * GROUPS,)),
            DMA((GROUPS,)),
            *sem(chips, GROUPS),
            *sem(chips, GROUPS),
            *sem(chips),
            *sem(2 * GROUPS),
            *sem(1 + GROUPS),
        ],
        compiler_params=pltpu.CompilerParams(
            collective_id=2, has_side_effects=True, vmem_limit_bytes=67043328
        ),
    )(lens, q3, kv, o3, l3, dog, wg, h1, rp, gmid, gfull, dg2, red, go)


def by_group(w):
    r = w.shape[0]
    w = w.reshape(r, 3, GROUPS, GH, HD).transpose(2, 0, 1, 3, 4)
    q, k, v = w[:, :, 0], w[:, :, 1], w[:, :, 2]
    zero = jnp.zeros_like(q[:, :, 0])
    return jnp.concatenate(
        [q[:, :, 0], q[:, :, 1], q[:, :, 2], zero, k[:, :, 0], k[:, :, 1], k[:, :, 2], v[:, :, 2],
         v[:, :, 0], v[:, :, 1]],
        axis=-1,
    )


def from_groups(g):
    r = g.shape[1]
    t = g.reshape(GROUPS, r, 10, HD).transpose(1, 0, 2, 3)
    q = t[:, :, 0:3]
    k = t[:, :, 4:7]
    v = jnp.stack([t[:, :, 8], t[:, :, 9], t[:, :, 7]], axis=2)
    return jnp.stack([q, k, v], axis=1).reshape(r, 3 * GROUPS * GH * HD)


def shards(n, resid, lengths, gain_one, w_qkv, w_out, gain_two, w_up, w_down, cotangent):
    _, rows, narrow = resid.shape
    width = narrow + 1
    ff = w_up.shape[1]
    c = lax.axis_index("ctx")
    pos = c * rows + jnp.arange(rows, dtype=jnp.int32)
    pad = ((0, 0), (0, 1))
    rp = jnp.pad(resid[0], pad)
    live = pos[:, None] < lengths[0]
    cp = jnp.pad(jnp.where(live, cotangent[0], jnp.zeros_like(cotangent[0])), pad)
    wo = jnp.pad(w_out, pad)
    wd = jnp.pad(w_down, pad)
    gains = jnp.pad(jnp.stack([gain_one, gain_two]).astype(F32), ((0, 6), (0, 0)))
    wg = by_group(w_qkv)
    meta = jnp.stack([c % (n // GROUPS), lengths[0]]).astype(jnp.int32)

    h1, q3, kv, _, woa, gfull = project(n, rp, gains, wg, wo)
    att, o3, l3 = attend(meta, q3, kv)
    out, gmid, red, go, dog, dg2 = mlp(n, att, rp, cp, gfull, woa, w_up, wd)
    gin, gq, gsum, res, goo = back(
        n, lengths, q3, kv, o3, l3, dog, wg, h1, rp, gmid, gfull, dg2, red, go
    )

    half = width // 2
    grad_qkv = from_groups(gq.reshape(GROUPS, half, -1).astype(F32))
    mine = lax.dynamic_slice_in_dim(gsum, lax.axis_index("fsdp") * half, half, 1)
    res = res.reshape(2, ff, width)
    up = jnp.concatenate([res[0, :width], res[0, width:]], axis=1).astype(F32)
    down = res[1, :, :narrow].astype(F32)
    gout = goo.reshape(half, width)[:, :narrow].astype(F32)
    return out[None], gin[None], mine[0], grad_qkv, gout, mine[1], up, down


def solution(mesh):
    n = mesh.shape["ctx"]
    return jax.shard_map(
        functools.partial(shards, n),
        mesh=mesh,
        in_specs=(
            P("fsdp", "ctx", None),
            P("fsdp"),
            P("fsdp"),
            P("fsdp", None),
            P("fsdp", None),
            P("fsdp"),
            P(None, "fsdp"),
            P("fsdp", None),
            P("fsdp", "ctx", None),
        ),
        out_specs=(
            P("fsdp", "ctx", None),
            P("fsdp", "ctx", None),
            P("fsdp"),
            P("fsdp", None),
            P("fsdp", None),
            P("fsdp"),
            P(None, "fsdp"),
            P("fsdp", None),
        ),
        check_vma=False,
    )
```

```python
import functools

import jax
import jax.numpy as jnp
from jax import lax
from jax.experimental import pallas as pl
from jax.experimental.pallas import tpu as pltpu
from jax.sharding import PartitionSpec as P

F32 = jnp.float32
BF16 = jnp.bfloat16
MESH = pl.DeviceIdType.MESH
NT = (((1,), (1,)), ((), ()))
TN = (((0,), (0,)), ((), ()))
EPS = 1e-05
MASKED = -1e30
LOG2E = 1.4426950408889634
SCALE = 0.125
GROUPS = 4
GH = 3
HD = 64
SUB = 1024
VLIM = 60 * 1024 * 1024

VM = pl.BlockSpec(memory_space=pltpu.VMEM)
SM = pl.BlockSpec(memory_space=pltpu.SMEM)
ANY = pl.BlockSpec(memory_space=pl.ANY)
DMA = pltpu.SemaphoreType.DMA


def dot(a, b):
    return jnp.dot(a, b, preferred_element_type=F32)


def dg(a, b, dims):
    return lax.dot_general(a, b, dims, preferred_element_type=F32)


def rcopy(src, dst, send, recv, dev):
    return pltpu.make_async_remote_copy(
        src_ref=src, dst_ref=dst, send_sem=send, recv_sem=recv, device_id=dev, device_id_type=MESH
    )


class Place:
    def __init__(self, n):
        self.n = n
        self.m = n // GROUPS
        self.chips = self.m // 2
        c = lax.axis_index("ctx")
        self.x = lax.axis_index("fsdp")
        self.a = c // self.m
        self.b = c % self.m
        self.chip = self.b // 2
        self.k = self.b % 2

    def xpeer(self):
        return {"fsdp": 1 - self.x}

    def sibling(self):
        return {"ctx": self.a * self.m + self.chip * 2 + 1 - self.k}

    def on_chip(self, chip):
        return {"ctx": self.a * self.m + chip * 2 + self.k}

    def on_line(self, a):
        return {"ctx": a * self.m + self.b}


def greet(p, xpeer=False, sibling=False, chips=False, line=False):
    bar = pltpu.get_barrier_semaphore()
    count = 0
    if xpeer:
        pl.semaphore_signal(bar, inc=1, device_id=p.xpeer(), device_id_type=MESH)
        count += 1
    if sibling:
        pl.semaphore_signal(bar, inc=1, device_id=p.sibling(), device_id_type=MESH)
        count += 1
    if chips:
        for d in range(1, p.chips):
            pl.semaphore_signal(
                bar, inc=1, device_id=p.on_chip((p.chip + d) % p.chips), device_id_type=MESH
            )
            count += 1
    if line:
        for d in range(1, GROUPS):
            pl.semaphore_signal(
                bar, inc=1, device_id=p.on_line((p.a + d) % GROUPS), device_id_type=MESH
            )
            count += 1
    return lambda: pl.semaphore_wait(bar, count)


def ext_of(v):
    last = lax.broadcasted_iota(jnp.int32, v.shape, 1) == v.shape[1] - 1
    return jnp.where(last, -jnp.sum(v, axis=1, keepdims=True), v)


def inv_rms(u):
    return lax.rsqrt(jnp.mean(u * u, axis=1, keepdims=True) + EPS)


def crms_back(u, inv, gain, dy):
    dx = dy * gain
    du = inv * (dx - u * (inv * inv * jnp.mean(dx * u, axis=1, keepdims=True)))
    width = u.shape[1]
    last = lax.broadcasted_iota(jnp.int32, u.shape, 1) == width - 1
    return jnp.where(last, 0.0, du - du[:, width - 1 :])


def low_half(shape):
    return lax.broadcasted_iota(jnp.int32, shape, len(shape) - 1) < HD


def pack_tail(t):
    half = t.shape[0] // 2
    top, bottom = t[:half], t[half:]
    return jnp.where(low_half(top.shape), pltpu.roll(bottom, HD, 1), top)


def unpack_tail(t):
    low = low_half(t.shape)
    zero = jnp.zeros_like(t)
    return jnp.where(low, zero, t), jnp.where(low, zero, pltpu.roll(t, HD, 1))


def causal(shape, sub, size, first_query):
    col = lax.broadcasted_iota(jnp.int32, shape, 1) + sub * size
    row = lax.broadcasted_iota(jnp.int32, shape, 0) + first_query
    return col <= row


def gelu_both(a):
    c = 0.7978845608028654
    a2 = a * a
    t = jnp.tanh(c * a * (1.0 + 0.044715 * a2))
    half = 0.5 * (1.0 + t)
    slope = half + 0.5 * a * (1.0 - t * t) * (c * (1.0 + 0.134145 * a2))
    return a * half, slope


def group_columns(wq, wg):
    width = wq.shape[1] // 3
    low = low_half((wq.shape[0], 128))
    zero = jnp.zeros((wq.shape[0], 128), wq.dtype)

    def swap(t):
        return pltpu.roll(t, HD, 1)

    for j in range(GROUPS // 2):
        a, b = 2 * j, 2 * j + 1
        for i in range(3):
            at = i * width + j * 384
            t0, t1, t2 = (wq[:, at + 128 * t : at + 128 * t + 128] for t in range(3))
            pair = (t0, swap(jnp.where(low, t2, t1)))
            if i < 2:
                third = (jnp.where(low, t1, zero), jnp.where(low, swap(t2), zero))
                for g, p, t in zip((a, b), pair, third):
                    wg[g, :, i * 256 : i * 256 + 128] = p
                    wg[g, :, i * 256 + 128 : i * 256 + 256] = t
            else:
                third = (jnp.where(low, zero, swap(t1)), jnp.where(low, zero, t2))
                for g, p, t in zip((a, b), pair, third):
                    wg[g, :, 512:640] = p
                    wg[g, :, 384:512] = wg[g, :, 384:512] + t


def front_kernel(
    n, lens, ri, ci, g1, g2, wq, wo, wuh, wdh,
    out, gmid, ysum, go, dog, dg2, rp, wg, h1, q3, kv, o3, l3, gfull,
    gains, wop, wa, woa, wu, wdr, wd, att, attg, attp, wide, hid, gmb, act, gpre, esum, dsend, gbb, mid, gk,
    ss, rs, ls, hs, hr, vs, kr, fs, xs, xr, cs, cr, ts, tr, as_, ar, ds_, dr, ks, ks_r,
):
    p = Place(n)
    rows, narrow = ri.shape
    width = narrow + 1
    half = width // 2
    ff = wuh.shape[1]
    pk = rows * 3 // 2
    keys = p.m * rows
    size = min(SUB, keys)
    subs = keys // size
    other = 1 - p.x
    others = [(p.chip + d) % p.chips for d in range(1, p.chips)]
    line = [(p.a + d) % GROUPS for d in range(1, GROUPS)]
    ready = greet(p, xpeer=True, sibling=True, chips=True, line=True)
    own_u = pltpu.make_async_copy(wuh, wu.at[p.x], ls.at[5])
    own_d = pltpu.make_async_copy(wdh, wdr.at[p.x], ls.at[6])
    own_u.start()
    own_d.start()

    rp[:, :narrow] = ri[...]
    rp[:, narrow:] = jnp.zeros((rows, 1), BF16)
    group_columns(wq, wg)
    gains[0:1, :] = g1[...].astype(F32).reshape(1, half)
    gains[1:2, :] = g2[...].astype(F32).reshape(1, half)
    gfull[p.x] = gains[...]
    ready()

    def xc(i, src, dst):
        return rcopy(src, dst, ss.at[i], rs.at[i], p.xpeer())

    at_x = pl.ds(pl.multiple_of(p.x * half, half), half)
    x_gain = xc(0, gains, gfull.at[p.x])
    x_gain.start()
    x_wa = xc(1, wg.at[p.a], wa.at[at_x])
    x_wa.start()

    def cut(i, chip, core):
        size_i = (width, ff)[i] // p.m
        return pl.ds(pl.multiple_of((chip * 2 + core) * size_i, size_i), size_i)

    def weight_x(i):
        at = cut(i, p.chip, p.k)
        return rcopy((wuh, wdh)[i].at[at], (wu, wdr)[i].at[p.x, at], xs.at[i], xr.at[i], p.xpeer())

    def weight_chip(i, owner, to):
        r = (wu, wdr)[i].at[other, cut(i, owner, p.k)]
        return rcopy(r, r, cs.at[i, to], cr.at[i, owner], p.on_chip(to))

    def weight_core(i, owner, core):
        r = (wu, wdr)[i].at[other, cut(i, owner, core)]
        return rcopy(r, r, ts.at[i, owner], tr.at[i, owner], p.sibling())

    def weight_spread(i):
        weight_x(i).wait_recv()
        for c in others:
            weight_chip(i, p.chip, c).start()
        weight_core(i, p.chip, p.k).start()

    def weight_pass(i):
        for c in others:
            weight_chip(i, c, c).wait_recv()
            weight_core(i, c, p.k).start()

    def weight_end(i):
        for c in range(p.chips):
            weight_core(i, c, 1 - p.k).wait_recv()

    weight_x(0).start()
    weight_x(1).start()

    wop[:, :narrow] = wo[...]
    wop[:, narrow:] = jnp.zeros((half, 1), BF16)
    xo = []
    local = []
    for i in range(2):
        g = p.x * 2 + i
        for j, (src, count, dst) in enumerate(((0, 128, 0), (128, 64, 192))):
            s_ = wop.at[pl.ds(i * 192 + src, count)]
            d_ = woa.at[pl.ds(pl.multiple_of(g * 256 + dst, 64), count)]
            xo.append(xc(2 + 2 * i + j, s_, d_))
            local.append(pltpu.make_async_copy(s_, d_, ls.at[1 + 2 * i + j]))
    zero_rows = jnp.zeros((HD, width), BF16)
    for g in range(GROUPS):
        woa[pl.ds(g * 256 + 128, HD), :] = zero_rows
    for c in xo:
        c.start()
    for c in local:
        c.start()
    slot = (p.a * p.m + p.b) * rows + lax.broadcasted_iota(jnp.int32, (rows, width), 0)
    live = slot < lens[0]
    gmb[0, :, :narrow] = ci[...]
    gmb[0, :, narrow:] = jnp.zeros((rows, 1), BF16)
    gmb[0] = jnp.where(live, gmb[0].astype(F32), 0.0).astype(BF16)
    x_gm = xc(6, gmb.at[0], gmb.at[1])
    x_gm.start()
    own_a = pltpu.make_async_copy(wg.at[p.a], wa.at[at_x], ls.at[0])
    own_a.start()
    u = ext_of(rp[...].astype(F32))
    normed = u * inv_rms(u)
    x_gain.wait()
    gain = jnp.concatenate([gfull[0, 0:1, :], gfull[1, 0:1, :]], axis=1)
    h1[p.a] = (normed * gain).astype(BF16)

    def line_copy(block, dst, sem):
        return rcopy(h1.at[block], h1.at[block], hs.at[sem], hr.at[block], p.on_line(dst))

    def kv_copy(block, b, dev, send):
        r = kv.at[pl.ds(pl.multiple_of((block * p.m + b) * rows, rows), rows)]
        return rcopy(r, r, send, kr.at[block, b], dev)

    def ac(i, to):
        return rcopy(att.at[to], attg.at[i], as_.at[to], ar.at[i], p.on_line(to))

    @pl.when(p.a < GROUPS - 1)
    def _():
        line_copy(p.a, p.a + 1, 0).start()

    @pl.when(p.a > 0)
    def _():
        line_copy(p.a, p.a - 1, 1).start()

    own_a.wait()
    x_wa.wait()

    def produce(block):
        y = dot(h1[block], wa[...]).astype(BF16)
        low = low_half((rows, 128))
        zero = jnp.zeros((rows, 128), BF16)
        at = pl.ds(pl.multiple_of(block * rows, rows), rows)
        q3[0, at, :] = jnp.where(low, y[:, :128], zero)
        q3[1, at, :] = jnp.where(low, zero, y[:, :128])
        q3[2, at, :] = y[:, 128:256]
        kv[pl.ds(pl.multiple_of((block * p.m + p.b) * rows, rows), rows), :] = y[:, 256:]
        for d in range(1, p.chips):
            kv_copy(block, p.b, p.on_chip((p.chip + d) % p.chips), vs.at[block, d]).start()
        kv_copy(block, p.b, p.sibling(), vs.at[block, 0]).start()

    def pass_on(block):
        for d in range(1, p.chips):
            b = ((p.chip + d) % p.chips) * 2 + p.k
            kv_copy(block, b, p.sibling(), fs.at[block, d]).wait_recv()
            kv_copy(block, b, p.sibling(), fs.at[block, d]).start()

    def complete(block):
        for c in range(p.chips):
            kv_copy(block, c * 2 + 1 - p.k, p.sibling(), vs.at[block, 0]).wait_recv()

    first_query = p.b * rows
    dead = jnp.where(lens[0] > keys, 0.0, 1.0).astype(F32)

    def pair(z, c, diagonal):
        at_q = pl.ds(pl.multiple_of(z * rows, rows), rows)
        gone = jnp.where(c > 0, dead, 0.0)
        for h in range(GH):
            kt = 128 * (h // 2)
            vt = 128 if h == 2 else 256
            q = q3[h, at_q, :]

            def keys_of(sub, first):
                at = pl.ds(pl.multiple_of(c * keys + sub * size, size), size)
                scores = dg(q, kv[at, kt : kt + 128], NT) * (SCALE * LOG2E)
                if diagonal:
                    scores = jnp.where(causal(scores.shape, sub, size, first_query), scores, MASKED)
                here = jnp.max(scores, axis=1, keepdims=True) + gone * MASKED
                if first:
                    newest = here
                else:
                    top = l3[h, at_q, 0:1]
                    newest = jnp.maximum(top, here)
                weights = jnp.exp2(scores - (newest - gone * (3.0 * MASKED)))
                sums = jnp.sum(weights, axis=1, keepdims=True)
                part = dot(weights.astype(BF16), kv[at, vt : vt + 128])
                if not first:
                    shrink = jnp.exp2(top - newest)
                    sums = sums + l3[h, at_q, HD : HD + 1] * shrink
                    part = part + o3[h, at_q, :] * shrink
                o3[h, at_q, :] = part
                l3[h, at_q, :] = jnp.where(low_half((rows, 128)), newest, sums)

            keys_of(0, diagonal)
            if subs > 1:

                def rest(sub, carry):
                    keys_of(sub, False)
                    return carry

                lax.fori_loop(1, subs, rest, 0)

    def finish_row(z):
        at_q = pl.ds(pl.multiple_of(z * rows, rows), rows)
        heads = []
        for h in range(GH):
            total = l3[h, at_q, HD : HD + 1]
            o = o3[h, at_q, :] / total
            o3[h, at_q, :] = o
            l3[h, at_q, :] = jnp.broadcast_to(l3[h, at_q, 0:1] + jnp.log2(total), (rows, 128))
            heads.append(o)
        att[z, 0:rows, :] = jnp.where(low_half((rows, 128)), heads[0], heads[1]).astype(BF16)
        att[z, rows:pk, :] = pack_tail(heads[2]).astype(BF16)

        @pl.when(z == p.a)
        def _():
            attg[z] = att[z]

        @pl.when(z != p.a)
        def _():
            ac(p.a, z).start()

    def far(z):
        return jnp.abs(z - p.a)

    def pairs(t):
        def row(z, carry):
            @pl.when(far(z) == t)
            def _():
                pair(z, z, True)

            def key(d, carry):
                @pl.when(jnp.maximum(far(z), far(z - d)) == t)
                def _():
                    pair(z, z - d, False)

                return carry

            lax.fori_loop(1, z + 1, key, 0)

            @pl.when(jnp.maximum(far(z), p.a) == t)
            def _():
                finish_row(z)

            return carry

        lax.fori_loop(0, GROUPS, row, 0)

    def step(s, carry):
        below = p.a - s
        above = p.a + s

        @pl.when((s > 0) & (below >= 0))
        def _():
            line_copy(below, p.a, 0).wait_recv()

            @pl.when(p.a < GROUPS - 1)
            def _():
                line_copy(below, p.a + 1, 2 * s).start()

        @pl.when((s > 0) & (above < GROUPS))
        def _():
            line_copy(above, p.a, 0).wait_recv()

            @pl.when(p.a > 0)
            def _():
                line_copy(above, p.a - 1, 2 * s + 1).start()

        @pl.when(s == GROUPS - 1)
        def _():
            weight_spread(0)

        @pl.when(s == GROUPS)
        def _():
            weight_spread(1)

        @pl.when(below >= 0)
        def _():
            produce(below)

        @pl.when((s > 0) & (above < GROUPS))
        def _():
            produce(above)

        @pl.when((s > 0) & (below + 1 >= 0))
        def _():
            pass_on(below + 1)
            complete(below + 1)

        @pl.when((s > 1) & (above - 1 < GROUPS))
        def _():
            pass_on(above - 1)
            complete(above - 1)

        @pl.when(s > 0)
        def _():
            pairs(s - 1)

        return carry

    lax.fori_loop(0, GROUPS + 1, step, 0)
    weight_pass(0)

    own_u.wait()
    own_d.wait()

    def pad_down(f):
        wd[f, :, :narrow] = wdr[f]
        wd[f, :, narrow:] = jnp.zeros((ff, 1), BF16)

    pad_down(p.x)
    for c in xo:
        c.wait()
    for c in local:
        c.wait()
    for g in line:
        ac(g, g).wait_recv()
    x_att = [xc(7 + i, attg.at[other * 2 + i], attp.at[i]) for i in range(2)]
    for g in range(GROUPS):
        wide[:, g * 256 : g * 256 + 128] = attg[g, 0:rows, :]
        top, bottom = unpack_tail(attg[g, rows:pk, :])
        wide[0 : rows // 2, g * 256 + 128 : g * 256 + 256] = top
        wide[rows // 2 : rows, g * 256 + 128 : g * 256 + 256] = bottom
    mid[...] = rp[...].astype(F32) + dot(wide[...], woa[...])
    u = ext_of(mid[...])
    gain = jnp.concatenate([gfull[0, 1:2, :], gfull[1, 1:2, :]], axis=1)
    hid[0] = (u * inv_rms(u) * gain).astype(BF16)
    x_hid = xc(9, hid.at[0], hid.at[1])
    x_hid.start()
    for c in x_att:
        c.start()
    tiles = ff // 256

    def up(slot, token, f):
        def tile(t, carry):
            at = pl.ds(pl.multiple_of(t * 256, 256), 256)
            a, slope = gelu_both(dot(hid[token], wu[f, :, at]))
            act[slot, :, at] = a.astype(BF16)
            gpre[slot, :, at] = (slope * dg(gmb[token], wd[f, at, :], NT)).astype(BF16)
            return carry

        lax.fori_loop(0, tiles, tile, 0)

    weight_pass(1)
    up(0, 0, p.x)
    weight_end(0)
    weight_end(1)
    pad_down(other)
    up(2, 0, other)

    def e_tile(t, carry):
        at = pl.ds(pl.multiple_of(t * 256, 256), 256)
        e = dg(gpre[0], wu[p.x, at, :], NT) + dg(gpre[2], wu[other, at, :], NT)
        esum[t] = e
        return carry

    lax.fori_loop(0, width // 256, e_tile, 0)
    e = jnp.concatenate([esum[t] for t in range(width // 256)], axis=1)
    u = ext_of(mid[...])
    inv = inv_rms(u)
    gmid[...] = gmb[0].astype(F32) + crms_back(u, inv, gain, e)
    gbb[0] = gmid[...].astype(BF16)
    x_gb = xc(10, gbb.at[0], gbb.at[1])
    x_gb.start()

    def dc(i, to):
        return rcopy(dsend.at[to], dog.at[i], ds_.at[to], dr.at[i], p.on_line(to))

    for d in range(1, GROUPS + 1):
        to = (p.a + d) % GROUPS
        w = woa[pl.ds(pl.multiple_of(to * 256, 256), 256), :]
        da = dg(gbb[0], w, NT).astype(BF16)
        if d < GROUPS:
            dsend[to, 0:rows, :] = da[:, 0:128]
            dsend[to, rows:pk, :] = pack_tail(da[:, 128:256])
            dc(p.a, to).start()
        else:
            dog[to, 0:rows, :] = da[:, 0:128]
            dog[to, rows:pk, :] = pack_tail(da[:, 128:256])
    x_gm.wait()
    x_hid.wait()
    up(1, 1, p.x)
    final = mid[...] + dot(act[0], wd[p.x]) + dot(act[2], wd[other])
    out[...] = final.astype(BF16)

    gm = wd
    piece = ysum.shape[2]
    part = GROUPS * piece

    def kc(chip):
        at = pl.ds(pl.multiple_of(chip * part, part), part)
        return rcopy(gm.at[1 - p.k, at], gk.at[at], ks.at[chip], ks_r.at[chip], p.sibling())

    def grad_up(t, carry):
        at = pl.ds(pl.multiple_of(t * 256, 256), 256)
        g = dg(hid[0], gpre[0, :, at], TN) + dg(hid[1], gpre[1, :, at], TN)
        per = width // 256
        r0 = pl.multiple_of((t // per) * width, width)
        c0 = pl.multiple_of((t % per) * 256, 256)
        gm[0, pl.ds(r0, width), pl.ds(c0, 256)] = g.astype(BF16)
        return carry

    def grad_down(t, carry):
        at = pl.ds(pl.multiple_of(t * 256, 256), 256)
        g = dg(act[0, :, at], gmb[0], TN) + dg(act[1, :, at], gmb[1], TN)
        gm[1, at, :] = g.astype(BF16)
        return carry

    @pl.when(p.k == 0)
    def _():
        lax.fori_loop(0, tiles, grad_down, 0)

    @pl.when(p.k == 1)
    def _():
        lax.fori_loop(0, tiles, grad_up, 0)

    for c in others:
        kc(c).start()
    kc(p.chip).start()

    @pl.when(p.k == 0)
    def _():
        lax.fori_loop(0, tiles, grad_up, 0)

    @pl.when(p.k == 1)
    def _():
        lax.fori_loop(0, tiles, grad_down, 0)

    for chip in others + [p.chip]:
        kc(chip).wait()
        for z in range(GROUPS):
            at = pl.ds(pl.multiple_of(chip * part + z * piece, 16), piece)
            ysum[chip, z] = (gm[p.k, at, :].astype(F32) + gk[at, :].astype(F32)).astype(BF16)
    dg2[...] = jnp.broadcast_to(jnp.sum(e * (u * inv), axis=0, keepdims=True), dg2.shape)
    for c in x_att:
        c.wait()
    x_gb.wait()
    for i in range(2):
        own_tail = jnp.concatenate(unpack_tail(attg[p.x * 2 + i, rows:pk, :]), axis=0)
        peer_tail = jnp.concatenate(unpack_tail(attp[i, rows:pk, :]), axis=0)
        g = dg(attg[p.x * 2 + i, 0:rows, :], gbb[0], TN) + dg(attp[i, 0:rows, :], gbb[1], TN)
        go[i * 192 : i * 192 + 128, :] = g.astype(BF16)
        g = dg(own_tail, gbb[0], TN) + dg(peer_tail, gbb[1], TN)
        go[i * 192 + 128 : i * 192 + 192, :] = g[HD:, :].astype(BF16)

    for g in line:
        ac(p.a, g).wait_send()
        dc(p.a, g).wait_send()
        dc(g, g).wait_recv()
    for block in range(GROUPS):
        kv_copy(block, p.b, p.sibling(), vs.at[block, 0]).wait_send()
        for d in range(1, p.chips):
            kv_copy(block, p.b, p.sibling(), vs.at[block, d]).wait_send()
            b = ((p.chip + d) % p.chips) * 2
            kv_copy(block, b + p.k, p.sibling(), fs.at[block, d]).wait_send()
    for s in range(GROUPS):

        @pl.when((p.a - s >= 0) & (p.a < GROUPS - 1))
        def _():
            line_copy(p.a - s, p.a + 1, 2 * s).wait_send()

        @pl.when((p.a + s < GROUPS) & (p.a > 0))
        def _():
            line_copy(p.a + s, p.a - 1, 2 * s + 1).wait_send()

    for i in range(2):
        weight_x(i).wait_send()
        for c in others:
            weight_chip(i, p.chip, c).wait_send()
        for c in range(p.chips):
            weight_core(i, c, p.k).wait_send()


def front(n, lens, ri, ci, g1, g2, wq, wo, wu, wd):
    rows, narrow = ri.shape
    width = narrow + 1
    half = width // 2
    ff = wu.shape[1]
    pk = rows * 3 // 2
    m = n // GROUPS
    chips = m // 2
    piece = ff // GROUPS // chips
    lanes = 640
    sds = jax.ShapeDtypeStruct
    v = pltpu.VMEM
    heads = (GH, GROUPS * rows, 128)
    sem = lambda *shape: [DMA(shape), DMA(shape)]
    return pl.pallas_call(
        functools.partial(front_kernel, n),
        name="front",
        out_shape=(
            sds((rows, width), BF16),
            sds((rows, width), F32),
            sds((chips, GROUPS, piece, width), BF16),
            sds((half, width), BF16),
            sds((GROUPS, pk, 128), BF16),
            sds((8, width), F32),
            sds((rows, width), BF16),
            sds((GROUPS, half, lanes), BF16),
            sds((GROUPS, rows, width), BF16),
            sds(heads, BF16),
            sds((n * rows, 384), BF16),
            sds(heads, F32),
            sds(heads, F32),
            sds((2, 8, half), F32),
        ),
        in_specs=[SM, VM, VM, VM, VM, VM, VM, ANY, ANY],
        out_specs=[VM] * 14,
        scratch_shapes=[
            v((8, half), F32),
            v((half, width), BF16),
            v((width, lanes), BF16),
            v((GROUPS * 256, width), BF16),
            v((2, width, ff), BF16),
            v((2, ff, narrow), BF16),
            v((2, ff, width), BF16),
            v((GROUPS, pk, 128), BF16),
            v((GROUPS, pk, 128), BF16),
            v((2, pk, 128), BF16),
            v((rows, GROUPS * 256), BF16),
            v((2, rows, width), BF16),
            v((2, rows, width), BF16),
            v((3, rows, ff), BF16),
            v((3, rows, ff), BF16),
            v((width // 256, rows, 256), F32),
            v((GROUPS, pk, 128), BF16),
            v((2, rows, width), BF16),
            v((rows, width), F32),
            v((ff, width), BF16),
            *sem(11),
            DMA((7,)),
            DMA((2 * GROUPS,)),
            DMA((GROUPS,)),
            DMA((GROUPS, chips)),
            DMA((GROUPS, m)),
            DMA((GROUPS, chips)),
            *sem(2),
            *sem(2, chips),
            *sem(2, chips),
            *sem(GROUPS),
            *sem(GROUPS),
            *sem(chips),
        ],
        compiler_params=pltpu.CompilerParams(
            collective_id=0, has_side_effects=True, vmem_limit_bytes=67043328
        ),
    )(lens, ri, ci, g1, g2, wq, wo, wu, wd)


def back_kernel(
    n, lens, q3, kv, o3, l3, dog, wg, h1, rp, gmid, gfull, dg2, ysum, go,
    gin, gq, gains, res, goo,
    red, ymine, yq, do3, dq3, kvc, dkv, dkvb, rk, ry, wfull, gps, gpr, gqb, qk, qx, qy,
    g0, gk, gx, gy, ga, left, right, sumr, suml, ok, os_, oy, oz, ozr,
    xs, xr, ls, vs, ks, kr, ys, yr, zs, zr, ws, wr, qs, qr, ns, nr, bs, br, cs, cr,
    rs_, rr, ls_, lr, as_, ar, es, er, fs, fr, ts, tr, us, ur, is_, ir, ps, pr,
):
    p = Place(n)
    rows, width = rp.shape
    half = width // 2
    quarter = width // 4
    last = GROUPS - 1
    keys = dkv.shape[0]
    size = min(SUB, keys)
    subs = keys // size
    slots = kvc.shape[0]
    others = [(p.chip + d) % p.chips for d in range(1, p.chips)]
    line = [(p.a + d) % GROUPS for d in range(1, GROUPS)]
    ready = greet(p, xpeer=True, sibling=True, chips=True, line=True)
    at_x = pl.ds(pl.multiple_of(p.x * half, half), half)
    local = [
        pltpu.make_async_copy(wg.at[g], wfull.at[g, at_x], ls.at[g]) for g in range(GROUPS)
    ]

    def chunk_of(i):
        return (p.a + 1 + i) % GROUPS

    def fetch(i):
        c = chunk_of(i)
        src = kv.at[pl.ds(pl.multiple_of(c * keys, keys), keys)]
        return pltpu.make_async_copy(src, kvc.at[i % slots], vs.at[i % slots])

    fetch(0).start()
    o_in = pltpu.make_async_copy(o3, dq3, ls.at[GROUPS])
    o_in.start()
    y_in = pltpu.make_async_copy(ysum.at[p.chip], ymine, ls.at[GROUPS + 1])
    y_in.start()
    for c in local:
        c.start()
    wx = [
        rcopy(wg.at[g], wfull.at[g, at_x], xs.at[g], xr.at[g], p.xpeer()) for g in range(GROUPS)
    ]

    def over_chips(chip, slot, z):
        return rcopy(ysum.at[chip, z], yq.at[slot, z], ps.at[chip, z], pr.at[slot, z], p.on_chip(chip))

    def turn(j):
        outer = jnp.where(p.a == 0, last - j, j)
        inner = (0, last, 1, last - 1)[j]
        return jnp.where((p.a == 0) | (p.a == last), outer, jnp.where(p.a == 1, last - inner, inner))

    def chip_sum(j):
        z = turn(j)
        total = ymine[z].astype(F32)
        for c in others:
            over_chips(c, c, z).wait_recv()
            total = total + yq[c, z].astype(F32)
        red[z] = total.astype(BF16)
        if j < last:

            @pl.when(p.a == 0)
            def _():
                rightward(z, red.at[z]).start()

            @pl.when(p.a == last)
            def _():
                leftward(z, red.at[z]).start()

    def rightward(z, src):
        return rcopy(src, left.at[z], rs_.at[z], rr.at[z], p.on_line(p.a + 1))

    def leftward(z, src):
        return rcopy(src, right.at[z], ls_.at[z], lr.at[z], p.on_line(p.a - 1))

    def reduce_step(s):
        @pl.when((p.a >= 1) & (p.a <= s))
        def _():
            z = last + p.a - s
            rightward(z, sumr.at[z]).wait_recv()
            if s < last:
                sumr[z] = (red[z].astype(F32) + left[z].astype(F32)).astype(BF16)
                rightward(z, sumr.at[z]).start()

        b = last - p.a

        @pl.when((b >= 1) & (b <= s))
        def _():
            z = s - b
            leftward(z, suml.at[z]).wait_recv()
            if s < last:
                suml[z] = (red[z].astype(F32) + right[z].astype(F32)).astype(BF16)
                leftward(z, suml.at[z]).start()

    def line_share(z, dst, sem):
        r = res.at[p.k, p.chip, z]
        return rcopy(r, r, as_.at[sem], ar.at[z], p.on_line(dst))

    def chip_share(chip, z, dst):
        r = res.at[p.k, chip, z]
        return rcopy(r, r, es.at[dst, z], er.at[chip, z], p.on_chip(dst))

    def core_share(core, chip, z):
        r = res.at[core, chip, z]
        return rcopy(r, r, fs.at[chip, z], fr.at[chip, z], p.sibling())

    def spread(z):
        for c in others:
            chip_share(p.chip, z, c).start()
        core_share(p.k, p.chip, z).start()

    def gather_first():
        z = p.a
        res[p.k, p.chip, z] = red[z]

        @pl.when(p.a > 0)
        def _():
            cur = res[p.k, p.chip, z].astype(F32)
            res[p.k, p.chip, z] = (cur + left[z].astype(F32)).astype(BF16)

        @pl.when(p.a < last)
        def _():
            cur = res[p.k, p.chip, z].astype(F32)
            res[p.k, p.chip, z] = (cur + right[z].astype(F32)).astype(BF16)
            line_share(z, p.a + 1, 0).start()

        @pl.when(p.a > 0)
        def _():
            line_share(z, p.a - 1, 1).start()

        spread(z)

    def gather_step(s):
        @pl.when(p.a - s >= 0)
        def _():
            line_share(p.a - s, p.a, 0).wait_recv()

            @pl.when(p.a < last)
            def _():
                line_share(p.a - s, p.a + 1, 2 * s).start()

            spread(p.a - s)

        @pl.when(p.a + s <= last)
        def _():
            line_share(p.a + s, p.a, 0).wait_recv()

            @pl.when(p.a > 0)
            def _():
                line_share(p.a + s, p.a - 1, 2 * s + 1).start()

            spread(p.a + s)

    def pass_on(z):
        for c in others:
            chip_share(c, z, c).wait_recv()
            core_share(p.k, c, z).start()

    orow = go.shape[0] // 2
    opart = orow // GROUPS

    def out_core():
        at = pl.ds(pl.multiple_of((1 - p.k) * orow, orow), orow)
        return rcopy(go.at[at], ok, is_.at[0], ir.at[0], p.sibling())

    def out_chip(chip, slot):
        return rcopy(os_, oy.at[slot], ts.at[chip], tr.at[slot], p.on_chip(chip))

    def out_line(slot, to):
        return rcopy(oz.at[to], ozr.at[slot], us.at[to], ur.at[slot], p.on_line(to))

    def out_back(slot, to):
        r = goo.at[p.k, slot]
        return rcopy(r, r, us.at[GROUPS + to], ur.at[GROUPS + slot], p.on_line(to))

    def out_share(core, z):
        r = goo.at[core, z]
        return rcopy(r, r, is_.at[1 + z], ir.at[1 + z], p.sibling())

    def out_1():
        out_core().wait()
        at = pl.ds(pl.multiple_of(p.k * orow, orow), orow)
        os_[...] = (go[at, :].astype(F32) + ok[...].astype(F32)).astype(BF16)
        for c in others:
            out_chip(c, p.chip).start()

    def out_2():
        total = os_[...].astype(F32)
        for c in others:
            out_chip(c, c).wait_recv()
            total = total + oy[c].astype(F32)
        for z in range(GROUPS):
            oz[z] = total[z * opart : (z + 1) * opart].astype(BF16)
        for z in line:
            out_line(p.a, z).start()

    def out_3():
        total = oz[p.a].astype(F32)
        for z in line:
            out_line(z, z).wait_recv()
            total = total + ozr[z].astype(F32)
        goo[p.k, p.a] = total.astype(BF16)
        for z in line:
            out_back(p.a, z).start()
        out_share(p.k, p.a).start()

    def kc(i, chip):
        c = chunk_of(i)
        at = pl.ds(pl.multiple_of((chip * 2 + 1 - p.k) * rows, rows), rows)
        return rcopy(
            dkvb.at[at], rk.at[c, chip], ks.at[c, chip], kr.at[c, chip], p.sibling()
        )

    def yc(c, chip, slot):
        return rcopy(rk.at[c, chip], ry.at[c, slot], ys.at[c, chip], yr.at[c, slot], p.on_chip(chip))

    def zkv(slot, to):
        lanes = pl.ds(256, 384)
        return rcopy(
            gps.at[to, :, lanes], gpr.at[slot, :, lanes], zs.at[to], zr.at[slot], p.on_line(to)
        )

    def zq(slot, to):
        lanes = pl.ds(0, 256)
        return rcopy(
            gps.at[to, :, lanes], gpr.at[slot, :, lanes], ws.at[to], wr.at[slot], p.on_line(to)
        )

    def mine(chip):
        at = pl.ds(pl.multiple_of((chip * 2 + p.k) * rows, rows), rows)
        return dkvb[at, :].astype(F32)

    def kv_1(i):
        dkvb[...] = dkv[...].astype(BF16)
        for c in others:
            kc(i, c).start()
        kc(i, p.chip).start()

    def kv_2(i):
        c = chunk_of(i)
        for chip in others:
            kc(i, chip).wait()
            rk[c, chip] = (mine(chip) + rk[c, chip].astype(F32)).astype(BF16)
            yc(c, chip, p.chip).start()
        kc(i, p.chip).wait()
        rk[c, p.chip] = (mine(p.chip) + rk[c, p.chip].astype(F32)).astype(BF16)

    def kv_3(i, send):
        c = chunk_of(i)
        total = rk[c, p.chip].astype(F32)
        for chip in others:
            yc(c, chip, chip).wait_recv()
            total = total + ry[c, chip].astype(F32)
        gps[c, :, 256:640] = total.astype(BF16)
        if send:
            zkv(p.a, c).start()

    ready()
    out_core().start()
    for j in range(GROUPS):
        for c in others:
            over_chips(c, p.chip, turn(j)).start()
    for c in wx:
        c.start()

    first_query = p.b * rows
    low = low_half((rows, 128))
    o_in.wait()
    y_in.wait()
    for z in range(GROUPS):
        at = pl.ds(z * rows, rows)
        both = dog[z, 0:rows, :]
        zero = jnp.zeros_like(both)
        do3[0, at, :] = jnp.where(low, both, zero)
        do3[1, at, :] = jnp.where(low, zero, both)
        top, bottom = unpack_tail(dog[z, rows:, :])
        do3[2, pl.ds(z * rows, rows // 2), :] = top
        do3[2, pl.ds(z * rows + rows // 2, rows // 2), :] = bottom
        for h in range(GH):
            delta = jnp.sum(dq3[h, at, :] * do3[h, at, :].astype(F32), axis=1, keepdims=True)
            gqb[h * rows : (h + 1) * rows, z * 128 : (z + 1) * 128] = jnp.broadcast_to(delta, (rows, 128))
    dq3[...] = jnp.zeros_like(dq3)
    gone = jnp.where(lens[0] > keys, 0.0, -MASKED).astype(F32)

    def chunk(i, carry):
        c = chunk_of(i)
        fetch(i).wait()

        if slots > 1:

            @pl.when(i < last)
            def _():
                fetch(i + 1).start()

        dead = jnp.where(c > 0, gone, 0.0)

        def head(h, carry):
            kt = pl.multiple_of(128 * (h // 2), 128)
            vt = pl.multiple_of(jnp.where(h == 2, 128, 256), 128)

            def step(z, masked):
                at_q = pl.ds(pl.multiple_of(z * rows, rows), rows)
                q = q3[h, at_q, :]
                do = do3[h, at_q, :]
                lse = l3[h, at_q, 0:1] + dead
                delta = gqb[
                    pl.ds(pl.multiple_of(h * rows, rows), rows),
                    pl.ds(pl.multiple_of(z * 128, 128), 128),
                ][:, 0:1]
                def keys_of(sub, carry):
                    at = pl.ds(pl.multiple_of(sub * size, size), size)
                    k = kvc[i % slots, at, pl.ds(kt, 128)]
                    v = kvc[i % slots, at, pl.ds(vt, 128)]
                    scores = dg(q, k, NT) * (SCALE * LOG2E)
                    if masked:
                        scores = jnp.where(
                            causal(scores.shape, sub, size, first_query), scores, MASKED
                        )
                    weights = jnp.exp2(scores - lse)
                    gp = dg(do, v, NT)
                    gs = (weights * (gp - delta)).astype(BF16)
                    dq3[h, at_q, :] += dot(gs, k)
                    gv = dg(weights.astype(BF16), do, TN)
                    gk_ = dg(gs, q, TN) * SCALE
                    if masked:
                        dkv[at, pl.ds(kt, 128)] = jnp.where(h == 1, dkv[at, pl.ds(kt, 128)], 0.0) + gk_
                        dkv[at, pl.ds(vt, 128)] = jnp.where(h == 0, 0.0, dkv[at, pl.ds(vt, 128)]) + gv
                    else:
                        dkv[at, pl.ds(kt, 128)] += gk_
                        dkv[at, pl.ds(vt, 128)] += gv
                    return carry

                if subs > 1:
                    lax.fori_loop(0, subs, keys_of, 0)
                else:
                    keys_of(0, 0)

            step(c, True)

            def rest(z, carry):
                step(z, False)
                return carry

            lax.fori_loop(c + 1, GROUPS, rest, 0)

            @pl.when(h == 0)
            def _():
                @pl.when(i >= 1)
                def _():
                    kv_2(i - 1)

            @pl.when(h == 1)
            def _():
                @pl.when(i >= 2)
                def _():
                    kv_3(i - 2, True)

                @pl.when(i == 2)
                def _():
                    chip_sum(2)
                    reduce_step(2)

            @pl.when(h == 2)
            def _():
                @pl.when(i == 0)
                def _():
                    out_1()
                    chip_sum(0)

                @pl.when(i == 1)
                def _():
                    chip_sum(1)
                    reduce_step(1)
                    out_2()

                @pl.when(i == 2)
                def _():
                    out_3()

                @pl.when(i == 3)
                def _():
                    chip_sum(3)
                    reduce_step(3)
                    gather_first()

            return carry

        lax.fori_loop(0, GH, head, 0)
        if slots == 1:

            @pl.when(i < last)
            def _():
                fetch(i + 1).start()

        kv_1(i)
        return carry

    lax.fori_loop(0, GROUPS, chunk, 0)
    kv_3(2, True)
    for d in range(1, GROUPS + 1):
        z = (p.a + d) % GROUPS
        at = pl.ds(pl.multiple_of(z * rows, rows), rows)
        gps[z, :, 0:128] = (jnp.where(low, dq3[0, at, :], dq3[1, at, :]) * SCALE).astype(BF16)
        gps[z, :, 128:256] = (jnp.where(low, dq3[2, at, :], 0.0) * SCALE).astype(BF16)
        if d < GROUPS:
            zq(p.a, z).start()
    kv_2(3)
    gather_step(1)
    kv_3(3, False)
    gpr[p.a] = gps[p.a]

    gqb[...] = jnp.zeros_like(gqb)

    def rowdot(z, carry):
        for t in range(width // 256):
            at = pl.ds(t * 256, 256)
            gqb[at, :] += dg(h1[z, :, at], gps[z], TN)
        return carry

    lax.fori_loop(0, GROUPS, rowdot, 0)

    def rows_of(i, core):
        return pl.ds(pl.multiple_of(i * half + core * quarter, quarter), quarter)

    for i in range(2):
        qk[0, i] = gqb[rows_of(i, 1 - p.k), :].astype(BF16)
    q_k = rcopy(qk.at[0], qk.at[1], qs.at[0], qr.at[0], p.sibling())
    q_k.start()
    for c in local:
        c.wait()
    q_k.wait()
    for i in range(2):
        gqb[rows_of(i, p.k), :] += qk[1, i].astype(F32)
    qx[0] = gqb[rows_of(1 - p.x, p.k), :].astype(BF16)
    q_x = rcopy(qx.at[0], qx.at[1], qs.at[1], qr.at[1], p.xpeer())
    q_x.start()
    gather_step(2)
    q_x.wait()
    gqb[rows_of(p.x, p.k), :] += qx[1].astype(F32)
    qy[p.chip] = gqb[rows_of(p.x, p.k), :].astype(BF16)

    def qc(chip, slot):
        return rcopy(qy.at[p.chip], qy.at[slot], ns.at[chip], nr.at[slot], p.on_chip(chip))

    for c in others:
        qc(c, p.chip).start()
    for c in wx:
        c.wait()
    h = dg(gpr[p.a], wfull[p.a], NT)
    for g in line:
        zkv(g, g).wait_recv()
        zq(g, g).wait_recv()
        h = h + dg(gpr[g], wfull[g], NT)
    total = gqb[rows_of(p.x, p.k), :]
    for c in others:
        qc(c, c).wait_recv()
        total = total + qy[c].astype(F32)
    gq[p.a, p.k] = total.astype(BF16)

    def bc(slot, to, sem):
        r = gq.at[slot, p.k]
        return rcopy(r, r, bs.at[sem], br.at[slot], p.on_line(to))

    def sc(slot, core):
        return rcopy(gq.at[slot, core], gq.at[slot, core], cs.at[slot], cr.at[slot], p.sibling())

    @pl.when(p.a < last)
    def _():
        bc(p.a, p.a + 1, 0).start()

    @pl.when(p.a > 0)
    def _():
        bc(p.a, p.a - 1, 1).start()

    sc(p.a, p.k).start()
    u = ext_of(rp[...].astype(F32))
    inv = inv_rms(u)
    gain = jnp.concatenate([gfull[0, 0:1, :], gfull[1, 0:1, :]], axis=1)
    result = gmid[...] + crms_back(u, inv, gain, h)
    gin[...] = result
    first = jnp.sum(h * (u * inv), axis=0, keepdims=True)
    which = lax.broadcasted_iota(jnp.int32, (8, width), 0)
    g0[...] = jnp.where(which == 0, first, dg2[...])
    g_k = rcopy(g0, gk, qs.at[2], qr.at[2], p.sibling())
    g_k.start()
    gather_step(3)
    for z in range(GROUPS):
        pass_on(z)
    g_k.wait()
    g0[...] += gk[...]
    g_x = rcopy(g0, gx, qs.at[3], qr.at[3], p.xpeer())
    g_x.start()
    for s in range(1, GROUPS):

        @pl.when(p.a - s >= 0)
        def _():
            bc(p.a - s, p.a, 0).wait_recv()

            @pl.when(p.a < last)
            def _():
                bc(p.a - s, p.a + 1, 2 * s).start()

            sc(p.a - s, p.k).start()

        @pl.when(p.a + s <= last)
        def _():
            bc(p.a + s, p.a, 0).wait_recv()

            @pl.when(p.a > 0)
            def _():
                bc(p.a + s, p.a - 1, 2 * s + 1).start()

            sc(p.a + s, p.k).start()

        if s == 1:
            g_x.wait()
            gy[p.chip] = g0[...] + gx[...]

            def gc(chip, slot):
                return rcopy(
                    gy.at[p.chip], gy.at[slot], ys.at[GROUPS, chip], yr.at[GROUPS, slot],
                    p.on_chip(chip),
                )

            for c in others:
                gc(c, p.chip).start()
        if s == 2:
            for c in others:
                gc(c, c).wait_recv()
            total = gy[0]
            for c in range(1, p.chips):
                total = total + gy[c]
            ga[p.a] = total

            def lc(slot, to):
                return rcopy(
                    ga.at[p.a], ga.at[slot], zs.at[GROUPS + to], zr.at[GROUPS + slot], p.on_line(to)
                )

            for g in line:
                lc(p.a, g).start()
    for g in line:
        lc(g, g).wait_recv()
    total = ga[0]
    for g in range(1, GROUPS):
        total = total + ga[g]
    gains[...] = total
    for g in line:
        out_back(g, g).wait_recv()
        out_share(p.k, g).start()
    for g in range(GROUPS):
        sc(g, 1 - p.k).wait_recv()
        sc(g, p.k).wait_send()
        out_share(1 - p.k, g).wait_recv()
        out_share(p.k, g).wait_send()
        for c in range(p.chips):
            core_share(1 - p.k, c, g).wait_recv()
            core_share(p.k, c, g).wait_send()
        for c in others:
            chip_share(p.chip, g, c).wait_send()
            yc(g, c, p.chip).wait_send()
            over_chips(c, p.chip, g).wait_send()
    for c in others:
        qc(c, p.chip).wait_send()
        gc(c, p.chip).wait_send()
        out_chip(c, p.chip).wait_send()
    for g in line:
        zkv(p.a, g).wait_send()
        zq(p.a, g).wait_send()
        lc(p.a, g).wait_send()
        out_line(p.a, g).wait_send()
        out_back(p.a, g).wait_send()
    for s in range(GROUPS):

        @pl.when((p.a - s >= 0) & (p.a < last))
        def _():
            bc(p.a - s, p.a + 1, 2 * s).wait_send()
            line_share(p.a - s, p.a + 1, 2 * s).wait_send()

        @pl.when((p.a + s <= last) & (p.a > 0))
        def _():
            bc(p.a + s, p.a - 1, 2 * s + 1).wait_send()
            line_share(p.a + s, p.a - 1, 2 * s + 1).wait_send()

        if s > 0:

            @pl.when(p.a + s <= last)
            def _():
                rightward(p.a + s, red.at[0]).wait_send()

            @pl.when(p.a - s >= 0)
            def _():
                leftward(p.a - s, red.at[0]).wait_send()


def back(n, lens, q3, kv, o3, l3, dog, wg, h1, rp, gmid, gfull, dg2, ysum, go):
    rows, width = rp.shape
    quarter = width // 4
    lanes = wg.shape[2]
    chips = n // GROUPS // 2
    keys = kv.shape[0] // GROUPS
    piece = ysum.shape[2]
    orow = go.shape[0] // 2
    sds = jax.ShapeDtypeStruct
    v = pltpu.VMEM
    sem = lambda *shape: [DMA(shape), DMA(shape)]
    return pl.pallas_call(
        functools.partial(back_kernel, n),
        name="back",
        out_shape=(
            sds((rows, width), F32),
            sds((GROUPS, 2, quarter, lanes), BF16),
            sds((8, width), F32),
            sds((2, chips, GROUPS, piece, width), BF16),
            sds((2, GROUPS, orow // GROUPS, width), BF16),
        ),
        in_specs=[SM, VM, ANY, ANY, VM, VM, ANY] + [VM] * 5 + [ANY, VM],
        out_specs=[VM] * 5,
        scratch_shapes=[
            v((GROUPS, piece, width), BF16),
            v((GROUPS, piece, width), BF16),
            v(ysum.shape, BF16),
            v(q3.shape, BF16),
            v(q3.shape, F32),
            v((2 if keys <= SUB else 1, keys, 384), BF16),
            v((keys, 384), F32),
            v((keys, 384), BF16),
            v((GROUPS, chips, rows, 384), BF16),
            v((GROUPS, chips, rows, 384), BF16),
            v((GROUPS, width, lanes), BF16),
            v((GROUPS, rows, lanes), BF16),
            v((GROUPS, rows, lanes), BF16),
            v((width, lanes), F32),
            v((2, 2, quarter, lanes), BF16),
            v((2, quarter, lanes), BF16),
            v((chips, quarter, lanes), BF16),
            v((8, width), F32),
            v((8, width), F32),
            v((8, width), F32),
            v((chips, 8, width), F32),
            v((GROUPS, 8, width), F32),
            v((GROUPS, piece, width), BF16),
            v((GROUPS, piece, width), BF16),
            v((GROUPS, piece, width), BF16),
            v((GROUPS, piece, width), BF16),
            v((orow, width), BF16),
            v((orow, width), BF16),
            v((chips, orow, width), BF16),
            v((GROUPS, orow // GROUPS, width), BF16),
            v((GROUPS, orow // GROUPS, width), BF16),
            *sem(GROUPS),
            DMA((GROUPS + 2,)),
            DMA((2,)),
            *sem(GROUPS, chips),
            *sem(GROUPS + 1, chips),
            *sem(2 * GROUPS),
            *sem(GROUPS),
            *sem(4),
            *sem(chips),
            DMA((2 * GROUPS,)),
            DMA((GROUPS,)),
            *sem(GROUPS),
            *sem(GROUPS),
            *sem(GROUPS),
            DMA((2 * GROUPS,)),
            DMA((GROUPS,)),
            *sem(chips, GROUPS),
            *sem(chips, GROUPS),
            *sem(chips),
            *sem(2 * GROUPS),
            *sem(1 + GROUPS),
            *sem(chips, GROUPS),
        ],
        compiler_params=pltpu.CompilerParams(
            collective_id=2, has_side_effects=True, vmem_limit_bytes=67043328
        ),
    )(lens, q3, kv, o3, l3, dog, wg, h1, rp, gmid, gfull, dg2, ysum, go)


def deliver_kernel(gq, ra, rb, rd, goo, gsum, gin, out, out_, gin_, g1_, qkv_, go_, g2_, up_, down_):
    narrow = gin_.shape[2]
    half = g1_.shape[0]
    width = 2 * half
    out_[0] = out[:, :narrow]
    gin_[0] = gin[:, :narrow]
    go_[...] = goo[:, :narrow].astype(F32)
    down_[...] = rd[0, :, :narrow].astype(F32)
    up_[:, :width] = ra[0].astype(F32)
    up_[:, width:] = rb[0].astype(F32)
    first = lax.axis_index("fsdp") == 0
    g1_[...] = jnp.where(first, gsum[0, :half], gsum[0, half:])
    g2_[...] = jnp.where(first, gsum[1, :half], gsum[1, half:])
    low = low_half((gq.shape[1], 128))

    def tile(g, t):
        return gq[g, :, t * 128 : (t + 1) * 128].astype(F32)

    def swap(t):
        return pltpu.roll(t, HD, 1)

    for j in range(GROUPS // 2):
        a, b = 2 * j, 2 * j + 1
        parts = []
        for t in (0, 2):
            pair = swap(tile(b, t))
            parts.append(
                (tile(a, t), jnp.where(low, tile(a, t + 1), pair), jnp.where(low, pair, swap(tile(b, t + 1))))
            )
        pair = swap(tile(b, 4))
        parts.append(
            (tile(a, 4), jnp.where(low, swap(tile(a, 3)), pair), jnp.where(low, pair, tile(b, 3)))
        )
        for i, three in enumerate(parts):
            for t, value in enumerate(three):
                at = i * width + j * 384 + t * 128
                qkv_[:, at : at + 128] = value


def deliver(gq, res, goo, gsum, gin, out):
    rows, width = gin.shape
    half = width // 2
    ff = res.shape[1]
    steps = 4
    sds = jax.ShapeDtypeStruct
    spec = pl.BlockSpec
    return pl.pallas_call(
        deliver_kernel,
        name="deliver",
        grid=(steps,),
        out_shape=(
            sds((1, rows, width - 1), BF16),
            sds((1, rows, width - 1), F32),
            sds((half,), F32),
            sds((half, 3 * width), F32),
            sds((half, width - 1), F32),
            sds((half,), F32),
            sds((width, ff), F32),
            sds((ff, width - 1), F32),
        ),
        in_specs=[
            spec((GROUPS, half // steps, gq.shape[2]), lambda i: (0, i, 0)),
            spec((1, width // steps, width), lambda i: (0, i, 0)),
            spec((1, width // steps, width), lambda i: (0, steps + i, 0)),
            spec((1, ff // steps, width), lambda i: (1, i, 0)),
            spec((half // steps, width), lambda i: (i, 0)),
            spec(gsum.shape, lambda i: (0, 0)),
            spec((rows // steps, width), lambda i: (i, 0)),
            spec((rows // steps, width), lambda i: (i, 0)),
        ],
        out_specs=[
            spec((1, rows // steps, width - 1), lambda i: (0, i, 0)),
            spec((1, rows // steps, width - 1), lambda i: (0, i, 0)),
            spec((half,), lambda i: (0,)),
            spec((half // steps, 3 * width), lambda i: (i, 0)),
            spec((half // steps, width - 1), lambda i: (i, 0)),
            spec((half,), lambda i: (0,)),
            spec((width // steps, ff), lambda i: (i, 0)),
            spec((ff // steps, width - 1), lambda i: (i, 0)),
        ],
        compiler_params=pltpu.CompilerParams(vmem_limit_bytes=VLIM),
    )(gq, res, res, res, goo, gsum, gin, out)


def shards(n, resid, lengths, gain_one, w_qkv, w_out, gain_two, w_up, w_down, cotangent):
    width = resid.shape[2] + 1
    ff = w_up.shape[1]
    out, gmid, ysum, go, dog, dg2, rp, wg, h1, q3, kv, o3, l3, gfull = front(
        n, lengths, resid[0], cotangent[0], gain_one, gain_two, w_qkv, w_out, w_up, w_down
    )
    gin, gq, gsum, res, goo = back(
        n, lengths, q3, kv, o3, l3, dog, wg, h1, rp, gmid, gfull, dg2, ysum, go
    )

    half = width // 2
    return deliver(
        gq.reshape(GROUPS, half, -1), res.reshape(2, ff, width), goo.reshape(half, width), gsum, gin, out
    )


def solution(mesh):
    n = mesh.shape["ctx"]
    return jax.shard_map(
        functools.partial(shards, n),
        mesh=mesh,
        in_specs=(
            P("fsdp", "ctx", None),
            P("fsdp"),
            P("fsdp"),
            P("fsdp", None),
            P("fsdp", None),
            P("fsdp"),
            P(None, "fsdp"),
            P("fsdp", None),
            P("fsdp", "ctx", None),
        ),
        out_specs=(
            P("fsdp", "ctx", None),
            P("fsdp", "ctx", None),
            P("fsdp"),
            P("fsdp", None),
            P("fsdp", None),
            P("fsdp"),
            P(None, "fsdp"),
            P("fsdp", None),
        ),
        check_vma=False,
    )
```

```python
import functools

import jax
import jax.numpy as jnp
from jax import lax
from jax.experimental import pallas as pl
from jax.experimental.pallas import tpu as pltpu
from jax.sharding import PartitionSpec as P

F32 = jnp.float32
BF16 = jnp.bfloat16
MESH = pl.DeviceIdType.MESH
NT = (((1,), (1,)), ((), ()))
TN = (((0,), (0,)), ((), ()))
EPS = 1e-05
MASKED = -1e30
LOG2E = 1.4426950408889634
SCALE = 0.125
GROUPS = 4
GH = 3
HD = 64
SUB = 1024
VLIM = 60 * 1024 * 1024

VM = pl.BlockSpec(memory_space=pltpu.VMEM)
SM = pl.BlockSpec(memory_space=pltpu.SMEM)
ANY = pl.BlockSpec(memory_space=pl.ANY)
DMA = pltpu.SemaphoreType.DMA


def dot(a, b):
    return jnp.dot(a, b, preferred_element_type=F32)


def dg(a, b, dims):
    return lax.dot_general(a, b, dims, preferred_element_type=F32)


def rcopy(src, dst, send, recv, dev):
    return pltpu.make_async_remote_copy(
        src_ref=src, dst_ref=dst, send_sem=send, recv_sem=recv, device_id=dev, device_id_type=MESH
    )


class Place:
    def __init__(self, n):
        self.n = n
        self.m = n // GROUPS
        self.chips = self.m // 2
        c = lax.axis_index("ctx")
        self.x = lax.axis_index("fsdp")
        self.a = c // self.m
        self.b = c % self.m
        self.chip = self.b // 2
        self.k = self.b % 2

    def xpeer(self):
        return {"fsdp": 1 - self.x}

    def sibling(self):
        return {"ctx": self.a * self.m + self.chip * 2 + 1 - self.k}

    def on_chip(self, chip):
        return {"ctx": self.a * self.m + chip * 2 + self.k}

    def on_line(self, a):
        return {"ctx": a * self.m + self.b}


def greet(p, xpeer=False, sibling=False, chips=False, line=False):
    bar = pltpu.get_barrier_semaphore()
    count = 0
    if xpeer:
        pl.semaphore_signal(bar, inc=1, device_id=p.xpeer(), device_id_type=MESH)
        count += 1
    if sibling:
        pl.semaphore_signal(bar, inc=1, device_id=p.sibling(), device_id_type=MESH)
        count += 1
    if chips:
        for d in range(1, p.chips):
            pl.semaphore_signal(
                bar, inc=1, device_id=p.on_chip((p.chip + d) % p.chips), device_id_type=MESH
            )
            count += 1
    if line:
        for d in range(1, GROUPS):
            pl.semaphore_signal(
                bar, inc=1, device_id=p.on_line((p.a + d) % GROUPS), device_id_type=MESH
            )
            count += 1
    return lambda: pl.semaphore_wait(bar, count)


def turn(p, j):
    last = GROUPS - 1
    outer = jnp.where(p.a == 0, last - j, j)
    inner = (0, last, 1, last - 1)[j]
    return jnp.where((p.a == 0) | (p.a == last), outer, jnp.where(p.a == 1, last - inner, inner))


def ext_of(v):
    last = lax.broadcasted_iota(jnp.int32, v.shape, 1) == v.shape[1] - 1
    return jnp.where(last, -jnp.sum(v, axis=1, keepdims=True), v)


def inv_rms(u):
    return lax.rsqrt(jnp.mean(u * u, axis=1, keepdims=True) + EPS)


def crms_back(u, inv, gain, dy):
    dx = dy * gain
    du = inv * (dx - u * (inv * inv * jnp.mean(dx * u, axis=1, keepdims=True)))
    width = u.shape[1]
    last = lax.broadcasted_iota(jnp.int32, u.shape, 1) == width - 1
    return jnp.where(last, 0.0, du - du[:, width - 1 :])


def low_half(shape):
    return lax.broadcasted_iota(jnp.int32, shape, len(shape) - 1) < HD


def pack_tail(t):
    half = t.shape[0] // 2
    top, bottom = t[:half], t[half:]
    return jnp.where(low_half(top.shape), pltpu.roll(bottom, HD, 1), top)


def unpack_tail(t):
    low = low_half(t.shape)
    zero = jnp.zeros_like(t)
    return jnp.where(low, zero, t), jnp.where(low, zero, pltpu.roll(t, HD, 1))


def causal(shape, sub, size, first_query):
    col = lax.broadcasted_iota(jnp.int32, shape, 1) + sub * size
    row = lax.broadcasted_iota(jnp.int32, shape, 0) + first_query
    return col <= row


def gelu_both(a):
    c = 0.7978845608028654
    a2 = a * a
    t = jnp.tanh(c * a * (1.0 + 0.044715 * a2))
    half = 0.5 * (1.0 + t)
    slope = half + 0.5 * a * (1.0 - t * t) * (c * (1.0 + 0.134145 * a2))
    return a * half, slope


def group_columns(wq, wg):
    width = wq.shape[1] // 3
    low = low_half((wq.shape[0], 128))
    zero = jnp.zeros((wq.shape[0], 128), wq.dtype)

    def swap(t):
        return pltpu.roll(t, HD, 1)

    for j in range(GROUPS // 2):
        a, b = 2 * j, 2 * j + 1
        for i in range(3):
            at = i * width + j * 384
            t0, t1, t2 = (wq[:, at + 128 * t : at + 128 * t + 128] for t in range(3))
            pair = (t0, swap(jnp.where(low, t2, t1)))
            if i < 2:
                third = (jnp.where(low, t1, zero), jnp.where(low, swap(t2), zero))
                for g, p, t in zip((a, b), pair, third):
                    wg[g, :, i * 256 : i * 256 + 128] = p
                    wg[g, :, i * 256 + 128 : i * 256 + 256] = t
            else:
                third = (jnp.where(low, zero, swap(t1)), jnp.where(low, zero, t2))
                for g, p, t in zip((a, b), pair, third):
                    wg[g, :, 512:640] = p
                    wg[g, :, 384:512] = wg[g, :, 384:512] + t


def front_kernel(
    n, lens, ri, ci, g1, g2, wq, wo, wuh, wdh,
    out, gmid_, ysum_, y0, gb_, attg, dog, dg2, rp_, wg_, h1_, q3_, kv_, o3_, l3_, gfull,
    gmid, ysum, rp, wg, h1, q3, kv, o3, l3, gains, wop, wa, woa, wu, wdr, wd, att, wide, hid, gmb, act, gpre, esum, dsend, gb, mid, gk,
    ss, rs, ls, hs, hr, vs, kr, fs, xs, xr, cs, cr, ts, tr, as_, ar, ds_, dr, ks, ks_r, ys, yr, us,
):
    p = Place(n)
    rows, narrow = ri.shape
    width = narrow + 1
    half = width // 2
    ff = wuh.shape[1]
    pk = rows * 3 // 2
    keys = p.m * rows
    size = min(SUB, keys)
    subs = keys // size
    other = 1 - p.x
    others = [(p.chip + d) % p.chips for d in range(1, p.chips)]
    line = [(p.a + d) % GROUPS for d in range(1, GROUPS)]
    ready = greet(p, xpeer=True, sibling=True, chips=True, line=True)
    own_u = pltpu.make_async_copy(wuh, wu.at[p.x], ls.at[5])
    own_d = pltpu.make_async_copy(wdh, wdr.at[p.x], ls.at[6])
    own_u.start()
    own_d.start()

    leaving = []

    def leave(src, dst):
        c = pltpu.make_async_copy(src, dst, us.at[len(leaving)])
        c.start()
        leaving.append(c)

    gains[0:1, :] = g1[...].astype(F32).reshape(1, half)
    gains[1:2, :] = g2[...].astype(F32).reshape(1, half)
    gfull[p.x] = gains[...]
    ready()

    def xc(i, src, dst):
        return rcopy(src, dst, ss.at[i], rs.at[i], p.xpeer())

    at_x = pl.ds(pl.multiple_of(p.x * half, half), half)
    x_gain = xc(0, gains, gfull.at[p.x])
    x_gain.start()
    rp[:, :narrow] = ri[...]
    rp[:, narrow:] = jnp.zeros((rows, 1), BF16)
    u = ext_of(rp[...].astype(F32))
    normed = u * inv_rms(u)
    x_gain.wait()
    gain = jnp.concatenate([gfull[0, 0:1, :], gfull[1, 0:1, :]], axis=1)
    h1[p.a] = (normed * gain).astype(BF16)

    def line_copy(block, dst, sem):
        return rcopy(h1.at[block], h1.at[block], hs.at[sem], hr.at[block], p.on_line(dst))

    @pl.when(p.a < GROUPS - 1)
    def _():
        line_copy(p.a, p.a + 1, 0).start()

    @pl.when(p.a > 0)
    def _():
        line_copy(p.a, p.a - 1, 1).start()

    group_columns(wq, wg)
    x_wa = xc(1, wg.at[p.a], wa.at[at_x])
    x_wa.start()
    own_a = pltpu.make_async_copy(wg.at[p.a], wa.at[at_x], ls.at[0])
    own_a.start()
    leave(rp, rp_)
    leave(wg, wg_)

    def up_rows(j, chip, core):
        size_i = width // p.m // 3
        return pl.ds(pl.multiple_of(((chip * 2 + core) * 3 + j) * size_i, size_i), size_i)

    def up_x(j):
        at = up_rows(j, p.chip, p.k)
        return rcopy(wuh.at[at], wu.at[p.x, at], xs.at[j], xr.at[j], p.xpeer())

    def up_chip(j, owner, to):
        r = wu.at[other, up_rows(j, owner, p.k)]
        return rcopy(r, r, cs.at[j, to], cr.at[j, owner], p.on_chip(to))

    def up_core(j, owner, core):
        r = wu.at[other, up_rows(j, owner, core)]
        return rcopy(r, r, ts.at[j, owner], tr.at[j, owner], p.sibling())

    def up_spread(j):
        up_x(j).wait_recv()
        for c in others:
            up_chip(j, p.chip, c).start()
        up_core(j, p.chip, p.k).start()

    def up_pass(j):
        for c in others:
            up_chip(j, c, c).wait_recv()
            up_core(j, c, p.k).start()

    def down_rows(chip, core):
        size_i = ff // p.m
        return pl.ds(pl.multiple_of((chip * 2 + core) * size_i, size_i), size_i)

    def down_x():
        at = down_rows(p.chip, p.k)
        return rcopy(wdh.at[at], wdr.at[p.x, at], xs.at[3], xr.at[3], p.xpeer())

    def down_chip(owner, to):
        r = wdr.at[other, down_rows(owner, p.k)]
        return rcopy(r, r, cs.at[3, to], cr.at[3, owner], p.on_chip(to))

    def down_core(owner, core):
        r = wdr.at[other, down_rows(owner, core)]
        return rcopy(r, r, ts.at[3, owner], tr.at[3, owner], p.sibling())

    for j in range(3):
        up_x(j).start()
    down_x().start()

    wop[:, :narrow] = wo[...]
    wop[:, narrow:] = jnp.zeros((half, 1), BF16)
    xo = []
    local = []
    for i in range(2):
        g = p.x * 2 + i
        for j, (src, count, dst) in enumerate(((0, 128, 0), (128, 64, 192))):
            s_ = wop.at[pl.ds(i * 192 + src, count)]
            d_ = woa.at[pl.ds(pl.multiple_of(g * 256 + dst, 64), count)]
            xo.append(xc(2 + 2 * i + j, s_, d_))
            local.append(pltpu.make_async_copy(s_, d_, ls.at[1 + 2 * i + j]))
    zero_rows = jnp.zeros((HD, width), BF16)
    for g in range(GROUPS):
        woa[pl.ds(g * 256 + 128, HD), :] = zero_rows
    for c in xo:
        c.start()
    for c in local:
        c.start()
    slot = (p.a * p.m + p.b) * rows + lax.broadcasted_iota(jnp.int32, (rows, width), 0)
    live = slot < lens[0]
    gmb[0, :, :narrow] = ci[...]
    gmb[0, :, narrow:] = jnp.zeros((rows, 1), BF16)
    gmb[0] = jnp.where(live, gmb[0].astype(F32), 0.0).astype(BF16)
    x_gm = xc(6, gmb.at[0], gmb.at[1])
    x_gm.start()
    def kv_copy(block, b, dev, send):
        r = kv.at[pl.ds(pl.multiple_of((block * p.m + b) * rows, rows), rows)]
        return rcopy(r, r, send, kr.at[block, b], dev)

    def ac(i, to):
        return rcopy(att.at[to], attg.at[i], as_.at[to], ar.at[i], p.on_line(to))

    own_a.wait()
    x_wa.wait()

    def produce(block):
        y = dot(h1[block], wa[...]).astype(BF16)
        low = low_half((rows, 128))
        zero = jnp.zeros((rows, 128), BF16)
        at = pl.ds(pl.multiple_of(block * rows, rows), rows)
        q3[0, at, :] = jnp.where(low, y[:, :128], zero)
        q3[1, at, :] = jnp.where(low, zero, y[:, :128])
        q3[2, at, :] = y[:, 128:256]
        kv[pl.ds(pl.multiple_of((block * p.m + p.b) * rows, rows), rows), :] = y[:, 256:]
        for d in range(1, p.chips):
            kv_copy(block, p.b, p.on_chip((p.chip + d) % p.chips), vs.at[block, d]).start()
        kv_copy(block, p.b, p.sibling(), vs.at[block, 0]).start()

    def pass_on(block):
        for d in range(1, p.chips):
            b = ((p.chip + d) % p.chips) * 2 + p.k
            kv_copy(block, b, p.sibling(), fs.at[block, d]).wait_recv()
            kv_copy(block, b, p.sibling(), fs.at[block, d]).start()

    def complete(block):
        for c in range(p.chips):
            kv_copy(block, c * 2 + 1 - p.k, p.sibling(), vs.at[block, 0]).wait_recv()

    first_query = p.b * rows
    dead = jnp.where(lens[0] > keys, 0.0, 1.0).astype(F32)

    def pair(z, c, diagonal):
        at_q = pl.ds(pl.multiple_of(z * rows, rows), rows)
        gone = jnp.where(c > 0, dead, 0.0)
        for h in range(GH):
            kt = 128 * (h // 2)
            vt = 128 if h == 2 else 256
            q = q3[h, at_q, :]

            def keys_of(sub, first):
                at = pl.ds(pl.multiple_of(c * keys + sub * size, size), size)
                scores = dg(q, kv[at, kt : kt + 128], NT) * (SCALE * LOG2E)
                if diagonal:
                    scores = jnp.where(causal(scores.shape, sub, size, first_query), scores, MASKED)
                here = jnp.max(scores, axis=1, keepdims=True) + gone * MASKED
                if first:
                    newest = here
                else:
                    top = l3[h, at_q, 0:1]
                    newest = jnp.maximum(top, here)
                weights = jnp.exp2(scores - (newest - gone * (3.0 * MASKED)))
                sums = jnp.sum(weights, axis=1, keepdims=True)
                part = dot(weights.astype(BF16), kv[at, vt : vt + 128])
                if not first:
                    shrink = jnp.exp2(top - newest)
                    sums = sums + l3[h, at_q, HD : HD + 1] * shrink
                    part = part + o3[h, at_q, :] * shrink
                o3[h, at_q, :] = part
                l3[h, at_q, :] = jnp.where(low_half((rows, 128)), newest, sums)

            keys_of(0, diagonal)
            if subs > 1:

                def rest(sub, carry):
                    keys_of(sub, False)
                    return carry

                lax.fori_loop(1, subs, rest, 0)

    def finish_row(z):
        at_q = pl.ds(pl.multiple_of(z * rows, rows), rows)
        heads = []
        for h in range(GH):
            total = l3[h, at_q, HD : HD + 1]
            o = o3[h, at_q, :] / total
            o3[h, at_q, :] = o
            l3[h, at_q, :] = jnp.broadcast_to(l3[h, at_q, 0:1] + jnp.log2(total), (rows, 128))
            heads.append(o)
        att[z, 0:rows, :] = jnp.where(low_half((rows, 128)), heads[0], heads[1]).astype(BF16)
        att[z, rows:pk, :] = pack_tail(heads[2]).astype(BF16)

        @pl.when(z == p.a)
        def _():
            attg[z] = att[z]

        @pl.when(z != p.a)
        def _():
            ac(p.a, z).start()

    def far(z):
        return jnp.abs(z - p.a)

    def pairs(t):
        def row(z, carry):
            @pl.when(far(z) == t)
            def _():
                pair(z, z, True)

            def key(d, carry):
                @pl.when(jnp.maximum(far(z), far(z - d)) == t)
                def _():
                    pair(z, z - d, False)

                return carry

            lax.fori_loop(1, z + 1, key, 0)

            @pl.when(jnp.maximum(far(z), p.a) == t)
            def _():
                finish_row(z)

            return carry

        lax.fori_loop(0, GROUPS, row, 0)

    def step(s, carry):
        below = p.a - s
        above = p.a + s

        @pl.when((s > 0) & (below >= 0))
        def _():
            line_copy(below, p.a, 0).wait_recv()

            @pl.when(p.a < GROUPS - 1)
            def _():
                line_copy(below, p.a + 1, 2 * s).start()

        @pl.when((s > 0) & (above < GROUPS))
        def _():
            line_copy(above, p.a, 0).wait_recv()

            @pl.when(p.a > 0)
            def _():
                line_copy(above, p.a - 1, 2 * s + 1).start()

        @pl.when(below >= 0)
        def _():
            produce(below)

        @pl.when((s > 0) & (above < GROUPS))
        def _():
            produce(above)

        for j in range(3):

            @pl.when(s == j + 1)
            def _():
                up_spread(j)

        @pl.when(s == GROUPS)
        def _():
            down_x().wait_recv()
            for c in others:
                down_chip(p.chip, c).start()
            down_core(p.chip, p.k).start()

        @pl.when((s > 0) & (below + 1 >= 0))
        def _():
            pass_on(below + 1)
            complete(below + 1)

        @pl.when((s > 1) & (above - 1 < GROUPS))
        def _():
            pass_on(above - 1)
            complete(above - 1)

        @pl.when(s > 0)
        def _():
            pairs(s - 1)

        for j in range(3):

            @pl.when(s == j + 2)
            def _():
                up_pass(j)

        return carry

    lax.fori_loop(0, GROUPS + 1, step, 0)
    for src, dst in ((h1, h1_), (q3, q3_), (kv, kv_), (o3, o3_), (l3, l3_)):
        leave(src, dst)

    own_u.wait()
    own_d.wait()

    def pad_down(f):
        wd[f, :, :narrow] = wdr[f]
        wd[f, :, narrow:] = jnp.zeros((ff, 1), BF16)

    pad_down(p.x)
    for c in xo:
        c.wait()
    for c in local:
        c.wait()
    for g in line:
        ac(g, g).wait_recv()
    for g in range(GROUPS):
        wide[:, g * 256 : g * 256 + 128] = attg[g, 0:rows, :]
        top, bottom = unpack_tail(attg[g, rows:pk, :])
        wide[0 : rows // 2, g * 256 + 128 : g * 256 + 256] = top
        wide[rows // 2 : rows, g * 256 + 128 : g * 256 + 256] = bottom
    mid[...] = rp[...].astype(F32) + dot(wide[...], woa[...])
    u = ext_of(mid[...])
    gain = jnp.concatenate([gfull[0, 1:2, :], gfull[1, 1:2, :]], axis=1)
    hid[0] = (u * inv_rms(u) * gain).astype(BF16)
    x_hid = xc(9, hid.at[0], hid.at[1])
    x_hid.start()
    tiles = ff // 256

    def up(slot, token, f):
        def tile(t, carry):
            at = pl.ds(pl.multiple_of(t * 256, 256), 256)
            a, slope = gelu_both(dot(hid[token], wu[f, :, at]))
            act[slot, :, at] = a.astype(BF16)
            gpre[slot, :, at] = (slope * dg(gmb[token], wd[f, at, :], NT)).astype(BF16)
            return carry

        lax.fori_loop(0, tiles, tile, 0)

    up(0, 0, p.x)
    for c in others:
        down_chip(c, c).wait_recv()
        down_core(c, p.k).start()
    for j in range(3):
        for c in range(p.chips):
            up_core(j, c, 1 - p.k).wait_recv()
    for c in range(p.chips):
        down_core(c, 1 - p.k).wait_recv()
    pad_down(other)
    up(2, 0, other)

    def e_tile(t, carry):
        at = pl.ds(pl.multiple_of(t * 256, 256), 256)
        e = dg(gpre[0], wu[p.x, at, :], NT) + dg(gpre[2], wu[other, at, :], NT)
        esum[t] = e
        return carry

    lax.fori_loop(0, width // 256, e_tile, 0)
    e = jnp.concatenate([esum[t] for t in range(width // 256)], axis=1)
    u = ext_of(mid[...])
    inv = inv_rms(u)
    gmid[...] = gmb[0].astype(F32) + crms_back(u, inv, gain, e)
    leave(gmid, gmid_)
    gb[...] = gmid[...].astype(BF16)
    leave(gb, gb_)

    def dc(i, to):
        return rcopy(dsend.at[to], dog.at[i], ds_.at[to], dr.at[i], p.on_line(to))

    for d in range(1, GROUPS + 1):
        to = (p.a + d) % GROUPS
        w = woa[pl.ds(pl.multiple_of(to * 256, 256), 256), :]
        da = dg(gb[...], w, NT).astype(BF16)
        if d < GROUPS:
            dsend[to, 0:rows, :] = da[:, 0:128]
            dsend[to, rows:pk, :] = pack_tail(da[:, 128:256])
            dc(p.a, to).start()
        else:
            dog[to, 0:rows, :] = da[:, 0:128]
            dog[to, rows:pk, :] = pack_tail(da[:, 128:256])
    x_gm.wait()
    x_hid.wait()
    up(1, 1, p.x)
    final = mid[...] + dot(act[0], wd[p.x]) + dot(act[2], wd[other])
    out[...] = final.astype(BF16)

    gm = wd
    piece = ysum.shape[2]
    part = GROUPS * piece

    def kc(chip):
        at = pl.ds(pl.multiple_of(chip * part, part), part)
        return rcopy(gm.at[1 - p.k, at], gk.at[at], ks.at[chip], ks_r.at[chip], p.sibling())

    def grad_up(t, carry):
        at = pl.ds(pl.multiple_of(t * 256, 256), 256)
        g = dg(hid[0], gpre[0, :, at], TN) + dg(hid[1], gpre[1, :, at], TN)
        per = width // 256
        r0 = pl.multiple_of((t // per) * width, width)
        c0 = pl.multiple_of((t % per) * 256, 256)
        gm[0, pl.ds(r0, width), pl.ds(c0, 256)] = g.astype(BF16)
        return carry

    def grad_down(t, carry):
        at = pl.ds(pl.multiple_of(t * 256, 256), 256)
        g = dg(act[0, :, at], gmb[0], TN) + dg(act[1, :, at], gmb[1], TN)
        gm[1, at, :] = g.astype(BF16)
        return carry

    @pl.when(p.k == 0)
    def _():
        lax.fori_loop(0, tiles, grad_down, 0)

    @pl.when(p.k == 1)
    def _():
        lax.fori_loop(0, tiles, grad_up, 0)

    for c in others:
        kc(c).start()
    kc(p.chip).start()

    @pl.when(p.k == 0)
    def _():
        lax.fori_loop(0, tiles, grad_up, 0)

    @pl.when(p.k == 1)
    def _():
        lax.fori_loop(0, tiles, grad_down, 0)

    def over_chips(chip, slot):
        return rcopy(ysum.at[chip, turn(p, 0)], y0.at[slot], ys.at[chip], yr.at[slot], p.on_chip(chip))

    def core_sum(chip, z):
        at = pl.ds(pl.multiple_of(chip * part + z * piece, 16), piece)
        ysum[chip, z] = (gm[p.k, at, :].astype(F32) + gk[at, :].astype(F32)).astype(BF16)

    for chip in others:
        kc(chip).wait()
        core_sum(chip, turn(p, 0))
        over_chips(chip, p.chip).start()
    for j in range(1, GROUPS):
        for chip in others:
            core_sum(chip, turn(p, j))
    kc(p.chip).wait()
    for j in range(GROUPS):
        core_sum(p.chip, turn(p, j))
    y0[p.chip] = ysum[p.chip, turn(p, 0)]
    leave(ysum, ysum_)
    dg2[...] = jnp.broadcast_to(jnp.sum(e * (u * inv), axis=0, keepdims=True), dg2.shape)

    for c in others:
        over_chips(c, p.chip).wait_send()
        over_chips(c, c).wait_recv()
    for g in line:
        ac(p.a, g).wait_send()
        dc(p.a, g).wait_send()
        dc(g, g).wait_recv()
    for block in range(GROUPS):
        kv_copy(block, p.b, p.sibling(), vs.at[block, 0]).wait_send()
        for d in range(1, p.chips):
            kv_copy(block, p.b, p.sibling(), vs.at[block, d]).wait_send()
            b = ((p.chip + d) % p.chips) * 2
            kv_copy(block, b + p.k, p.sibling(), fs.at[block, d]).wait_send()
    for s in range(GROUPS):

        @pl.when((p.a - s >= 0) & (p.a < GROUPS - 1))
        def _():
            line_copy(p.a - s, p.a + 1, 2 * s).wait_send()

        @pl.when((p.a + s < GROUPS) & (p.a > 0))
        def _():
            line_copy(p.a + s, p.a - 1, 2 * s + 1).wait_send()

    for j in range(3):
        up_x(j).wait_send()
        for c in others:
            up_chip(j, p.chip, c).wait_send()
        for c in range(p.chips):
            up_core(j, c, p.k).wait_send()
    down_x().wait_send()
    for c in others:
        down_chip(p.chip, c).wait_send()
    for c in range(p.chips):
        down_core(c, p.k).wait_send()
    for c in leaving:
        c.wait()


def front(n, lens, ri, ci, g1, g2, wq, wo, wu, wd):
    rows, narrow = ri.shape
    width = narrow + 1
    half = width // 2
    ff = wu.shape[1]
    pk = rows * 3 // 2
    m = n // GROUPS
    chips = m // 2
    piece = ff // GROUPS // chips
    lanes = 640
    sds = jax.ShapeDtypeStruct
    v = pltpu.VMEM
    heads = (GH, GROUPS * rows, 128)
    sem = lambda *shape: [DMA(shape), DMA(shape)]
    return pl.pallas_call(
        functools.partial(front_kernel, n),
        name="front",
        out_shape=(
            sds((rows, width), BF16),
            sds((rows, width), F32),
            sds((chips, GROUPS, piece, width), BF16),
            sds((chips, piece, width), BF16),
            sds((rows, width), BF16),
            sds((GROUPS, pk, 128), BF16),
            sds((GROUPS, pk, 128), BF16),
            sds((8, width), F32),
            sds((rows, width), BF16),
            sds((GROUPS, half, lanes), BF16),
            sds((GROUPS, rows, width), BF16),
            sds(heads, BF16),
            sds((n * rows, 384), BF16),
            sds(heads, F32),
            sds(heads, F32),
            sds((2, 8, half), F32),
        ),
        in_specs=[SM, VM, VM, VM, VM, VM, VM, ANY, ANY],
        out_specs=[VM, ANY, ANY, VM, ANY] + [VM] * 3 + [ANY] * 7 + [VM],
        scratch_shapes=[
            v((rows, width), F32),
            v((chips, GROUPS, piece, width), BF16),
            v((rows, width), BF16),
            v((GROUPS, half, lanes), BF16),
            v((GROUPS, rows, width), BF16),
            v(heads, BF16),
            v((n * rows, 384), BF16),
            v(heads, F32),
            v(heads, F32),
            v((8, half), F32),
            v((half, width), BF16),
            v((width, lanes), BF16),
            v((GROUPS * 256, width), BF16),
            v((2, width, ff), BF16),
            v((2, ff, narrow), BF16),
            v((2, ff, width), BF16),
            v((GROUPS, pk, 128), BF16),
            v((rows, GROUPS * 256), BF16),
            v((2, rows, width), BF16),
            v((2, rows, width), BF16),
            v((3, rows, ff), BF16),
            v((3, rows, ff), BF16),
            v((width // 256, rows, 256), F32),
            v((GROUPS, pk, 128), BF16),
            v((rows, width), BF16),
            v((rows, width), F32),
            v((ff, width), BF16),
            *sem(10),
            DMA((7,)),
            DMA((2 * GROUPS,)),
            DMA((GROUPS,)),
            DMA((GROUPS, chips)),
            DMA((GROUPS, m)),
            DMA((GROUPS, chips)),
            *sem(4),
            *sem(4, chips),
            *sem(4, chips),
            *sem(GROUPS),
            *sem(GROUPS),
            *sem(chips),
            *sem(chips),
            DMA((10,)),
        ],
        compiler_params=pltpu.CompilerParams(
            collective_id=0, has_side_effects=True, vmem_limit_bytes=67043328
        ),
    )(lens, ri, ci, g1, g2, wq, wo, wu, wd)


def back_kernel(
    n, lens, q3, kv, o3, l3, dog, wg, h1_, rp_, gmid_, gfull, dg2, ysum, y0, gb_, att_,
    gin, gq, gains, res, goo,
    h1, rp, gmid, go, gb, att, red, ymine, yq, do3, dq3, kvc, dkv, dkvb, rk, ry, wfull, gps, gpr, gqb, qk, qx, qy,
    g0, gk, gx, gy, ga, left, right, sumr, suml, ok, os_, oy, oz, ozr,
    xs, xr, ls, vs, ks, kr, ys, yr, zs, zr, ws, wr, qs, qr, ns, nr, bs, br, cs, cr,
    rs_, rr, ls_, lr, as_, ar, es, er, fs, fr, ts, tr, us, ur, is_, ir, ps, pr, ws2, wr2, zs2, zr2,
):
    p = Place(n)
    rows, width = rp_.shape
    half = width // 2
    quarter = width // 4
    last = GROUPS - 1
    keys = dkv.shape[0]
    size = min(SUB, keys)
    subs = keys // size
    slots = kvc.shape[0]
    others = [(p.chip + d) % p.chips for d in range(1, p.chips)]
    line = [(p.a + d) % GROUPS for d in range(1, GROUPS)]
    ready = greet(p, xpeer=True, sibling=True, chips=True, line=True)
    at_x = pl.ds(pl.multiple_of(p.x * half, half), half)
    local = [
        pltpu.make_async_copy(wg.at[g], wfull.at[g, at_x], ls.at[g]) for g in range(GROUPS)
    ]

    def chunk_of(i):
        return (p.a + 1 + i) % GROUPS

    def fetch(i):
        c = chunk_of(i)
        src = kv.at[pl.ds(pl.multiple_of(c * keys, keys), keys)]
        return pltpu.make_async_copy(src, kvc.at[i % slots], vs.at[i % slots])

    fetch(0).start()
    o_in = pltpu.make_async_copy(o3, dq3, ls.at[GROUPS])
    o_in.start()
    y_in = pltpu.make_async_copy(ysum.at[p.chip], ymine, ls.at[GROUPS + 1])
    y_in.start()
    late = [
        pltpu.make_async_copy(src, dst, ls.at[GROUPS + 2 + i])
        for i, (src, dst) in enumerate(((h1_, h1), (rp_, rp), (gmid_, gmid)))
    ]
    for c in late:
        c.start()
    gos = [
        pltpu.make_async_copy(src, dst, ls.at[GROUPS + 5 + i])
        for i, (src, dst) in enumerate(((gb_, gb.at[0]), (att_.at[pl.ds(p.x * 2, 2)], att.at[0])))
    ]
    for c in gos:
        c.start()
    gox = [
        rcopy(src, dst, zs2.at[i], zr2.at[i], p.xpeer())
        for i, (src, dst) in enumerate(((gb_, gb.at[1]), (att_.at[pl.ds((1 - p.x) * 2, 2)], att.at[1])))
    ]
    for c in local:
        c.start()

    def weight_rows(x, core):
        return pl.ds(pl.multiple_of(x * half + core * quarter, quarter), quarter)

    def weight_x(g):
        src = wg.at[g, pl.ds(pl.multiple_of(p.k * quarter, quarter), quarter)]
        return rcopy(src, wfull.at[g, weight_rows(p.x, p.k)], xs.at[g], xr.at[g], p.xpeer())

    def weight_core(g, core):
        r = wfull.at[g, weight_rows(1 - p.x, core)]
        return rcopy(r, r, ws2.at[g], wr2.at[g], p.sibling())

    def over_chips(chip, slot, z):
        return rcopy(ysum.at[chip, z], yq.at[slot, z], ps.at[chip, z], pr.at[slot, z], p.on_chip(chip))

    def chip_sum(j):
        z = turn(p, j)
        total = ymine[z].astype(F32)
        for c in others:
            if j > 0:
                over_chips(c, c, z).wait_recv()
                total = total + yq[c, z].astype(F32)
            else:
                total = total + y0[c].astype(F32)
        red[z] = total.astype(BF16)
        if j < last:

            @pl.when(p.a == 0)
            def _():
                rightward(z, red.at[z]).start()

            @pl.when(p.a == last)
            def _():
                leftward(z, red.at[z]).start()

    def rightward(z, src):
        return rcopy(src, left.at[z], rs_.at[z], rr.at[z], p.on_line(p.a + 1))

    def leftward(z, src):
        return rcopy(src, right.at[z], ls_.at[z], lr.at[z], p.on_line(p.a - 1))

    def reduce_step(s):
        @pl.when((p.a >= 1) & (p.a <= s))
        def _():
            z = last + p.a - s
            rightward(z, sumr.at[z]).wait_recv()
            if s < last:
                sumr[z] = (red[z].astype(F32) + left[z].astype(F32)).astype(BF16)
                rightward(z, sumr.at[z]).start()

        b = last - p.a

        @pl.when((b >= 1) & (b <= s))
        def _():
            z = s - b
            leftward(z, suml.at[z]).wait_recv()
            if s < last:
                suml[z] = (red[z].astype(F32) + right[z].astype(F32)).astype(BF16)
                leftward(z, suml.at[z]).start()

    def line_share(z, dst, sem):
        r = res.at[p.k, p.chip, z]
        return rcopy(r, r, as_.at[sem], ar.at[z], p.on_line(dst))

    def chip_share(chip, z, dst):
        r = res.at[p.k, chip, z]
        return rcopy(r, r, es.at[dst, z], er.at[chip, z], p.on_chip(dst))

    def core_share(core, chip, z):
        r = res.at[core, chip, z]
        return rcopy(r, r, fs.at[chip, z], fr.at[chip, z], p.sibling())

    def spread(z):
        for c in others:
            chip_share(p.chip, z, c).start()
        core_share(p.k, p.chip, z).start()

    def gather_first():
        z = p.a
        res[p.k, p.chip, z] = red[z]

        @pl.when(p.a > 0)
        def _():
            cur = res[p.k, p.chip, z].astype(F32)
            res[p.k, p.chip, z] = (cur + left[z].astype(F32)).astype(BF16)

        @pl.when(p.a < last)
        def _():
            cur = res[p.k, p.chip, z].astype(F32)
            res[p.k, p.chip, z] = (cur + right[z].astype(F32)).astype(BF16)
            line_share(z, p.a + 1, 0).start()

        @pl.when(p.a > 0)
        def _():
            line_share(z, p.a - 1, 1).start()

    def gather_step(s):
        @pl.when(p.a - s >= 0)
        def _():
            line_share(p.a - s, p.a, 0).wait_recv()

            @pl.when(p.a < last)
            def _():
                line_share(p.a - s, p.a + 1, 2 * s).start()

            spread(p.a - s)

        @pl.when(p.a + s <= last)
        def _():
            line_share(p.a + s, p.a, 0).wait_recv()

            @pl.when(p.a > 0)
            def _():
                line_share(p.a + s, p.a - 1, 2 * s + 1).start()

            spread(p.a + s)

    def pass_on(z):
        for c in others:
            chip_share(c, z, c).wait_recv()
            core_share(p.k, c, z).start()

    orow = half // 2
    opart = orow // GROUPS

    def out_core():
        at = pl.ds(pl.multiple_of((1 - p.k) * orow, orow), orow)
        return rcopy(go.at[at], ok, is_.at[0], ir.at[0], p.sibling())

    def out_line(slot, to):
        return rcopy(oz.at[to], ozr.at[slot], us.at[to], ur.at[slot], p.on_line(to))

    def out_chip(chip, slot):
        return rcopy(os_, oy.at[slot], ts.at[chip], tr.at[slot], p.on_chip(chip))

    def out_back(slot, to):
        r = goo.at[p.k, slot]
        return rcopy(r, r, us.at[GROUPS + to], ur.at[GROUPS + slot], p.on_line(to))

    def out_share(core, z):
        r = goo.at[core, z]
        return rcopy(r, r, is_.at[1 + z], ir.at[1 + z], p.sibling())

    def out_0():
        for c in gos + gox:
            c.wait()
        for i in range(2):
            tails = [jnp.concatenate(unpack_tail(att[s, i, rows:, :]), axis=0) for s in range(2)]
            g = dg(att[0, i, 0:rows, :], gb[0], TN) + dg(att[1, i, 0:rows, :], gb[1], TN)
            go[i * 192 : i * 192 + 128, :] = g.astype(BF16)
            g = dg(tails[0], gb[0], TN) + dg(tails[1], gb[1], TN)
            go[i * 192 + 128 : i * 192 + 192, :] = g[HD:, :].astype(BF16)
        out_core().start()

    def out_1():
        out_core().wait()
        at = pl.ds(pl.multiple_of(p.k * orow, orow), orow)
        total = go[at, :].astype(F32) + ok[...].astype(F32)
        for z in range(GROUPS):
            oz[z] = total[z * opart : (z + 1) * opart].astype(BF16)
        for z in line:
            out_line(p.a, z).start()

    def out_2():
        total = oz[p.a].astype(F32)
        for z in line:
            out_line(z, z).wait_recv()
            total = total + ozr[z].astype(F32)
        os_[...] = total.astype(BF16)
        for c in others:
            out_chip(c, p.chip).start()

    def out_3():
        total = os_[...].astype(F32)
        for c in others:
            out_chip(c, c).wait_recv()
            total = total + oy[c].astype(F32)
        goo[p.k, p.a] = total.astype(BF16)
        for z in line:
            out_back(p.a, z).start()
        out_share(p.k, p.a).start()

    def kc(i, chip):
        c = chunk_of(i)
        at = pl.ds(pl.multiple_of((chip * 2 + 1 - p.k) * rows, rows), rows)
        return rcopy(
            dkvb.at[at], rk.at[c, chip], ks.at[c, chip], kr.at[c, chip], p.sibling()
        )

    def yc(c, chip, slot):
        return rcopy(rk.at[c, chip], ry.at[c, slot], ys.at[c, chip], yr.at[c, slot], p.on_chip(chip))

    def zkv(slot, to):
        lanes = pl.ds(256, 384)
        return rcopy(
            gps.at[to, :, lanes], gpr.at[slot, :, lanes], zs.at[to], zr.at[slot], p.on_line(to)
        )

    def zq(slot, to):
        lanes = pl.ds(0, 256)
        return rcopy(
            gps.at[to, :, lanes], gpr.at[slot, :, lanes], ws.at[to], wr.at[slot], p.on_line(to)
        )

    def mine(chip):
        at = pl.ds(pl.multiple_of((chip * 2 + p.k) * rows, rows), rows)
        return dkvb[at, :].astype(F32)

    def kv_1(i):
        dkvb[...] = dkv[...].astype(BF16)
        for c in others:
            kc(i, c).start()
        kc(i, p.chip).start()

    def kv_2(i):
        c = chunk_of(i)
        for chip in others:
            kc(i, chip).wait()
            rk[c, chip] = (mine(chip) + rk[c, chip].astype(F32)).astype(BF16)
            yc(c, chip, p.chip).start()
        kc(i, p.chip).wait()
        rk[c, p.chip] = (mine(p.chip) + rk[c, p.chip].astype(F32)).astype(BF16)

    def kv_3(i, send):
        c = chunk_of(i)
        total = rk[c, p.chip].astype(F32)
        for chip in others:
            yc(c, chip, chip).wait_recv()
            total = total + ry[c, chip].astype(F32)
        gps[c, :, 256:640] = total.astype(BF16)
        if send:
            zkv(p.a, c).start()

    ready()
    for j in range(1, last):
        for c in others:
            over_chips(c, p.chip, turn(p, j)).start()
    for c in gox:
        c.start()
    for g in range(GROUPS):
        weight_x(g).start()

    first_query = p.b * rows
    low = low_half((rows, 128))
    o_in.wait()
    y_in.wait()
    chip_sum(0)
    for z in range(GROUPS):
        at = pl.ds(z * rows, rows)
        both = dog[z, 0:rows, :]
        zero = jnp.zeros_like(both)
        do3[0, at, :] = jnp.where(low, both, zero)
        do3[1, at, :] = jnp.where(low, zero, both)
        top, bottom = unpack_tail(dog[z, rows:, :])
        do3[2, pl.ds(z * rows, rows // 2), :] = top
        do3[2, pl.ds(z * rows + rows // 2, rows // 2), :] = bottom
        for h in range(GH):
            delta = jnp.sum(dq3[h, at, :] * do3[h, at, :].astype(F32), axis=1, keepdims=True)
            gqb[h * rows : (h + 1) * rows, z * 128 : (z + 1) * 128] = jnp.broadcast_to(delta, (rows, 128))
    dq3[...] = jnp.zeros_like(dq3)
    gone = jnp.where(lens[0] > keys, 0.0, -MASKED).astype(F32)

    def chunk(i, carry):
        c = chunk_of(i)
        fetch(i).wait()

        if slots > 1:

            @pl.when(i < last)
            def _():
                fetch(i + 1).start()

        dead = jnp.where(c > 0, gone, 0.0)

        def head(h, carry):
            kt = pl.multiple_of(128 * (h // 2), 128)
            vt = pl.multiple_of(jnp.where(h == 2, 128, 256), 128)

            def step(z, masked):
                at_q = pl.ds(pl.multiple_of(z * rows, rows), rows)
                q = q3[h, at_q, :]
                do = do3[h, at_q, :]
                lse = l3[h, at_q, 0:1] + dead
                delta = gqb[
                    pl.ds(pl.multiple_of(h * rows, rows), rows),
                    pl.ds(pl.multiple_of(z * 128, 128), 128),
                ][:, 0:1]
                def keys_of(sub, carry):
                    at = pl.ds(pl.multiple_of(sub * size, size), size)
                    k = kvc[i % slots, at, pl.ds(kt, 128)]
                    v = kvc[i % slots, at, pl.ds(vt, 128)]
                    scores = dg(q, k, NT) * (SCALE * LOG2E)
                    if masked:
                        scores = jnp.where(
                            causal(scores.shape, sub, size, first_query), scores, MASKED
                        )
                    weights = jnp.exp2(scores - lse)
                    gp = dg(do, v, NT)
                    gs = (weights * (gp - delta)).astype(BF16)
                    dq3[h, at_q, :] += dot(gs, k)
                    gv = dg(weights.astype(BF16), do, TN)
                    gk_ = dg(gs, q, TN) * SCALE
                    if masked:
                        dkv[at, pl.ds(kt, 128)] = jnp.where(h == 1, dkv[at, pl.ds(kt, 128)], 0.0) + gk_
                        dkv[at, pl.ds(vt, 128)] = jnp.where(h == 0, 0.0, dkv[at, pl.ds(vt, 128)]) + gv
                    else:
                        dkv[at, pl.ds(kt, 128)] += gk_
                        dkv[at, pl.ds(vt, 128)] += gv
                    return carry

                if subs > 1:
                    lax.fori_loop(0, subs, keys_of, 0)
                else:
                    keys_of(0, 0)

            step(c, True)

            def rest(z, carry):
                step(z, False)
                return carry

            lax.fori_loop(c + 1, GROUPS, rest, 0)

            @pl.when(h == 0)
            def _():
                @pl.when(i >= 1)
                def _():
                    kv_2(i - 1)

                @pl.when(i == 1)
                def _():
                    for c in others:
                        over_chips(c, p.chip, turn(p, last)).start()
                    chip_sum(1)
                    reduce_step(1)

                @pl.when(i == 2)
                def _():
                    reduce_step(2)

                @pl.when(i == 3)
                def _():
                    chip_sum(3)
                    reduce_step(3)
                    gather_first()

            @pl.when((h == 1) & (i >= 2))
            def _():
                kv_3(i - 2, True)

            @pl.when(h == 2)
            def _():
                @pl.when(i == 1)
                def _():
                    chip_sum(2)
                    out_0()

                @pl.when(i == 2)
                def _():
                    out_1()

                @pl.when(i == last)
                def _():
                    for g in range(GROUPS):
                        weight_x(g).wait_recv()
                        weight_core(g, p.k).start()

            return carry

        lax.fori_loop(0, GH, head, 0)
        if slots == 1:

            @pl.when(i < last)
            def _():
                fetch(i + 1).start()

        kv_1(i)
        return carry

    lax.fori_loop(0, GROUPS, chunk, 0)
    kv_2(3)
    spread(p.a)
    kv_3(2, True)
    for d in range(1, GROUPS + 1):
        z = (p.a + d) % GROUPS
        at = pl.ds(pl.multiple_of(z * rows, rows), rows)
        gps[z, :, 0:128] = (jnp.where(low, dq3[0, at, :], dq3[1, at, :]) * SCALE).astype(BF16)
        gps[z, :, 128:256] = (jnp.where(low, dq3[2, at, :], 0.0) * SCALE).astype(BF16)
        if d < GROUPS:
            zq(p.a, z).start()

    def rows_of(i, core):
        return pl.ds(pl.multiple_of(i * half + core * quarter, quarter), quarter)

    for c in late:
        c.wait()
    for t in range(width // 256):
        at = pl.ds(t * 256, 256)
        gqb[at, 0:256] = dg(h1[p.a, :, at], gps[p.a, :, 0:256], TN)
        gqb[at, 256:640] = jnp.zeros((256, 384), F32)

    def rowdot(d, carry):
        z = (p.a + d) % GROUPS
        for t in range(width // 256):
            at = pl.ds(t * 256, 256)
            gqb[at, :] += dg(h1[z, :, at], gps[z], TN)
        return carry

    lax.fori_loop(1, GROUPS, rowdot, 0)
    gather_step(1)
    kv_3(3, False)
    gpr[p.a] = gps[p.a]
    for t in range(width // 256):
        at = pl.ds(t * 256, 256)
        gqb[at, 256:640] += dg(h1[p.a, :, at], gps[p.a, :, 256:640], TN)
    for i in range(2):
        qk[0, i] = gqb[rows_of(i, 1 - p.k), :].astype(BF16)
    q_k = rcopy(qk.at[0], qk.at[1], qs.at[0], qr.at[0], p.sibling())
    q_k.start()
    for c in local:
        c.wait()
    q_k.wait()
    for i in range(2):
        gqb[rows_of(i, p.k), :] += qk[1, i].astype(F32)
    qx[0] = gqb[rows_of(1 - p.x, p.k), :].astype(BF16)
    q_x = rcopy(qx.at[0], qx.at[1], qs.at[1], qr.at[1], p.xpeer())
    q_x.start()
    out_2()
    q_x.wait()
    gqb[rows_of(p.x, p.k), :] += qx[1].astype(F32)
    qy[p.chip] = gqb[rows_of(p.x, p.k), :].astype(BF16)

    def qc(chip, slot):
        return rcopy(qy.at[p.chip], qy.at[slot], ns.at[chip], nr.at[slot], p.on_chip(chip))

    for c in others:
        qc(c, p.chip).start()
    gather_step(2)
    for g in range(GROUPS):
        weight_core(g, 1 - p.k).wait_recv()
        weight_core(g, p.k).wait_send()
        weight_x(g).wait_send()
    h = dg(gpr[p.a], wfull[p.a], NT)
    for g in line:
        zkv(g, g).wait_recv()
        zq(g, g).wait_recv()
        h = h + dg(gpr[g], wfull[g], NT)
    total = gqb[rows_of(p.x, p.k), :]
    for c in others:
        qc(c, c).wait_recv()
        total = total + qy[c].astype(F32)
    gq[p.a, p.k] = total.astype(BF16)

    def bc(slot, to, sem):
        r = gq.at[slot, p.k]
        return rcopy(r, r, bs.at[sem], br.at[slot], p.on_line(to))

    def sc(slot, core):
        return rcopy(gq.at[slot, core], gq.at[slot, core], cs.at[slot], cr.at[slot], p.sibling())

    @pl.when(p.a < last)
    def _():
        bc(p.a, p.a + 1, 0).start()

    @pl.when(p.a > 0)
    def _():
        bc(p.a, p.a - 1, 1).start()

    sc(p.a, p.k).start()
    out_3()
    u = ext_of(rp[...].astype(F32))
    inv = inv_rms(u)
    gain = jnp.concatenate([gfull[0, 0:1, :], gfull[1, 0:1, :]], axis=1)
    result = gmid[...] + crms_back(u, inv, gain, h)
    gin[...] = result.T
    first = jnp.sum(h * (u * inv), axis=0, keepdims=True)
    which = lax.broadcasted_iota(jnp.int32, (8, width), 0)
    g0[...] = jnp.where(which == 0, first, dg2[...])
    g_k = rcopy(g0, gk, qs.at[2], qr.at[2], p.sibling())
    g_k.start()
    gather_step(3)
    g_k.wait()
    g0[...] += gk[...]
    g_x = rcopy(g0, gx, qs.at[3], qr.at[3], p.xpeer())
    g_x.start()
    for s in range(1, GROUPS):

        @pl.when(p.a - s >= 0)
        def _():
            bc(p.a - s, p.a, 0).wait_recv()

            @pl.when(p.a < last)
            def _():
                bc(p.a - s, p.a + 1, 2 * s).start()

            sc(p.a - s, p.k).start()

        @pl.when(p.a + s <= last)
        def _():
            bc(p.a + s, p.a, 0).wait_recv()

            @pl.when(p.a > 0)
            def _():
                bc(p.a + s, p.a - 1, 2 * s + 1).start()

            sc(p.a + s, p.k).start()

        if s == 1:
            g_x.wait()
            gy[p.chip] = g0[...] + gx[...]

            def gc(chip, slot):
                return rcopy(
                    gy.at[p.chip], gy.at[slot], ys.at[GROUPS, chip], yr.at[GROUPS, slot],
                    p.on_chip(chip),
                )

            for c in others:
                gc(c, p.chip).start()
        if s == 2:
            for z in range(GROUPS):
                pass_on(z)
            for c in others:
                gc(c, c).wait_recv()
            total = gy[0]
            for c in range(1, p.chips):
                total = total + gy[c]
            ga[p.a] = total

            def lc(slot, to):
                return rcopy(
                    ga.at[p.a], ga.at[slot], zs.at[GROUPS + to], zr.at[GROUPS + slot], p.on_line(to)
                )

            for g in line:
                lc(p.a, g).start()
    for g in line:
        lc(g, g).wait_recv()
    total = ga[0]
    for g in range(1, GROUPS):
        total = total + ga[g]
    gains[...] = total
    for g in line:
        out_back(g, g).wait_recv()
        out_share(p.k, g).start()
    for g in range(GROUPS):
        sc(g, 1 - p.k).wait_recv()
        sc(g, p.k).wait_send()
        out_share(1 - p.k, g).wait_recv()
        out_share(p.k, g).wait_send()
        for c in range(p.chips):
            core_share(1 - p.k, c, g).wait_recv()
            core_share(p.k, c, g).wait_send()
        for c in others:
            chip_share(p.chip, g, c).wait_send()
            yc(g, c, p.chip).wait_send()
    for c in others:
        for j in range(1, GROUPS):
            over_chips(c, p.chip, turn(p, j)).wait_send()
        qc(c, p.chip).wait_send()
        gc(c, p.chip).wait_send()
        out_chip(c, p.chip).wait_send()
    for g in line:
        zkv(p.a, g).wait_send()
        zq(p.a, g).wait_send()
        lc(p.a, g).wait_send()
        out_line(p.a, g).wait_send()
        out_back(p.a, g).wait_send()
    for s in range(GROUPS):

        @pl.when((p.a - s >= 0) & (p.a < last))
        def _():
            bc(p.a - s, p.a + 1, 2 * s).wait_send()
            line_share(p.a - s, p.a + 1, 2 * s).wait_send()

        @pl.when((p.a + s <= last) & (p.a > 0))
        def _():
            bc(p.a + s, p.a - 1, 2 * s + 1).wait_send()
            line_share(p.a + s, p.a - 1, 2 * s + 1).wait_send()

        if s > 0:

            @pl.when(p.a + s <= last)
            def _():
                rightward(p.a + s, red.at[0]).wait_send()

            @pl.when(p.a - s >= 0)
            def _():
                leftward(p.a - s, red.at[0]).wait_send()


def back(n, lens, q3, kv, o3, l3, dog, wg, h1, rp, gmid, gfull, dg2, ysum, y0, gb, att):
    rows, width = rp.shape
    quarter = width // 4
    lanes = wg.shape[2]
    chips = n // GROUPS // 2
    keys = kv.shape[0] // GROUPS
    piece = ysum.shape[2]
    half = width // 2
    orow = half // 2
    sds = jax.ShapeDtypeStruct
    v = pltpu.VMEM
    sem = lambda *shape: [DMA(shape), DMA(shape)]
    return pl.pallas_call(
        functools.partial(back_kernel, n),
        name="back",
        out_shape=(
            sds((width, rows), F32),
            sds((GROUPS, 2, quarter, lanes), BF16),
            sds((8, width), F32),
            sds((2, chips, GROUPS, piece, width), BF16),
            sds((2, GROUPS, orow // GROUPS, width), BF16),
        ),
        in_specs=[SM, VM, ANY, ANY, VM, VM, ANY, ANY, ANY, ANY, VM, VM, ANY, VM, ANY, ANY],
        out_specs=[VM] * 5,
        scratch_shapes=[
            v(h1.shape, BF16),
            v(rp.shape, BF16),
            v(gmid.shape, F32),
            v((half, width), BF16),
            v((2, rows, width), BF16),
            v((2, 2) + att.shape[1:], BF16),
            v((GROUPS, piece, width), BF16),
            v((GROUPS, piece, width), BF16),
            v(ysum.shape, BF16),
            v(q3.shape, BF16),
            v(q3.shape, F32),
            v((2 if keys <= SUB else 1, keys, 384), BF16),
            v((keys, 384), F32),
            v((keys, 384), BF16),
            v((GROUPS, chips, rows, 384), BF16),
            v((GROUPS, chips, rows, 384), BF16),
            v((GROUPS, width, lanes), BF16),
            v((GROUPS, rows, lanes), BF16),
            v((GROUPS, rows, lanes), BF16),
            v((width, lanes), F32),
            v((2, 2, quarter, lanes), BF16),
            v((2, quarter, lanes), BF16),
            v((chips, quarter, lanes), BF16),
            v((8, width), F32),
            v((8, width), F32),
            v((8, width), F32),
            v((chips, 8, width), F32),
            v((GROUPS, 8, width), F32),
            v((GROUPS, piece, width), BF16),
            v((GROUPS, piece, width), BF16),
            v((GROUPS, piece, width), BF16),
            v((GROUPS, piece, width), BF16),
            v((orow, width), BF16),
            v((orow // GROUPS, width), BF16),
            v((chips, orow // GROUPS, width), BF16),
            v((GROUPS, orow // GROUPS, width), BF16),
            v((GROUPS, orow // GROUPS, width), BF16),
            *sem(GROUPS),
            DMA((GROUPS + 7,)),
            DMA((2,)),
            *sem(GROUPS, chips),
            *sem(GROUPS + 1, chips),
            *sem(2 * GROUPS),
            *sem(GROUPS),
            *sem(4),
            *sem(chips),
            DMA((2 * GROUPS,)),
            DMA((GROUPS,)),
            *sem(GROUPS),
            *sem(GROUPS),
            *sem(GROUPS),
            DMA((2 * GROUPS,)),
            DMA((GROUPS,)),
            *sem(chips, GROUPS),
            *sem(chips, GROUPS),
            *sem(chips),
            *sem(2 * GROUPS),
            *sem(1 + GROUPS),
            *sem(chips, GROUPS),
            *sem(GROUPS),
            *sem(2),
        ],
        compiler_params=pltpu.CompilerParams(
            collective_id=2, has_side_effects=True, vmem_limit_bytes=67043328
        ),
    )(lens, q3, kv, o3, l3, dog, wg, h1, rp, gmid, gfull, dg2, ysum, y0, gb, att)


def deliver_kernel(gq, ra, rb, rd, goo, gsum, gin, out, out_, gin_, g1_, qkv_, go_, g2_, up_, down_):
    narrow = gin_.shape[0]
    half = g1_.shape[0]
    width = 2 * half
    out_[0] = out[:, :narrow]
    gin_[:, 0, :] = gin[:narrow, :]
    go_[...] = goo[:, :narrow].astype(F32)
    down_[...] = rd[0, :, :narrow].astype(F32)
    up_[:, :width] = ra[0].astype(F32)
    up_[:, width:] = rb[0].astype(F32)
    first = lax.axis_index("fsdp") == 0
    g1_[...] = jnp.where(first, gsum[0, :half], gsum[0, half:])
    g2_[...] = jnp.where(first, gsum[1, :half], gsum[1, half:])
    low = low_half((gq.shape[1], 128))

    def tile(g, t):
        return gq[g, :, t * 128 : (t + 1) * 128].astype(F32)

    def swap(t):
        return pltpu.roll(t, HD, 1)

    for j in range(GROUPS // 2):
        a, b = 2 * j, 2 * j + 1
        parts = []
        for t in (0, 2):
            pair = swap(tile(b, t))
            parts.append(
                (tile(a, t), jnp.where(low, tile(a, t + 1), pair), jnp.where(low, pair, swap(tile(b, t + 1))))
            )
        pair = swap(tile(b, 4))
        parts.append(
            (tile(a, 4), jnp.where(low, swap(tile(a, 3)), pair), jnp.where(low, pair, tile(b, 3)))
        )
        for i, three in enumerate(parts):
            for t, value in enumerate(three):
                at = i * width + j * 384 + t * 128
                qkv_[:, at : at + 128] = value


def deliver(gq, res, goo, gsum, gin, out):
    width, rows = gin.shape
    half = width // 2
    ff = res.shape[1]
    steps = 4
    sds = jax.ShapeDtypeStruct
    spec = pl.BlockSpec
    return pl.pallas_call(
        deliver_kernel,
        name="deliver",
        grid=(steps,),
        out_shape=(
            sds((1, rows, width - 1), BF16),
            sds((width - 1, 1, rows), F32),
            sds((half,), F32),
            sds((half, 3 * width), F32),
            sds((half, width - 1), F32),
            sds((half,), F32),
            sds((width, ff), F32),
            sds((ff, width - 1), F32),
        ),
        in_specs=[
            spec((GROUPS, half // steps, gq.shape[2]), lambda i: (0, i, 0)),
            spec((1, width // steps, width), lambda i: (0, i, 0)),
            spec((1, width // steps, width), lambda i: (0, steps + i, 0)),
            spec((1, ff // steps, width), lambda i: (1, i, 0)),
            spec((half // steps, width), lambda i: (i, 0)),
            spec(gsum.shape, lambda i: (0, 0)),
            spec((width, rows), lambda i: (0, 0)),
            spec((rows // steps, width), lambda i: (i, 0)),
        ],
        out_specs=[
            spec((1, rows // steps, width - 1), lambda i: (0, i, 0)),
            spec((width - 1, 1, rows), lambda i: (0, 0, 0)),
            spec((half,), lambda i: (0,)),
            spec((half // steps, 3 * width), lambda i: (i, 0)),
            spec((half // steps, width - 1), lambda i: (i, 0)),
            spec((half,), lambda i: (0,)),
            spec((width // steps, ff), lambda i: (i, 0)),
            spec((ff // steps, width - 1), lambda i: (i, 0)),
        ],
        compiler_params=pltpu.CompilerParams(vmem_limit_bytes=VLIM),
    )(gq, res, res, res, goo, gsum, gin, out)


def shards(n, resid, lengths, gain_one, w_qkv, w_out, gain_two, w_up, w_down, cotangent):
    width = resid.shape[2] + 1
    ff = w_up.shape[1]
    out, gmid, ysum, y0, gb, attg, dog, dg2, rp, wg, h1, q3, kv, o3, l3, gfull = front(
        n, lengths, resid[0], cotangent[0], gain_one, gain_two, w_qkv, w_out, w_up, w_down
    )
    gin, gq, gsum, res, goo = back(
        n, lengths, q3, kv, o3, l3, dog, wg, h1, rp, gmid, gfull, dg2, ysum, y0, gb, attg
    )

    half = width // 2
    delivered = deliver(
        gq.reshape(GROUPS, half, -1), res.reshape(2, ff, width), goo.reshape(half, width), gsum, gin, out
    )
    return delivered[0], jnp.transpose(delivered[1], (1, 2, 0)), *delivered[2:]


def solution(mesh):
    n = mesh.shape["ctx"]
    return jax.shard_map(
        functools.partial(shards, n),
        mesh=mesh,
        in_specs=(
            P("fsdp", "ctx", None),
            P("fsdp"),
            P("fsdp"),
            P("fsdp", None),
            P("fsdp", None),
            P("fsdp"),
            P(None, "fsdp"),
            P("fsdp", None),
            P("fsdp", "ctx", None),
        ),
        out_specs=(
            P("fsdp", "ctx", None),
            P("fsdp", "ctx", None),
            P("fsdp"),
            P("fsdp", None),
            P("fsdp", None),
            P("fsdp"),
            P(None, "fsdp"),
            P("fsdp", None),
        ),
        check_vma=False,
    )
```

```python
import functools

import jax
import jax.numpy as jnp
from jax import lax
from jax.experimental import pallas as pl
from jax.experimental.pallas import tpu as pltpu
from jax.sharding import PartitionSpec as P

F32 = jnp.float32
BF16 = jnp.bfloat16
MESH = pl.DeviceIdType.MESH
NT = (((1,), (1,)), ((), ()))
TN = (((0,), (0,)), ((), ()))
EPS = 1e-05
MASKED = -1e30
LOG2E = 1.4426950408889634
SCALE = 0.125
GROUPS = 4
GH = 3
HD = 64
SUB = 1024
VLIM = 60 * 1024 * 1024

VM = pl.BlockSpec(memory_space=pltpu.VMEM)
SM = pl.BlockSpec(memory_space=pltpu.SMEM)
ANY = pl.BlockSpec(memory_space=pl.ANY)
DMA = pltpu.SemaphoreType.DMA


def dot(a, b):
    return jnp.dot(a, b, preferred_element_type=F32)


def dg(a, b, dims):
    return lax.dot_general(a, b, dims, preferred_element_type=F32)


def rcopy(src, dst, send, recv, dev):
    return pltpu.make_async_remote_copy(
        src_ref=src, dst_ref=dst, send_sem=send, recv_sem=recv, device_id=dev, device_id_type=MESH
    )


class Place:
    def __init__(self, n):
        self.n = n
        self.m = n // GROUPS
        self.chips = self.m // 2
        c = lax.axis_index("ctx")
        self.x = lax.axis_index("fsdp")
        self.a = c // self.m
        self.b = c % self.m
        self.chip = self.b // 2
        self.k = self.b % 2

    def xpeer(self):
        return {"fsdp": 1 - self.x}

    def sibling(self):
        return {"ctx": self.a * self.m + self.chip * 2 + 1 - self.k}

    def on_chip(self, chip):
        return {"ctx": self.a * self.m + chip * 2 + self.k}

    def on_line(self, a):
        return {"ctx": a * self.m + self.b}


def greet(p, xpeer=False, sibling=False, chips=False, line=False):
    bar = pltpu.get_barrier_semaphore()
    count = 0
    if xpeer:
        pl.semaphore_signal(bar, inc=1, device_id=p.xpeer(), device_id_type=MESH)
        count += 1
    if sibling:
        pl.semaphore_signal(bar, inc=1, device_id=p.sibling(), device_id_type=MESH)
        count += 1
    if chips:
        for d in range(1, p.chips):
            pl.semaphore_signal(
                bar, inc=1, device_id=p.on_chip((p.chip + d) % p.chips), device_id_type=MESH
            )
            count += 1
    if line:
        for d in range(1, GROUPS):
            pl.semaphore_signal(
                bar, inc=1, device_id=p.on_line((p.a + d) % GROUPS), device_id_type=MESH
            )
            count += 1
    return lambda: pl.semaphore_wait(bar, count)


def turn(p, j):
    last = GROUPS - 1
    outer = jnp.where(p.a == 0, last - j, j)
    inner = (0, last, 1, last - 1)[j]
    return jnp.where((p.a == 0) | (p.a == last), outer, jnp.where(p.a == 1, last - inner, inner))


def ext_of(v):
    last = lax.broadcasted_iota(jnp.int32, v.shape, 1) == v.shape[1] - 1
    return jnp.where(last, -jnp.sum(v, axis=1, keepdims=True), v)


def inv_rms(u):
    return lax.rsqrt(jnp.mean(u * u, axis=1, keepdims=True) + EPS)


def crms_back(u, inv, gain, dy):
    dx = dy * gain
    du = inv * (dx - u * (inv * inv * jnp.mean(dx * u, axis=1, keepdims=True)))
    width = u.shape[1]
    last = lax.broadcasted_iota(jnp.int32, u.shape, 1) == width - 1
    return jnp.where(last, 0.0, du - du[:, width - 1 :])


def low_half(shape):
    return lax.broadcasted_iota(jnp.int32, shape, len(shape) - 1) < HD


def pack_tail(t):
    half = t.shape[0] // 2
    top, bottom = t[:half], t[half:]
    return jnp.where(low_half(top.shape), pltpu.roll(bottom, HD, 1), top)


def unpack_tail(t):
    low = low_half(t.shape)
    zero = jnp.zeros_like(t)
    return jnp.where(low, zero, t), jnp.where(low, zero, pltpu.roll(t, HD, 1))


def causal(shape, sub, size, first_query):
    col = lax.broadcasted_iota(jnp.int32, shape, 1) + sub * size
    row = lax.broadcasted_iota(jnp.int32, shape, 0) + first_query
    return col <= row


def gelu_both(a):
    c = 0.7978845608028654
    a2 = a * a
    t = jnp.tanh(c * a * (1.0 + 0.044715 * a2))
    half = 0.5 * (1.0 + t)
    slope = half + 0.5 * a * (1.0 - t * t) * (c * (1.0 + 0.134145 * a2))
    return a * half, slope


def group_columns(wq, wg):
    width = wq.shape[1] // 3
    low = low_half((wq.shape[0], 128))
    zero = jnp.zeros((wq.shape[0], 128), wq.dtype)

    def swap(t):
        return pltpu.roll(t, HD, 1)

    for j in range(GROUPS // 2):
        a, b = 2 * j, 2 * j + 1
        for i in range(3):
            at = i * width + j * 384
            t0, t1, t2 = (wq[:, at + 128 * t : at + 128 * t + 128] for t in range(3))
            pair = (t0, swap(jnp.where(low, t2, t1)))
            if i < 2:
                third = (jnp.where(low, t1, zero), jnp.where(low, swap(t2), zero))
                for g, p, t in zip((a, b), pair, third):
                    wg[g, :, i * 256 : i * 256 + 128] = p
                    wg[g, :, i * 256 + 128 : i * 256 + 256] = t
            else:
                third = (jnp.where(low, zero, swap(t1)), jnp.where(low, zero, t2))
                for g, p, t in zip((a, b), pair, third):
                    wg[g, :, 512:640] = p
                    wg[g, :, 384:512] = wg[g, :, 384:512] + t


def front_kernel(
    n, lens, ri, ci, g1, g2, wq, wo, wuh, wdh,
    out, gmid_, ysum_, y0, gb_, attg, dog, dg2, rp_, wg_, h1_, q3_, kv_, o3_, l3_, gfull,
    gmid, ysum, rp, wg, h1, q3, kv, o3, l3, gains, wop, wa, woa, wu, wdr, wd, att, wide, hid, gmb, act, gpre, esum, dsend, gb, mid, gk,
    ss, rs, ls, hs, hr, vs, kr, fs, xs, xr, cs, cr, ts, tr, as_, ar, ds_, dr, ks, ks_r, ys, yr, us,
):
    p = Place(n)
    rows, narrow = ri.shape
    width = narrow + 1
    half = width // 2
    ff = wuh.shape[1]
    pk = rows * 3 // 2
    keys = p.m * rows
    size = min(SUB, keys)
    subs = keys // size
    other = 1 - p.x
    others = [(p.chip + d) % p.chips for d in range(1, p.chips)]
    line = [(p.a + d) % GROUPS for d in range(1, GROUPS)]
    ready = greet(p, xpeer=True, sibling=True, chips=True, line=True)
    own_u = pltpu.make_async_copy(wuh, wu.at[p.x], ls.at[5])
    own_d = pltpu.make_async_copy(wdh, wdr.at[p.x], ls.at[6])
    own_u.start()
    own_d.start()

    leaving = []

    def leave(src, dst):
        c = pltpu.make_async_copy(src, dst, us.at[len(leaving)])
        c.start()
        leaving.append(c)

    gains[0:1, :] = g1[...].astype(F32).reshape(1, half)
    gains[1:2, :] = g2[...].astype(F32).reshape(1, half)
    gfull[p.x] = gains[...]
    ready()

    def xc(i, src, dst):
        return rcopy(src, dst, ss.at[i], rs.at[i], p.xpeer())

    at_x = pl.ds(pl.multiple_of(p.x * half, half), half)
    x_gain = xc(0, gains, gfull.at[p.x])
    x_gain.start()
    rp[:, :narrow] = ri[...]
    rp[:, narrow:] = jnp.zeros((rows, 1), BF16)
    u = ext_of(rp[...].astype(F32))
    normed = u * inv_rms(u)
    x_gain.wait()
    gain = jnp.concatenate([gfull[0, 0:1, :], gfull[1, 0:1, :]], axis=1)
    h1[p.a] = (normed * gain).astype(BF16)

    def line_copy(block, dst, sem):
        return rcopy(h1.at[block], h1.at[block], hs.at[sem], hr.at[block], p.on_line(dst))

    @pl.when(p.a < GROUPS - 1)
    def _():
        line_copy(p.a, p.a + 1, 0).start()

    @pl.when(p.a > 0)
    def _():
        line_copy(p.a, p.a - 1, 1).start()

    group_columns(wq, wg)
    x_wa = xc(1, wg.at[p.a], wa.at[at_x])
    x_wa.start()
    own_a = pltpu.make_async_copy(wg.at[p.a], wa.at[at_x], ls.at[0])
    own_a.start()
    leave(rp, rp_)
    leave(wg, wg_)

    def up_rows(j, chip, core):
        size_i = width // p.m // 3
        return pl.ds(pl.multiple_of(((chip * 2 + core) * 3 + j) * size_i, size_i), size_i)

    def up_x(j):
        at = up_rows(j, p.chip, p.k)
        return rcopy(wuh.at[at], wu.at[p.x, at], xs.at[j], xr.at[j], p.xpeer())

    def up_chip(j, owner, to):
        r = wu.at[other, up_rows(j, owner, p.k)]
        return rcopy(r, r, cs.at[j, to], cr.at[j, owner], p.on_chip(to))

    def up_core(j, owner, core):
        r = wu.at[other, up_rows(j, owner, core)]
        return rcopy(r, r, ts.at[j, owner], tr.at[j, owner], p.sibling())

    def up_spread(j):
        up_x(j).wait_recv()
        for c in others:
            up_chip(j, p.chip, c).start()
        up_core(j, p.chip, p.k).start()

    def up_pass(j):
        for c in others:
            up_chip(j, c, c).wait_recv()
            up_core(j, c, p.k).start()

    def down_rows(chip, core):
        size_i = ff // p.m
        return pl.ds(pl.multiple_of((chip * 2 + core) * size_i, size_i), size_i)

    def down_x():
        at = down_rows(p.chip, p.k)
        return rcopy(wdh.at[at], wdr.at[p.x, at], xs.at[3], xr.at[3], p.xpeer())

    def down_chip(owner, to):
        r = wdr.at[other, down_rows(owner, p.k)]
        return rcopy(r, r, cs.at[3, to], cr.at[3, owner], p.on_chip(to))

    def down_core(owner, core):
        r = wdr.at[other, down_rows(owner, core)]
        return rcopy(r, r, ts.at[3, owner], tr.at[3, owner], p.sibling())

    for j in range(3):
        up_x(j).start()
    down_x().start()

    wop[:, :narrow] = wo[...]
    wop[:, narrow:] = jnp.zeros((half, 1), BF16)
    xo = []
    local = []
    for i in range(2):
        g = p.x * 2 + i
        for j, (src, count, dst) in enumerate(((0, 128, 0), (128, 64, 192))):
            s_ = wop.at[pl.ds(i * 192 + src, count)]
            d_ = woa.at[pl.ds(pl.multiple_of(g * 256 + dst, 64), count)]
            xo.append(xc(2 + 2 * i + j, s_, d_))
            local.append(pltpu.make_async_copy(s_, d_, ls.at[1 + 2 * i + j]))
    zero_rows = jnp.zeros((HD, width), BF16)
    for g in range(GROUPS):
        woa[pl.ds(g * 256 + 128, HD), :] = zero_rows
    for c in xo:
        c.start()
    for c in local:
        c.start()
    slot = (p.a * p.m + p.b) * rows + lax.broadcasted_iota(jnp.int32, (rows, width), 0)
    live = slot < lens[0]
    gmb[0, :, :narrow] = ci[...]
    gmb[0, :, narrow:] = jnp.zeros((rows, 1), BF16)
    gmb[0] = jnp.where(live, gmb[0].astype(F32), 0.0).astype(BF16)
    x_gm = xc(6, gmb.at[0], gmb.at[1])
    x_gm.start()
    def kv_copy(block, b, dev, send):
        r = kv.at[pl.ds(pl.multiple_of((block * p.m + b) * rows, rows), rows)]
        return rcopy(r, r, send, kr.at[block, b], dev)

    def ac(i, to):
        return rcopy(att.at[to], attg.at[i], as_.at[to], ar.at[i], p.on_line(to))

    own_a.wait()
    x_wa.wait()

    def produce(block):
        y = dot(h1[block], wa[...]).astype(BF16)
        low = low_half((rows, 128))
        zero = jnp.zeros((rows, 128), BF16)
        at = pl.ds(pl.multiple_of(block * rows, rows), rows)
        q3[0, at, :] = jnp.where(low, y[:, :128], zero)
        q3[1, at, :] = jnp.where(low, zero, y[:, :128])
        q3[2, at, :] = y[:, 128:256]
        kv[pl.ds(pl.multiple_of((block * p.m + p.b) * rows, rows), rows), :] = y[:, 256:]
        for d in range(1, p.chips):
            kv_copy(block, p.b, p.on_chip((p.chip + d) % p.chips), vs.at[block, d]).start()
        kv_copy(block, p.b, p.sibling(), vs.at[block, 0]).start()

    def pass_on(block):
        for d in range(1, p.chips):
            b = ((p.chip + d) % p.chips) * 2 + p.k
            kv_copy(block, b, p.sibling(), fs.at[block, d]).wait_recv()
            kv_copy(block, b, p.sibling(), fs.at[block, d]).start()

    def complete(block):
        for c in range(p.chips):
            kv_copy(block, c * 2 + 1 - p.k, p.sibling(), vs.at[block, 0]).wait_recv()

    first_query = p.b * rows
    dead = jnp.where(lens[0] > keys, 0.0, 1.0).astype(F32)

    def pair(z, c, diagonal):
        at_q = pl.ds(pl.multiple_of(z * rows, rows), rows)
        gone = jnp.where(c > 0, dead, 0.0)
        for h in range(GH):
            kt = 128 * (h // 2)
            vt = 128 if h == 2 else 256
            q = q3[h, at_q, :]

            def keys_of(sub, first):
                at = pl.ds(pl.multiple_of(c * keys + sub * size, size), size)
                scores = dg(q, kv[at, kt : kt + 128], NT) * (SCALE * LOG2E)
                if diagonal:
                    scores = jnp.where(causal(scores.shape, sub, size, first_query), scores, MASKED)
                here = jnp.max(scores, axis=1, keepdims=True) + gone * MASKED
                if first:
                    newest = here
                else:
                    top = l3[h, at_q, 0:1]
                    newest = jnp.maximum(top, here)
                weights = jnp.exp2(scores - (newest - gone * (3.0 * MASKED)))
                sums = jnp.sum(weights, axis=1, keepdims=True)
                part = dot(weights.astype(BF16), kv[at, vt : vt + 128])
                if not first:
                    shrink = jnp.exp2(top - newest)
                    sums = sums + l3[h, at_q, HD : HD + 1] * shrink
                    part = part + o3[h, at_q, :] * shrink
                o3[h, at_q, :] = part
                l3[h, at_q, :] = jnp.where(low_half((rows, 128)), newest, sums)

            keys_of(0, diagonal)
            if subs > 1:

                def rest(sub, carry):
                    keys_of(sub, False)
                    return carry

                lax.fori_loop(1, subs, rest, 0)

    def finish_row(z):
        at_q = pl.ds(pl.multiple_of(z * rows, rows), rows)
        heads = []
        for h in range(GH):
            total = l3[h, at_q, HD : HD + 1]
            o = o3[h, at_q, :] / total
            o3[h, at_q, :] = o
            l3[h, at_q, :] = jnp.broadcast_to(l3[h, at_q, 0:1] + jnp.log2(total), (rows, 128))
            heads.append(o)
        att[z, 0:rows, :] = jnp.where(low_half((rows, 128)), heads[0], heads[1]).astype(BF16)
        att[z, rows:pk, :] = pack_tail(heads[2]).astype(BF16)

        @pl.when(z == p.a)
        def _():
            attg[z] = att[z]

        @pl.when(z != p.a)
        def _():
            ac(p.a, z).start()

    def far(z):
        return jnp.abs(z - p.a)

    def pairs(t):
        def row(z, carry):
            @pl.when(far(z) == t)
            def _():
                pair(z, z, True)

            def key(d, carry):
                @pl.when(jnp.maximum(far(z), far(z - d)) == t)
                def _():
                    pair(z, z - d, False)

                return carry

            lax.fori_loop(1, z + 1, key, 0)

            @pl.when(jnp.maximum(far(z), p.a) == t)
            def _():
                finish_row(z)

            return carry

        lax.fori_loop(0, GROUPS, row, 0)

    def step(s, carry):
        below = p.a - s
        above = p.a + s

        @pl.when((s > 0) & (below >= 0))
        def _():
            line_copy(below, p.a, 0).wait_recv()

            @pl.when(p.a < GROUPS - 1)
            def _():
                line_copy(below, p.a + 1, 2 * s).start()

        @pl.when((s > 0) & (above < GROUPS))
        def _():
            line_copy(above, p.a, 0).wait_recv()

            @pl.when(p.a > 0)
            def _():
                line_copy(above, p.a - 1, 2 * s + 1).start()

        @pl.when(below >= 0)
        def _():
            produce(below)

        @pl.when((s > 0) & (above < GROUPS))
        def _():
            produce(above)

        for j in range(3):

            @pl.when(s == j + 1)
            def _():
                up_spread(j)

        @pl.when(s == GROUPS)
        def _():
            down_x().wait_recv()
            for c in others:
                down_chip(p.chip, c).start()
            down_core(p.chip, p.k).start()

        @pl.when((s > 0) & (below + 1 >= 0))
        def _():
            pass_on(below + 1)
            complete(below + 1)

        @pl.when((s > 1) & (above - 1 < GROUPS))
        def _():
            pass_on(above - 1)
            complete(above - 1)

        @pl.when(s > 0)
        def _():
            pairs(s - 1)

        for j in range(3):

            @pl.when(s == j + 2)
            def _():
                up_pass(j)

        return carry

    lax.fori_loop(0, GROUPS + 1, step, 0)
    for src, dst in ((h1, h1_), (q3, q3_), (kv, kv_), (o3, o3_), (l3, l3_)):
        leave(src, dst)

    own_u.wait()
    own_d.wait()

    def pad_down(f):
        wd[f, :, :narrow] = wdr[f]
        wd[f, :, narrow:] = jnp.zeros((ff, 1), BF16)

    pad_down(p.x)
    for c in xo:
        c.wait()
    for c in local:
        c.wait()
    for g in line:
        ac(g, g).wait_recv()
    for g in range(GROUPS):
        wide[:, g * 256 : g * 256 + 128] = attg[g, 0:rows, :]
        top, bottom = unpack_tail(attg[g, rows:pk, :])
        wide[0 : rows // 2, g * 256 + 128 : g * 256 + 256] = top
        wide[rows // 2 : rows, g * 256 + 128 : g * 256 + 256] = bottom
    mid[...] = rp[...].astype(F32) + dot(wide[...], woa[...])
    u = ext_of(mid[...])
    gain = jnp.concatenate([gfull[0, 1:2, :], gfull[1, 1:2, :]], axis=1)
    hid[0] = (u * inv_rms(u) * gain).astype(BF16)
    x_hid = xc(9, hid.at[0], hid.at[1])
    x_hid.start()
    tiles = ff // 256

    def up(slot, token, f):
        def tile(t, carry):
            at = pl.ds(pl.multiple_of(t * 256, 256), 256)
            a, slope = gelu_both(dot(hid[token], wu[f, :, at]))
            act[slot, :, at] = a.astype(BF16)
            gpre[slot, :, at] = (slope * dg(gmb[token], wd[f, at, :], NT)).astype(BF16)
            return carry

        lax.fori_loop(0, tiles, tile, 0)

    up(0, 0, p.x)
    for c in others:
        down_chip(c, c).wait_recv()
        down_core(c, p.k).start()
    for j in range(3):
        for c in range(p.chips):
            up_core(j, c, 1 - p.k).wait_recv()
    for c in range(p.chips):
        down_core(c, 1 - p.k).wait_recv()
    pad_down(other)
    up(2, 0, other)

    def e_tile(t, carry):
        at = pl.ds(pl.multiple_of(t * 256, 256), 256)
        e = dg(gpre[0], wu[p.x, at, :], NT) + dg(gpre[2], wu[other, at, :], NT)
        esum[t] = e
        return carry

    lax.fori_loop(0, width // 256, e_tile, 0)
    e = jnp.concatenate([esum[t] for t in range(width // 256)], axis=1)
    u = ext_of(mid[...])
    inv = inv_rms(u)
    gmid[...] = gmb[0].astype(F32) + crms_back(u, inv, gain, e)
    leave(gmid, gmid_)
    gb[...] = gmid[...].astype(BF16)
    leave(gb, gb_)

    def dc(i, to):
        return rcopy(dsend.at[to], dog.at[i], ds_.at[to], dr.at[i], p.on_line(to))

    for d in range(1, GROUPS + 1):
        to = (p.a + d) % GROUPS
        w = woa[pl.ds(pl.multiple_of(to * 256, 256), 256), :]
        da = dg(gb[...], w, NT).astype(BF16)
        if d < GROUPS:
            dsend[to, 0:rows, :] = da[:, 0:128]
            dsend[to, rows:pk, :] = pack_tail(da[:, 128:256])
            dc(p.a, to).start()
        else:
            dog[to, 0:rows, :] = da[:, 0:128]
            dog[to, rows:pk, :] = pack_tail(da[:, 128:256])
    x_gm.wait()
    x_hid.wait()
    up(1, 1, p.x)
    final = mid[...] + dot(act[0], wd[p.x]) + dot(act[2], wd[other])
    out[...] = final.astype(BF16)

    gm = wd
    piece = ysum.shape[2]
    part = GROUPS * piece

    def kc(chip):
        at = pl.ds(pl.multiple_of(chip * part, part), part)
        return rcopy(gm.at[1 - p.k, at], gk.at[at], ks.at[chip], ks_r.at[chip], p.sibling())

    def grad_up(t, carry):
        at = pl.ds(pl.multiple_of(t * 256, 256), 256)
        g = dg(hid[0], gpre[0, :, at], TN) + dg(hid[1], gpre[1, :, at], TN)
        per = width // 256
        r0 = pl.multiple_of((t // per) * width, width)
        c0 = pl.multiple_of((t % per) * 256, 256)
        gm[0, pl.ds(r0, width), pl.ds(c0, 256)] = g.astype(BF16)
        return carry

    def grad_down(t, carry):
        at = pl.ds(pl.multiple_of(t * 256, 256), 256)
        g = dg(act[0, :, at], gmb[0], TN) + dg(act[1, :, at], gmb[1], TN)
        gm[1, at, :] = g.astype(BF16)
        return carry

    @pl.when(p.k == 0)
    def _():
        lax.fori_loop(0, tiles, grad_down, 0)

    @pl.when(p.k == 1)
    def _():
        lax.fori_loop(0, tiles, grad_up, 0)

    for c in others:
        kc(c).start()
    kc(p.chip).start()

    @pl.when(p.k == 0)
    def _():
        lax.fori_loop(0, tiles, grad_up, 0)

    @pl.when(p.k == 1)
    def _():
        lax.fori_loop(0, tiles, grad_down, 0)

    def over_chips(chip, slot):
        return rcopy(ysum.at[chip, turn(p, 0)], y0.at[slot], ys.at[chip], yr.at[slot], p.on_chip(chip))

    def core_sum(chip, z):
        at = pl.ds(pl.multiple_of(chip * part + z * piece, 16), piece)
        ysum[chip, z] = (gm[p.k, at, :].astype(F32) + gk[at, :].astype(F32)).astype(BF16)

    for chip in others:
        kc(chip).wait()
        core_sum(chip, turn(p, 0))
        over_chips(chip, p.chip).start()
    for j in range(1, GROUPS):
        for chip in others:
            core_sum(chip, turn(p, j))
    kc(p.chip).wait()
    for j in range(GROUPS):
        core_sum(p.chip, turn(p, j))
    y0[p.chip] = ysum[p.chip, turn(p, 0)]
    leave(ysum, ysum_)
    dg2[...] = jnp.broadcast_to(jnp.sum(e * (u * inv), axis=0, keepdims=True), dg2.shape)

    for c in others:
        over_chips(c, p.chip).wait_send()
        over_chips(c, c).wait_recv()
    for g in line:
        ac(p.a, g).wait_send()
        dc(p.a, g).wait_send()
        dc(g, g).wait_recv()
    for block in range(GROUPS):
        kv_copy(block, p.b, p.sibling(), vs.at[block, 0]).wait_send()
        for d in range(1, p.chips):
            kv_copy(block, p.b, p.sibling(), vs.at[block, d]).wait_send()
            b = ((p.chip + d) % p.chips) * 2
            kv_copy(block, b + p.k, p.sibling(), fs.at[block, d]).wait_send()
    for s in range(GROUPS):

        @pl.when((p.a - s >= 0) & (p.a < GROUPS - 1))
        def _():
            line_copy(p.a - s, p.a + 1, 2 * s).wait_send()

        @pl.when((p.a + s < GROUPS) & (p.a > 0))
        def _():
            line_copy(p.a + s, p.a - 1, 2 * s + 1).wait_send()

    for j in range(3):
        up_x(j).wait_send()
        for c in others:
            up_chip(j, p.chip, c).wait_send()
        for c in range(p.chips):
            up_core(j, c, p.k).wait_send()
    down_x().wait_send()
    for c in others:
        down_chip(p.chip, c).wait_send()
    for c in range(p.chips):
        down_core(c, p.k).wait_send()
    for c in leaving:
        c.wait()


def front(n, lens, ri, ci, g1, g2, wq, wo, wu, wd):
    rows, narrow = ri.shape
    width = narrow + 1
    half = width // 2
    ff = wu.shape[1]
    pk = rows * 3 // 2
    m = n // GROUPS
    chips = m // 2
    piece = ff // GROUPS // chips
    lanes = 640
    sds = jax.ShapeDtypeStruct
    v = pltpu.VMEM
    heads = (GH, GROUPS * rows, 128)
    sem = lambda *shape: [DMA(shape), DMA(shape)]
    return pl.pallas_call(
        functools.partial(front_kernel, n),
        name="front",
        out_shape=(
            sds((rows, width), BF16),
            sds((rows, width), F32),
            sds((chips, GROUPS, piece, width), BF16),
            sds((chips, piece, width), BF16),
            sds((rows, width), BF16),
            sds((GROUPS, pk, 128), BF16),
            sds((GROUPS, pk, 128), BF16),
            sds((8, width), F32),
            sds((rows, width), BF16),
            sds((GROUPS, half, lanes), BF16),
            sds((GROUPS, rows, width), BF16),
            sds(heads, BF16),
            sds((n * rows, 384), BF16),
            sds(heads, F32),
            sds(heads, F32),
            sds((2, 8, half), F32),
        ),
        in_specs=[SM, VM, VM, VM, VM, VM, VM, ANY, ANY],
        out_specs=[VM, ANY, ANY, VM, ANY] + [VM] * 3 + [ANY] * 7 + [VM],
        scratch_shapes=[
            v((rows, width), F32),
            v((chips, GROUPS, piece, width), BF16),
            v((rows, width), BF16),
            v((GROUPS, half, lanes), BF16),
            v((GROUPS, rows, width), BF16),
            v(heads, BF16),
            v((n * rows, 384), BF16),
            v(heads, F32),
            v(heads, F32),
            v((8, half), F32),
            v((half, width), BF16),
            v((width, lanes), BF16),
            v((GROUPS * 256, width), BF16),
            v((2, width, ff), BF16),
            v((2, ff, narrow), BF16),
            v((2, ff, width), BF16),
            v((GROUPS, pk, 128), BF16),
            v((rows, GROUPS * 256), BF16),
            v((2, rows, width), BF16),
            v((2, rows, width), BF16),
            v((3, rows, ff), BF16),
            v((3, rows, ff), BF16),
            v((width // 256, rows, 256), F32),
            v((GROUPS, pk, 128), BF16),
            v((rows, width), BF16),
            v((rows, width), F32),
            v((ff, width), BF16),
            *sem(10),
            DMA((7,)),
            DMA((2 * GROUPS,)),
            DMA((GROUPS,)),
            DMA((GROUPS, chips)),
            DMA((GROUPS, m)),
            DMA((GROUPS, chips)),
            *sem(4),
            *sem(4, chips),
            *sem(4, chips),
            *sem(GROUPS),
            *sem(GROUPS),
            *sem(chips),
            *sem(chips),
            DMA((10,)),
        ],
        compiler_params=pltpu.CompilerParams(
            collective_id=0, has_side_effects=True, vmem_limit_bytes=67043328
        ),
    )(lens, ri, ci, g1, g2, wq, wo, wu, wd)


def back_kernel(
    n, lens, q3, kv, o3, l3, dog, wg, h1_, rp_, gmid_, gfull, dg2, ysum, y0, gb_, att_,
    gin, gq, gains, res, goo,
    h1, rp, gmid, go, gb, att, red, ymine, yq, do3, dq3, kvc, dkv, dkvb, rk, ry, wfull, gps, gpr, gqb, qk, qx, qy,
    qs_, qz_, qr_, g0, gk, gx, gy, ga, left, right, sumr, suml, ok, os_, oy, oz, ozr,
    xs, xr, ls, vs, ks, kr, ys, yr, zs, zr, ws, wr, qs, qr, ns, nr, bs, br, cs, cr,
    rs_, rr, ls_, lr, as_, ar, es, er, fs, fr, ts, tr, us, ur, is_, ir, ps, pr, ws2, wr2, zs2, zr2, vs2, vr2, fs2, fr2,
):
    p = Place(n)
    rows, width = rp_.shape
    half = width // 2
    quarter = width // 4
    last = GROUPS - 1
    keys = dkv.shape[0]
    size = min(SUB, keys)
    subs = keys // size
    slots = kvc.shape[0]
    others = [(p.chip + d) % p.chips for d in range(1, p.chips)]
    line = [(p.a + d) % GROUPS for d in range(1, GROUPS)]
    ready = greet(p, xpeer=True, sibling=True, chips=True, line=True)
    at_x = pl.ds(pl.multiple_of(p.x * half, half), half)
    local = [
        pltpu.make_async_copy(wg.at[g], wfull.at[g, at_x], ls.at[g]) for g in range(GROUPS)
    ]

    def chunk_of(i):
        return (p.a + 1 + i) % GROUPS

    def fetch(i):
        c = chunk_of(i)
        src = kv.at[pl.ds(pl.multiple_of(c * keys, keys), keys)]
        return pltpu.make_async_copy(src, kvc.at[i % slots], vs.at[i % slots])

    fetch(0).start()
    o_in = pltpu.make_async_copy(o3, dq3, ls.at[GROUPS])
    o_in.start()
    y_in = pltpu.make_async_copy(ysum.at[p.chip], ymine, ls.at[GROUPS + 1])
    y_in.start()
    late = [
        pltpu.make_async_copy(src, dst, ls.at[GROUPS + 2 + i])
        for i, (src, dst) in enumerate(((h1_, h1), (rp_, rp), (gmid_, gmid)))
    ]
    for c in late:
        c.start()
    gos = [
        pltpu.make_async_copy(src, dst, ls.at[GROUPS + 5 + i])
        for i, (src, dst) in enumerate(((gb_, gb.at[0]), (att_.at[pl.ds(p.x * 2, 2)], att.at[0])))
    ]
    for c in gos:
        c.start()
    gox = [
        rcopy(src, dst, zs2.at[i], zr2.at[i], p.xpeer())
        for i, (src, dst) in enumerate(((gb_, gb.at[1]), (att_.at[pl.ds((1 - p.x) * 2, 2)], att.at[1])))
    ]
    for c in local:
        c.start()

    def weight_rows(x, core):
        return pl.ds(pl.multiple_of(x * half + core * quarter, quarter), quarter)

    def weight_x(g):
        src = wg.at[g, pl.ds(pl.multiple_of(p.k * quarter, quarter), quarter)]
        return rcopy(src, wfull.at[g, weight_rows(p.x, p.k)], xs.at[g], xr.at[g], p.xpeer())

    def weight_core(g, core):
        r = wfull.at[g, weight_rows(1 - p.x, core)]
        return rcopy(r, r, ws2.at[g], wr2.at[g], p.sibling())

    def over_chips(chip, slot, z):
        return rcopy(ysum.at[chip, z], yq.at[slot, z], ps.at[chip, z], pr.at[slot, z], p.on_chip(chip))

    def chip_sum(j):
        z = turn(p, j)
        total = ymine[z].astype(F32)
        for c in others:
            if j > 0:
                over_chips(c, c, z).wait_recv()
                total = total + yq[c, z].astype(F32)
            else:
                total = total + y0[c].astype(F32)
        red[z] = total.astype(BF16)
        if j < last:

            @pl.when(p.a == 0)
            def _():
                rightward(z, red.at[z]).start()

            @pl.when(p.a == last)
            def _():
                leftward(z, red.at[z]).start()

    def rightward(z, src):
        return rcopy(src, left.at[z], rs_.at[z], rr.at[z], p.on_line(p.a + 1))

    def leftward(z, src):
        return rcopy(src, right.at[z], ls_.at[z], lr.at[z], p.on_line(p.a - 1))

    def reduce_step(s):
        @pl.when((p.a >= 1) & (p.a <= s))
        def _():
            z = last + p.a - s
            rightward(z, sumr.at[z]).wait_recv()
            if s < last:
                sumr[z] = (red[z].astype(F32) + left[z].astype(F32)).astype(BF16)
                rightward(z, sumr.at[z]).start()

        b = last - p.a

        @pl.when((b >= 1) & (b <= s))
        def _():
            z = s - b
            leftward(z, suml.at[z]).wait_recv()
            if s < last:
                suml[z] = (red[z].astype(F32) + right[z].astype(F32)).astype(BF16)
                leftward(z, suml.at[z]).start()

    def line_share(z, dst, sem):
        r = res.at[p.k, p.chip, z]
        return rcopy(r, r, as_.at[sem], ar.at[z], p.on_line(dst))

    def chip_share(chip, z, dst):
        r = res.at[p.k, chip, z]
        return rcopy(r, r, es.at[dst, z], er.at[chip, z], p.on_chip(dst))

    def core_share(core, chip, z):
        r = res.at[core, chip, z]
        return rcopy(r, r, fs.at[chip, z], fr.at[chip, z], p.sibling())

    def spread(z):
        for c in others:
            chip_share(p.chip, z, c).start()
        core_share(p.k, p.chip, z).start()

    def gather_first():
        z = p.a
        res[p.k, p.chip, z] = red[z]

        @pl.when(p.a > 0)
        def _():
            cur = res[p.k, p.chip, z].astype(F32)
            res[p.k, p.chip, z] = (cur + left[z].astype(F32)).astype(BF16)

        @pl.when(p.a < last)
        def _():
            cur = res[p.k, p.chip, z].astype(F32)
            res[p.k, p.chip, z] = (cur + right[z].astype(F32)).astype(BF16)
            line_share(z, p.a + 1, 0).start()

        @pl.when(p.a > 0)
        def _():
            line_share(z, p.a - 1, 1).start()

    def gather_step(s):
        @pl.when(p.a - s >= 0)
        def _():
            line_share(p.a - s, p.a, 0).wait_recv()

            @pl.when(p.a < last)
            def _():
                line_share(p.a - s, p.a + 1, 2 * s).start()

            if s > 1:
                spread(p.a - s)
            else:

                @pl.when(p.a == last)
                def _():
                    spread(p.a - s)

        @pl.when(p.a + s <= last)
        def _():
            line_share(p.a + s, p.a, 0).wait_recv()

            @pl.when(p.a > 0)
            def _():
                line_share(p.a + s, p.a - 1, 2 * s + 1).start()

            spread(p.a + s)

    def pass_on(z):
        for c in others:
            chip_share(c, z, c).wait_recv()
            core_share(p.k, c, z).start()

    orow = half // 2
    oc = os_.shape[0]
    oyrow = orow // oc
    opart = oyrow // GROUPS
    my = p.chip if oc > 1 else 0

    def out_core():
        at = pl.ds(pl.multiple_of((1 - p.k) * orow, orow), orow)
        return rcopy(go.at[at], ok, is_.at[0], ir.at[0], p.sibling())

    def out_chip(chip, slot):
        return rcopy(os_.at[chip if oc > 1 else 0], oy.at[slot], ts.at[chip], tr.at[slot], p.on_chip(chip))

    def out_line(slot, to):
        return rcopy(oz.at[to], ozr.at[slot], us.at[to], ur.at[slot], p.on_line(to))

    def out_back(slot, to):
        r = goo.at[p.k, my, slot]
        return rcopy(r, r, us.at[GROUPS + to], ur.at[GROUPS + slot], p.on_line(to))

    def out_spread(chip, z, to):
        r = goo.at[p.k, chip, z]
        return rcopy(r, r, fs2.at[z, to], fr2.at[z, chip], p.on_chip(to))

    def out_share(core, chip, z):
        r = goo.at[core, chip, z]
        i = 1 + chip * GROUPS + z
        return rcopy(r, r, is_.at[i], ir.at[i], p.sibling())

    def out_0():
        for c in gos + gox:
            c.wait()
        for i in range(2):
            tails = [jnp.concatenate(unpack_tail(att[s, i, rows:, :]), axis=0) for s in range(2)]
            g = dg(att[0, i, 0:rows, :], gb[0], TN) + dg(att[1, i, 0:rows, :], gb[1], TN)
            go[i * 192 : i * 192 + 128, :] = g.astype(BF16)
            g = dg(tails[0], gb[0], TN) + dg(tails[1], gb[1], TN)
            go[i * 192 + 128 : i * 192 + 192, :] = g[HD:, :].astype(BF16)
        out_core().start()

    def out_1():
        out_core().wait()
        at = pl.ds(pl.multiple_of(p.k * orow, orow), orow)
        total = go[at, :].astype(F32) + ok[...].astype(F32)
        for c in range(oc):
            os_[c] = total[c * oyrow : (c + 1) * oyrow].astype(BF16)
        for c in others:
            out_chip(c, p.chip).start()

    def out_2():
        total = os_[my].astype(F32)
        for c in others:
            out_chip(c, c).wait_recv()
            total = total + oy[c].astype(F32)
        for z in range(GROUPS):
            oz[z] = total[z * opart : (z + 1) * opart].astype(BF16)
        for z in line:
            out_line(p.a, z).start()

    def out_3():
        total = oz[p.a].astype(F32)
        for z in line:
            out_line(z, z).wait_recv()
            total = total + ozr[z].astype(F32)
        goo[p.k, my, p.a] = total.astype(BF16)
        for z in line:
            out_back(p.a, z).start()

    def out_4():
        for z in line:
            out_back(z, z).wait_recv()
        for z in range(GROUPS):
            if oc > 1:
                for c in others:
                    out_spread(p.chip, z, c).start()
            out_share(p.k, my, z).start()

    def kc(i, chip):
        c = chunk_of(i)
        at = pl.ds(pl.multiple_of((chip * 2 + 1 - p.k) * rows, rows), rows)
        return rcopy(
            dkvb.at[at], rk.at[c, chip], ks.at[c, chip], kr.at[c, chip], p.sibling()
        )

    def yc(c, chip, slot):
        return rcopy(rk.at[c, chip], ry.at[c, slot], ys.at[c, chip], yr.at[c, slot], p.on_chip(chip))

    def zkv(slot, to):
        lanes = pl.ds(256, 384)
        return rcopy(
            gps.at[to, :, lanes], gpr.at[slot, :, lanes], zs.at[to], zr.at[slot], p.on_line(to)
        )

    def zq(slot, to):
        return rcopy(qz_.at[to], qr_.at[slot], ws.at[to], wr.at[slot], p.on_line(to))

    def mine(chip):
        at = pl.ds(pl.multiple_of((chip * 2 + p.k) * rows, rows), rows)
        return dkvb[at, :].astype(F32)

    def kv_1(i):
        dkvb[...] = dkv[...].astype(BF16)
        for c in others:
            kc(i, c).start()
        kc(i, p.chip).start()

    def kv_2(i):
        c = chunk_of(i)
        for chip in others:
            kc(i, chip).wait()
            rk[c, chip] = (mine(chip) + rk[c, chip].astype(F32)).astype(BF16)
            yc(c, chip, p.chip).start()
        kc(i, p.chip).wait()
        rk[c, p.chip] = (mine(p.chip) + rk[c, p.chip].astype(F32)).astype(BF16)

    def kv_3(i, send):
        c = chunk_of(i)
        total = rk[c, p.chip].astype(F32)
        for chip in others:
            yc(c, chip, chip).wait_recv()
            total = total + ry[c, chip].astype(F32)
        gps[c, :, 256:640] = total.astype(BF16)
        if send:
            zkv(p.a, c).start()

    ready()
    for j in range(1, last):
        for c in others:
            over_chips(c, p.chip, turn(p, j)).start()
    for c in gox:
        c.start()
    for g in range(GROUPS):
        weight_x(g).start()

    first_query = p.b * rows
    low = low_half((rows, 128))
    o_in.wait()
    y_in.wait()
    chip_sum(0)
    for z in range(GROUPS):
        at = pl.ds(z * rows, rows)
        both = dog[z, 0:rows, :]
        zero = jnp.zeros_like(both)
        do3[0, at, :] = jnp.where(low, both, zero)
        do3[1, at, :] = jnp.where(low, zero, both)
        top, bottom = unpack_tail(dog[z, rows:, :])
        do3[2, pl.ds(z * rows, rows // 2), :] = top
        do3[2, pl.ds(z * rows + rows // 2, rows // 2), :] = bottom
        for h in range(GH):
            delta = jnp.sum(dq3[h, at, :] * do3[h, at, :].astype(F32), axis=1, keepdims=True)
            gqb[h * rows : (h + 1) * rows, z * 128 : (z + 1) * 128] = jnp.broadcast_to(delta, (rows, 128))
    dq3[...] = jnp.zeros_like(dq3)
    gone = jnp.where(lens[0] > keys, 0.0, -MASKED).astype(F32)

    def chunk(i, carry):
        c = chunk_of(i)
        fetch(i).wait()

        if slots > 1:

            @pl.when(i < last)
            def _():
                fetch(i + 1).start()

        dead = jnp.where(c > 0, gone, 0.0)

        def head(h, carry):
            kt = pl.multiple_of(128 * (h // 2), 128)
            vt = pl.multiple_of(jnp.where(h == 2, 128, 256), 128)

            def step(z, masked):
                at_q = pl.ds(pl.multiple_of(z * rows, rows), rows)
                q = q3[h, at_q, :]
                do = do3[h, at_q, :]
                lse = l3[h, at_q, 0:1] + dead
                delta = gqb[
                    pl.ds(pl.multiple_of(h * rows, rows), rows),
                    pl.ds(pl.multiple_of(z * 128, 128), 128),
                ][:, 0:1]
                def keys_of(sub, carry):
                    at = pl.ds(pl.multiple_of(sub * size, size), size)
                    k = kvc[i % slots, at, pl.ds(kt, 128)]
                    v = kvc[i % slots, at, pl.ds(vt, 128)]
                    scores = dg(q, k, NT) * (SCALE * LOG2E)
                    if masked:
                        scores = jnp.where(
                            causal(scores.shape, sub, size, first_query), scores, MASKED
                        )
                    weights = jnp.exp2(scores - lse)
                    gp = dg(do, v, NT)
                    gs = (weights * (gp - delta)).astype(BF16)
                    dq3[h, at_q, :] += dot(gs, k)
                    gv = dg(weights.astype(BF16), do, TN)
                    gk_ = dg(gs, q, TN) * SCALE
                    if masked:
                        dkv[at, pl.ds(kt, 128)] = jnp.where(h == 1, dkv[at, pl.ds(kt, 128)], 0.0) + gk_
                        dkv[at, pl.ds(vt, 128)] = jnp.where(h == 0, 0.0, dkv[at, pl.ds(vt, 128)]) + gv
                    else:
                        dkv[at, pl.ds(kt, 128)] += gk_
                        dkv[at, pl.ds(vt, 128)] += gv
                    return carry

                if subs > 1:
                    lax.fori_loop(0, subs, keys_of, 0)
                else:
                    keys_of(0, 0)

            step(c, True)

            def rest(z, carry):
                step(z, False)
                return carry

            lax.fori_loop(c + 1, GROUPS, rest, 0)

            @pl.when(h == 0)
            def _():
                @pl.when(i >= 1)
                def _():
                    kv_2(i - 1)

                @pl.when(i == 1)
                def _():
                    for c in others:
                        over_chips(c, p.chip, turn(p, last)).start()
                    chip_sum(1)
                    reduce_step(1)

                @pl.when(i == 2)
                def _():
                    reduce_step(2)

                @pl.when(i == 3)
                def _():
                    chip_sum(3)
                    reduce_step(3)
                    gather_first()

            @pl.when((h == 1) & (i >= 2))
            def _():
                kv_3(i - 2, True)

            @pl.when(h == 2)
            def _():
                @pl.when(i == 1)
                def _():
                    chip_sum(2)
                    out_0()

                @pl.when(i == 2)
                def _():
                    out_1()

                @pl.when(i == last)
                def _():
                    for g in range(GROUPS):
                        weight_x(g).wait_recv()
                        weight_core(g, p.k).start()

            return carry

        lax.fori_loop(0, GH, head, 0)
        if slots == 1:

            @pl.when(i < last)
            def _():
                fetch(i + 1).start()

        kv_1(i)
        return carry

    lax.fori_loop(0, GROUPS, chunk, 0)
    kv_2(3)
    spread(p.a)
    kv_3(2, True)
    for d in range(1, GROUPS + 1):
        z = (p.a + d) % GROUPS
        at = pl.ds(pl.multiple_of(z * rows, rows), rows)
        gps[z, :, 0:128] = (jnp.where(low, dq3[0, at, :], dq3[1, at, :]) * SCALE).astype(BF16)
        third = (jnp.where(low, dq3[2, at, :], 0.0) * SCALE).astype(BF16)
        gps[z, :, 128:256] = third
        if d < GROUPS:
            qz_[z, 0:rows, :] = gps[z, :, 0:128]
            bottom = pltpu.roll(third[rows // 2 :], HD, 1)
            qz_[z, rows:, :] = jnp.where(low[: rows // 2], third[: rows // 2], bottom)
            zq(p.a, z).start()
    out_2()

    def rows_of(i, core):
        return pl.ds(pl.multiple_of(i * half + core * quarter, quarter), quarter)

    for c in late:
        c.wait()
    for t in range(width // 256):
        at = pl.ds(t * 256, 256)
        gqb[at, 0:256] = dg(h1[p.a, :, at], gps[p.a, :, 0:256], TN)
        gqb[at, 256:640] = jnp.zeros((256, 384), F32)

    def rowdot(d, carry):
        z = (p.a + d) % GROUPS
        for t in range(width // 256):
            at = pl.ds(t * 256, 256)
            gqb[at, :] += dg(h1[z, :, at], gps[z], TN)
        return carry

    lax.fori_loop(1, GROUPS, rowdot, 0)
    gather_step(1)
    kv_3(3, False)
    gpr[p.a] = gps[p.a]
    for t in range(width // 256):
        at = pl.ds(t * 256, 256)
        gqb[at, 256:640] += dg(h1[p.a, :, at], gps[p.a, :, 256:640], TN)
    for i in range(2):
        qk[0, i] = gqb[rows_of(i, 1 - p.k), :].astype(BF16)
    q_k = rcopy(qk.at[0], qk.at[1], qs.at[0], qr.at[0], p.sibling())
    q_k.start()
    for c in local:
        c.wait()
    q_k.wait()
    for i in range(2):
        gqb[rows_of(i, p.k), :] += qk[1, i].astype(F32)
    qk[0, 0] = gqb[rows_of(1 - p.x, p.k), :].astype(BF16)
    q_x = rcopy(qk.at[0, 0], qx, qs.at[1], qr.at[1], p.xpeer())
    q_x.start()
    q_x.wait()
    gqb[rows_of(p.x, p.k), :] += qx[...].astype(F32)
    share = quarter // p.chips

    def own_rows(chip):
        start = p.x * half + p.k * quarter + chip * share
        return pl.ds(pl.multiple_of(start, share), share)

    def qc(chip, slot):
        return rcopy(qs_.at[chip], qy.at[slot], ns.at[chip], nr.at[slot], p.on_chip(chip))

    for c in others:
        qs_[c] = gqb[own_rows(c), :].astype(BF16)
        qc(c, p.chip).start()

    @pl.when((p.a > 0) & (p.a < last))
    def _():
        spread(p.a - 1)

    out_3()
    gather_step(2)
    total = gqb[own_rows(p.chip), :]
    for c in others:
        qc(c, c).wait_recv()
        total = total + qy[c].astype(F32)
    gq[p.a, p.k, p.chip] = total.astype(BF16)

    def bc(slot, to, sem):
        r = gq.at[slot, p.k, p.chip]
        return rcopy(r, r, bs.at[sem], br.at[slot], p.on_line(to))

    def qshare(slot, chip, to):
        r = gq.at[slot, p.k, chip]
        return rcopy(r, r, vs2.at[slot, to], vr2.at[slot, chip], p.on_chip(to))

    def sc(slot, core, chip):
        r = gq.at[slot, core, chip]
        return rcopy(r, r, cs.at[slot, chip], cr.at[slot, chip], p.sibling())

    def qspread(slot):
        for c in others:
            qshare(slot, p.chip, c).start()
        sc(slot, p.k, p.chip).start()

    @pl.when(p.a < last)
    def _():
        bc(p.a, p.a + 1, 0).start()

    @pl.when(p.a > 0)
    def _():
        bc(p.a, p.a - 1, 1).start()

    qspread(p.a)
    for g in range(GROUPS):
        weight_core(g, 1 - p.k).wait_recv()
        weight_core(g, p.k).wait_send()
        weight_x(g).wait_send()
    h = dg(gpr[p.a], wfull[p.a], NT)
    for g in line:
        zkv(g, g).wait_recv()
        zq(g, g).wait_recv()
        gpr[g, :, 0:128] = qr_[g, 0:rows, :]
        t = qr_[g, rows:, :]
        zero = jnp.zeros_like(t)
        at_low = low_half(t.shape)
        gpr[g, 0 : rows // 2, 128:256] = jnp.where(at_low, t, zero)
        gpr[g, rows // 2 :, 128:256] = jnp.where(at_low, pltpu.roll(t, HD, 1), zero)
        h = h + dg(gpr[g], wfull[g], NT)
    out_4()
    u = ext_of(rp[...].astype(F32))
    inv = inv_rms(u)
    gain = jnp.concatenate([gfull[0, 0:1, :], gfull[1, 0:1, :]], axis=1)
    result = gmid[...] + crms_back(u, inv, gain, h)
    gin[...] = result.T
    first = jnp.sum(h * (u * inv), axis=0, keepdims=True)
    which = lax.broadcasted_iota(jnp.int32, (8, width), 0)
    g0[...] = jnp.where(which == 0, first, dg2[...])
    g_k = rcopy(g0, gk, qs.at[2], qr.at[2], p.sibling())
    g_k.start()
    gather_step(3)
    g_k.wait()
    g0[...] += gk[...]
    g_x = rcopy(g0, gx, qs.at[3], qr.at[3], p.xpeer())
    g_x.start()
    for s in range(1, GROUPS):

        @pl.when(p.a - s >= 0)
        def _():
            bc(p.a - s, p.a, 0).wait_recv()

            @pl.when(p.a < last)
            def _():
                bc(p.a - s, p.a + 1, 2 * s).start()

            qspread(p.a - s)

        @pl.when(p.a + s <= last)
        def _():
            bc(p.a + s, p.a, 0).wait_recv()

            @pl.when(p.a > 0)
            def _():
                bc(p.a + s, p.a - 1, 2 * s + 1).start()

            qspread(p.a + s)

        if s == 1:
            g_x.wait()
            gy[p.chip] = g0[...] + gx[...]

            def gc(chip, slot):
                return rcopy(
                    gy.at[p.chip], gy.at[slot], ys.at[GROUPS, chip], yr.at[GROUPS, slot],
                    p.on_chip(chip),
                )

            for c in others:
                gc(c, p.chip).start()
        if s == 2:
            for z in range(GROUPS):
                pass_on(z)
            for c in others:
                gc(c, c).wait_recv()
            total = gy[0]
            for c in range(1, p.chips):
                total = total + gy[c]
            ga[p.a] = total

            def lc(slot, to):
                return rcopy(
                    ga.at[p.a], ga.at[slot], zs.at[GROUPS + to], zr.at[GROUPS + slot], p.on_line(to)
                )

            for g in line:
                lc(p.a, g).start()
    for g in line:
        lc(g, g).wait_recv()
    total = ga[0]
    for g in range(1, GROUPS):
        total = total + ga[g]
    gains[...] = total
    for c in others:
        if oc > 1:
            for g in range(GROUPS):
                out_spread(c, g, c).wait_recv()
                out_share(p.k, c, g).start()
    for g in [p.a] + line:
        for c in others:
            qshare(g, c, c).wait_recv()
            sc(g, p.k, c).start()
    for g in range(GROUPS):
        for c in range(p.chips):
            sc(g, 1 - p.k, c).wait_recv()
            sc(g, p.k, c).wait_send()
        for c in others:
            qshare(g, p.chip, c).wait_send()
            if oc > 1:
                out_spread(p.chip, g, c).wait_send()
        for c in range(oc):
            out_share(1 - p.k, c, g).wait_recv()
            out_share(p.k, c, g).wait_send()
        for c in range(p.chips):
            core_share(1 - p.k, c, g).wait_recv()
            core_share(p.k, c, g).wait_send()
        for c in others:
            chip_share(p.chip, g, c).wait_send()
            yc(g, c, p.chip).wait_send()
    for c in others:
        for j in range(1, GROUPS):
            over_chips(c, p.chip, turn(p, j)).wait_send()
        qc(c, p.chip).wait_send()
        gc(c, p.chip).wait_send()
        out_chip(c, p.chip).wait_send()
    for g in line:
        zkv(p.a, g).wait_send()
        zq(p.a, g).wait_send()
        lc(p.a, g).wait_send()
        out_line(p.a, g).wait_send()
        out_back(p.a, g).wait_send()
    for s in range(GROUPS):

        @pl.when((p.a - s >= 0) & (p.a < last))
        def _():
            bc(p.a - s, p.a + 1, 2 * s).wait_send()
            line_share(p.a - s, p.a + 1, 2 * s).wait_send()

        @pl.when((p.a + s <= last) & (p.a > 0))
        def _():
            bc(p.a + s, p.a - 1, 2 * s + 1).wait_send()
            line_share(p.a + s, p.a - 1, 2 * s + 1).wait_send()

        if s > 0:

            @pl.when(p.a + s <= last)
            def _():
                rightward(p.a + s, red.at[0]).wait_send()

            @pl.when(p.a - s >= 0)
            def _():
                leftward(p.a - s, red.at[0]).wait_send()


def back(n, lens, q3, kv, o3, l3, dog, wg, h1, rp, gmid, gfull, dg2, ysum, y0, gb, att):
    rows, width = rp.shape
    quarter = width // 4
    lanes = wg.shape[2]
    chips = n // GROUPS // 2
    keys = kv.shape[0] // GROUPS
    piece = ysum.shape[2]
    half = width // 2
    orow = half // 2
    oc = chips if orow % (chips * GROUPS * 8) == 0 else 1
    oyrow = orow // oc
    sds = jax.ShapeDtypeStruct
    v = pltpu.VMEM
    sem = lambda *shape: [DMA(shape), DMA(shape)]
    return pl.pallas_call(
        functools.partial(back_kernel, n),
        name="back",
        out_shape=(
            sds((width, rows), F32),
            sds((GROUPS, 2, chips, quarter // chips, lanes), BF16),
            sds((8, width), F32),
            sds((2, chips, GROUPS, piece, width), BF16),
            sds((2, oc, GROUPS, oyrow // GROUPS, width), BF16),
        ),
        in_specs=[SM, VM, ANY, ANY, VM, VM, ANY, ANY, ANY, ANY, VM, VM, ANY, VM, ANY, ANY],
        out_specs=[VM] * 5,
        scratch_shapes=[
            v(h1.shape, BF16),
            v(rp.shape, BF16),
            v(gmid.shape, F32),
            v((half, width), BF16),
            v((2, rows, width), BF16),
            v((2, 2) + att.shape[1:], BF16),
            v((GROUPS, piece, width), BF16),
            v((GROUPS, piece, width), BF16),
            v(ysum.shape, BF16),
            v(q3.shape, BF16),
            v(q3.shape, F32),
            v((2 if keys <= SUB else 1, keys, 384), BF16),
            v((keys, 384), F32),
            v((keys, 384), BF16),
            v((GROUPS, chips, rows, 384), BF16),
            v((GROUPS, chips, rows, 384), BF16),
            v((GROUPS, width, lanes), BF16),
            v((GROUPS, rows, lanes), BF16),
            v((GROUPS, rows, lanes), BF16),
            v((width, lanes), F32),
            v((2, 2, quarter, lanes), BF16),
            v((quarter, lanes), BF16),
            v((chips, quarter // chips, lanes), BF16),
            v((chips, quarter // chips, lanes), BF16),
            v((GROUPS, rows * 3 // 2, 128), BF16),
            v((GROUPS, rows * 3 // 2, 128), BF16),
            v((8, width), F32),
            v((8, width), F32),
            v((8, width), F32),
            v((chips, 8, width), F32),
            v((GROUPS, 8, width), F32),
            v((GROUPS, piece, width), BF16),
            v((GROUPS, piece, width), BF16),
            v((GROUPS, piece, width), BF16),
            v((GROUPS, piece, width), BF16),
            v((orow, width), BF16),
            v((oc, oyrow, width), BF16),
            v((chips, oyrow, width), BF16),
            v((GROUPS, oyrow // GROUPS, width), BF16),
            v((GROUPS, oyrow // GROUPS, width), BF16),
            *sem(GROUPS),
            DMA((GROUPS + 7,)),
            DMA((2,)),
            *sem(GROUPS, chips),
            *sem(GROUPS + 1, chips),
            *sem(2 * GROUPS),
            *sem(GROUPS),
            *sem(4),
            *sem(chips),
            DMA((2 * GROUPS,)),
            DMA((GROUPS,)),
            *sem(GROUPS, chips),
            *sem(GROUPS),
            *sem(GROUPS),
            DMA((2 * GROUPS,)),
            DMA((GROUPS,)),
            *sem(chips, GROUPS),
            *sem(chips, GROUPS),
            *sem(chips),
            *sem(2 * GROUPS),
            *sem(1 + chips * GROUPS),
            *sem(chips, GROUPS),
            *sem(GROUPS),
            *sem(2),
            *sem(GROUPS, chips),
            *sem(GROUPS, chips),
        ],
        compiler_params=pltpu.CompilerParams(
            collective_id=2, has_side_effects=True, vmem_limit_bytes=67043328
        ),
    )(lens, q3, kv, o3, l3, dog, wg, h1, rp, gmid, gfull, dg2, ysum, y0, gb, att)


def deliver_kernel(gq, ra, rb, rd, goo, gsum, gin, out, out_, gin_, g1_, qkv_, go_, g2_, up_, down_):
    narrow = gin_.shape[0]
    half = g1_.shape[0]
    width = 2 * half
    out_[0] = out[:, :narrow]
    gin_[:, 0, :] = gin[:narrow, :]
    go_[...] = goo[:, :narrow].astype(F32)
    down_[...] = rd[0, :, :narrow].astype(F32)
    up_[:, :width] = ra[0].astype(F32)
    up_[:, width:] = rb[0].astype(F32)
    first = lax.axis_index("fsdp") == 0
    g1_[...] = jnp.where(first, gsum[0, :half], gsum[0, half:])
    g2_[...] = jnp.where(first, gsum[1, :half], gsum[1, half:])
    low = low_half((gq.shape[1], 128))

    def tile(g, t):
        return gq[g, :, t * 128 : (t + 1) * 128].astype(F32)

    def swap(t):
        return pltpu.roll(t, HD, 1)

    for j in range(GROUPS // 2):
        a, b = 2 * j, 2 * j + 1
        parts = []
        for t in (0, 2):
            pair = swap(tile(b, t))
            parts.append(
                (tile(a, t), jnp.where(low, tile(a, t + 1), pair), jnp.where(low, pair, swap(tile(b, t + 1))))
            )
        pair = swap(tile(b, 4))
        parts.append(
            (tile(a, 4), jnp.where(low, swap(tile(a, 3)), pair), jnp.where(low, pair, tile(b, 3)))
        )
        for i, three in enumerate(parts):
            for t, value in enumerate(three):
                at = i * width + j * 384 + t * 128
                qkv_[:, at : at + 128] = value


def deliver(gq, res, goo, gsum, gin, out):
    width, rows = gin.shape
    half = width // 2
    ff = res.shape[1]
    steps = 4
    sds = jax.ShapeDtypeStruct
    spec = pl.BlockSpec
    return pl.pallas_call(
        deliver_kernel,
        name="deliver",
        grid=(steps,),
        out_shape=(
            sds((1, rows, width - 1), BF16),
            sds((width - 1, 1, rows), F32),
            sds((half,), F32),
            sds((half, 3 * width), F32),
            sds((half, width - 1), F32),
            sds((half,), F32),
            sds((width, ff), F32),
            sds((ff, width - 1), F32),
        ),
        in_specs=[
            spec((GROUPS, half // steps, gq.shape[2]), lambda i: (0, i, 0)),
            spec((1, width // steps, width), lambda i: (0, i, 0)),
            spec((1, width // steps, width), lambda i: (0, steps + i, 0)),
            spec((1, ff // steps, width), lambda i: (1, i, 0)),
            spec((half // steps, width), lambda i: (i, 0)),
            spec(gsum.shape, lambda i: (0, 0)),
            spec((width, rows), lambda i: (0, 0)),
            spec((rows // steps, width), lambda i: (i, 0)),
        ],
        out_specs=[
            spec((1, rows // steps, width - 1), lambda i: (0, i, 0)),
            spec((width - 1, 1, rows), lambda i: (0, 0, 0)),
            spec((half,), lambda i: (0,)),
            spec((half // steps, 3 * width), lambda i: (i, 0)),
            spec((half // steps, width - 1), lambda i: (i, 0)),
            spec((half,), lambda i: (0,)),
            spec((width // steps, ff), lambda i: (i, 0)),
            spec((ff // steps, width - 1), lambda i: (i, 0)),
        ],
        compiler_params=pltpu.CompilerParams(vmem_limit_bytes=VLIM),
    )(gq, res, res, res, goo, gsum, gin, out)


def shards(n, resid, lengths, gain_one, w_qkv, w_out, gain_two, w_up, w_down, cotangent):
    width = resid.shape[2] + 1
    ff = w_up.shape[1]
    out, gmid, ysum, y0, gb, attg, dog, dg2, rp, wg, h1, q3, kv, o3, l3, gfull = front(
        n, lengths, resid[0], cotangent[0], gain_one, gain_two, w_qkv, w_out, w_up, w_down
    )
    gin, gq, gsum, res, goo = back(
        n, lengths, q3, kv, o3, l3, dog, wg, h1, rp, gmid, gfull, dg2, ysum, y0, gb, attg
    )

    half = width // 2
    delivered = deliver(
        gq.reshape(GROUPS, half, -1), res.reshape(2, ff, width), goo.reshape(half, width), gsum, gin, out
    )
    return delivered[0], jnp.transpose(delivered[1], (1, 2, 0)), *delivered[2:]


def solution(mesh):
    n = mesh.shape["ctx"]
    return jax.shard_map(
        functools.partial(shards, n),
        mesh=mesh,
        in_specs=(
            P("fsdp", "ctx", None),
            P("fsdp"),
            P("fsdp"),
            P("fsdp", None),
            P("fsdp", None),
            P("fsdp"),
            P(None, "fsdp"),
            P("fsdp", None),
            P("fsdp", "ctx", None),
        ),
        out_specs=(
            P("fsdp", "ctx", None),
            P("fsdp", "ctx", None),
            P("fsdp"),
            P("fsdp", None),
            P("fsdp", None),
            P("fsdp"),
            P(None, "fsdp"),
            P("fsdp", None),
        ),
        check_vma=False,
    )
```

```python
import functools

import jax
import jax.numpy as jnp
from jax import lax
from jax.experimental import pallas as pl
from jax.experimental.pallas import tpu as pltpu
from jax.sharding import PartitionSpec as P

F32 = jnp.float32
BF16 = jnp.bfloat16
MESH = pl.DeviceIdType.MESH
NT = (((1,), (1,)), ((), ()))
TN = (((0,), (0,)), ((), ()))
EPS = 1e-05
MASKED = -1e30
LOG2E = 1.4426950408889634
SCALE = 0.125
GROUPS = 4
GH = 3
HD = 64
SUB = 1024
VLIM = 60 * 1024 * 1024

VM = pl.BlockSpec(memory_space=pltpu.VMEM)
SM = pl.BlockSpec(memory_space=pltpu.SMEM)
ANY = pl.BlockSpec(memory_space=pl.ANY)
DMA = pltpu.SemaphoreType.DMA


def dot(a, b):
    return jnp.dot(a, b, preferred_element_type=F32)


def dg(a, b, dims):
    return lax.dot_general(a, b, dims, preferred_element_type=F32)


def rcopy(src, dst, send, recv, dev):
    return pltpu.make_async_remote_copy(
        src_ref=src, dst_ref=dst, send_sem=send, recv_sem=recv, device_id=dev, device_id_type=MESH
    )


class Place:
    def __init__(self, n):
        self.n = n
        self.m = n // GROUPS
        self.chips = self.m // 2
        c = lax.axis_index("ctx")
        self.x = lax.axis_index("fsdp")
        self.a = c // self.m
        self.b = c % self.m
        self.chip = self.b // 2
        self.k = self.b % 2

    def xpeer(self):
        return {"fsdp": 1 - self.x}

    def sibling(self):
        return {"ctx": self.a * self.m + self.chip * 2 + 1 - self.k}

    def on_chip(self, chip):
        return {"ctx": self.a * self.m + chip * 2 + self.k}

    def on_line(self, a):
        return {"ctx": a * self.m + self.b}


def greet(p, xpeer=False, sibling=False, chips=False, line=False):
    bar = pltpu.get_barrier_semaphore()
    count = 0
    if xpeer:
        pl.semaphore_signal(bar, inc=1, device_id=p.xpeer(), device_id_type=MESH)
        count += 1
    if sibling:
        pl.semaphore_signal(bar, inc=1, device_id=p.sibling(), device_id_type=MESH)
        count += 1
    if chips:
        for d in range(1, p.chips):
            pl.semaphore_signal(
                bar, inc=1, device_id=p.on_chip((p.chip + d) % p.chips), device_id_type=MESH
            )
            count += 1
    if line:
        for d in range(1, GROUPS):
            pl.semaphore_signal(
                bar, inc=1, device_id=p.on_line((p.a + d) % GROUPS), device_id_type=MESH
            )
            count += 1
    return lambda: pl.semaphore_wait(bar, count)


def turn(p, j):
    last = GROUPS - 1
    outer = jnp.where(p.a == 0, last - j, j)
    inner = (0, last, 1, last - 1)[j]
    return jnp.where((p.a == 0) | (p.a == last), outer, jnp.where(p.a == 1, last - inner, inner))


def ext_of(v):
    last = lax.broadcasted_iota(jnp.int32, v.shape, 1) == v.shape[1] - 1
    return jnp.where(last, -jnp.sum(v, axis=1, keepdims=True), v)


def inv_rms(u):
    return lax.rsqrt(jnp.mean(u * u, axis=1, keepdims=True) + EPS)


def crms_back(u, inv, gain, dy):
    dx = dy * gain
    du = inv * (dx - u * (inv * inv * jnp.mean(dx * u, axis=1, keepdims=True)))
    width = u.shape[1]
    last = lax.broadcasted_iota(jnp.int32, u.shape, 1) == width - 1
    return jnp.where(last, 0.0, du - du[:, width - 1 :])


def low_half(shape):
    return lax.broadcasted_iota(jnp.int32, shape, len(shape) - 1) < HD


def pack_tail(t):
    half = t.shape[0] // 2
    top, bottom = t[:half], t[half:]
    return jnp.where(low_half(top.shape), pltpu.roll(bottom, HD, 1), top)


def unpack_tail(t):
    low = low_half(t.shape)
    zero = jnp.zeros_like(t)
    return jnp.where(low, zero, t), jnp.where(low, zero, pltpu.roll(t, HD, 1))


def causal(shape, sub, size, first_query):
    col = lax.broadcasted_iota(jnp.int32, shape, 1) + sub * size
    row = lax.broadcasted_iota(jnp.int32, shape, 0) + first_query
    return col <= row


def gelu_both(a):
    c = 0.7978845608028654
    a2 = a * a
    t = jnp.tanh(c * a * (1.0 + 0.044715 * a2))
    half = 0.5 * (1.0 + t)
    slope = half + 0.5 * a * (1.0 - t * t) * (c * (1.0 + 0.134145 * a2))
    return a * half, slope


def group_columns(wq, wg):
    width = wq.shape[1] // 3
    low = low_half((wq.shape[0], 128))
    zero = jnp.zeros((wq.shape[0], 128), wq.dtype)

    def swap(t):
        return pltpu.roll(t, HD, 1)

    for j in range(GROUPS // 2):
        a, b = 2 * j, 2 * j + 1
        for i in range(3):
            at = i * width + j * 384
            t0, t1, t2 = (wq[:, at + 128 * t : at + 128 * t + 128] for t in range(3))
            pair = (t0, swap(jnp.where(low, t2, t1)))
            if i < 2:
                third = (jnp.where(low, t1, zero), jnp.where(low, swap(t2), zero))
                for g, p, t in zip((a, b), pair, third):
                    wg[g, :, i * 256 : i * 256 + 128] = p
                    wg[g, :, i * 256 + 128 : i * 256 + 256] = t
            else:
                third = (jnp.where(low, zero, swap(t1)), jnp.where(low, zero, t2))
                for g, p, t in zip((a, b), pair, third):
                    wg[g, :, 512:640] = p
                    wg[g, :, 384:512] = wg[g, :, 384:512] + t


def front_kernel(
    n, lens, ri, ci, g1, g2, wq, wo, wuh, wdh,
    out, gmid_, ysum_, y0, gb_, attg, dog, dg2, rp_, wg_, h1_, q3_, kv_, o3_, l3_, gfull,
    gmid, ysum, rp, wg, h1, q3, kv, o3, l3, gains, wop, wa, woa, wu, wdr, wd, att, wide, hid, gmb, act, gpre, esum, dsend, gb, mid, gk, grads,
    ss, rs, ls, hs, hr, vs, kr, fs, xs, xr, cs, cr, ts, tr, as_, ar, ds_, dr, ks, ks_r, ys, yr, us,
):
    p = Place(n)
    rows, narrow = ri.shape
    width = narrow + 1
    half = width // 2
    ff = wuh.shape[1]
    pk = rows * 3 // 2
    keys = p.m * rows
    size = min(SUB, keys)
    subs = keys // size
    other = 1 - p.x
    others = [(p.chip + d) % p.chips for d in range(1, p.chips)]
    line = [(p.a + d) % GROUPS for d in range(1, GROUPS)]
    ready = greet(p, xpeer=True, sibling=True, chips=True, line=True)
    own_u = pltpu.make_async_copy(wuh, wu.at[p.x], ls.at[5])
    own_d = pltpu.make_async_copy(wdh, wdr.at[p.x], ls.at[6])
    own_u.start()
    own_d.start()

    leaving = []

    def leave(src, dst):
        c = pltpu.make_async_copy(src, dst, us.at[len(leaving)])
        c.start()
        leaving.append(c)

    gains[0:1, :] = g1[...].astype(F32).reshape(1, half)
    gains[1:2, :] = g2[...].astype(F32).reshape(1, half)
    gfull[p.x] = gains[...]
    ready()

    def xc(i, src, dst):
        return rcopy(src, dst, ss.at[i], rs.at[i], p.xpeer())

    at_x = pl.ds(pl.multiple_of(p.x * half, half), half)
    x_gain = xc(0, gains, gfull.at[p.x])
    x_gain.start()
    rp[:, :narrow] = ri[...]
    rp[:, narrow:] = jnp.zeros((rows, 1), BF16)
    u = ext_of(rp[...].astype(F32))
    normed = u * inv_rms(u)
    x_gain.wait()
    gain = jnp.concatenate([gfull[0, 0:1, :], gfull[1, 0:1, :]], axis=1)
    h1[p.a] = (normed * gain).astype(BF16)

    def line_copy(block, dst, sem):
        return rcopy(h1.at[block], h1.at[block], hs.at[sem], hr.at[block], p.on_line(dst))

    @pl.when(p.a < GROUPS - 1)
    def _():
        line_copy(p.a, p.a + 1, 0).start()

    @pl.when(p.a > 0)
    def _():
        line_copy(p.a, p.a - 1, 1).start()

    group_columns(wq, wg)
    x_wa = xc(1, wg.at[p.a], wa.at[at_x])
    x_wa.start()
    own_a = pltpu.make_async_copy(wg.at[p.a], wa.at[at_x], ls.at[0])
    own_a.start()
    leave(rp, rp_)
    leave(wg, wg_)

    def up_rows(j, chip, core):
        size_i = width // p.m // 3
        return pl.ds(pl.multiple_of(((chip * 2 + core) * 3 + j) * size_i, size_i), size_i)

    def up_x(j):
        at = up_rows(j, p.chip, p.k)
        return rcopy(wuh.at[at], wu.at[p.x, at], xs.at[j], xr.at[j], p.xpeer())

    def up_chip(j, owner, to):
        r = wu.at[other, up_rows(j, owner, p.k)]
        return rcopy(r, r, cs.at[j, to], cr.at[j, owner], p.on_chip(to))

    def up_core(j, owner, core):
        r = wu.at[other, up_rows(j, owner, core)]
        return rcopy(r, r, ts.at[j, owner], tr.at[j, owner], p.sibling())

    def up_spread(j):
        up_x(j).wait_recv()
        for c in others:
            up_chip(j, p.chip, c).start()
        up_core(j, p.chip, p.k).start()

    def up_pass(j):
        for c in others:
            up_chip(j, c, c).wait_recv()
            up_core(j, c, p.k).start()

    def down_rows(chip, core):
        size_i = ff // p.m
        return pl.ds(pl.multiple_of((chip * 2 + core) * size_i, size_i), size_i)

    def down_x():
        at = down_rows(p.chip, p.k)
        return rcopy(wdh.at[at], wdr.at[p.x, at], xs.at[3], xr.at[3], p.xpeer())

    def down_chip(owner, to):
        r = wdr.at[other, down_rows(owner, p.k)]
        return rcopy(r, r, cs.at[3, to], cr.at[3, owner], p.on_chip(to))

    def down_core(owner, core):
        r = wdr.at[other, down_rows(owner, core)]
        return rcopy(r, r, ts.at[3, owner], tr.at[3, owner], p.sibling())

    for j in range(3):
        up_x(j).start()
    down_x().start()

    wop[:, :narrow] = wo[...]
    wop[:, narrow:] = jnp.zeros((half, 1), BF16)
    xo = []
    local = []
    for i in range(2):
        g = p.x * 2 + i
        for j, (src, count, dst) in enumerate(((0, 128, 0), (128, 64, 192))):
            s_ = wop.at[pl.ds(i * 192 + src, count)]
            d_ = woa.at[pl.ds(pl.multiple_of(g * 256 + dst, 64), count)]
            xo.append(xc(2 + 2 * i + j, s_, d_))
            local.append(pltpu.make_async_copy(s_, d_, ls.at[1 + 2 * i + j]))
    zero_rows = jnp.zeros((HD, width), BF16)
    for g in range(GROUPS):
        woa[pl.ds(g * 256 + 128, HD), :] = zero_rows
    for c in xo:
        c.start()
    for c in local:
        c.start()
    slot = (p.a * p.m + p.b) * rows + lax.broadcasted_iota(jnp.int32, (rows, width), 0)
    live = slot < lens[0]
    gmb[0, :, :narrow] = ci[...]
    gmb[0, :, narrow:] = jnp.zeros((rows, 1), BF16)
    gmb[0] = jnp.where(live, gmb[0].astype(F32), 0.0).astype(BF16)
    x_gm = xc(6, gmb.at[0], gmb.at[1])
    x_gm.start()
    def kv_copy(block, b, dev, send):
        r = kv.at[pl.ds(pl.multiple_of((block * p.m + b) * rows, rows), rows)]
        return rcopy(r, r, send, kr.at[block, b], dev)

    def ac(i, to):
        return rcopy(att.at[to], attg.at[i], as_.at[to], ar.at[i], p.on_line(to))

    own_a.wait()
    x_wa.wait()

    def produce(block):
        y = dot(h1[block], wa[...]).astype(BF16)
        low = low_half((rows, 128))
        zero = jnp.zeros((rows, 128), BF16)
        at = pl.ds(pl.multiple_of(block * rows, rows), rows)
        q3[0, at, :] = jnp.where(low, y[:, :128], zero)
        q3[1, at, :] = jnp.where(low, zero, y[:, :128])
        q3[2, at, :] = y[:, 128:256]
        kv[pl.ds(pl.multiple_of((block * p.m + p.b) * rows, rows), rows), :] = y[:, 256:]
        for d in range(1, p.chips):
            kv_copy(block, p.b, p.on_chip((p.chip + d) % p.chips), vs.at[block, d]).start()
        kv_copy(block, p.b, p.sibling(), vs.at[block, 0]).start()

    def pass_on(block):
        for d in range(1, p.chips):
            b = ((p.chip + d) % p.chips) * 2 + p.k
            kv_copy(block, b, p.sibling(), fs.at[block, d]).wait_recv()
            kv_copy(block, b, p.sibling(), fs.at[block, d]).start()

    def complete(block):
        for c in range(p.chips):
            kv_copy(block, c * 2 + 1 - p.k, p.sibling(), vs.at[block, 0]).wait_recv()

    first_query = p.b * rows
    dead = jnp.where(lens[0] > keys, 0.0, 1.0).astype(F32)

    def pair(z, c, diagonal):
        at_q = pl.ds(pl.multiple_of(z * rows, rows), rows)
        gone = jnp.where(c > 0, dead, 0.0)
        for h in range(GH):
            kt = 128 * (h // 2)
            vt = 128 if h == 2 else 256
            q = q3[h, at_q, :]

            def keys_of(sub, first):
                at = pl.ds(pl.multiple_of(c * keys + sub * size, size), size)
                scores = dg(q, kv[at, kt : kt + 128], NT) * (SCALE * LOG2E)
                if diagonal:
                    scores = jnp.where(causal(scores.shape, sub, size, first_query), scores, MASKED)
                here = jnp.max(scores, axis=1, keepdims=True) + gone * MASKED
                if first:
                    newest = here
                else:
                    top = l3[h, at_q, 0:1]
                    newest = jnp.maximum(top, here)
                weights = jnp.exp2(scores - (newest - gone * (3.0 * MASKED)))
                sums = jnp.sum(weights, axis=1, keepdims=True)
                part = dot(weights.astype(BF16), kv[at, vt : vt + 128])
                if not first:
                    shrink = jnp.exp2(top - newest)
                    sums = sums + l3[h, at_q, HD : HD + 1] * shrink
                    part = part + o3[h, at_q, :] * shrink
                o3[h, at_q, :] = part
                l3[h, at_q, :] = jnp.where(low_half((rows, 128)), newest, sums)

            keys_of(0, diagonal)
            if subs > 1:

                def rest(sub, carry):
                    keys_of(sub, False)
                    return carry

                lax.fori_loop(1, subs, rest, 0)

    def finish_row(z):
        at_q = pl.ds(pl.multiple_of(z * rows, rows), rows)
        heads = []
        for h in range(GH):
            total = l3[h, at_q, HD : HD + 1]
            o = o3[h, at_q, :] / total
            o3[h, at_q, :] = o
            l3[h, at_q, :] = jnp.broadcast_to(l3[h, at_q, 0:1] + jnp.log2(total), (rows, 128))
            heads.append(o)
        att[z, 0:rows, :] = jnp.where(low_half((rows, 128)), heads[0], heads[1]).astype(BF16)
        att[z, rows:pk, :] = pack_tail(heads[2]).astype(BF16)

        @pl.when(z == p.a)
        def _():
            attg[z] = att[z]

        @pl.when(z != p.a)
        def _():
            ac(p.a, z).start()

    def far(z):
        return jnp.abs(z - p.a)

    def pairs(t):
        def row(z, carry):
            @pl.when(far(z) == t)
            def _():
                pair(z, z, True)

            def key(d, carry):
                @pl.when(jnp.maximum(far(z), far(z - d)) == t)
                def _():
                    pair(z, z - d, False)

                return carry

            lax.fori_loop(1, z + 1, key, 0)

            @pl.when(jnp.maximum(far(z), p.a) == t)
            def _():
                finish_row(z)

            return carry

        lax.fori_loop(0, GROUPS, row, 0)

    def step(s, carry):
        below = p.a - s
        above = p.a + s

        @pl.when((s > 0) & (below >= 0))
        def _():
            line_copy(below, p.a, 0).wait_recv()

            @pl.when(p.a < GROUPS - 1)
            def _():
                line_copy(below, p.a + 1, 2 * s).start()

        @pl.when((s > 0) & (above < GROUPS))
        def _():
            line_copy(above, p.a, 0).wait_recv()

            @pl.when(p.a > 0)
            def _():
                line_copy(above, p.a - 1, 2 * s + 1).start()

        @pl.when(below >= 0)
        def _():
            produce(below)

        @pl.when((s > 0) & (above < GROUPS))
        def _():
            produce(above)

        for j in range(3):

            @pl.when(s == j + 1)
            def _():
                up_spread(j)

        @pl.when(s == GROUPS)
        def _():
            down_x().wait_recv()
            for c in others:
                down_chip(p.chip, c).start()
            down_core(p.chip, p.k).start()

        @pl.when((s > 0) & (below + 1 >= 0))
        def _():
            pass_on(below + 1)
            complete(below + 1)

        @pl.when((s > 1) & (above - 1 < GROUPS))
        def _():
            pass_on(above - 1)
            complete(above - 1)

        @pl.when(s > 0)
        def _():
            pairs(s - 1)

        for j in range(3):

            @pl.when(s == j + 2)
            def _():
                up_pass(j)

        return carry

    lax.fori_loop(0, GROUPS + 1, step, 0)
    for src, dst in ((h1, h1_), (q3, q3_), (kv, kv_), (o3, o3_), (l3, l3_)):
        leave(src, dst)

    own_u.wait()
    own_d.wait()

    def pad_down(f):
        wd[f, :, :narrow] = wdr[f]
        wd[f, :, narrow:] = jnp.zeros((ff, 1), BF16)

    pad_down(p.x)
    for c in xo:
        c.wait()
    for c in local:
        c.wait()
    for g in line:
        ac(g, g).wait_recv()
    for g in range(GROUPS):
        wide[:, g * 256 : g * 256 + 128] = attg[g, 0:rows, :]
        top, bottom = unpack_tail(attg[g, rows:pk, :])
        wide[0 : rows // 2, g * 256 + 128 : g * 256 + 256] = top
        wide[rows // 2 : rows, g * 256 + 128 : g * 256 + 256] = bottom
    mid[...] = rp[...].astype(F32) + dot(wide[...], woa[...])
    u = ext_of(mid[...])
    gain = jnp.concatenate([gfull[0, 1:2, :], gfull[1, 1:2, :]], axis=1)
    hid[0] = (u * inv_rms(u) * gain).astype(BF16)
    x_hid = xc(9, hid.at[0], hid.at[1])
    x_hid.start()
    tiles = ff // 256
    wide_tile = 512

    def up(slot, token, f):
        def tile(t, carry):
            at = pl.ds(pl.multiple_of(t * wide_tile, wide_tile), wide_tile)
            a, slope = gelu_both(dot(hid[token], wu[f, :, at]))
            act[slot, :, at] = a.astype(BF16)
            gpre[slot, :, at] = (slope * dg(gmb[token], wd[f, at, :], NT)).astype(BF16)
            return carry

        lax.fori_loop(0, ff // wide_tile, tile, 0)

    up(0, 0, p.x)
    for c in others:
        down_chip(c, c).wait_recv()
        down_core(c, p.k).start()
    for j in range(3):
        for c in range(p.chips):
            up_core(j, c, 1 - p.k).wait_recv()
    for c in range(p.chips):
        down_core(c, 1 - p.k).wait_recv()
    pad_down(other)
    up(2, 0, other)

    def e_tile(t, carry):
        at = pl.ds(pl.multiple_of(t * 256, 256), 256)
        e = dg(gpre[0], wu[p.x, at, :], NT) + dg(gpre[2], wu[other, at, :], NT)
        esum[t] = e
        return carry

    lax.fori_loop(0, width // 256, e_tile, 0)
    e = jnp.concatenate([esum[t] for t in range(width // 256)], axis=1)
    u = ext_of(mid[...])
    inv = inv_rms(u)
    gmid[...] = gmb[0].astype(F32) + crms_back(u, inv, gain, e)
    leave(gmid, gmid_)
    gb[...] = gmid[...].astype(BF16)
    leave(gb, gb_)

    def dc(i, to):
        return rcopy(dsend.at[to], dog.at[i], ds_.at[to], dr.at[i], p.on_line(to))

    for d in range(1, GROUPS + 1):
        to = (p.a + d) % GROUPS
        w = woa[pl.ds(pl.multiple_of(to * 256, 256), 256), :]
        da = dg(gb[...], w, NT).astype(BF16)
        if d < GROUPS:
            dsend[to, 0:rows, :] = da[:, 0:128]
            dsend[to, rows:pk, :] = pack_tail(da[:, 128:256])
            dc(p.a, to).start()
        else:
            dog[to, 0:rows, :] = da[:, 0:128]
            dog[to, rows:pk, :] = pack_tail(da[:, 128:256])
    x_gm.wait()
    x_hid.wait()
    up(1, 1, p.x)

    def finish_out():
        final = mid[...] + dot(act[0], wd[p.x]) + dot(act[2], wd[other])
        out[...] = final.astype(BF16)

    shared = grads.shape != wd.shape
    gm = wd if shared else grads
    if shared:
        finish_out()
    piece = ysum.shape[2]
    part = GROUPS * piece

    def kc(chip):
        at = pl.ds(pl.multiple_of(chip * part, part), part)
        return rcopy(gm.at[1 - p.k, at], gk.at[at], ks.at[chip], ks_r.at[chip], p.sibling())

    def grad_up(t, carry):
        at = pl.ds(pl.multiple_of(t * 256, 256), 256)
        g = dg(hid[0], gpre[0, :, at], TN) + dg(hid[1], gpre[1, :, at], TN)
        per = width // 256
        r0 = pl.multiple_of((t // per) * width, width)
        c0 = pl.multiple_of((t % per) * 256, 256)
        gm[0, pl.ds(r0, width), pl.ds(c0, 256)] = g.astype(BF16)
        return carry

    def grad_down(t, carry):
        at = pl.ds(pl.multiple_of(t * 256, 256), 256)
        g = dg(act[0, :, at], gmb[0], TN) + dg(act[1, :, at], gmb[1], TN)
        gm[1, at, :] = g.astype(BF16)
        return carry

    @pl.when(p.k == 0)
    def _():
        lax.fori_loop(0, tiles, grad_down, 0)

    @pl.when(p.k == 1)
    def _():
        lax.fori_loop(0, tiles, grad_up, 0)

    for c in others:
        kc(c).start()
    kc(p.chip).start()

    @pl.when(p.k == 0)
    def _():
        lax.fori_loop(0, tiles, grad_up, 0)

    @pl.when(p.k == 1)
    def _():
        lax.fori_loop(0, tiles, grad_down, 0)

    def over_chips(chip, slot):
        return rcopy(ysum.at[chip, turn(p, 0)], y0.at[slot], ys.at[chip], yr.at[slot], p.on_chip(chip))

    def core_sum(chip, z):
        at = pl.ds(pl.multiple_of(chip * part + z * piece, 16), piece)
        ysum[chip, z] = (gm[p.k, at, :].astype(F32) + gk[at, :].astype(F32)).astype(BF16)

    for chip in others:
        kc(chip).wait()
        core_sum(chip, turn(p, 0))
        over_chips(chip, p.chip).start()
    if not shared:
        finish_out()
    for j in range(1, GROUPS):
        for chip in others:
            core_sum(chip, turn(p, j))
    kc(p.chip).wait()
    for j in range(GROUPS):
        core_sum(p.chip, turn(p, j))
    y0[p.chip] = ysum[p.chip, turn(p, 0)]
    leave(ysum, ysum_)
    dg2[...] = jnp.broadcast_to(jnp.sum(e * (u * inv), axis=0, keepdims=True), dg2.shape)

    for c in others:
        over_chips(c, p.chip).wait_send()
        over_chips(c, c).wait_recv()
    for g in line:
        ac(p.a, g).wait_send()
        dc(p.a, g).wait_send()
        dc(g, g).wait_recv()
    for block in range(GROUPS):
        kv_copy(block, p.b, p.sibling(), vs.at[block, 0]).wait_send()
        for d in range(1, p.chips):
            kv_copy(block, p.b, p.sibling(), vs.at[block, d]).wait_send()
            b = ((p.chip + d) % p.chips) * 2
            kv_copy(block, b + p.k, p.sibling(), fs.at[block, d]).wait_send()
    for s in range(GROUPS):

        @pl.when((p.a - s >= 0) & (p.a < GROUPS - 1))
        def _():
            line_copy(p.a - s, p.a + 1, 2 * s).wait_send()

        @pl.when((p.a + s < GROUPS) & (p.a > 0))
        def _():
            line_copy(p.a + s, p.a - 1, 2 * s + 1).wait_send()

    for j in range(3):
        up_x(j).wait_send()
        for c in others:
            up_chip(j, p.chip, c).wait_send()
        for c in range(p.chips):
            up_core(j, c, p.k).wait_send()
    down_x().wait_send()
    for c in others:
        down_chip(p.chip, c).wait_send()
    for c in range(p.chips):
        down_core(c, p.k).wait_send()
    for c in leaving:
        c.wait()


def front(n, lens, ri, ci, g1, g2, wq, wo, wu, wd):
    rows, narrow = ri.shape
    width = narrow + 1
    half = width // 2
    ff = wu.shape[1]
    pk = rows * 3 // 2
    m = n // GROUPS
    chips = m // 2
    piece = ff // GROUPS // chips
    lanes = 640
    sds = jax.ShapeDtypeStruct
    v = pltpu.VMEM
    heads = (GH, GROUPS * rows, 128)
    sem = lambda *shape: [DMA(shape), DMA(shape)]
    return pl.pallas_call(
        functools.partial(front_kernel, n),
        name="front",
        out_shape=(
            sds((rows, width), BF16),
            sds((rows, width), F32),
            sds((chips, GROUPS, piece, width), BF16),
            sds((chips, piece, width), BF16),
            sds((rows, width), BF16),
            sds((GROUPS, pk, 128), BF16),
            sds((GROUPS, pk, 128), BF16),
            sds((8, width), F32),
            sds((rows, width), BF16),
            sds((GROUPS, half, lanes), BF16),
            sds((GROUPS, rows, width), BF16),
            sds(heads, BF16),
            sds((n * rows, 384), BF16),
            sds(heads, F32),
            sds(heads, F32),
            sds((2, 8, half), F32),
        ),
        in_specs=[SM, VM, VM, VM, VM, VM, VM, ANY, ANY],
        out_specs=[VM, ANY, ANY, VM, ANY] + [VM] * 3 + [ANY] * 7 + [VM],
        scratch_shapes=[
            v((rows, width), F32),
            v((chips, GROUPS, piece, width), BF16),
            v((rows, width), BF16),
            v((GROUPS, half, lanes), BF16),
            v((GROUPS, rows, width), BF16),
            v(heads, BF16),
            v((n * rows, 384), BF16),
            v(heads, F32),
            v(heads, F32),
            v((8, half), F32),
            v((half, width), BF16),
            v((width, lanes), BF16),
            v((GROUPS * 256, width), BF16),
            v((2, width, ff), BF16),
            v((2, ff, narrow), BF16),
            v((2, ff, width), BF16),
            v((GROUPS, pk, 128), BF16),
            v((rows, GROUPS * 256), BF16),
            v((2, rows, width), BF16),
            v((2, rows, width), BF16),
            v((3, rows, ff), BF16),
            v((3, rows, ff), BF16),
            v((width // 256, rows, 256), F32),
            v((GROUPS, pk, 128), BF16),
            v((rows, width), BF16),
            v((rows, width), F32),
            v((ff, width), BF16),
            v((2, ff, width) if m * rows <= SUB else (8, 128), BF16),
            *sem(10),
            DMA((7,)),
            DMA((2 * GROUPS,)),
            DMA((GROUPS,)),
            DMA((GROUPS, chips)),
            DMA((GROUPS, m)),
            DMA((GROUPS, chips)),
            *sem(4),
            *sem(4, chips),
            *sem(4, chips),
            *sem(GROUPS),
            *sem(GROUPS),
            *sem(chips),
            *sem(chips),
            DMA((10,)),
        ],
        compiler_params=pltpu.CompilerParams(
            collective_id=0, has_side_effects=True, vmem_limit_bytes=67043328
        ),
    )(lens, ri, ci, g1, g2, wq, wo, wu, wd)


def back_kernel(
    n, lens, q3_, kv, o3, l3_, dog_, wg, h1_, rp_, gmid_, gfull, dg2, ysum, y0, gb_, att_,
    gin, gq, gains, res_, goo,
    q3, l3, dog, res, h1, rp, gmid, go, gb, att, red, ymine, yq, do3, dq3, kvc, dkv, dkvb, rk, ry, wfull, gps, gpr, gqb, qk, qx, qy,
    qs_, qz_, qr_, g0, gk, gx, gy, ga, left, right, sumr, suml, ok, os_, oy, oz, ozr,
    xs, xr, ls, vs, ks, kr, ys, yr, zs, zr, ws, wr, qs, qr, ns, nr, bs, br, cs, cr,
    rs_, rr, ls_, lr, as_, ar, es, er, fs, fr, ts, tr, us, ur, is_, ir, ps, pr, ws2, wr2, zs2, zr2, vs2, vr2, fs2, fr2,
):
    p = Place(n)
    rows, width = rp_.shape
    half = width // 2
    quarter = width // 4
    last = GROUPS - 1
    keys = dkv.shape[0]
    size = min(SUB, keys)
    subs = keys // size
    slots = kvc.shape[0]
    others = [(p.chip + d) % p.chips for d in range(1, p.chips)]
    line = [(p.a + d) % GROUPS for d in range(1, GROUPS)]
    ready = greet(p, xpeer=True, sibling=True, chips=True, line=True)
    at_x = pl.ds(pl.multiple_of(p.x * half, half), half)
    local = [
        pltpu.make_async_copy(wg.at[g], wfull.at[g, at_x], ls.at[g]) for g in range(GROUPS)
    ]

    def chunk_of(i):
        return (p.a + 1 + i) % GROUPS

    def fetch(i):
        c = chunk_of(i)
        src = kv.at[pl.ds(pl.multiple_of(c * keys, keys), keys)]
        return pltpu.make_async_copy(src, kvc.at[i % slots], vs.at[i % slots])

    first_in = [
        pltpu.make_async_copy(src, dst, ls.at[GROUPS + 7 + i])
        for i, (src, dst) in enumerate(((dog_, dog), (q3_, q3), (l3_, l3)))
    ]
    for c in first_in:
        c.start()
    fetch(0).start()
    o_in = pltpu.make_async_copy(o3, dq3, ls.at[GROUPS])
    o_in.start()
    y_in = pltpu.make_async_copy(ysum.at[p.chip], ymine, ls.at[GROUPS + 1])
    y_in.start()
    late = [
        pltpu.make_async_copy(src, dst, ls.at[GROUPS + 2 + i])
        for i, (src, dst) in enumerate(((h1_, h1), (rp_, rp), (gmid_, gmid)))
    ]
    for c in late:
        c.start()
    gos = [
        pltpu.make_async_copy(src, dst, ls.at[GROUPS + 5 + i])
        for i, (src, dst) in enumerate(((gb_, gb.at[0]), (att_.at[pl.ds(p.x * 2, 2)], att.at[0])))
    ]
    for c in gos:
        c.start()
    gox = [
        rcopy(src, dst, zs2.at[i], zr2.at[i], p.xpeer())
        for i, (src, dst) in enumerate(((gb_, gb.at[1]), (att_.at[pl.ds((1 - p.x) * 2, 2)], att.at[1])))
    ]
    for c in local:
        c.start()

    def weight_rows(x, core):
        return pl.ds(pl.multiple_of(x * half + core * quarter, quarter), quarter)

    def weight_x(g):
        src = wg.at[g, pl.ds(pl.multiple_of(p.k * quarter, quarter), quarter)]
        return rcopy(src, wfull.at[g, weight_rows(p.x, p.k)], xs.at[g], xr.at[g], p.xpeer())

    def weight_core(g, core):
        r = wfull.at[g, weight_rows(1 - p.x, core)]
        return rcopy(r, r, ws2.at[g], wr2.at[g], p.sibling())

    def over_chips(chip, slot, z):
        return rcopy(ysum.at[chip, z], yq.at[slot, z], ps.at[chip, z], pr.at[slot, z], p.on_chip(chip))

    def chip_sum(j):
        z = turn(p, j)
        total = ymine[z].astype(F32)
        for c in others:
            if j > 0:
                over_chips(c, c, z).wait_recv()
                total = total + yq[c, z].astype(F32)
            else:
                total = total + y0[c].astype(F32)
        red[z] = total.astype(BF16)
        if j < last:

            @pl.when(p.a == 0)
            def _():
                rightward(z, red.at[z]).start()

            @pl.when(p.a == last)
            def _():
                leftward(z, red.at[z]).start()

    def rightward(z, src):
        return rcopy(src, left.at[z], rs_.at[z], rr.at[z], p.on_line(p.a + 1))

    def leftward(z, src):
        return rcopy(src, right.at[z], ls_.at[z], lr.at[z], p.on_line(p.a - 1))

    def reduce_step(s):
        @pl.when((p.a >= 1) & (p.a <= s))
        def _():
            z = last + p.a - s
            rightward(z, sumr.at[z]).wait_recv()
            if s < last:
                sumr[z] = (red[z].astype(F32) + left[z].astype(F32)).astype(BF16)
                rightward(z, sumr.at[z]).start()

        b = last - p.a

        @pl.when((b >= 1) & (b <= s))
        def _():
            z = s - b
            leftward(z, suml.at[z]).wait_recv()
            if s < last:
                suml[z] = (red[z].astype(F32) + right[z].astype(F32)).astype(BF16)
                leftward(z, suml.at[z]).start()

    def line_share(z, dst, sem):
        r = res.at[p.k, p.chip, z]
        return rcopy(r, r, as_.at[sem], ar.at[z], p.on_line(dst))

    def chip_share(chip, z, dst):
        r = res.at[p.k, chip, z]
        return rcopy(r, r, es.at[dst, z], er.at[chip, z], p.on_chip(dst))

    def core_share(core, chip, z):
        r = res.at[core, chip, z]
        return rcopy(r, r, fs.at[chip, z], fr.at[chip, z], p.sibling())

    def spread(z):
        for c in others:
            chip_share(p.chip, z, c).start()
        core_share(p.k, p.chip, z).start()

    def gather_first():
        z = p.a
        res[p.k, p.chip, z] = red[z]

        @pl.when(p.a > 0)
        def _():
            cur = res[p.k, p.chip, z].astype(F32)
            res[p.k, p.chip, z] = (cur + left[z].astype(F32)).astype(BF16)

        @pl.when(p.a < last)
        def _():
            cur = res[p.k, p.chip, z].astype(F32)
            res[p.k, p.chip, z] = (cur + right[z].astype(F32)).astype(BF16)
            line_share(z, p.a + 1, 0).start()

        @pl.when(p.a > 0)
        def _():
            line_share(z, p.a - 1, 1).start()

    def gather_step(s):
        @pl.when(p.a - s >= 0)
        def _():
            line_share(p.a - s, p.a, 0).wait_recv()

            @pl.when(p.a < last)
            def _():
                line_share(p.a - s, p.a + 1, 2 * s).start()

            if s > 1:
                spread(p.a - s)
            else:

                @pl.when(p.a == last)
                def _():
                    spread(p.a - s)

        @pl.when(p.a + s <= last)
        def _():
            line_share(p.a + s, p.a, 0).wait_recv()

            @pl.when(p.a > 0)
            def _():
                line_share(p.a + s, p.a - 1, 2 * s + 1).start()

            spread(p.a + s)

    def pass_on(z):
        for c in others:
            chip_share(c, z, c).wait_recv()
            core_share(p.k, c, z).start()

    orow = half // 2
    oc = os_.shape[0]
    oyrow = orow // oc
    opart = oyrow // GROUPS
    my = p.chip if oc > 1 else 0

    def out_core():
        at = pl.ds(pl.multiple_of((1 - p.k) * orow, orow), orow)
        return rcopy(go.at[at], ok, is_.at[0], ir.at[0], p.sibling())

    def out_chip(chip, slot):
        return rcopy(os_.at[chip if oc > 1 else 0], oy.at[slot], ts.at[chip], tr.at[slot], p.on_chip(chip))

    def out_line(slot, to):
        return rcopy(oz.at[to], ozr.at[slot], us.at[to], ur.at[slot], p.on_line(to))

    def out_back(slot, to):
        r = goo.at[p.k, my, slot]
        return rcopy(r, r, us.at[GROUPS + to], ur.at[GROUPS + slot], p.on_line(to))

    def out_spread(chip, z, to):
        r = goo.at[p.k, chip, z]
        return rcopy(r, r, fs2.at[z, to], fr2.at[z, chip], p.on_chip(to))

    def out_share(core, chip, z):
        r = goo.at[core, chip, z]
        i = 1 + chip * GROUPS + z
        return rcopy(r, r, is_.at[i], ir.at[i], p.sibling())

    def out_0():
        for c in gos + gox:
            c.wait()
        for i in range(2):
            tails = [jnp.concatenate(unpack_tail(att[s, i, rows:, :]), axis=0) for s in range(2)]
            g = dg(att[0, i, 0:rows, :], gb[0], TN) + dg(att[1, i, 0:rows, :], gb[1], TN)
            go[i * 192 : i * 192 + 128, :] = g.astype(BF16)
            g = dg(tails[0], gb[0], TN) + dg(tails[1], gb[1], TN)
            go[i * 192 + 128 : i * 192 + 192, :] = g[HD:, :].astype(BF16)
        out_core().start()

    def out_1():
        out_core().wait()
        at = pl.ds(pl.multiple_of(p.k * orow, orow), orow)
        total = go[at, :].astype(F32) + ok[...].astype(F32)
        for c in range(oc):
            os_[c] = total[c * oyrow : (c + 1) * oyrow].astype(BF16)
        for c in others:
            out_chip(c, p.chip).start()

    def out_2():
        total = os_[my].astype(F32)
        for c in others:
            out_chip(c, c).wait_recv()
            total = total + oy[c].astype(F32)
        for z in range(GROUPS):
            oz[z] = total[z * opart : (z + 1) * opart].astype(BF16)
        for z in line:
            out_line(p.a, z).start()

    def out_3():
        total = oz[p.a].astype(F32)
        for z in line:
            out_line(z, z).wait_recv()
            total = total + ozr[z].astype(F32)
        goo[p.k, my, p.a] = total.astype(BF16)
        for z in line:
            out_back(p.a, z).start()

    def out_4():
        for z in line:
            out_back(z, z).wait_recv()
        for z in range(GROUPS):
            if oc > 1:
                for c in others:
                    out_spread(p.chip, z, c).start()
            out_share(p.k, my, z).start()

    def kc(i, chip):
        c = chunk_of(i)
        at = pl.ds(pl.multiple_of((chip * 2 + 1 - p.k) * rows, rows), rows)
        return rcopy(
            dkvb.at[at], rk.at[c, chip], ks.at[c, chip], kr.at[c, chip], p.sibling()
        )

    def yc(c, chip, slot):
        return rcopy(rk.at[c, chip], ry.at[c, slot], ys.at[c, chip], yr.at[c, slot], p.on_chip(chip))

    def zkv(slot, to):
        lanes = pl.ds(256, 384)
        return rcopy(
            gps.at[to, :, lanes], gpr.at[slot, :, lanes], zs.at[to], zr.at[slot], p.on_line(to)
        )

    def zq(slot, to):
        return rcopy(qz_.at[to], qr_.at[slot], ws.at[to], wr.at[slot], p.on_line(to))

    def mine(chip):
        at = pl.ds(pl.multiple_of((chip * 2 + p.k) * rows, rows), rows)
        return dkvb[at, :].astype(F32)

    def kv_1(i):
        dkvb[...] = dkv[...].astype(BF16)
        for c in others:
            kc(i, c).start()
        kc(i, p.chip).start()

    def kv_2(i):
        c = chunk_of(i)
        for chip in others:
            kc(i, chip).wait()
            rk[c, chip] = (mine(chip) + rk[c, chip].astype(F32)).astype(BF16)
            yc(c, chip, p.chip).start()
        kc(i, p.chip).wait()
        rk[c, p.chip] = (mine(p.chip) + rk[c, p.chip].astype(F32)).astype(BF16)

    def kv_3(i, send):
        c = chunk_of(i)
        total = rk[c, p.chip].astype(F32)
        for chip in others:
            yc(c, chip, chip).wait_recv()
            total = total + ry[c, chip].astype(F32)
        gps[c, :, 256:640] = total.astype(BF16)
        if send:
            zkv(p.a, c).start()

    ready()
    for j in range(1, last):
        for c in others:
            over_chips(c, p.chip, turn(p, j)).start()
    for c in gox:
        c.start()
    for g in range(GROUPS):
        weight_x(g).start()

    first_query = p.b * rows
    low = low_half((rows, 128))
    for c in first_in:
        c.wait()
    o_in.wait()
    y_in.wait()
    chip_sum(0)
    for z in range(GROUPS):
        at = pl.ds(z * rows, rows)
        both = dog[z, 0:rows, :]
        zero = jnp.zeros_like(both)
        do3[0, at, :] = jnp.where(low, both, zero)
        do3[1, at, :] = jnp.where(low, zero, both)
        top, bottom = unpack_tail(dog[z, rows:, :])
        do3[2, pl.ds(z * rows, rows // 2), :] = top
        do3[2, pl.ds(z * rows + rows // 2, rows // 2), :] = bottom
        for h in range(GH):
            delta = jnp.sum(dq3[h, at, :] * do3[h, at, :].astype(F32), axis=1, keepdims=True)
            gqb[h * rows : (h + 1) * rows, z * 128 : (z + 1) * 128] = jnp.broadcast_to(delta, (rows, 128))
    dq3[...] = jnp.zeros_like(dq3)
    gone = jnp.where(lens[0] > keys, 0.0, -MASKED).astype(F32)

    def chunk(i, carry):
        c = chunk_of(i)
        fetch(i).wait()

        if slots > 1:

            @pl.when(i < last)
            def _():
                fetch(i + 1).start()

        dead = jnp.where(c > 0, gone, 0.0)

        def head(h, carry):
            kt = pl.multiple_of(128 * (h // 2), 128)
            vt = pl.multiple_of(jnp.where(h == 2, 128, 256), 128)

            def step(z, masked):
                at_q = pl.ds(pl.multiple_of(z * rows, rows), rows)
                q = q3[h, at_q, :]
                do = do3[h, at_q, :]
                lse = l3[h, at_q, 0:1] + dead
                delta = gqb[
                    pl.ds(pl.multiple_of(h * rows, rows), rows),
                    pl.ds(pl.multiple_of(z * 128, 128), 128),
                ][:, 0:1]
                def keys_of(sub, carry):
                    at = pl.ds(pl.multiple_of(sub * size, size), size)
                    k = kvc[i % slots, at, pl.ds(kt, 128)]
                    v = kvc[i % slots, at, pl.ds(vt, 128)]
                    scores = dg(q, k, NT) * (SCALE * LOG2E)
                    if masked:
                        scores = jnp.where(
                            causal(scores.shape, sub, size, first_query), scores, MASKED
                        )
                    weights = jnp.exp2(scores - lse)
                    gp = dg(do, v, NT)
                    gs = (weights * (gp - delta)).astype(BF16)
                    dq3[h, at_q, :] += dot(gs, k)
                    gv = dg(weights.astype(BF16), do, TN)
                    gk_ = dg(gs, q, TN) * SCALE
                    if masked:
                        dkv[at, pl.ds(kt, 128)] = jnp.where(h == 1, dkv[at, pl.ds(kt, 128)], 0.0) + gk_
                        dkv[at, pl.ds(vt, 128)] = jnp.where(h == 0, 0.0, dkv[at, pl.ds(vt, 128)]) + gv
                    else:
                        dkv[at, pl.ds(kt, 128)] += gk_
                        dkv[at, pl.ds(vt, 128)] += gv
                    return carry

                if subs > 1:
                    lax.fori_loop(0, subs, keys_of, 0)
                else:
                    keys_of(0, 0)

            step(c, True)

            def rest(z, carry):
                step(z, False)
                return carry

            lax.fori_loop(c + 1, GROUPS, rest, 0)

            @pl.when(h == 0)
            def _():
                @pl.when(i >= 1)
                def _():
                    kv_2(i - 1)

                @pl.when(i == 1)
                def _():
                    for c in others:
                        over_chips(c, p.chip, turn(p, last)).start()
                    chip_sum(1)
                    reduce_step(1)

                @pl.when(i == 2)
                def _():
                    reduce_step(2)

                @pl.when(i == 3)
                def _():
                    chip_sum(3)
                    reduce_step(3)
                    gather_first()

            @pl.when((h == 1) & (i >= 2))
            def _():
                kv_3(i - 2, True)

            @pl.when(h == 2)
            def _():
                @pl.when(i == 1)
                def _():
                    chip_sum(2)
                    out_0()

                @pl.when(i == last)
                def _():
                    for g in range(GROUPS):
                        weight_x(g).wait_recv()
                        weight_core(g, p.k).start()

            return carry

        lax.fori_loop(0, GH, head, 0)
        if slots == 1:

            @pl.when(i < last)
            def _():
                fetch(i + 1).start()

        kv_1(i)
        return carry

    lax.fori_loop(0, GROUPS, chunk, 0)
    kv_2(3)
    spread(p.a)
    out_1()
    for d in range(1, GROUPS + 1):
        z = (p.a + d) % GROUPS
        at = pl.ds(pl.multiple_of(z * rows, rows), rows)
        gps[z, :, 0:128] = (jnp.where(low, dq3[0, at, :], dq3[1, at, :]) * SCALE).astype(BF16)
        third = (jnp.where(low, dq3[2, at, :], 0.0) * SCALE).astype(BF16)
        gps[z, :, 128:256] = third
        if d < GROUPS:
            qz_[z, 0:rows, :] = gps[z, :, 0:128]
            bottom = pltpu.roll(third[rows // 2 :], HD, 1)
            qz_[z, rows:, :] = jnp.where(low[: rows // 2], third[: rows // 2], bottom)
            zq(p.a, z).start()
    kv_3(2, True)

    def rows_of(i, core):
        return pl.ds(pl.multiple_of(i * half + core * quarter, quarter), quarter)

    for c in late:
        c.wait()
    for t in range(width // 256):
        at = pl.ds(t * 256, 256)
        gqb[at, 0:256] = dg(h1[p.a, :, at], gps[p.a, :, 0:256], TN)
        gqb[at, 256:640] = jnp.zeros((256, 384), F32)

    def rowdot(d, carry):
        z = (p.a + d) % GROUPS
        for t in range(width // 256):
            at = pl.ds(t * 256, 256)
            gqb[at, :] += dg(h1[z, :, at], gps[z], TN)
        return carry

    lax.fori_loop(1, GROUPS, rowdot, 0)
    kv_3(3, False)
    gpr[p.a] = gps[p.a]
    for t in range(width // 256):
        at = pl.ds(t * 256, 256)
        gqb[at, 256:640] += dg(h1[p.a, :, at], gps[p.a, :, 256:640], TN)
    for i in range(2):
        qk[0, i] = gqb[rows_of(i, 1 - p.k), :].astype(BF16)
    q_k = rcopy(qk.at[0], qk.at[1], qs.at[0], qr.at[0], p.sibling())
    q_k.start()
    gather_step(1)
    for c in local:
        c.wait()
    q_k.wait()
    for i in range(2):
        gqb[rows_of(i, p.k), :] += qk[1, i].astype(F32)
    qk[0, 0] = gqb[rows_of(1 - p.x, p.k), :].astype(BF16)
    q_x = rcopy(qk.at[0, 0], qx, qs.at[1], qr.at[1], p.xpeer())
    q_x.start()
    out_2()
    q_x.wait()
    gqb[rows_of(p.x, p.k), :] += qx[...].astype(F32)
    share = quarter // p.chips

    def own_rows(chip):
        start = p.x * half + p.k * quarter + chip * share
        return pl.ds(pl.multiple_of(start, share), share)

    def qc(chip, slot):
        return rcopy(qs_.at[chip], qy.at[slot], ns.at[chip], nr.at[slot], p.on_chip(chip))

    for c in others:
        qs_[c] = gqb[own_rows(c), :].astype(BF16)
        qc(c, p.chip).start()

    @pl.when((p.a > 0) & (p.a < last))
    def _():
        spread(p.a - 1)

    gather_step(2)
    total = gqb[own_rows(p.chip), :]
    for c in others:
        qc(c, c).wait_recv()
        total = total + qy[c].astype(F32)
    gq[p.a, p.k, p.chip] = total.astype(BF16)

    def bc(slot, to, sem):
        r = gq.at[slot, p.k, p.chip]
        return rcopy(r, r, bs.at[sem], br.at[slot], p.on_line(to))

    def qshare(slot, chip, to):
        r = gq.at[slot, p.k, chip]
        return rcopy(r, r, vs2.at[slot, to], vr2.at[slot, chip], p.on_chip(to))

    def sc(slot, core, chip):
        r = gq.at[slot, core, chip]
        return rcopy(r, r, cs.at[slot, chip], cr.at[slot, chip], p.sibling())

    def qspread(slot):
        for c in others:
            qshare(slot, p.chip, c).start()
        sc(slot, p.k, p.chip).start()

    @pl.when(p.a < last)
    def _():
        bc(p.a, p.a + 1, 0).start()

    @pl.when(p.a > 0)
    def _():
        bc(p.a, p.a - 1, 1).start()

    qspread(p.a)
    for g in range(GROUPS):
        weight_core(g, 1 - p.k).wait_recv()
        weight_core(g, p.k).wait_send()
        weight_x(g).wait_send()
    h = dg(gpr[p.a], wfull[p.a], NT)
    for g in line:
        zkv(g, g).wait_recv()
        zq(g, g).wait_recv()
        gpr[g, :, 0:128] = qr_[g, 0:rows, :]
        t = qr_[g, rows:, :]
        zero = jnp.zeros_like(t)
        at_low = low_half(t.shape)
        gpr[g, 0 : rows // 2, 128:256] = jnp.where(at_low, t, zero)
        gpr[g, rows // 2 :, 128:256] = jnp.where(at_low, pltpu.roll(t, HD, 1), zero)
        h = h + dg(gpr[g], wfull[g], NT)
    out_3()
    u = ext_of(rp[...].astype(F32))
    inv = inv_rms(u)
    gain = jnp.concatenate([gfull[0, 0:1, :], gfull[1, 0:1, :]], axis=1)
    result = gmid[...] + crms_back(u, inv, gain, h)
    gin[...] = result.T
    first = jnp.sum(h * (u * inv), axis=0, keepdims=True)
    which = lax.broadcasted_iota(jnp.int32, (8, width), 0)
    g0[...] = jnp.where(which == 0, first, dg2[...])
    g_k = rcopy(g0, gk, qs.at[2], qr.at[2], p.sibling())
    g_k.start()
    gather_step(3)
    g_k.wait()
    g0[...] += gk[...]
    g_x = rcopy(g0, gx, qs.at[3], qr.at[3], p.xpeer())
    g_x.start()
    for s in range(1, GROUPS):

        @pl.when(p.a - s >= 0)
        def _():
            bc(p.a - s, p.a, 0).wait_recv()

            @pl.when(p.a < last)
            def _():
                bc(p.a - s, p.a + 1, 2 * s).start()

            qspread(p.a - s)

        @pl.when(p.a + s <= last)
        def _():
            bc(p.a + s, p.a, 0).wait_recv()

            @pl.when(p.a > 0)
            def _():
                bc(p.a + s, p.a - 1, 2 * s + 1).start()

            qspread(p.a + s)

        if s == 1:
            out_4()
            g_x.wait()
            gy[p.chip] = g0[...] + gx[...]

            def gc(chip, slot):
                return rcopy(
                    gy.at[p.chip], gy.at[slot], ys.at[GROUPS, chip], yr.at[GROUPS, slot],
                    p.on_chip(chip),
                )

            for c in others:
                gc(c, p.chip).start()
        if s == 2:
            for z in range(GROUPS):
                pass_on(z)
            for c in others:
                gc(c, c).wait_recv()
            total = gy[0]
            for c in range(1, p.chips):
                total = total + gy[c]
            ga[p.a] = total

            def lc(slot, to):
                return rcopy(
                    ga.at[p.a], ga.at[slot], zs.at[GROUPS + to], zr.at[GROUPS + slot], p.on_line(to)
                )

            for g in line:
                lc(p.a, g).start()
    for g in range(GROUPS):
        for c in range(p.chips):
            core_share(1 - p.k, c, g).wait_recv()
    res_out = pltpu.make_async_copy(res, res_, ls.at[0])
    res_out.start()
    for g in line:
        lc(g, g).wait_recv()
    total = ga[0]
    for g in range(1, GROUPS):
        total = total + ga[g]
    gains[...] = total
    for c in others:
        if oc > 1:
            for g in range(GROUPS):
                out_spread(c, g, c).wait_recv()
                out_share(p.k, c, g).start()
    for g in [p.a] + line:
        for c in others:
            qshare(g, c, c).wait_recv()
            sc(g, p.k, c).start()
    for g in range(GROUPS):
        for c in range(p.chips):
            sc(g, 1 - p.k, c).wait_recv()
            sc(g, p.k, c).wait_send()
        for c in others:
            qshare(g, p.chip, c).wait_send()
            if oc > 1:
                out_spread(p.chip, g, c).wait_send()
        for c in range(oc):
            out_share(1 - p.k, c, g).wait_recv()
            out_share(p.k, c, g).wait_send()
        for c in range(p.chips):
            core_share(p.k, c, g).wait_send()
        for c in others:
            chip_share(p.chip, g, c).wait_send()
            yc(g, c, p.chip).wait_send()
    for c in others:
        for j in range(1, GROUPS):
            over_chips(c, p.chip, turn(p, j)).wait_send()
        qc(c, p.chip).wait_send()
        gc(c, p.chip).wait_send()
        out_chip(c, p.chip).wait_send()
    for g in line:
        zkv(p.a, g).wait_send()
        zq(p.a, g).wait_send()
        lc(p.a, g).wait_send()
        out_line(p.a, g).wait_send()
        out_back(p.a, g).wait_send()
    for s in range(GROUPS):

        @pl.when((p.a - s >= 0) & (p.a < last))
        def _():
            bc(p.a - s, p.a + 1, 2 * s).wait_send()
            line_share(p.a - s, p.a + 1, 2 * s).wait_send()

        @pl.when((p.a + s <= last) & (p.a > 0))
        def _():
            bc(p.a + s, p.a - 1, 2 * s + 1).wait_send()
            line_share(p.a + s, p.a - 1, 2 * s + 1).wait_send()

        if s > 0:

            @pl.when(p.a + s <= last)
            def _():
                rightward(p.a + s, red.at[0]).wait_send()

            @pl.when(p.a - s >= 0)
            def _():
                leftward(p.a - s, red.at[0]).wait_send()

    res_out.wait()


def back(n, lens, q3, kv, o3, l3, dog, wg, h1, rp, gmid, gfull, dg2, ysum, y0, gb, att):
    rows, width = rp.shape
    quarter = width // 4
    lanes = wg.shape[2]
    chips = n // GROUPS // 2
    keys = kv.shape[0] // GROUPS
    piece = ysum.shape[2]
    half = width // 2
    orow = half // 2
    oc = chips if orow % (chips * GROUPS * 8) == 0 else 1
    oyrow = orow // oc
    sds = jax.ShapeDtypeStruct
    v = pltpu.VMEM
    sem = lambda *shape: [DMA(shape), DMA(shape)]
    return pl.pallas_call(
        functools.partial(back_kernel, n),
        name="back",
        out_shape=(
            sds((width, rows), F32),
            sds((GROUPS, 2, chips, quarter // chips, lanes), BF16),
            sds((8, width), F32),
            sds((2, chips, GROUPS, piece, width), BF16),
            sds((2, oc, GROUPS, oyrow // GROUPS, width), BF16),
        ),
        in_specs=[SM, ANY, ANY, ANY, ANY, ANY, ANY, ANY, ANY, ANY, VM, VM, ANY, VM, ANY, ANY],
        out_specs=[VM, VM, VM, ANY, VM],
        scratch_shapes=[
            v(q3.shape, BF16),
            v(l3.shape, F32),
            v(dog.shape, BF16),
            v((2, chips, GROUPS, piece, width), BF16),
            v(h1.shape, BF16),
            v(rp.shape, BF16),
            v(gmid.shape, F32),
            v((half, width), BF16),
            v((2, rows, width), BF16),
            v((2, 2) + att.shape[1:], BF16),
            v((GROUPS, piece, width), BF16),
            v((GROUPS, piece, width), BF16),
            v(ysum.shape, BF16),
            v(q3.shape, BF16),
            v(q3.shape, F32),
            v((2 if keys <= SUB else 1, keys, 384), BF16),
            v((keys, 384), F32),
            v((keys, 384), BF16),
            v((GROUPS, chips, rows, 384), BF16),
            v((GROUPS, chips, rows, 384), BF16),
            v((GROUPS, width, lanes), BF16),
            v((GROUPS, rows, lanes), BF16),
            v((GROUPS, rows, lanes), BF16),
            v((width, lanes), F32),
            v((2, 2, quarter, lanes), BF16),
            v((quarter, lanes), BF16),
            v((chips, quarter // chips, lanes), BF16),
            v((chips, quarter // chips, lanes), BF16),
            v((GROUPS, rows * 3 // 2, 128), BF16),
            v((GROUPS, rows * 3 // 2, 128), BF16),
            v((8, width), F32),
            v((8, width), F32),
            v((8, width), F32),
            v((chips, 8, width), F32),
            v((GROUPS, 8, width), F32),
            v((GROUPS, piece, width), BF16),
            v((GROUPS, piece, width), BF16),
            v((GROUPS, piece, width), BF16),
            v((GROUPS, piece, width), BF16),
            v((orow, width), BF16),
            v((oc, oyrow, width), BF16),
            v((chips, oyrow, width), BF16),
            v((GROUPS, oyrow // GROUPS, width), BF16),
            v((GROUPS, oyrow // GROUPS, width), BF16),
            *sem(GROUPS),
            DMA((GROUPS + 10,)),
            DMA((2,)),
            *sem(GROUPS, chips),
            *sem(GROUPS + 1, chips),
            *sem(2 * GROUPS),
            *sem(GROUPS),
            *sem(4),
            *sem(chips),
            DMA((2 * GROUPS,)),
            DMA((GROUPS,)),
            *sem(GROUPS, chips),
            *sem(GROUPS),
            *sem(GROUPS),
            DMA((2 * GROUPS,)),
            DMA((GROUPS,)),
            *sem(chips, GROUPS),
            *sem(chips, GROUPS),
            *sem(chips),
            *sem(2 * GROUPS),
            *sem(1 + chips * GROUPS),
            *sem(chips, GROUPS),
            *sem(GROUPS),
            *sem(2),
            *sem(GROUPS, chips),
            *sem(GROUPS, chips),
        ],
        compiler_params=pltpu.CompilerParams(
            collective_id=2, has_side_effects=True, vmem_limit_bytes=67043328
        ),
    )(lens, q3, kv, o3, l3, dog, wg, h1, rp, gmid, gfull, dg2, ysum, y0, gb, att)


def deliver_kernel(gq, ra, rb, rd, goo, gsum, gin, out, out_, gin_, g1_, qkv_, go_, g2_, up_, down_):
    narrow = gin_.shape[0]
    half = g1_.shape[0]
    width = 2 * half
    out_[0] = out[:, :narrow]

    @pl.when(pl.program_id(0) == 0)
    def _():
        gin_[:, 0, :] = gin[:narrow, :]

    go_[...] = goo[:, :narrow].astype(F32)
    down_[...] = rd[0, :, :narrow].astype(F32)
    up_[:, :width] = ra[0].astype(F32)
    up_[:, width:] = rb[0].astype(F32)
    first = lax.axis_index("fsdp") == 0
    g1_[...] = jnp.where(first, gsum[0, :half], gsum[0, half:])
    g2_[...] = jnp.where(first, gsum[1, :half], gsum[1, half:])
    low = low_half((gq.shape[1], 128))

    def tile(g, t):
        return gq[g, :, t * 128 : (t + 1) * 128].astype(F32)

    def swap(t):
        return pltpu.roll(t, HD, 1)

    for j in range(GROUPS // 2):
        a, b = 2 * j, 2 * j + 1
        parts = []
        for t in (0, 2):
            pair = swap(tile(b, t))
            parts.append(
                (tile(a, t), jnp.where(low, tile(a, t + 1), pair), jnp.where(low, pair, swap(tile(b, t + 1))))
            )
        pair = swap(tile(b, 4))
        parts.append(
            (tile(a, 4), jnp.where(low, swap(tile(a, 3)), pair), jnp.where(low, pair, tile(b, 3)))
        )
        for i, three in enumerate(parts):
            for t, value in enumerate(three):
                at = i * width + j * 384 + t * 128
                qkv_[:, at : at + 128] = value


def deliver(gq, res, goo, gsum, gin, out):
    width, rows = gin.shape
    half = width // 2
    ff = res.shape[1]
    steps = 2
    sds = jax.ShapeDtypeStruct
    spec = pl.BlockSpec
    return pl.pallas_call(
        deliver_kernel,
        name="deliver",
        grid=(steps,),
        out_shape=(
            sds((1, rows, width - 1), BF16),
            sds((width - 1, 1, rows), F32),
            sds((half,), F32),
            sds((half, 3 * width), F32),
            sds((half, width - 1), F32),
            sds((half,), F32),
            sds((width, ff), F32),
            sds((ff, width - 1), F32),
        ),
        in_specs=[
            spec((GROUPS, half // steps, gq.shape[2]), lambda i: (0, i, 0)),
            spec((1, width // steps, width), lambda i: (0, i, 0)),
            spec((1, width // steps, width), lambda i: (0, steps + i, 0)),
            spec((1, ff // steps, width), lambda i: (1, i, 0)),
            spec((half // steps, width), lambda i: (i, 0)),
            spec(gsum.shape, lambda i: (0, 0)),
            spec((width, rows), lambda i: (0, 0)),
            spec((rows // steps, width), lambda i: (i, 0)),
        ],
        out_specs=[
            spec((1, rows // steps, width - 1), lambda i: (0, i, 0)),
            spec((width - 1, 1, rows), lambda i: (0, 0, 0)),
            spec((half,), lambda i: (0,)),
            spec((half // steps, 3 * width), lambda i: (i, 0)),
            spec((half // steps, width - 1), lambda i: (i, 0)),
            spec((half,), lambda i: (0,)),
            spec((width // steps, ff), lambda i: (i, 0)),
            spec((ff // steps, width - 1), lambda i: (i, 0)),
        ],
        compiler_params=pltpu.CompilerParams(vmem_limit_bytes=VLIM),
    )(gq, res, res, res, goo, gsum, gin, out)


def shards(n, resid, lengths, gain_one, w_qkv, w_out, gain_two, w_up, w_down, cotangent):
    width = resid.shape[2] + 1
    ff = w_up.shape[1]
    out, gmid, ysum, y0, gb, attg, dog, dg2, rp, wg, h1, q3, kv, o3, l3, gfull = front(
        n, lengths, resid[0], cotangent[0], gain_one, gain_two, w_qkv, w_out, w_up, w_down
    )
    gin, gq, gsum, res, goo = back(
        n, lengths, q3, kv, o3, l3, dog, wg, h1, rp, gmid, gfull, dg2, ysum, y0, gb, attg
    )

    half = width // 2
    delivered = deliver(
        gq.reshape(GROUPS, half, -1), res.reshape(2, ff, width), goo.reshape(half, width), gsum, gin, out
    )
    return delivered[0], jnp.transpose(delivered[1], (1, 2, 0)), *delivered[2:]


def solution(mesh):
    n = mesh.shape["ctx"]
    return jax.shard_map(
        functools.partial(shards, n),
        mesh=mesh,
        in_specs=(
            P("fsdp", "ctx", None),
            P("fsdp"),
            P("fsdp"),
            P("fsdp", None),
            P("fsdp", None),
            P("fsdp"),
            P(None, "fsdp"),
            P("fsdp", None),
            P("fsdp", "ctx", None),
        ),
        out_specs=(
            P("fsdp", "ctx", None),
            P("fsdp", "ctx", None),
            P("fsdp"),
            P("fsdp", None),
            P("fsdp", None),
            P("fsdp"),
            P(None, "fsdp"),
            P("fsdp", None),
        ),
        check_vma=False,
    )
```

```python
import functools

import jax
import jax.numpy as jnp
from jax import lax
from jax.experimental import pallas as pl
from jax.experimental.pallas import tpu as pltpu
from jax.sharding import PartitionSpec as P

F32 = jnp.float32
BF16 = jnp.bfloat16
MESH = pl.DeviceIdType.MESH
NT = (((1,), (1,)), ((), ()))
TN = (((0,), (0,)), ((), ()))
EPS = 1e-05
MASKED = -1e30
LOG2E = 1.4426950408889634
SCALE = 0.125
GROUPS = 4
GH = 3
HD = 64
SUB = 1024
VLIM = 60 * 1024 * 1024

VM = pl.BlockSpec(memory_space=pltpu.VMEM)
SM = pl.BlockSpec(memory_space=pltpu.SMEM)
ANY = pl.BlockSpec(memory_space=pl.ANY)
DMA = pltpu.SemaphoreType.DMA


def dot(a, b):
    return jnp.dot(a, b, preferred_element_type=F32)


def dg(a, b, dims):
    return lax.dot_general(a, b, dims, preferred_element_type=F32)


def rcopy(src, dst, send, recv, dev):
    return pltpu.make_async_remote_copy(
        src_ref=src, dst_ref=dst, send_sem=send, recv_sem=recv, device_id=dev, device_id_type=MESH
    )


class Place:
    def __init__(self, n):
        self.n = n
        self.m = n // GROUPS
        self.chips = self.m // 2
        c = lax.axis_index("ctx")
        self.x = lax.axis_index("fsdp")
        self.a = c // self.m
        self.b = c % self.m
        self.chip = self.b // 2
        self.k = self.b % 2

    def xpeer(self):
        return {"fsdp": 1 - self.x}

    def sibling(self):
        return {"ctx": self.a * self.m + self.chip * 2 + 1 - self.k}

    def on_chip(self, chip):
        return {"ctx": self.a * self.m + chip * 2 + self.k}

    def on_line(self, a):
        return {"ctx": a * self.m + self.b}


def greet(p, xpeer=False, sibling=False, chips=False, line=False):
    bar = pltpu.get_barrier_semaphore()
    count = 0
    if xpeer:
        pl.semaphore_signal(bar, inc=1, device_id=p.xpeer(), device_id_type=MESH)
        count += 1
    if sibling:
        pl.semaphore_signal(bar, inc=1, device_id=p.sibling(), device_id_type=MESH)
        count += 1
    if chips:
        for d in range(1, p.chips):
            pl.semaphore_signal(
                bar, inc=1, device_id=p.on_chip((p.chip + d) % p.chips), device_id_type=MESH
            )
            count += 1
    if line:
        for d in range(1, GROUPS):
            pl.semaphore_signal(
                bar, inc=1, device_id=p.on_line((p.a + d) % GROUPS), device_id_type=MESH
            )
            count += 1
    return lambda: pl.semaphore_wait(bar, count)


def turn(p, j):
    last = GROUPS - 1
    outer = jnp.where(p.a == 0, last - j, j)
    inner = (0, last, 1, last - 1)[j]
    return jnp.where((p.a == 0) | (p.a == last), outer, jnp.where(p.a == 1, last - inner, inner))


def ext_of(v):
    last = lax.broadcasted_iota(jnp.int32, v.shape, 1) == v.shape[1] - 1
    return jnp.where(last, -jnp.sum(v, axis=1, keepdims=True), v)


def inv_rms(u):
    return lax.rsqrt(jnp.mean(u * u, axis=1, keepdims=True) + EPS)


def crms_back(u, inv, gain, dy):
    dx = dy * gain
    du = inv * (dx - u * (inv * inv * jnp.mean(dx * u, axis=1, keepdims=True)))
    width = u.shape[1]
    last = lax.broadcasted_iota(jnp.int32, u.shape, 1) == width - 1
    return jnp.where(last, 0.0, du - du[:, width - 1 :])


def low_half(shape):
    return lax.broadcasted_iota(jnp.int32, shape, len(shape) - 1) < HD


def pack_tail(t):
    half = t.shape[0] // 2
    top, bottom = t[:half], t[half:]
    return jnp.where(low_half(top.shape), pltpu.roll(bottom, HD, 1), top)


def unpack_tail(t):
    low = low_half(t.shape)
    zero = jnp.zeros_like(t)
    return jnp.where(low, zero, t), jnp.where(low, zero, pltpu.roll(t, HD, 1))


def causal(shape, sub, size, first_query):
    col = lax.broadcasted_iota(jnp.int32, shape, 1) + sub * size
    row = lax.broadcasted_iota(jnp.int32, shape, 0) + first_query
    return col <= row


def gelu_both(a):
    c = 0.7978845608028654
    a2 = a * a
    t = jnp.tanh(c * a * (1.0 + 0.044715 * a2))
    half = 0.5 * (1.0 + t)
    slope = half + 0.5 * a * (1.0 - t * t) * (c * (1.0 + 0.134145 * a2))
    return a * half, slope


def group_columns(wq, wg):
    width = wq.shape[1] // 3
    low = low_half((wq.shape[0], 128))
    zero = jnp.zeros((wq.shape[0], 128), wq.dtype)

    def swap(t):
        return pltpu.roll(t, HD, 1)

    for j in range(GROUPS // 2):
        a, b = 2 * j, 2 * j + 1
        for i in range(3):
            at = i * width + j * 384
            t0, t1, t2 = (wq[:, at + 128 * t : at + 128 * t + 128] for t in range(3))
            pair = (t0, swap(jnp.where(low, t2, t1)))
            if i < 2:
                third = (jnp.where(low, t1, zero), jnp.where(low, swap(t2), zero))
                for g, p, t in zip((a, b), pair, third):
                    wg[g, :, i * 256 : i * 256 + 128] = p
                    wg[g, :, i * 256 + 128 : i * 256 + 256] = t
            else:
                third = (jnp.where(low, zero, swap(t1)), jnp.where(low, zero, t2))
                for g, p, t in zip((a, b), pair, third):
                    wg[g, :, 512:640] = p
                    wg[g, :, 384:512] = wg[g, :, 384:512] + t


def front_kernel(
    n, lens, ri, ci, g1, g2, wq, wo, wuh, wdh,
    out, gmid_, ysum_, y0, gb_, attg, dog, dg2, rp_, wg_, h1_, q3_, kv_, o3_, l3_, gfull,
    gmid, ysum, rp, wg, h1, q3, kv, o3, l3, gains, wop, wa, woa, wu, wdr, wd, att, wide, hid, gmb, act, gpre, esum, dsend, gb, mid, gk, grads,
    ss, rs, ls, hs, hr, vs, kr, fs, xs, xr, cs, cr, ts, tr, as_, ar, ds_, dr, ks, ks_r, ys, yr, us,
):
    p = Place(n)
    rows, narrow = ri.shape
    width = narrow + 1
    half = width // 2
    ff = wuh.shape[1]
    pk = rows * 3 // 2
    keys = p.m * rows
    size = min(SUB, keys)
    subs = keys // size
    other = 1 - p.x
    others = [(p.chip + d) % p.chips for d in range(1, p.chips)]
    line = [(p.a + d) % GROUPS for d in range(1, GROUPS)]
    ready = greet(p, xpeer=True, sibling=True, chips=True, line=True)
    own_u = pltpu.make_async_copy(wuh, wu.at[p.x], ls.at[5])
    own_d = pltpu.make_async_copy(wdh, wdr.at[p.x], ls.at[6])
    own_u.start()
    own_d.start()

    leaving = []

    def leave(src, dst):
        c = pltpu.make_async_copy(src, dst, us.at[len(leaving)])
        c.start()
        leaving.append(c)

    gains[0:1, :] = g1[...].astype(F32).reshape(1, half)
    gains[1:2, :] = g2[...].astype(F32).reshape(1, half)
    gfull[p.x] = gains[...]
    ready()

    def xc(i, src, dst):
        return rcopy(src, dst, ss.at[i], rs.at[i], p.xpeer())

    at_x = pl.ds(pl.multiple_of(p.x * half, half), half)
    x_gain = xc(0, gains, gfull.at[p.x])
    x_gain.start()
    rp[:, :narrow] = ri[...]
    rp[:, narrow:] = jnp.zeros((rows, 1), BF16)
    u = ext_of(rp[...].astype(F32))
    normed = u * inv_rms(u)
    x_gain.wait()
    gain = jnp.concatenate([gfull[0, 0:1, :], gfull[1, 0:1, :]], axis=1)
    h1[p.a] = (normed * gain).astype(BF16)

    def line_copy(block, dst, sem):
        return rcopy(h1.at[block], h1.at[block], hs.at[sem], hr.at[block], p.on_line(dst))

    @pl.when(p.a < GROUPS - 1)
    def _():
        line_copy(p.a, p.a + 1, 0).start()

    @pl.when(p.a > 0)
    def _():
        line_copy(p.a, p.a - 1, 1).start()

    group_columns(wq, wg)
    x_wa = xc(1, wg.at[p.a], wa.at[at_x])
    x_wa.start()
    own_a = pltpu.make_async_copy(wg.at[p.a], wa.at[at_x], ls.at[0])
    own_a.start()
    leave(rp, rp_)
    leave(wg, wg_)

    def up_rows(j, chip, core):
        size_i = width // p.m // 3
        return pl.ds(pl.multiple_of(((chip * 2 + core) * 3 + j) * size_i, size_i), size_i)

    def up_x(j):
        at = up_rows(j, p.chip, p.k)
        return rcopy(wuh.at[at], wu.at[p.x, at], xs.at[j], xr.at[j], p.xpeer())

    def up_chip(j, owner, to):
        r = wu.at[other, up_rows(j, owner, p.k)]
        return rcopy(r, r, cs.at[j, to], cr.at[j, owner], p.on_chip(to))

    def up_core(j, owner, core):
        r = wu.at[other, up_rows(j, owner, core)]
        return rcopy(r, r, ts.at[j, owner], tr.at[j, owner], p.sibling())

    def up_spread(j):
        up_x(j).wait_recv()
        for c in others:
            up_chip(j, p.chip, c).start()
        up_core(j, p.chip, p.k).start()

    def up_pass(j):
        for c in others:
            up_chip(j, c, c).wait_recv()
            up_core(j, c, p.k).start()

    def down_rows(chip, core):
        size_i = ff // p.m
        return pl.ds(pl.multiple_of((chip * 2 + core) * size_i, size_i), size_i)

    def down_x():
        at = down_rows(p.chip, p.k)
        return rcopy(wdh.at[at], wdr.at[p.x, at], xs.at[3], xr.at[3], p.xpeer())

    def down_chip(owner, to):
        r = wdr.at[other, down_rows(owner, p.k)]
        return rcopy(r, r, cs.at[3, to], cr.at[3, owner], p.on_chip(to))

    def down_core(owner, core):
        r = wdr.at[other, down_rows(owner, core)]
        return rcopy(r, r, ts.at[3, owner], tr.at[3, owner], p.sibling())

    for j in range(3):
        up_x(j).start()
    down_x().start()

    wop[:, :narrow] = wo[...]
    wop[:, narrow:] = jnp.zeros((half, 1), BF16)
    xo = []
    local = []
    for i in range(2):
        g = p.x * 2 + i
        for j, (src, count, dst) in enumerate(((0, 128, 0), (128, 64, 192))):
            s_ = wop.at[pl.ds(i * 192 + src, count)]
            d_ = woa.at[pl.ds(pl.multiple_of(g * 256 + dst, 64), count)]
            xo.append(xc(2 + 2 * i + j, s_, d_))
            local.append(pltpu.make_async_copy(s_, d_, ls.at[1 + 2 * i + j]))
    zero_rows = jnp.zeros((HD, width), BF16)
    for g in range(GROUPS):
        woa[pl.ds(g * 256 + 128, HD), :] = zero_rows
    for c in xo:
        c.start()
    for c in local:
        c.start()
    slot = (p.a * p.m + p.b) * rows + lax.broadcasted_iota(jnp.int32, (rows, width), 0)
    live = slot < lens[0]
    gmb[0, :, :narrow] = ci[...]
    gmb[0, :, narrow:] = jnp.zeros((rows, 1), BF16)
    gmb[0] = jnp.where(live, gmb[0].astype(F32), 0.0).astype(BF16)
    x_gm = xc(6, gmb.at[0], gmb.at[1])
    x_gm.start()
    def kv_copy(block, b, dev, send):
        r = kv.at[pl.ds(pl.multiple_of((block * p.m + b) * rows, rows), rows)]
        return rcopy(r, r, send, kr.at[block, b], dev)

    def ac(i, to):
        return rcopy(att.at[to], attg.at[i], as_.at[to], ar.at[i], p.on_line(to))

    own_a.wait()
    x_wa.wait()

    def produce(block):
        y = dot(h1[block], wa[...]).astype(BF16)
        low = low_half((rows, 128))
        zero = jnp.zeros((rows, 128), BF16)
        at = pl.ds(pl.multiple_of(block * rows, rows), rows)
        q3[0, at, :] = jnp.where(low, y[:, :128], zero)
        q3[1, at, :] = jnp.where(low, zero, y[:, :128])
        q3[2, at, :] = y[:, 128:256]
        kv[pl.ds(pl.multiple_of((block * p.m + p.b) * rows, rows), rows), :] = y[:, 256:]
        for d in range(1, p.chips):
            kv_copy(block, p.b, p.on_chip((p.chip + d) % p.chips), vs.at[block, d]).start()
        kv_copy(block, p.b, p.sibling(), vs.at[block, 0]).start()

    def pass_on(block):
        for d in range(1, p.chips):
            b = ((p.chip + d) % p.chips) * 2 + p.k
            kv_copy(block, b, p.sibling(), fs.at[block, d]).wait_recv()
            kv_copy(block, b, p.sibling(), fs.at[block, d]).start()

    def complete(block):
        for c in range(p.chips):
            kv_copy(block, c * 2 + 1 - p.k, p.sibling(), vs.at[block, 0]).wait_recv()

    first_query = p.b * rows
    dead = jnp.where(lens[0] > keys, 0.0, 1.0).astype(F32)

    def pair(z, c, diagonal):
        at_q = pl.ds(pl.multiple_of(z * rows, rows), rows)
        gone = jnp.where(c > 0, dead, 0.0)
        for h in range(GH):
            kt = 128 * (h // 2)
            vt = 128 if h == 2 else 256
            q = q3[h, at_q, :]

            def keys_of(sub, first):
                at = pl.ds(pl.multiple_of(c * keys + sub * size, size), size)
                scores = dg(q, kv[at, kt : kt + 128], NT) * (SCALE * LOG2E)
                if diagonal:
                    scores = jnp.where(causal(scores.shape, sub, size, first_query), scores, MASKED)
                here = jnp.max(scores, axis=1, keepdims=True) + gone * MASKED
                if first:
                    newest = here
                else:
                    top = l3[h, at_q, 0:1]
                    newest = jnp.maximum(top, here)
                weights = jnp.exp2(scores - (newest - gone * (3.0 * MASKED)))
                sums = jnp.sum(weights, axis=1, keepdims=True)
                part = dot(weights.astype(BF16), kv[at, vt : vt + 128])
                if not first:
                    shrink = jnp.exp2(top - newest)
                    sums = sums + l3[h, at_q, HD : HD + 1] * shrink
                    part = part + o3[h, at_q, :] * shrink
                o3[h, at_q, :] = part
                l3[h, at_q, :] = jnp.where(low_half((rows, 128)), newest, sums)

            keys_of(0, diagonal)
            if subs > 1:

                def rest(sub, carry):
                    keys_of(sub, False)
                    return carry

                lax.fori_loop(1, subs, rest, 0)

    def finish_row(z):
        at_q = pl.ds(pl.multiple_of(z * rows, rows), rows)
        heads = []
        for h in range(GH):
            total = l3[h, at_q, HD : HD + 1]
            o = o3[h, at_q, :] / total
            o3[h, at_q, :] = o
            l3[h, at_q, :] = jnp.broadcast_to(l3[h, at_q, 0:1] + jnp.log2(total), (rows, 128))
            heads.append(o)
        att[z, 0:rows, :] = jnp.where(low_half((rows, 128)), heads[0], heads[1]).astype(BF16)
        att[z, rows:pk, :] = pack_tail(heads[2]).astype(BF16)

        @pl.when(z == p.a)
        def _():
            attg[z] = att[z]

        @pl.when(z != p.a)
        def _():
            ac(p.a, z).start()

    def far(z):
        return jnp.abs(z - p.a)

    def pairs(t):
        def row(z, carry):
            @pl.when(far(z) == t)
            def _():
                pair(z, z, True)

            def key(d, carry):
                @pl.when(jnp.maximum(far(z), far(z - d)) == t)
                def _():
                    pair(z, z - d, False)

                return carry

            lax.fori_loop(1, z + 1, key, 0)

            @pl.when(jnp.maximum(far(z), p.a) == t)
            def _():
                finish_row(z)

            return carry

        lax.fori_loop(0, GROUPS, row, 0)

    def step(s, carry):
        below = p.a - s
        above = p.a + s

        @pl.when((s > 0) & (below >= 0))
        def _():
            line_copy(below, p.a, 0).wait_recv()

            @pl.when(p.a < GROUPS - 1)
            def _():
                line_copy(below, p.a + 1, 2 * s).start()

        @pl.when((s > 0) & (above < GROUPS))
        def _():
            line_copy(above, p.a, 0).wait_recv()

            @pl.when(p.a > 0)
            def _():
                line_copy(above, p.a - 1, 2 * s + 1).start()

        @pl.when(below >= 0)
        def _():
            produce(below)

        @pl.when((s > 0) & (above < GROUPS))
        def _():
            produce(above)

        for j in range(3):

            @pl.when(s == j + 1)
            def _():
                up_spread(j)

        @pl.when(s == GROUPS)
        def _():
            down_x().wait_recv()
            for c in others:
                down_chip(p.chip, c).start()
            down_core(p.chip, p.k).start()

        @pl.when((s > 0) & (below + 1 >= 0))
        def _():
            pass_on(below + 1)
            complete(below + 1)

        @pl.when((s > 1) & (above - 1 < GROUPS))
        def _():
            pass_on(above - 1)
            complete(above - 1)

        @pl.when(s > 0)
        def _():
            pairs(s - 1)

        for j in range(3):

            @pl.when(s == j + 2)
            def _():
                up_pass(j)

        return carry

    lax.fori_loop(0, GROUPS + 1, step, 0)
    for src, dst in ((h1, h1_), (q3, q3_), (kv, kv_), (o3, o3_), (l3, l3_)):
        leave(src, dst)

    own_u.wait()
    own_d.wait()

    def pad_down(f):
        wd[f, :, :narrow] = wdr[f]
        wd[f, :, narrow:] = jnp.zeros((ff, 1), BF16)

    pad_down(p.x)
    for c in xo:
        c.wait()
    for c in local:
        c.wait()
    for g in line:
        ac(g, g).wait_recv()
    for g in range(GROUPS):
        wide[:, g * 256 : g * 256 + 128] = attg[g, 0:rows, :]
        top, bottom = unpack_tail(attg[g, rows:pk, :])
        wide[0 : rows // 2, g * 256 + 128 : g * 256 + 256] = top
        wide[rows // 2 : rows, g * 256 + 128 : g * 256 + 256] = bottom
    mid[...] = rp[...].astype(F32) + dot(wide[...], woa[...])
    u = ext_of(mid[...])
    gain = jnp.concatenate([gfull[0, 1:2, :], gfull[1, 1:2, :]], axis=1)
    hid[0] = (u * inv_rms(u) * gain).astype(BF16)
    x_hid = xc(9, hid.at[0], hid.at[1])
    x_hid.start()
    wide_tile = 512

    def up(slot, token, f):
        def tile(t, carry):
            at = pl.ds(pl.multiple_of(t * wide_tile, wide_tile), wide_tile)
            a, slope = gelu_both(dot(hid[token], wu[f, :, at]))
            act[slot, :, at] = a.astype(BF16)
            gpre[slot, :, at] = (slope * dg(gmb[token], wd[f, at, :], NT)).astype(BF16)
            return carry

        lax.fori_loop(0, ff // wide_tile, tile, 0)

    up(0, 0, p.x)
    for c in others:
        down_chip(c, c).wait_recv()
        down_core(c, p.k).start()
    for j in range(3):
        for c in range(p.chips):
            up_core(j, c, 1 - p.k).wait_recv()
    for c in range(p.chips):
        down_core(c, 1 - p.k).wait_recv()
    pad_down(other)
    up(2, 0, other)

    def e_tile(t, carry):
        at = pl.ds(pl.multiple_of(t * 256, 256), 256)
        e = dg(gpre[0], wu[p.x, at, :], NT) + dg(gpre[2], wu[other, at, :], NT)
        esum[t] = e
        return carry

    lax.fori_loop(0, width // 256, e_tile, 0)
    e = jnp.concatenate([esum[t] for t in range(width // 256)], axis=1)
    u = ext_of(mid[...])
    inv = inv_rms(u)
    gmid[...] = gmb[0].astype(F32) + crms_back(u, inv, gain, e)
    leave(gmid, gmid_)
    gb[...] = gmid[...].astype(BF16)
    leave(gb, gb_)

    def dc(i, to):
        return rcopy(dsend.at[to], dog.at[i], ds_.at[to], dr.at[i], p.on_line(to))

    for d in range(1, GROUPS + 1):
        to = (p.a + d) % GROUPS
        w = woa[pl.ds(pl.multiple_of(to * 256, 256), 256), :]
        da = dg(gb[...], w, NT).astype(BF16)
        if d < GROUPS:
            dsend[to, 0:rows, :] = da[:, 0:128]
            dsend[to, rows:pk, :] = pack_tail(da[:, 128:256])
            dc(p.a, to).start()
        else:
            dog[to, 0:rows, :] = da[:, 0:128]
            dog[to, rows:pk, :] = pack_tail(da[:, 128:256])
    x_gm.wait()
    x_hid.wait()
    up(1, 1, p.x)

    def finish_out():
        final = mid[...] + dot(act[0], wd[p.x]) + dot(act[2], wd[other])
        out[...] = final.astype(BF16)

    shared = grads.shape != wd.shape
    gm = wd if shared else grads
    if shared:
        finish_out()
    piece = ysum.shape[2]
    part = GROUPS * piece

    def kc(chip):
        at = pl.ds(pl.multiple_of(chip * part, part), part)
        return rcopy(gm.at[1 - p.k, at], gk.at[at], ks.at[chip], ks_r.at[chip], p.sibling())

    def grad_up(t, carry):
        at = pl.ds(pl.multiple_of(t * 384, 384), 384)
        g = dg(hid[0], gpre[0, :, at], TN) + dg(hid[1], gpre[1, :, at], TN)
        per = width // 384
        r0 = pl.multiple_of((t // per) * width, width)
        c0 = pl.multiple_of((t % per) * 384, 384)
        gm[0, pl.ds(r0, width), pl.ds(c0, 384)] = g.astype(BF16)
        return carry

    def grad_down(t, carry):
        at = pl.ds(pl.multiple_of(t * 384, 384), 384)
        g = dg(act[0, :, at], gmb[0], TN) + dg(act[1, :, at], gmb[1], TN)
        gm[1, at, :] = g.astype(BF16)
        return carry

    @pl.when(p.k == 0)
    def _():
        lax.fori_loop(0, ff // 384, grad_down, 0)

    @pl.when(p.k == 1)
    def _():
        lax.fori_loop(0, ff // 384, grad_up, 0)

    for c in others:
        kc(c).start()
    kc(p.chip).start()

    @pl.when(p.k == 0)
    def _():
        lax.fori_loop(0, ff // 384, grad_up, 0)

    @pl.when(p.k == 1)
    def _():
        lax.fori_loop(0, ff // 384, grad_down, 0)

    def over_chips(chip, slot):
        return rcopy(ysum.at[chip, turn(p, 0)], y0.at[slot], ys.at[chip], yr.at[slot], p.on_chip(chip))

    def core_sum(chip, z):
        at = pl.ds(pl.multiple_of(chip * part + z * piece, 16), piece)
        ysum[chip, z] = (gm[p.k, at, :].astype(F32) + gk[at, :].astype(F32)).astype(BF16)

    for chip in others:
        kc(chip).wait()
        core_sum(chip, turn(p, 0))
        over_chips(chip, p.chip).start()
    if not shared:
        finish_out()
    for j in range(1, GROUPS):
        for chip in others:
            core_sum(chip, turn(p, j))
    kc(p.chip).wait()
    for j in range(GROUPS):
        core_sum(p.chip, turn(p, j))
    y0[p.chip] = ysum[p.chip, turn(p, 0)]
    leave(ysum, ysum_)
    dg2[...] = jnp.broadcast_to(jnp.sum(e * (u * inv), axis=0, keepdims=True), dg2.shape)

    for c in others:
        over_chips(c, p.chip).wait_send()
        over_chips(c, c).wait_recv()
    for g in line:
        ac(p.a, g).wait_send()
        dc(p.a, g).wait_send()
        dc(g, g).wait_recv()
    for block in range(GROUPS):
        kv_copy(block, p.b, p.sibling(), vs.at[block, 0]).wait_send()
        for d in range(1, p.chips):
            kv_copy(block, p.b, p.sibling(), vs.at[block, d]).wait_send()
            b = ((p.chip + d) % p.chips) * 2
            kv_copy(block, b + p.k, p.sibling(), fs.at[block, d]).wait_send()
    for s in range(GROUPS):

        @pl.when((p.a - s >= 0) & (p.a < GROUPS - 1))
        def _():
            line_copy(p.a - s, p.a + 1, 2 * s).wait_send()

        @pl.when((p.a + s < GROUPS) & (p.a > 0))
        def _():
            line_copy(p.a + s, p.a - 1, 2 * s + 1).wait_send()

    for j in range(3):
        up_x(j).wait_send()
        for c in others:
            up_chip(j, p.chip, c).wait_send()
        for c in range(p.chips):
            up_core(j, c, p.k).wait_send()
    down_x().wait_send()
    for c in others:
        down_chip(p.chip, c).wait_send()
    for c in range(p.chips):
        down_core(c, p.k).wait_send()
    for c in leaving:
        c.wait()


def front(n, lens, ri, ci, g1, g2, wq, wo, wu, wd):
    rows, narrow = ri.shape
    width = narrow + 1
    half = width // 2
    ff = wu.shape[1]
    pk = rows * 3 // 2
    m = n // GROUPS
    chips = m // 2
    piece = ff // GROUPS // chips
    lanes = 640
    sds = jax.ShapeDtypeStruct
    v = pltpu.VMEM
    heads = (GH, GROUPS * rows, 128)
    sem = lambda *shape: [DMA(shape), DMA(shape)]
    return pl.pallas_call(
        functools.partial(front_kernel, n),
        name="front",
        out_shape=(
            sds((rows, width), BF16),
            sds((rows, width), F32),
            sds((chips, GROUPS, piece, width), BF16),
            sds((chips, piece, width), BF16),
            sds((rows, width), BF16),
            sds((GROUPS, pk, 128), BF16),
            sds((GROUPS, pk, 128), BF16),
            sds((8, width), F32),
            sds((rows, width), BF16),
            sds((GROUPS, half, lanes), BF16),
            sds((GROUPS, rows, width), BF16),
            sds(heads, BF16),
            sds((n * rows, 384), BF16),
            sds(heads, F32),
            sds(heads, F32),
            sds((2, 8, half), F32),
        ),
        in_specs=[SM, VM, VM, VM, VM, VM, VM, ANY, ANY],
        out_specs=[VM, ANY, ANY, VM, ANY] + [VM] * 3 + [ANY] * 7 + [VM],
        scratch_shapes=[
            v((rows, width), F32),
            v((chips, GROUPS, piece, width), BF16),
            v((rows, width), BF16),
            v((GROUPS, half, lanes), BF16),
            v((GROUPS, rows, width), BF16),
            v(heads, BF16),
            v((n * rows, 384), BF16),
            v(heads, F32),
            v(heads, F32),
            v((8, half), F32),
            v((half, width), BF16),
            v((width, lanes), BF16),
            v((GROUPS * 256, width), BF16),
            v((2, width, ff), BF16),
            v((2, ff, narrow), BF16),
            v((2, ff, width), BF16),
            v((GROUPS, pk, 128), BF16),
            v((rows, GROUPS * 256), BF16),
            v((2, rows, width), BF16),
            v((2, rows, width), BF16),
            v((3, rows, ff), BF16),
            v((3, rows, ff), BF16),
            v((width // 256, rows, 256), F32),
            v((GROUPS, pk, 128), BF16),
            v((rows, width), BF16),
            v((rows, width), F32),
            v((ff, width), BF16),
            v((2, ff, width) if m * rows <= SUB else (8, 128), BF16),
            *sem(10),
            DMA((7,)),
            DMA((2 * GROUPS,)),
            DMA((GROUPS,)),
            DMA((GROUPS, chips)),
            DMA((GROUPS, m)),
            DMA((GROUPS, chips)),
            *sem(4),
            *sem(4, chips),
            *sem(4, chips),
            *sem(GROUPS),
            *sem(GROUPS),
            *sem(chips),
            *sem(chips),
            DMA((10,)),
        ],
        compiler_params=pltpu.CompilerParams(
            collective_id=0, has_side_effects=True, vmem_limit_bytes=67043328
        ),
    )(lens, ri, ci, g1, g2, wq, wo, wu, wd)


def back_kernel(
    n, lens, q3_, kv, o3, l3_, dog_, wg, h1_, rp_, gmid_, gfull, dg2, ysum, y0, gb_, att_,
    gin, gq, gains, res_, goo,
    q3, l3, dog, res, h1, rp, gmid, go, gb, att, red, ymine, yq, do3, dq3, kvc, dkv, dkvb, rk, ry, wfull, gps, gpr, gqb, qk, qx, qy,
    qs_, qz_, qr_, g0, gk, gx, gy, ga, left, right, sumr, suml, ok, os_, oy, oz, ozr,
    xs, xr, ls, vs, ks, kr, ys, yr, zs, zr, ws, wr, qs, qr, ns, nr, bs, br, cs, cr,
    rs_, rr, ls_, lr, as_, ar, es, er, fs, fr, ts, tr, us, ur, is_, ir, ps, pr, ws2, wr2, zs2, zr2, vs2, vr2, fs2, fr2,
):
    p = Place(n)
    rows, width = rp_.shape
    half = width // 2
    quarter = width // 4
    last = GROUPS - 1
    keys = dkv.shape[0]
    size = min(SUB, keys)
    subs = keys // size
    slots = kvc.shape[0]
    others = [(p.chip + d) % p.chips for d in range(1, p.chips)]
    line = [(p.a + d) % GROUPS for d in range(1, GROUPS)]
    ready = greet(p, xpeer=True, sibling=True, chips=True, line=True)
    at_x = pl.ds(pl.multiple_of(p.x * half, half), half)
    local = [
        pltpu.make_async_copy(wg.at[g], wfull.at[g, at_x], ls.at[g]) for g in range(GROUPS)
    ]

    def chunk_of(i):
        return (p.a + 1 + i) % GROUPS

    def fetch(i):
        c = chunk_of(i)
        src = kv.at[pl.ds(pl.multiple_of(c * keys, keys), keys)]
        return pltpu.make_async_copy(src, kvc.at[i % slots], vs.at[i % slots])

    first_in = [
        pltpu.make_async_copy(src, dst, ls.at[GROUPS + 7 + i])
        for i, (src, dst) in enumerate(((dog_, dog), (q3_, q3), (l3_, l3)))
    ]
    for c in first_in:
        c.start()
    fetch(0).start()
    o_in = pltpu.make_async_copy(o3, dq3, ls.at[GROUPS])
    o_in.start()
    y_in = pltpu.make_async_copy(ysum.at[p.chip], ymine, ls.at[GROUPS + 1])
    y_in.start()
    late = [
        pltpu.make_async_copy(src, dst, ls.at[GROUPS + 2 + i])
        for i, (src, dst) in enumerate(((h1_, h1), (rp_, rp), (gmid_, gmid)))
    ]
    for c in late:
        c.start()
    gos = [
        pltpu.make_async_copy(src, dst, ls.at[GROUPS + 5 + i])
        for i, (src, dst) in enumerate(((gb_, gb.at[0]), (att_.at[pl.ds(p.x * 2, 2)], att.at[0])))
    ]
    for c in gos:
        c.start()
    gox = [
        rcopy(src, dst, zs2.at[i], zr2.at[i], p.xpeer())
        for i, (src, dst) in enumerate(((gb_, gb.at[1]), (att_.at[pl.ds((1 - p.x) * 2, 2)], att.at[1])))
    ]
    for c in local:
        c.start()

    def weight_rows(x, core):
        return pl.ds(pl.multiple_of(x * half + core * quarter, quarter), quarter)

    def weight_x(g):
        src = wg.at[g, pl.ds(pl.multiple_of(p.k * quarter, quarter), quarter)]
        return rcopy(src, wfull.at[g, weight_rows(p.x, p.k)], xs.at[g], xr.at[g], p.xpeer())

    def weight_core(g, core):
        r = wfull.at[g, weight_rows(1 - p.x, core)]
        return rcopy(r, r, ws2.at[g], wr2.at[g], p.sibling())

    def over_chips(chip, slot, z):
        return rcopy(ysum.at[chip, z], yq.at[slot, z], ps.at[chip, z], pr.at[slot, z], p.on_chip(chip))

    def chip_sum(j):
        z = turn(p, j)
        total = ymine[z].astype(F32)
        for c in others:
            if j > 0:
                over_chips(c, c, z).wait_recv()
                total = total + yq[c, z].astype(F32)
            else:
                total = total + y0[c].astype(F32)
        red[z] = total.astype(BF16)
        if j < last:

            @pl.when(p.a == 0)
            def _():
                rightward(z, red.at[z]).start()

            @pl.when(p.a == last)
            def _():
                leftward(z, red.at[z]).start()

    def rightward(z, src):
        return rcopy(src, left.at[z], rs_.at[z], rr.at[z], p.on_line(jnp.minimum(p.a + 1, last)))

    def leftward(z, src):
        return rcopy(src, right.at[z], ls_.at[z], lr.at[z], p.on_line(jnp.maximum(p.a - 1, 0)))

    def reduce_step(s):
        @pl.when((p.a >= 1) & (p.a <= s))
        def _():
            z = last + p.a - s
            rightward(z, sumr.at[z]).wait_recv()
            if s < last:
                sumr[z] = (red[z].astype(F32) + left[z].astype(F32)).astype(BF16)
                rightward(z, sumr.at[z]).start()

        b = last - p.a

        @pl.when((b >= 1) & (b <= s))
        def _():
            z = s - b
            leftward(z, suml.at[z]).wait_recv()
            if s < last:
                suml[z] = (red[z].astype(F32) + right[z].astype(F32)).astype(BF16)
                leftward(z, suml.at[z]).start()

    def line_share(z, dst, sem):
        r = res.at[p.k, p.chip, z]
        return rcopy(r, r, as_.at[sem], ar.at[z], p.on_line(dst))

    def chip_share(chip, z, dst):
        r = res.at[p.k, chip, z]
        return rcopy(r, r, es.at[dst, z], er.at[chip, z], p.on_chip(dst))

    def core_share(core, chip, z):
        r = res.at[core, chip, z]
        return rcopy(r, r, fs.at[chip, z], fr.at[chip, z], p.sibling())

    def spread(z):
        for c in others:
            chip_share(p.chip, z, c).start()
        core_share(p.k, p.chip, z).start()

    def gather_first():
        z = p.a
        res[p.k, p.chip, z] = red[z]

        @pl.when(p.a > 0)
        def _():
            cur = res[p.k, p.chip, z].astype(F32)
            res[p.k, p.chip, z] = (cur + left[z].astype(F32)).astype(BF16)

        @pl.when(p.a < last)
        def _():
            cur = res[p.k, p.chip, z].astype(F32)
            res[p.k, p.chip, z] = (cur + right[z].astype(F32)).astype(BF16)
            line_share(z, p.a + 1, 0).start()

        @pl.when(p.a > 0)
        def _():
            line_share(z, p.a - 1, 1).start()

    def gather_step(s):
        @pl.when(p.a - s >= 0)
        def _():
            line_share(p.a - s, p.a, 0).wait_recv()

            @pl.when(p.a < last)
            def _():
                line_share(p.a - s, p.a + 1, 2 * s).start()

            if s > 1:
                spread(p.a - s)
            else:

                @pl.when(p.a == last)
                def _():
                    spread(p.a - s)

        @pl.when(p.a + s <= last)
        def _():
            line_share(p.a + s, p.a, 0).wait_recv()

            @pl.when(p.a > 0)
            def _():
                line_share(p.a + s, p.a - 1, 2 * s + 1).start()

            spread(p.a + s)

    def pass_on(z):
        for c in others:
            chip_share(c, z, c).wait_recv()
            core_share(p.k, c, z).start()

    orow = half // 2
    oc = os_.shape[0]
    oyrow = orow // oc
    opart = oyrow // GROUPS
    my = p.chip if oc > 1 else 0

    def out_core():
        at = pl.ds(pl.multiple_of((1 - p.k) * orow, orow), orow)
        return rcopy(go.at[at], ok, is_.at[0], ir.at[0], p.sibling())

    def out_chip(chip, slot):
        return rcopy(os_.at[chip if oc > 1 else 0], oy.at[slot], ts.at[chip], tr.at[slot], p.on_chip(chip))

    def out_line(slot, to):
        return rcopy(oz.at[to], ozr.at[slot], us.at[to], ur.at[slot], p.on_line(to))

    def out_back(slot, to):
        r = goo.at[p.k, my, slot]
        return rcopy(r, r, us.at[GROUPS + to], ur.at[GROUPS + slot], p.on_line(to))

    def out_spread(chip, z, to):
        r = goo.at[p.k, chip, z]
        return rcopy(r, r, fs2.at[z, to], fr2.at[z, chip], p.on_chip(to))

    def out_share(core, chip, z):
        r = goo.at[core, chip, z]
        i = 1 + chip * GROUPS + z
        return rcopy(r, r, is_.at[i], ir.at[i], p.sibling())

    def out_0():
        for c in gos + gox:
            c.wait()
        for i in range(2):
            tails = [jnp.concatenate(unpack_tail(att[s, i, rows:, :]), axis=0) for s in range(2)]
            g = dg(att[0, i, 0:rows, :], gb[0], TN) + dg(att[1, i, 0:rows, :], gb[1], TN)
            go[i * 192 : i * 192 + 128, :] = g.astype(BF16)
            g = dg(tails[0], gb[0], TN) + dg(tails[1], gb[1], TN)
            go[i * 192 + 128 : i * 192 + 192, :] = g[HD:, :].astype(BF16)
        out_core().start()

    def out_1():
        out_core().wait()
        at = pl.ds(pl.multiple_of(p.k * orow, orow), orow)
        total = go[at, :].astype(F32) + ok[...].astype(F32)
        for c in range(oc):
            os_[c] = total[c * oyrow : (c + 1) * oyrow].astype(BF16)
        for c in others:
            out_chip(c, p.chip).start()

    def out_2():
        total = os_[my].astype(F32)
        for c in others:
            out_chip(c, c).wait_recv()
            total = total + oy[c].astype(F32)
        for z in range(GROUPS):
            oz[z] = total[z * opart : (z + 1) * opart].astype(BF16)
        for z in line:
            out_line(p.a, z).start()

    def out_3():
        total = oz[p.a].astype(F32)
        for z in line:
            out_line(z, z).wait_recv()
            total = total + ozr[z].astype(F32)
        goo[p.k, my, p.a] = total.astype(BF16)
        for z in line:
            out_back(p.a, z).start()

    def out_4():
        for z in line:
            out_back(z, z).wait_recv()
        for z in range(GROUPS):
            if oc > 1:
                for c in others:
                    out_spread(p.chip, z, c).start()
            out_share(p.k, my, z).start()

    def kc(i, chip):
        c = chunk_of(i)
        at = pl.ds(pl.multiple_of((chip * 2 + 1 - p.k) * rows, rows), rows)
        return rcopy(
            dkvb.at[at], rk.at[c, chip], ks.at[c, chip], kr.at[c, chip], p.sibling()
        )

    def yc(c, chip, slot):
        return rcopy(rk.at[c, chip], ry.at[c, slot], ys.at[c, chip], yr.at[c, slot], p.on_chip(chip))

    def zkv(slot, to):
        lanes = pl.ds(256, 384)
        return rcopy(
            gps.at[to, :, lanes], gpr.at[slot, :, lanes], zs.at[to], zr.at[slot], p.on_line(to)
        )

    def zq(slot, to):
        return rcopy(qz_.at[to], qr_.at[slot], ws.at[to], wr.at[slot], p.on_line(to))

    def mine(chip):
        at = pl.ds(pl.multiple_of((chip * 2 + p.k) * rows, rows), rows)
        return dkvb[at, :].astype(F32)

    def kv_1(i):
        dkvb[...] = dkv[...].astype(BF16)
        for c in others:
            kc(i, c).start()
        kc(i, p.chip).start()

    def kv_2(i):
        c = chunk_of(i)
        for chip in others:
            kc(i, chip).wait()
            rk[c, chip] = (mine(chip) + rk[c, chip].astype(F32)).astype(BF16)
            yc(c, chip, p.chip).start()
        kc(i, p.chip).wait()
        rk[c, p.chip] = (mine(p.chip) + rk[c, p.chip].astype(F32)).astype(BF16)

    def kv_3(i, send):
        c = chunk_of(i)
        total = rk[c, p.chip].astype(F32)
        for chip in others:
            yc(c, chip, chip).wait_recv()
            total = total + ry[c, chip].astype(F32)
        gps[c, :, 256:640] = total.astype(BF16)
        if send:
            zkv(p.a, c).start()

    ready()
    for j in range(1, last):
        for c in others:
            over_chips(c, p.chip, turn(p, j)).start()
    for c in gox:
        c.start()
    for g in range(GROUPS):
        weight_x(g).start()

    first_query = p.b * rows
    low = low_half((rows, 128))
    for c in first_in:
        c.wait()
    o_in.wait()
    y_in.wait()
    chip_sum(0)
    for z in range(GROUPS):
        at = pl.ds(z * rows, rows)
        both = dog[z, 0:rows, :]
        zero = jnp.zeros_like(both)
        do3[0, at, :] = jnp.where(low, both, zero)
        do3[1, at, :] = jnp.where(low, zero, both)
        top, bottom = unpack_tail(dog[z, rows:, :])
        do3[2, pl.ds(z * rows, rows // 2), :] = top
        do3[2, pl.ds(z * rows + rows // 2, rows // 2), :] = bottom
        for h in range(GH):
            delta = jnp.sum(dq3[h, at, :] * do3[h, at, :].astype(F32), axis=1, keepdims=True)
            gqb[h * rows : (h + 1) * rows, z * 128 : (z + 1) * 128] = jnp.broadcast_to(delta, (rows, 128))
    dq3[...] = jnp.zeros_like(dq3)
    gone = jnp.where(lens[0] > keys, 0.0, -MASKED).astype(F32)

    def chunk(i, carry):
        c = chunk_of(i)
        fetch(i).wait()

        if slots > 1:

            @pl.when(i < last)
            def _():
                fetch(i + 1).start()

        dead = jnp.where(c > 0, gone, 0.0)

        def head(h, carry):
            kt = pl.multiple_of(128 * (h // 2), 128)
            vt = pl.multiple_of(jnp.where(h == 2, 128, 256), 128)

            def step(z, masked):
                at_q = pl.ds(pl.multiple_of(z * rows, rows), rows)
                q = q3[h, at_q, :]
                do = do3[h, at_q, :]
                lse = l3[h, at_q, 0:1] + dead
                delta = gqb[
                    pl.ds(pl.multiple_of(h * rows, rows), rows),
                    pl.ds(pl.multiple_of(z * 128, 128), 128),
                ][:, 0:1]
                def keys_of(sub, carry):
                    at = pl.ds(pl.multiple_of(sub * size, size), size)
                    k = kvc[i % slots, at, pl.ds(kt, 128)]
                    v = kvc[i % slots, at, pl.ds(vt, 128)]
                    scores = dg(q, k, NT) * (SCALE * LOG2E)
                    if masked:
                        scores = jnp.where(
                            causal(scores.shape, sub, size, first_query), scores, MASKED
                        )
                    weights = jnp.exp2(scores - lse)
                    gp = dg(do, v, NT)
                    gs = (weights * (gp - delta)).astype(BF16)
                    dq3[h, at_q, :] += dot(gs, k)
                    gv = dg(weights.astype(BF16), do, TN)
                    gk_ = dg(gs, q, TN) * SCALE
                    if masked:
                        dkv[at, pl.ds(kt, 128)] = jnp.where(h == 1, dkv[at, pl.ds(kt, 128)], 0.0) + gk_
                        dkv[at, pl.ds(vt, 128)] = jnp.where(h == 0, 0.0, dkv[at, pl.ds(vt, 128)]) + gv
                    else:
                        dkv[at, pl.ds(kt, 128)] += gk_
                        dkv[at, pl.ds(vt, 128)] += gv
                    return carry

                if subs > 1:
                    lax.fori_loop(0, subs, keys_of, 0)
                else:
                    keys_of(0, 0)

            step(c, True)

            def rest(z, carry):
                step(z, False)
                return carry

            lax.fori_loop(c + 1, GROUPS, rest, 0)

            @pl.when(h == 0)
            def _():
                @pl.when(i >= 1)
                def _():
                    kv_2(i - 1)

                @pl.when(i == 1)
                def _():
                    for c in others:
                        over_chips(c, p.chip, turn(p, last)).start()
                    chip_sum(1)
                    reduce_step(1)

                @pl.when(i == 2)
                def _():
                    reduce_step(2)

                @pl.when(i == 3)
                def _():
                    chip_sum(3)
                    reduce_step(3)
                    gather_first()

            @pl.when((h == 1) & (i >= 2))
            def _():
                kv_3(i - 2, True)

            @pl.when(h == 2)
            def _():
                @pl.when(i == 1)
                def _():
                    chip_sum(2)
                    out_0()

                @pl.when(i == last)
                def _():
                    for g in range(GROUPS):
                        weight_x(g).wait_recv()
                        weight_core(g, p.k).start()

            return carry

        lax.fori_loop(0, GH, head, 0)
        if slots == 1:

            @pl.when(i < last)
            def _():
                fetch(i + 1).start()

        kv_1(i)
        return carry

    lax.fori_loop(0, GROUPS, chunk, 0)
    kv_2(3)
    spread(p.a)
    out_1()
    for d in range(1, GROUPS + 1):
        z = (p.a + d) % GROUPS
        at = pl.ds(pl.multiple_of(z * rows, rows), rows)
        gps[z, :, 0:128] = (jnp.where(low, dq3[0, at, :], dq3[1, at, :]) * SCALE).astype(BF16)
        third = (jnp.where(low, dq3[2, at, :], 0.0) * SCALE).astype(BF16)
        gps[z, :, 128:256] = third
        if d < GROUPS:
            qz_[z, 0:rows, :] = gps[z, :, 0:128]
            bottom = pltpu.roll(third[rows // 2 :], HD, 1)
            qz_[z, rows:, :] = jnp.where(low[: rows // 2], third[: rows // 2], bottom)
            zq(p.a, z).start()
    kv_3(2, True)

    def rows_of(i, core):
        return pl.ds(pl.multiple_of(i * half + core * quarter, quarter), quarter)

    for c in late:
        c.wait()
    for t in range(width // 256):
        at = pl.ds(t * 256, 256)
        gqb[at, 0:256] = dg(h1[p.a, :, at], gps[p.a, :, 0:256], TN)
        gqb[at, 256:640] = jnp.zeros((256, 384), F32)

    def rowdot(d, carry):
        z = (p.a + d) % GROUPS
        for t in range(width // 256):
            at = pl.ds(t * 256, 256)
            gqb[at, :] += dg(h1[z, :, at], gps[z], TN)
        return carry

    lax.fori_loop(1, GROUPS, rowdot, 0)
    kv_3(3, False)
    gpr[p.a] = gps[p.a]
    for t in range(width // 256):
        at = pl.ds(t * 256, 256)
        gqb[at, 256:640] += dg(h1[p.a, :, at], gps[p.a, :, 256:640], TN)
    for i in range(2):
        qk[0, i] = gqb[rows_of(i, 1 - p.k), :].astype(BF16)
    q_k = rcopy(qk.at[0], qk.at[1], qs.at[0], qr.at[0], p.sibling())
    q_k.start()
    gather_step(1)
    for c in local:
        c.wait()
    q_k.wait()
    for i in range(2):
        gqb[rows_of(i, p.k), :] += qk[1, i].astype(F32)
    qk[0, 0] = gqb[rows_of(1 - p.x, p.k), :].astype(BF16)
    q_x = rcopy(qk.at[0, 0], qx, qs.at[1], qr.at[1], p.xpeer())
    q_x.start()
    out_2()
    q_x.wait()
    gqb[rows_of(p.x, p.k), :] += qx[...].astype(F32)
    share = quarter // p.chips

    def own_rows(chip):
        start = p.x * half + p.k * quarter + chip * share
        return pl.ds(pl.multiple_of(start, share), share)

    def qc(chip, slot):
        return rcopy(qs_.at[chip], qy.at[slot], ns.at[chip], nr.at[slot], p.on_chip(chip))

    for c in others:
        qs_[c] = gqb[own_rows(c), :].astype(BF16)
        qc(c, p.chip).start()

    @pl.when((p.a > 0) & (p.a < last))
    def _():
        spread(p.a - 1)

    gather_step(2)
    total = gqb[own_rows(p.chip), :]
    for c in others:
        qc(c, c).wait_recv()
        total = total + qy[c].astype(F32)
    gq[p.a, p.k, p.chip] = total.astype(BF16)

    def bc(slot, to, sem):
        r = gq.at[slot, p.k, p.chip]
        return rcopy(r, r, bs.at[sem], br.at[slot], p.on_line(to))

    def qshare(slot, chip, to):
        r = gq.at[slot, p.k, chip]
        return rcopy(r, r, vs2.at[slot, to], vr2.at[slot, chip], p.on_chip(to))

    def sc(slot, core, chip):
        r = gq.at[slot, core, chip]
        return rcopy(r, r, cs.at[slot, chip], cr.at[slot, chip], p.sibling())

    def qspread(slot):
        for c in others:
            qshare(slot, p.chip, c).start()
        sc(slot, p.k, p.chip).start()

    @pl.when(p.a < last)
    def _():
        bc(p.a, p.a + 1, 0).start()

    @pl.when(p.a > 0)
    def _():
        bc(p.a, p.a - 1, 1).start()

    qspread(p.a)
    for g in range(GROUPS):
        weight_core(g, 1 - p.k).wait_recv()
        weight_core(g, p.k).wait_send()
        weight_x(g).wait_send()
    h = dg(gpr[p.a], wfull[p.a], NT)
    for g in line:
        zkv(g, g).wait_recv()
        zq(g, g).wait_recv()
        gpr[g, :, 0:128] = qr_[g, 0:rows, :]
        t = qr_[g, rows:, :]
        zero = jnp.zeros_like(t)
        at_low = low_half(t.shape)
        gpr[g, 0 : rows // 2, 128:256] = jnp.where(at_low, t, zero)
        gpr[g, rows // 2 :, 128:256] = jnp.where(at_low, pltpu.roll(t, HD, 1), zero)
        h = h + dg(gpr[g], wfull[g], NT)
    out_3()
    u = ext_of(rp[...].astype(F32))
    inv = inv_rms(u)
    gain = jnp.concatenate([gfull[0, 0:1, :], gfull[1, 0:1, :]], axis=1)
    result = gmid[...] + crms_back(u, inv, gain, h)
    gin[...] = result.T
    first = jnp.sum(h * (u * inv), axis=0, keepdims=True)
    which = lax.broadcasted_iota(jnp.int32, (8, width), 0)
    g0[...] = jnp.where(which == 0, first, dg2[...])
    g_k = rcopy(g0, gk, qs.at[2], qr.at[2], p.sibling())
    g_k.start()
    gather_step(3)
    g_k.wait()
    g0[...] += gk[...]
    g_x = rcopy(g0, gx, qs.at[3], qr.at[3], p.xpeer())
    g_x.start()
    for s in range(1, GROUPS):

        @pl.when(p.a - s >= 0)
        def _():
            bc(p.a - s, p.a, 0).wait_recv()

            @pl.when(p.a < last)
            def _():
                bc(p.a - s, p.a + 1, 2 * s).start()

            qspread(p.a - s)

        @pl.when(p.a + s <= last)
        def _():
            bc(p.a + s, p.a, 0).wait_recv()

            @pl.when(p.a > 0)
            def _():
                bc(p.a + s, p.a - 1, 2 * s + 1).start()

            qspread(p.a + s)

        if s == 1:
            out_4()
            g_x.wait()
            gy[p.chip] = g0[...] + gx[...]

            def gc(chip, slot):
                return rcopy(
                    gy.at[p.chip], gy.at[slot], ys.at[GROUPS, chip], yr.at[GROUPS, slot],
                    p.on_chip(chip),
                )

            for c in others:
                gc(c, p.chip).start()
        if s == 2:
            for z in range(GROUPS):
                pass_on(z)
            for c in others:
                gc(c, c).wait_recv()
            total = gy[0]
            for c in range(1, p.chips):
                total = total + gy[c]
            ga[p.a] = total

            def lc(slot, to):
                return rcopy(
                    ga.at[p.a], ga.at[slot], zs.at[GROUPS + to], zr.at[GROUPS + slot], p.on_line(to)
                )

            for g in line:
                lc(p.a, g).start()
    for g in range(GROUPS):
        for c in range(p.chips):
            core_share(1 - p.k, c, g).wait_recv()
    res_out = pltpu.make_async_copy(res, res_, ls.at[0])
    res_out.start()
    for g in line:
        lc(g, g).wait_recv()
    total = ga[0]
    for g in range(1, GROUPS):
        total = total + ga[g]
    gains[...] = total
    for c in others:
        if oc > 1:
            for g in range(GROUPS):
                out_spread(c, g, c).wait_recv()
                out_share(p.k, c, g).start()
    for g in [p.a] + line:
        for c in others:
            qshare(g, c, c).wait_recv()
            sc(g, p.k, c).start()
    for g in range(GROUPS):
        for c in range(p.chips):
            sc(g, 1 - p.k, c).wait_recv()
            sc(g, p.k, c).wait_send()
        for c in others:
            qshare(g, p.chip, c).wait_send()
            if oc > 1:
                out_spread(p.chip, g, c).wait_send()
        for c in range(oc):
            out_share(1 - p.k, c, g).wait_recv()
            out_share(p.k, c, g).wait_send()
        for c in range(p.chips):
            core_share(p.k, c, g).wait_send()
        for c in others:
            chip_share(p.chip, g, c).wait_send()
            yc(g, c, p.chip).wait_send()
    for c in others:
        for j in range(1, GROUPS):
            over_chips(c, p.chip, turn(p, j)).wait_send()
        qc(c, p.chip).wait_send()
        gc(c, p.chip).wait_send()
        out_chip(c, p.chip).wait_send()
    for g in line:
        zkv(p.a, g).wait_send()
        zq(p.a, g).wait_send()
        lc(p.a, g).wait_send()
        out_line(p.a, g).wait_send()
        out_back(p.a, g).wait_send()
    for s in range(GROUPS):

        @pl.when((p.a - s >= 0) & (p.a < last))
        def _():
            bc(p.a - s, p.a + 1, 2 * s).wait_send()
            line_share(p.a - s, p.a + 1, 2 * s).wait_send()

        @pl.when((p.a + s <= last) & (p.a > 0))
        def _():
            bc(p.a + s, p.a - 1, 2 * s + 1).wait_send()
            line_share(p.a + s, p.a - 1, 2 * s + 1).wait_send()

        if s > 0:

            @pl.when(p.a + s <= last)
            def _():
                rightward(p.a + s, red.at[0]).wait_send()

            @pl.when(p.a - s >= 0)
            def _():
                leftward(p.a - s, red.at[0]).wait_send()

    res_out.wait()


def back(n, lens, q3, kv, o3, l3, dog, wg, h1, rp, gmid, gfull, dg2, ysum, y0, gb, att):
    rows, width = rp.shape
    quarter = width // 4
    lanes = wg.shape[2]
    chips = n // GROUPS // 2
    keys = kv.shape[0] // GROUPS
    piece = ysum.shape[2]
    half = width // 2
    orow = half // 2
    oc = chips if orow % (chips * GROUPS * 8) == 0 else 1
    oyrow = orow // oc
    sds = jax.ShapeDtypeStruct
    v = pltpu.VMEM
    sem = lambda *shape: [DMA(shape), DMA(shape)]
    return pl.pallas_call(
        functools.partial(back_kernel, n),
        name="back",
        out_shape=(
            sds((width, rows), F32),
            sds((GROUPS, 2, chips, quarter // chips, lanes), BF16),
            sds((8, width), F32),
            sds((2, chips, GROUPS, piece, width), BF16),
            sds((2, oc, GROUPS, oyrow // GROUPS, width), BF16),
        ),
        in_specs=[SM, ANY, ANY, ANY, ANY, ANY, ANY, ANY, ANY, ANY, VM, VM, ANY, VM, ANY, ANY],
        out_specs=[VM, VM, VM, ANY, VM],
        scratch_shapes=[
            v(q3.shape, BF16),
            v(l3.shape, F32),
            v(dog.shape, BF16),
            v((2, chips, GROUPS, piece, width), BF16),
            v(h1.shape, BF16),
            v(rp.shape, BF16),
            v(gmid.shape, F32),
            v((half, width), BF16),
            v((2, rows, width), BF16),
            v((2, 2) + att.shape[1:], BF16),
            v((GROUPS, piece, width), BF16),
            v((GROUPS, piece, width), BF16),
            v(ysum.shape, BF16),
            v(q3.shape, BF16),
            v(q3.shape, F32),
            v((2 if keys <= SUB else 1, keys, 384), BF16),
            v((keys, 384), F32),
            v((keys, 384), BF16),
            v((GROUPS, chips, rows, 384), BF16),
            v((GROUPS, chips, rows, 384), BF16),
            v((GROUPS, width, lanes), BF16),
            v((GROUPS, rows, lanes), BF16),
            v((GROUPS, rows, lanes), BF16),
            v((width, lanes), F32),
            v((2, 2, quarter, lanes), BF16),
            v((quarter, lanes), BF16),
            v((chips, quarter // chips, lanes), BF16),
            v((chips, quarter // chips, lanes), BF16),
            v((GROUPS, rows * 3 // 2, 128), BF16),
            v((GROUPS, rows * 3 // 2, 128), BF16),
            v((8, width), F32),
            v((8, width), F32),
            v((8, width), F32),
            v((chips, 8, width), F32),
            v((GROUPS, 8, width), F32),
            v((GROUPS, piece, width), BF16),
            v((GROUPS, piece, width), BF16),
            v((GROUPS, piece, width), BF16),
            v((GROUPS, piece, width), BF16),
            v((orow, width), BF16),
            v((oc, oyrow, width), BF16),
            v((chips, oyrow, width), BF16),
            v((GROUPS, oyrow // GROUPS, width), BF16),
            v((GROUPS, oyrow // GROUPS, width), BF16),
            *sem(GROUPS),
            DMA((GROUPS + 10,)),
            DMA((2,)),
            *sem(GROUPS, chips),
            *sem(GROUPS + 1, chips),
            *sem(2 * GROUPS),
            *sem(GROUPS),
            *sem(4),
            *sem(chips),
            DMA((2 * GROUPS,)),
            DMA((GROUPS,)),
            *sem(GROUPS, chips),
            *sem(GROUPS),
            *sem(GROUPS),
            DMA((2 * GROUPS,)),
            DMA((GROUPS,)),
            *sem(chips, GROUPS),
            *sem(chips, GROUPS),
            *sem(chips),
            *sem(2 * GROUPS),
            *sem(1 + chips * GROUPS),
            *sem(chips, GROUPS),
            *sem(GROUPS),
            *sem(2),
            *sem(GROUPS, chips),
            *sem(GROUPS, chips),
        ],
        compiler_params=pltpu.CompilerParams(
            collective_id=2, has_side_effects=True, vmem_limit_bytes=67043328
        ),
    )(lens, q3, kv, o3, l3, dog, wg, h1, rp, gmid, gfull, dg2, ysum, y0, gb, att)


def deliver_kernel(gq, ra, rb, rd, goo, gsum, gin, out, out_, gin_, g1_, qkv_, go_, g2_, up_, down_):
    narrow = gin_.shape[0]
    half = g1_.shape[0]
    width = 2 * half
    out_[0] = out[:, :narrow]

    @pl.when(pl.program_id(0) == 0)
    def _():
        gin_[:, 0, :] = gin[:narrow, :]

    go_[...] = goo[:, :narrow].astype(F32)
    down_[...] = rd[0, :, :narrow].astype(F32)
    up_[:, :width] = ra[0].astype(F32)
    up_[:, width:] = rb[0].astype(F32)
    first = lax.axis_index("fsdp") == 0
    g1_[...] = jnp.where(first, gsum[0, :half], gsum[0, half:])
    g2_[...] = jnp.where(first, gsum[1, :half], gsum[1, half:])
    low = low_half((gq.shape[1], 128))

    def tile(g, t):
        return gq[g, :, t * 128 : (t + 1) * 128].astype(F32)

    def swap(t):
        return pltpu.roll(t, HD, 1)

    for j in range(GROUPS // 2):
        a, b = 2 * j, 2 * j + 1
        parts = []
        for t in (0, 2):
            pair = swap(tile(b, t))
            parts.append(
                (tile(a, t), jnp.where(low, tile(a, t + 1), pair), jnp.where(low, pair, swap(tile(b, t + 1))))
            )
        pair = swap(tile(b, 4))
        parts.append(
            (tile(a, 4), jnp.where(low, swap(tile(a, 3)), pair), jnp.where(low, pair, tile(b, 3)))
        )
        for i, three in enumerate(parts):
            for t, value in enumerate(three):
                at = i * width + j * 384 + t * 128
                qkv_[:, at : at + 128] = value


def deliver(gq, res, goo, gsum, gin, out):
    width, rows = gin.shape
    half = width // 2
    ff = res.shape[1]
    steps = 2
    sds = jax.ShapeDtypeStruct
    spec = pl.BlockSpec
    return pl.pallas_call(
        deliver_kernel,
        name="deliver",
        grid=(steps,),
        out_shape=(
            sds((1, rows, width - 1), BF16),
            sds((width - 1, 1, rows), F32),
            sds((half,), F32),
            sds((half, 3 * width), F32),
            sds((half, width - 1), F32),
            sds((half,), F32),
            sds((width, ff), F32),
            sds((ff, width - 1), F32),
        ),
        in_specs=[
            spec((GROUPS, half // steps, gq.shape[2]), lambda i: (0, i, 0)),
            spec((1, width // steps, width), lambda i: (0, i, 0)),
            spec((1, width // steps, width), lambda i: (0, steps + i, 0)),
            spec((1, ff // steps, width), lambda i: (1, i, 0)),
            spec((half // steps, width), lambda i: (i, 0)),
            spec(gsum.shape, lambda i: (0, 0)),
            spec((width, rows), lambda i: (0, 0)),
            spec((rows // steps, width), lambda i: (i, 0)),
        ],
        out_specs=[
            spec((1, rows // steps, width - 1), lambda i: (0, i, 0)),
            spec((width - 1, 1, rows), lambda i: (0, 0, 0)),
            spec((half,), lambda i: (0,)),
            spec((half // steps, 3 * width), lambda i: (i, 0)),
            spec((half // steps, width - 1), lambda i: (i, 0)),
            spec((half,), lambda i: (0,)),
            spec((width // steps, ff), lambda i: (i, 0)),
            spec((ff // steps, width - 1), lambda i: (i, 0)),
        ],
        compiler_params=pltpu.CompilerParams(vmem_limit_bytes=VLIM),
    )(gq, res, res, res, goo, gsum, gin, out)


def shards(n, resid, lengths, gain_one, w_qkv, w_out, gain_two, w_up, w_down, cotangent):
    width = resid.shape[2] + 1
    ff = w_up.shape[1]
    out, gmid, ysum, y0, gb, attg, dog, dg2, rp, wg, h1, q3, kv, o3, l3, gfull = front(
        n, lengths, resid[0], cotangent[0], gain_one, gain_two, w_qkv, w_out, w_up, w_down
    )
    gin, gq, gsum, res, goo = back(
        n, lengths, q3, kv, o3, l3, dog, wg, h1, rp, gmid, gfull, dg2, ysum, y0, gb, attg
    )

    half = width // 2
    delivered = deliver(
        gq.reshape(GROUPS, half, -1), res.reshape(2, ff, width), goo.reshape(half, width), gsum, gin, out
    )
    return delivered[0], jnp.transpose(delivered[1], (1, 2, 0)), *delivered[2:]


def solution(mesh):
    n = mesh.shape["ctx"]
    return jax.shard_map(
        functools.partial(shards, n),
        mesh=mesh,
        in_specs=(
            P("fsdp", "ctx", None),
            P("fsdp"),
            P("fsdp"),
            P("fsdp", None),
            P("fsdp", None),
            P("fsdp"),
            P(None, "fsdp"),
            P("fsdp", None),
            P("fsdp", "ctx", None),
        ),
        out_specs=(
            P("fsdp", "ctx", None),
            P("fsdp", "ctx", None),
            P("fsdp"),
            P("fsdp", None),
            P("fsdp", None),
            P("fsdp"),
            P(None, "fsdp"),
            P("fsdp", None),
        ),
        check_vma=False,
    )
```

```python
import functools

import jax
import jax.numpy as jnp
from jax import lax
from jax.experimental import pallas as pl
from jax.experimental.pallas import tpu as pltpu
from jax.sharding import PartitionSpec as P

F32 = jnp.float32
BF16 = jnp.bfloat16
MESH = pl.DeviceIdType.MESH
NT = (((1,), (1,)), ((), ()))
TN = (((0,), (0,)), ((), ()))
EPS = 1e-05
MASKED = -1e30
LOG2E = 1.4426950408889634
SCALE = 0.125
GROUPS = 4
GH = 3
HD = 64
SUB = 1024
VLIM = 60 * 1024 * 1024

VM = pl.BlockSpec(memory_space=pltpu.VMEM)
SM = pl.BlockSpec(memory_space=pltpu.SMEM)
ANY = pl.BlockSpec(memory_space=pl.ANY)
DMA = pltpu.SemaphoreType.DMA


def dot(a, b):
    return jnp.dot(a, b, preferred_element_type=F32)


def dg(a, b, dims):
    return lax.dot_general(a, b, dims, preferred_element_type=F32)


def rcopy(src, dst, send, recv, dev):
    return pltpu.make_async_remote_copy(
        src_ref=src, dst_ref=dst, send_sem=send, recv_sem=recv, device_id=dev, device_id_type=MESH
    )


class Place:
    def __init__(self, n):
        self.n = n
        self.m = n // GROUPS
        self.chips = self.m // 2
        c = lax.axis_index("ctx")
        self.x = lax.axis_index("fsdp")
        self.a = c // self.m
        self.b = c % self.m
        self.chip = self.b // 2
        self.k = self.b % 2

    def xpeer(self):
        return {"fsdp": 1 - self.x}

    def sibling(self):
        return {"ctx": self.a * self.m + self.chip * 2 + 1 - self.k}

    def on_chip(self, chip):
        return {"ctx": self.a * self.m + chip * 2 + self.k}

    def on_line(self, a):
        return {"ctx": a * self.m + self.b}


def greet(p, xpeer=False, sibling=False, chips=False, line=False):
    bar = pltpu.get_barrier_semaphore()
    count = 0
    if xpeer:
        pl.semaphore_signal(bar, inc=1, device_id=p.xpeer(), device_id_type=MESH)
        count += 1
    if sibling:
        pl.semaphore_signal(bar, inc=1, device_id=p.sibling(), device_id_type=MESH)
        count += 1
    if chips:
        for d in range(1, p.chips):
            pl.semaphore_signal(
                bar, inc=1, device_id=p.on_chip((p.chip + d) % p.chips), device_id_type=MESH
            )
            count += 1
    if line:
        for d in range(1, GROUPS):
            pl.semaphore_signal(
                bar, inc=1, device_id=p.on_line((p.a + d) % GROUPS), device_id_type=MESH
            )
            count += 1
    return lambda: pl.semaphore_wait(bar, count)


def turn(p, j):
    last = GROUPS - 1
    outer = jnp.where(p.a == 0, last - j, j)
    inner = (0, last, 1, last - 1)[j]
    return jnp.where((p.a == 0) | (p.a == last), outer, jnp.where(p.a == 1, last - inner, inner))


def ext_of(v):
    last = lax.broadcasted_iota(jnp.int32, v.shape, 1) == v.shape[1] - 1
    return jnp.where(last, -jnp.sum(v, axis=1, keepdims=True), v)


def inv_rms(u):
    return lax.rsqrt(jnp.mean(u * u, axis=1, keepdims=True) + EPS)


def crms_back(u, inv, gain, dy):
    dx = dy * gain
    du = inv * (dx - u * (inv * inv * jnp.mean(dx * u, axis=1, keepdims=True)))
    width = u.shape[1]
    last = lax.broadcasted_iota(jnp.int32, u.shape, 1) == width - 1
    return jnp.where(last, 0.0, du - du[:, width - 1 :])


def low_half(shape):
    return lax.broadcasted_iota(jnp.int32, shape, len(shape) - 1) < HD


def pack_tail(t):
    half = t.shape[0] // 2
    top, bottom = t[:half], t[half:]
    return jnp.where(low_half(top.shape), pltpu.roll(bottom, HD, 1), top)


def unpack_tail(t):
    low = low_half(t.shape)
    zero = jnp.zeros_like(t)
    return jnp.where(low, zero, t), jnp.where(low, zero, pltpu.roll(t, HD, 1))


def causal(shape, sub, size, first_query):
    col = lax.broadcasted_iota(jnp.int32, shape, 1) + sub * size
    row = lax.broadcasted_iota(jnp.int32, shape, 0) + first_query
    return col <= row


def gelu_both(a):
    c = 0.7978845608028654
    a2 = a * a
    t = jnp.tanh(c * a * (1.0 + 0.044715 * a2))
    half = 0.5 * (1.0 + t)
    slope = half + 0.5 * a * (1.0 - t * t) * (c * (1.0 + 0.134145 * a2))
    return a * half, slope


def group_columns(wq, wg):
    width = wq.shape[1] // 3
    low = low_half((wq.shape[0], 128))
    zero = jnp.zeros((wq.shape[0], 128), wq.dtype)

    def swap(t):
        return pltpu.roll(t, HD, 1)

    for j in range(GROUPS // 2):
        a, b = 2 * j, 2 * j + 1
        for i in range(3):
            at = i * width + j * 384
            t0, t1, t2 = (wq[:, at + 128 * t : at + 128 * t + 128] for t in range(3))
            pair = (t0, swap(jnp.where(low, t2, t1)))
            if i < 2:
                third = (jnp.where(low, t1, zero), jnp.where(low, swap(t2), zero))
                for g, p, t in zip((a, b), pair, third):
                    wg[g, :, i * 256 : i * 256 + 128] = p
                    wg[g, :, i * 256 + 128 : i * 256 + 256] = t
            else:
                third = (jnp.where(low, zero, swap(t1)), jnp.where(low, zero, t2))
                for g, p, t in zip((a, b), pair, third):
                    wg[g, :, 512:640] = p
                    wg[g, :, 384:512] = wg[g, :, 384:512] + t


def front_kernel(
    n, lens, ri, ci, g1, g2, wq, wo, wuh, wdh,
    out, gmid_, ysum_, y0, gb_, attg, dog, dg2, rp_, wg_, h1_, q3_, kv_, o3_, l3_, gfull,
    gmid, ysum, rp, wg, h1, q3, kv, o3, l3, gains, wop, wa, woa, wu, wdr, wd, att, wide, hid, gmb, act, gpre, esum, dsend, gb, mid, gk, grads,
    ss, rs, ls, hs, hr, vs, kr, fs, xs, xr, cs, cr, ts, tr, as_, ar, ds_, dr, ks, ks_r, ys, yr, us,
):
    p = Place(n)
    rows, narrow = ri.shape
    width = narrow + 1
    half = width // 2
    ff = wuh.shape[1]
    pk = rows * 3 // 2
    keys = p.m * rows
    size = min(SUB, keys)
    subs = keys // size
    other = 1 - p.x
    others = [(p.chip + d) % p.chips for d in range(1, p.chips)]
    line = [(p.a + d) % GROUPS for d in range(1, GROUPS)]
    ready = greet(p, xpeer=True, sibling=True, chips=True, line=True)
    own_u = pltpu.make_async_copy(wuh, wu.at[p.x], ls.at[5])
    own_d = pltpu.make_async_copy(wdh, wdr.at[p.x], ls.at[6])
    own_u.start()
    own_d.start()

    leaving = []

    def leave(src, dst):
        c = pltpu.make_async_copy(src, dst, us.at[len(leaving)])
        c.start()
        leaving.append(c)

    gains[0:1, :] = g1[...].astype(F32).reshape(1, half)
    gains[1:2, :] = g2[...].astype(F32).reshape(1, half)
    gfull[p.x] = gains[...]
    ready()

    def xc(i, src, dst):
        return rcopy(src, dst, ss.at[i], rs.at[i], p.xpeer())

    at_x = pl.ds(pl.multiple_of(p.x * half, half), half)
    x_gain = xc(0, gains, gfull.at[p.x])
    x_gain.start()
    rp[:, :narrow] = ri[...]
    rp[:, narrow:] = jnp.zeros((rows, 1), BF16)
    u = ext_of(rp[...].astype(F32))
    normed = u * inv_rms(u)
    x_gain.wait()
    gain = jnp.concatenate([gfull[0, 0:1, :], gfull[1, 0:1, :]], axis=1)
    h1[p.a] = (normed * gain).astype(BF16)

    def line_copy(block, dst, sem):
        return rcopy(h1.at[block], h1.at[block], hs.at[sem], hr.at[block], p.on_line(dst))

    @pl.when(p.a < GROUPS - 1)
    def _():
        line_copy(p.a, p.a + 1, 0).start()

    @pl.when(p.a > 0)
    def _():
        line_copy(p.a, p.a - 1, 1).start()

    group_columns(wq, wg)
    x_wa = xc(1, wg.at[p.a], wa.at[at_x])
    x_wa.start()
    own_a = pltpu.make_async_copy(wg.at[p.a], wa.at[at_x], ls.at[0])
    own_a.start()
    leave(rp, rp_)
    leave(wg, wg_)

    def up_rows(j, chip, core):
        size_i = width // p.m // 3
        return pl.ds(pl.multiple_of(((chip * 2 + core) * 3 + j) * size_i, size_i), size_i)

    def up_x(j):
        at = up_rows(j, p.chip, p.k)
        return rcopy(wuh.at[at], wu.at[p.x, at], xs.at[j], xr.at[j], p.xpeer())

    def up_chip(j, owner, to):
        r = wu.at[other, up_rows(j, owner, p.k)]
        return rcopy(r, r, cs.at[j, to], cr.at[j, owner], p.on_chip(to))

    def up_core(j, owner, core):
        r = wu.at[other, up_rows(j, owner, core)]
        return rcopy(r, r, ts.at[j, owner], tr.at[j, owner], p.sibling())

    def up_spread(j):
        up_x(j).wait_recv()
        for c in others:
            up_chip(j, p.chip, c).start()
        up_core(j, p.chip, p.k).start()

    def up_pass(j):
        for c in others:
            up_chip(j, c, c).wait_recv()
            up_core(j, c, p.k).start()

    def down_rows(chip, core):
        size_i = ff // p.m
        return pl.ds(pl.multiple_of((chip * 2 + core) * size_i, size_i), size_i)

    def down_x():
        at = down_rows(p.chip, p.k)
        return rcopy(wdh.at[at], wdr.at[p.x, at], xs.at[3], xr.at[3], p.xpeer())

    def down_chip(owner, to):
        r = wdr.at[other, down_rows(owner, p.k)]
        return rcopy(r, r, cs.at[3, to], cr.at[3, owner], p.on_chip(to))

    def down_core(owner, core):
        r = wdr.at[other, down_rows(owner, core)]
        return rcopy(r, r, ts.at[3, owner], tr.at[3, owner], p.sibling())

    for j in range(3):
        up_x(j).start()
    down_x().start()

    wop[:, :narrow] = wo[...]
    wop[:, narrow:] = jnp.zeros((half, 1), BF16)
    xo = []
    local = []
    for i in range(2):
        g = p.x * 2 + i
        for j, (src, count, dst) in enumerate(((0, 128, 0), (128, 64, 192))):
            s_ = wop.at[pl.ds(i * 192 + src, count)]
            d_ = woa.at[pl.ds(pl.multiple_of(g * 256 + dst, 64), count)]
            xo.append(xc(2 + 2 * i + j, s_, d_))
            local.append(pltpu.make_async_copy(s_, d_, ls.at[1 + 2 * i + j]))
    zero_rows = jnp.zeros((HD, width), BF16)
    for g in range(GROUPS):
        woa[pl.ds(g * 256 + 128, HD), :] = zero_rows
    for c in xo:
        c.start()
    for c in local:
        c.start()
    slot = (p.a * p.m + p.b) * rows + lax.broadcasted_iota(jnp.int32, (rows, width), 0)
    live = slot < lens[0]
    gmb[0, :, :narrow] = ci[...]
    gmb[0, :, narrow:] = jnp.zeros((rows, 1), BF16)
    gmb[0] = jnp.where(live, gmb[0].astype(F32), 0.0).astype(BF16)
    x_gm = xc(6, gmb.at[0], gmb.at[1])
    x_gm.start()
    def kv_copy(block, b, dev, send):
        r = kv.at[pl.ds(pl.multiple_of((block * p.m + b) * rows, rows), rows)]
        return rcopy(r, r, send, kr.at[block, b], dev)

    def ac(i, to):
        return rcopy(att.at[to], attg.at[i], as_.at[to], ar.at[i], p.on_line(to))

    own_a.wait()
    x_wa.wait()

    def produce(block):
        y = dot(h1[block], wa[...]).astype(BF16)
        low = low_half((rows, 128))
        zero = jnp.zeros((rows, 128), BF16)
        at = pl.ds(pl.multiple_of(block * rows, rows), rows)
        q3[0, at, :] = jnp.where(low, y[:, :128], zero)
        q3[1, at, :] = jnp.where(low, zero, y[:, :128])
        q3[2, at, :] = y[:, 128:256]
        kv[pl.ds(pl.multiple_of((block * p.m + p.b) * rows, rows), rows), :] = y[:, 256:]
        for d in range(1, p.chips):
            kv_copy(block, p.b, p.on_chip((p.chip + d) % p.chips), vs.at[block, d]).start()
        kv_copy(block, p.b, p.sibling(), vs.at[block, 0]).start()

    def pass_on(block):
        for d in range(1, p.chips):
            b = ((p.chip + d) % p.chips) * 2 + p.k
            kv_copy(block, b, p.sibling(), fs.at[block, d]).wait_recv()
            kv_copy(block, b, p.sibling(), fs.at[block, d]).start()

    def complete(block):
        for c in range(p.chips):
            kv_copy(block, c * 2 + 1 - p.k, p.sibling(), vs.at[block, 0]).wait_recv()

    first_query = p.b * rows
    dead = jnp.where(lens[0] > keys, 0.0, 1.0).astype(F32)

    def pair(z, c, diagonal):
        at_q = pl.ds(pl.multiple_of(z * rows, rows), rows)
        gone = jnp.where(c > 0, dead, 0.0)
        for h in range(GH):
            kt = 128 * (h // 2)
            vt = 128 if h == 2 else 256
            q = q3[h, at_q, :]

            def keys_of(sub, first):
                at = pl.ds(pl.multiple_of(c * keys + sub * size, size), size)
                scores = dg(q, kv[at, kt : kt + 128], NT) * (SCALE * LOG2E)
                if diagonal:
                    scores = jnp.where(causal(scores.shape, sub, size, first_query), scores, MASKED)
                here = jnp.max(scores, axis=1, keepdims=True) + gone * MASKED
                if first:
                    newest = here
                else:
                    top = l3[h, at_q, 0:1]
                    newest = jnp.maximum(top, here)
                weights = jnp.exp2(scores - (newest - gone * (3.0 * MASKED)))
                sums = jnp.sum(weights, axis=1, keepdims=True)
                part = dot(weights.astype(BF16), kv[at, vt : vt + 128])
                if not first:
                    shrink = jnp.exp2(top - newest)
                    sums = sums + l3[h, at_q, HD : HD + 1] * shrink
                    part = part + o3[h, at_q, :] * shrink
                o3[h, at_q, :] = part
                l3[h, at_q, :] = jnp.where(low_half((rows, 128)), newest, sums)

            keys_of(0, diagonal)
            if subs > 1:

                def rest(sub, carry):
                    keys_of(sub, False)
                    return carry

                lax.fori_loop(1, subs, rest, 0)

    def finish_row(z):
        at_q = pl.ds(pl.multiple_of(z * rows, rows), rows)
        heads = []
        for h in range(GH):
            total = l3[h, at_q, HD : HD + 1]
            o = o3[h, at_q, :] / total
            o3[h, at_q, :] = o
            l3[h, at_q, :] = jnp.broadcast_to(l3[h, at_q, 0:1] + jnp.log2(total), (rows, 128))
            heads.append(o)
        att[z, 0:rows, :] = jnp.where(low_half((rows, 128)), heads[0], heads[1]).astype(BF16)
        att[z, rows:pk, :] = pack_tail(heads[2]).astype(BF16)

        @pl.when(z == p.a)
        def _():
            attg[z] = att[z]

        @pl.when(z != p.a)
        def _():
            ac(p.a, z).start()

    def far(z):
        return jnp.abs(z - p.a)

    def pairs(t):
        def row(z, carry):
            @pl.when(far(z) == t)
            def _():
                pair(z, z, True)

            def key(d, carry):
                @pl.when(jnp.maximum(far(z), far(z - d)) == t)
                def _():
                    pair(z, z - d, False)

                return carry

            lax.fori_loop(1, z + 1, key, 0)

            @pl.when(jnp.maximum(far(z), p.a) == t)
            def _():
                finish_row(z)

            return carry

        lax.fori_loop(0, GROUPS, row, 0)

    def step(s, carry):
        below = p.a - s
        above = p.a + s

        @pl.when((s > 0) & (below >= 0))
        def _():
            line_copy(below, p.a, 0).wait_recv()

            @pl.when(p.a < GROUPS - 1)
            def _():
                line_copy(below, p.a + 1, 2 * s).start()

        @pl.when((s > 0) & (above < GROUPS))
        def _():
            line_copy(above, p.a, 0).wait_recv()

            @pl.when(p.a > 0)
            def _():
                line_copy(above, p.a - 1, 2 * s + 1).start()

        @pl.when(below >= 0)
        def _():
            produce(below)

        @pl.when((s > 0) & (above < GROUPS))
        def _():
            produce(above)

        for j in range(3):

            @pl.when(s == j + 1)
            def _():
                up_spread(j)

        @pl.when(s == GROUPS)
        def _():
            down_x().wait_recv()
            for c in others:
                down_chip(p.chip, c).start()
            down_core(p.chip, p.k).start()

        @pl.when((s > 0) & (below + 1 >= 0))
        def _():
            pass_on(below + 1)
            complete(below + 1)

        @pl.when((s > 1) & (above - 1 < GROUPS))
        def _():
            pass_on(above - 1)
            complete(above - 1)

        @pl.when(s > 0)
        def _():
            pairs(s - 1)

        for j in range(3):

            @pl.when(s == j + 2)
            def _():
                up_pass(j)

        return carry

    lax.fori_loop(0, GROUPS + 1, step, 0)
    for src, dst in ((h1, h1_), (q3, q3_), (kv, kv_), (o3, o3_), (l3, l3_)):
        leave(src, dst)

    own_u.wait()
    own_d.wait()

    def pad_down(f):
        wd[f, :, :narrow] = wdr[f]
        wd[f, :, narrow:] = jnp.zeros((ff, 1), BF16)

    pad_down(p.x)
    for c in xo:
        c.wait()
    for c in local:
        c.wait()
    for g in line:
        ac(g, g).wait_recv()
    for g in range(GROUPS):
        wide[:, g * 256 : g * 256 + 128] = attg[g, 0:rows, :]
        top, bottom = unpack_tail(attg[g, rows:pk, :])
        wide[0 : rows // 2, g * 256 + 128 : g * 256 + 256] = top
        wide[rows // 2 : rows, g * 256 + 128 : g * 256 + 256] = bottom
    mid[...] = rp[...].astype(F32) + dot(wide[...], woa[...])
    u = ext_of(mid[...])
    gain = jnp.concatenate([gfull[0, 1:2, :], gfull[1, 1:2, :]], axis=1)
    hid[0] = (u * inv_rms(u) * gain).astype(BF16)
    x_hid = xc(9, hid.at[0], hid.at[1])
    x_hid.start()
    wide_tile = 512

    def up(slot, token, f):
        def tile(t, carry):
            at = pl.ds(pl.multiple_of(t * wide_tile, wide_tile), wide_tile)
            a, slope = gelu_both(dot(hid[token], wu[f, :, at]))
            act[slot, :, at] = a.astype(BF16)
            gpre[slot, :, at] = (slope * dg(gmb[token], wd[f, at, :], NT)).astype(BF16)
            return carry

        lax.fori_loop(0, ff // wide_tile, tile, 0)

    up(0, 0, p.x)
    for c in others:
        down_chip(c, c).wait_recv()
        down_core(c, p.k).start()
    for j in range(3):
        for c in range(p.chips):
            up_core(j, c, 1 - p.k).wait_recv()
    for c in range(p.chips):
        down_core(c, 1 - p.k).wait_recv()
    pad_down(other)
    up(2, 0, other)

    def e_tile(t, carry):
        at = pl.ds(pl.multiple_of(t * 256, 256), 256)
        e = dg(gpre[0], wu[p.x, at, :], NT) + dg(gpre[2], wu[other, at, :], NT)
        esum[t] = e
        return carry

    lax.fori_loop(0, width // 256, e_tile, 0)
    e = jnp.concatenate([esum[t] for t in range(width // 256)], axis=1)
    u = ext_of(mid[...])
    inv = inv_rms(u)
    gmid[...] = gmb[0].astype(F32) + crms_back(u, inv, gain, e)
    leave(gmid, gmid_)
    gb[...] = gmid[...].astype(BF16)
    leave(gb, gb_)

    def dc(i, to):
        return rcopy(dsend.at[to], dog.at[i], ds_.at[to], dr.at[i], p.on_line(to))

    for d in range(1, GROUPS + 1):
        to = (p.a + d) % GROUPS
        w = woa[pl.ds(pl.multiple_of(to * 256, 256), 256), :]
        da = dg(gb[...], w, NT).astype(BF16)
        if d < GROUPS:
            dsend[to, 0:rows, :] = da[:, 0:128]
            dsend[to, rows:pk, :] = pack_tail(da[:, 128:256])
            dc(p.a, to).start()
        else:
            dog[to, 0:rows, :] = da[:, 0:128]
            dog[to, rows:pk, :] = pack_tail(da[:, 128:256])
    x_gm.wait()
    x_hid.wait()
    up(1, 1, p.x)

    def finish_out():
        final = mid[...] + dot(act[0], wd[p.x]) + dot(act[2], wd[other])
        out[...] = final.astype(BF16)

    shared = grads.shape != wd.shape
    gm = wd if shared else grads
    if shared:
        finish_out()
    piece = ysum.shape[2]
    part = GROUPS * piece

    def kc(chip):
        at = pl.ds(pl.multiple_of(chip * part, part), part)
        return rcopy(gm.at[1 - p.k, at], gk.at[at], ks.at[chip], ks_r.at[chip], p.sibling())

    def grad_up(t, carry):
        at = pl.ds(pl.multiple_of(t * 384, 384), 384)
        g = dg(hid[0], gpre[0, :, at], TN) + dg(hid[1], gpre[1, :, at], TN)
        per = width // 384
        r0 = pl.multiple_of((t // per) * width, width)
        c0 = pl.multiple_of((t % per) * 384, 384)
        gm[0, pl.ds(r0, width), pl.ds(c0, 384)] = g.astype(BF16)
        return carry

    def grad_down(t, carry):
        at = pl.ds(pl.multiple_of(t * 384, 384), 384)
        g = dg(act[0, :, at], gmb[0], TN) + dg(act[1, :, at], gmb[1], TN)
        gm[1, at, :] = g.astype(BF16)
        return carry

    @pl.when(p.k == 0)
    def _():
        lax.fori_loop(0, ff // 384, grad_down, 0)

    @pl.when(p.k == 1)
    def _():
        lax.fori_loop(0, ff // 384, grad_up, 0)

    for c in others:
        kc(c).start()
    kc(p.chip).start()

    @pl.when(p.k == 0)
    def _():
        lax.fori_loop(0, ff // 384, grad_up, 0)

    @pl.when(p.k == 1)
    def _():
        lax.fori_loop(0, ff // 384, grad_down, 0)

    def over_chips(chip, slot):
        return rcopy(ysum.at[chip, turn(p, 0)], y0.at[slot], ys.at[chip], yr.at[slot], p.on_chip(chip))

    def core_sum(chip, z):
        at = pl.ds(pl.multiple_of(chip * part + z * piece, 16), piece)
        ysum[chip, z] = (gm[p.k, at, :].astype(F32) + gk[at, :].astype(F32)).astype(BF16)

    for chip in others:
        kc(chip).wait()
        core_sum(chip, turn(p, 0))
        over_chips(chip, p.chip).start()
    if not shared:
        finish_out()
    for j in range(1, GROUPS):
        for chip in others:
            core_sum(chip, turn(p, j))
    kc(p.chip).wait()
    for j in range(GROUPS):
        core_sum(p.chip, turn(p, j))
    y0[p.chip] = ysum[p.chip, turn(p, 0)]
    leave(ysum, ysum_)
    dg2[...] = jnp.broadcast_to(jnp.sum(e * (u * inv), axis=0, keepdims=True), dg2.shape)

    for c in others:
        over_chips(c, p.chip).wait_send()
        over_chips(c, c).wait_recv()
    for g in line:
        ac(p.a, g).wait_send()
        dc(p.a, g).wait_send()
        dc(g, g).wait_recv()
    for block in range(GROUPS):
        kv_copy(block, p.b, p.sibling(), vs.at[block, 0]).wait_send()
        for d in range(1, p.chips):
            kv_copy(block, p.b, p.sibling(), vs.at[block, d]).wait_send()
            b = ((p.chip + d) % p.chips) * 2
            kv_copy(block, b + p.k, p.sibling(), fs.at[block, d]).wait_send()
    for s in range(GROUPS):

        @pl.when((p.a - s >= 0) & (p.a < GROUPS - 1))
        def _():
            line_copy(p.a - s, p.a + 1, 2 * s).wait_send()

        @pl.when((p.a + s < GROUPS) & (p.a > 0))
        def _():
            line_copy(p.a + s, p.a - 1, 2 * s + 1).wait_send()

    for j in range(3):
        up_x(j).wait_send()
        for c in others:
            up_chip(j, p.chip, c).wait_send()
        for c in range(p.chips):
            up_core(j, c, p.k).wait_send()
    down_x().wait_send()
    for c in others:
        down_chip(p.chip, c).wait_send()
    for c in range(p.chips):
        down_core(c, p.k).wait_send()
    for c in leaving:
        c.wait()


def front(n, lens, ri, ci, g1, g2, wq, wo, wu, wd):
    rows, narrow = ri.shape
    width = narrow + 1
    half = width // 2
    ff = wu.shape[1]
    pk = rows * 3 // 2
    m = n // GROUPS
    chips = m // 2
    piece = ff // GROUPS // chips
    lanes = 640
    sds = jax.ShapeDtypeStruct
    v = pltpu.VMEM
    heads = (GH, GROUPS * rows, 128)
    sem = lambda *shape: [DMA(shape), DMA(shape)]
    return pl.pallas_call(
        functools.partial(front_kernel, n),
        name="front",
        out_shape=(
            sds((rows, width), BF16),
            sds((rows, width), F32),
            sds((chips, GROUPS, piece, width), BF16),
            sds((chips, piece, width), BF16),
            sds((rows, width), BF16),
            sds((GROUPS, pk, 128), BF16),
            sds((GROUPS, pk, 128), BF16),
            sds((8, width), F32),
            sds((rows, width), BF16),
            sds((GROUPS, half, lanes), BF16),
            sds((GROUPS, rows, width), BF16),
            sds(heads, BF16),
            sds((n * rows, 384), BF16),
            sds(heads, F32),
            sds(heads, F32),
            sds((2, 8, half), F32),
        ),
        in_specs=[SM, VM, VM, VM, VM, VM, VM, ANY, ANY],
        out_specs=[VM, ANY, ANY, VM, ANY] + [VM] * 3 + [ANY] * 7 + [VM],
        scratch_shapes=[
            v((rows, width), F32),
            v((chips, GROUPS, piece, width), BF16),
            v((rows, width), BF16),
            v((GROUPS, half, lanes), BF16),
            v((GROUPS, rows, width), BF16),
            v(heads, BF16),
            v((n * rows, 384), BF16),
            v(heads, F32),
            v(heads, F32),
            v((8, half), F32),
            v((half, width), BF16),
            v((width, lanes), BF16),
            v((GROUPS * 256, width), BF16),
            v((2, width, ff), BF16),
            v((2, ff, narrow), BF16),
            v((2, ff, width), BF16),
            v((GROUPS, pk, 128), BF16),
            v((rows, GROUPS * 256), BF16),
            v((2, rows, width), BF16),
            v((2, rows, width), BF16),
            v((3, rows, ff), BF16),
            v((3, rows, ff), BF16),
            v((width // 256, rows, 256), F32),
            v((GROUPS, pk, 128), BF16),
            v((rows, width), BF16),
            v((rows, width), F32),
            v((ff, width), BF16),
            v((2, ff, width) if m * rows <= SUB else (8, 128), BF16),
            *sem(10),
            DMA((7,)),
            DMA((2 * GROUPS,)),
            DMA((GROUPS,)),
            DMA((GROUPS, chips)),
            DMA((GROUPS, m)),
            DMA((GROUPS, chips)),
            *sem(4),
            *sem(4, chips),
            *sem(4, chips),
            *sem(GROUPS),
            *sem(GROUPS),
            *sem(chips),
            *sem(chips),
            DMA((10,)),
        ],
        compiler_params=pltpu.CompilerParams(
            collective_id=0, has_side_effects=True, vmem_limit_bytes=67043328
        ),
    )(lens, ri, ci, g1, g2, wq, wo, wu, wd)


def back_kernel(
    n, lens, q3_, kv, o3, l3_, dog_, wg, h1_, rp_, gmid_, gfull, dg2, ysum, y0, gb_, att_,
    gin, gq, gains, res_, goo,
    q3, l3, dog, res, h1, rp, gmid, go, gb, att, red, ymine, yq, do3, dq3, kvc, dkv, dkvb, rk, ry, wfull, gps, gpr, gqb, qk, qx, qy,
    qs_, qz_, qr_, g0, gk, gx, gy, ga, left, right, sumr, suml, ok, os_, oy, oz, ozr,
    xs, xr, ls, vs, ks, kr, ys, yr, zs, zr, ws, wr, qs, qr, ns, nr, bs, br, cs, cr,
    rs_, rr, ls_, lr, as_, ar, es, er, fs, fr, ts, tr, us, ur, is_, ir, ps, pr, ws2, wr2, zs2, zr2, vs2, vr2, fs2, fr2,
):
    p = Place(n)
    rows, width = rp_.shape
    half = width // 2
    quarter = width // 4
    last = GROUPS - 1
    keys = dkv.shape[0]
    size = min(SUB, keys)
    subs = keys // size
    slots = kvc.shape[0]
    others = [(p.chip + d) % p.chips for d in range(1, p.chips)]
    line = [(p.a + d) % GROUPS for d in range(1, GROUPS)]
    ready = greet(p, xpeer=True, sibling=True, chips=True, line=True)
    at_x = pl.ds(pl.multiple_of(p.x * half, half), half)
    local = [
        pltpu.make_async_copy(wg.at[g], wfull.at[g, at_x], ls.at[g]) for g in range(GROUPS)
    ]

    def chunk_of(i):
        return (p.a + 1 + i) % GROUPS

    def fetch(i):
        c = chunk_of(i)
        src = kv.at[pl.ds(pl.multiple_of(c * keys, keys), keys)]
        return pltpu.make_async_copy(src, kvc.at[i % slots], vs.at[i % slots])

    first_in = [
        pltpu.make_async_copy(src, dst, ls.at[GROUPS + 7 + i])
        for i, (src, dst) in enumerate(((dog_, dog), (q3_, q3), (l3_, l3)))
    ]
    for c in first_in:
        c.start()
    fetch(0).start()
    o_in = pltpu.make_async_copy(o3, dq3, ls.at[GROUPS])
    o_in.start()
    y_in = pltpu.make_async_copy(ysum.at[p.chip], ymine, ls.at[GROUPS + 1])
    y_in.start()
    late = [
        pltpu.make_async_copy(src, dst, ls.at[GROUPS + 2 + i])
        for i, (src, dst) in enumerate(((h1_, h1), (rp_, rp), (gmid_, gmid)))
    ]
    for c in late:
        c.start()
    gos = [
        pltpu.make_async_copy(src, dst, ls.at[GROUPS + 5 + i])
        for i, (src, dst) in enumerate(((gb_, gb.at[0]), (att_.at[pl.ds(p.x * 2, 2)], att.at[0])))
    ]
    for c in gos:
        c.start()
    gox = [
        rcopy(src, dst, zs2.at[i], zr2.at[i], p.xpeer())
        for i, (src, dst) in enumerate(((gb_, gb.at[1]), (att_.at[pl.ds((1 - p.x) * 2, 2)], att.at[1])))
    ]
    for c in local:
        c.start()

    def weight_rows(x, core):
        return pl.ds(pl.multiple_of(x * half + core * quarter, quarter), quarter)

    def weight_x(g):
        src = wg.at[g, pl.ds(pl.multiple_of(p.k * quarter, quarter), quarter)]
        return rcopy(src, wfull.at[g, weight_rows(p.x, p.k)], xs.at[g], xr.at[g], p.xpeer())

    def weight_core(g, core):
        r = wfull.at[g, weight_rows(1 - p.x, core)]
        return rcopy(r, r, ws2.at[g], wr2.at[g], p.sibling())

    def over_chips(chip, slot, z):
        return rcopy(ysum.at[chip, z], yq.at[slot, z], ps.at[chip, z], pr.at[slot, z], p.on_chip(chip))

    def chip_sum(j):
        z = turn(p, j)
        total = ymine[z].astype(F32)
        for c in others:
            if j > 0:
                over_chips(c, c, z).wait_recv()
                total = total + yq[c, z].astype(F32)
            else:
                total = total + y0[c].astype(F32)
        red[z] = total.astype(BF16)
        if j < last:

            @pl.when(p.a == 0)
            def _():
                rightward(z, red.at[z]).start()

            @pl.when(p.a == last)
            def _():
                leftward(z, red.at[z]).start()

    def rightward(z, src):
        return rcopy(src, left.at[z], rs_.at[z], rr.at[z], p.on_line(jnp.minimum(p.a + 1, last)))

    def leftward(z, src):
        return rcopy(src, right.at[z], ls_.at[z], lr.at[z], p.on_line(jnp.maximum(p.a - 1, 0)))

    def reduce_step(s):
        @pl.when((p.a >= 1) & (p.a <= s))
        def _():
            z = last + p.a - s
            rightward(z, sumr.at[z]).wait_recv()
            if s < last:
                sumr[z] = (red[z].astype(F32) + left[z].astype(F32)).astype(BF16)
                rightward(z, sumr.at[z]).start()

        b = last - p.a

        @pl.when((b >= 1) & (b <= s))
        def _():
            z = s - b
            leftward(z, suml.at[z]).wait_recv()
            if s < last:
                suml[z] = (red[z].astype(F32) + right[z].astype(F32)).astype(BF16)
                leftward(z, suml.at[z]).start()

    def line_share(z, dst, sem):
        r = res.at[p.k, p.chip, z]
        return rcopy(r, r, as_.at[sem], ar.at[z], p.on_line(dst))

    def chip_share(chip, z, dst):
        r = res.at[p.k, chip, z]
        return rcopy(r, r, es.at[dst, z], er.at[chip, z], p.on_chip(dst))

    def core_share(core, chip, z):
        r = res.at[core, chip, z]
        return rcopy(r, r, fs.at[chip, z], fr.at[chip, z], p.sibling())

    def spread(z):
        for c in others:
            chip_share(p.chip, z, c).start()
        core_share(p.k, p.chip, z).start()

    def gather_first():
        z = p.a
        res[p.k, p.chip, z] = red[z]

        @pl.when(p.a > 0)
        def _():
            cur = res[p.k, p.chip, z].astype(F32)
            res[p.k, p.chip, z] = (cur + left[z].astype(F32)).astype(BF16)

        @pl.when(p.a < last)
        def _():
            cur = res[p.k, p.chip, z].astype(F32)
            res[p.k, p.chip, z] = (cur + right[z].astype(F32)).astype(BF16)
            line_share(z, p.a + 1, 0).start()

        @pl.when(p.a > 0)
        def _():
            line_share(z, p.a - 1, 1).start()

    def gather_step(s):
        @pl.when(p.a - s >= 0)
        def _():
            line_share(p.a - s, p.a, 0).wait_recv()

            @pl.when(p.a < last)
            def _():
                line_share(p.a - s, p.a + 1, 2 * s).start()

            if s > 1:
                spread(p.a - s)
            else:

                @pl.when(p.a == last)
                def _():
                    spread(p.a - s)

        @pl.when(p.a + s <= last)
        def _():
            line_share(p.a + s, p.a, 0).wait_recv()

            @pl.when(p.a > 0)
            def _():
                line_share(p.a + s, p.a - 1, 2 * s + 1).start()

            spread(p.a + s)

    def pass_on(z):
        for c in others:
            chip_share(c, z, c).wait_recv()
            core_share(p.k, c, z).start()

    orow = half // 2
    oc = os_.shape[0]
    oyrow = orow // oc
    opart = oyrow // GROUPS
    my = p.chip if oc > 1 else 0

    def out_core():
        at = pl.ds(pl.multiple_of((1 - p.k) * orow, orow), orow)
        return rcopy(go.at[at], ok, is_.at[0], ir.at[0], p.sibling())

    def out_chip(chip, slot):
        return rcopy(os_.at[chip if oc > 1 else 0], oy.at[slot], ts.at[chip], tr.at[slot], p.on_chip(chip))

    def out_line(slot, to):
        return rcopy(oz.at[to], ozr.at[slot], us.at[to], ur.at[slot], p.on_line(to))

    def out_back(slot, to):
        r = goo.at[p.k, my, slot]
        return rcopy(r, r, us.at[GROUPS + to], ur.at[GROUPS + slot], p.on_line(to))

    def out_spread(chip, z, to):
        r = goo.at[p.k, chip, z]
        return rcopy(r, r, fs2.at[z, to], fr2.at[z, chip], p.on_chip(to))

    def out_share(core, chip, z):
        r = goo.at[core, chip, z]
        i = 1 + chip * GROUPS + z
        return rcopy(r, r, is_.at[i], ir.at[i], p.sibling())

    def out_0():
        for c in gos + gox:
            c.wait()
        for i in range(2):
            tails = [jnp.concatenate(unpack_tail(att[s, i, rows:, :]), axis=0) for s in range(2)]
            g = dg(att[0, i, 0:rows, :], gb[0], TN) + dg(att[1, i, 0:rows, :], gb[1], TN)
            go[i * 192 : i * 192 + 128, :] = g.astype(BF16)
            g = dg(tails[0], gb[0], TN) + dg(tails[1], gb[1], TN)
            go[i * 192 + 128 : i * 192 + 192, :] = g[HD:, :].astype(BF16)
        out_core().start()

    def out_1():
        out_core().wait()
        at = pl.ds(pl.multiple_of(p.k * orow, orow), orow)
        total = go[at, :].astype(F32) + ok[...].astype(F32)
        for c in range(oc):
            os_[c] = total[c * oyrow : (c + 1) * oyrow].astype(BF16)
        for c in others:
            out_chip(c, p.chip).start()

    def out_2():
        total = os_[my].astype(F32)
        for c in others:
            out_chip(c, c).wait_recv()
            total = total + oy[c].astype(F32)
        for z in range(GROUPS):
            oz[z] = total[z * opart : (z + 1) * opart].astype(BF16)
        for z in line:
            out_line(p.a, z).start()

    def out_3():
        total = oz[p.a].astype(F32)
        for z in line:
            out_line(z, z).wait_recv()
            total = total + ozr[z].astype(F32)
        goo[p.k, my, p.a] = total.astype(BF16)
        for z in line:
            out_back(p.a, z).start()

    def out_4():
        for z in line:
            out_back(z, z).wait_recv()
        for z in range(GROUPS):
            if oc > 1:
                for c in others:
                    out_spread(p.chip, z, c).start()
            out_share(p.k, my, z).start()

    def kc(i, chip):
        c = chunk_of(i)
        at = pl.ds(pl.multiple_of((chip * 2 + 1 - p.k) * rows, rows), rows)
        return rcopy(
            dkvb.at[at], rk.at[c, chip], ks.at[c, chip], kr.at[c, chip], p.sibling()
        )

    def yc(c, chip, slot):
        return rcopy(rk.at[c, chip], ry.at[c, slot], ys.at[c, chip], yr.at[c, slot], p.on_chip(chip))

    def zkv(slot, to):
        lanes = pl.ds(256, 384)
        return rcopy(
            gps.at[to, :, lanes], gpr.at[slot, :, lanes], zs.at[to], zr.at[slot], p.on_line(to)
        )

    def zq(slot, to):
        return rcopy(qz_.at[to], qr_.at[slot], ws.at[to], wr.at[slot], p.on_line(to))

    def mine(chip):
        at = pl.ds(pl.multiple_of((chip * 2 + p.k) * rows, rows), rows)
        return dkvb[at, :].astype(F32)

    def kv_1(i):
        dkvb[...] = dkv[...].astype(BF16)
        for c in others:
            kc(i, c).start()
        kc(i, p.chip).start()

    def kv_2(i):
        c = chunk_of(i)
        for chip in others:
            kc(i, chip).wait()
            rk[c, chip] = (mine(chip) + rk[c, chip].astype(F32)).astype(BF16)
            yc(c, chip, p.chip).start()
        kc(i, p.chip).wait()
        rk[c, p.chip] = (mine(p.chip) + rk[c, p.chip].astype(F32)).astype(BF16)

    def kv_3(i, send):
        c = chunk_of(i)
        total = rk[c, p.chip].astype(F32)
        for chip in others:
            yc(c, chip, chip).wait_recv()
            total = total + ry[c, chip].astype(F32)
        gps[c, :, 256:640] = total.astype(BF16)
        if send:
            zkv(p.a, c).start()

    ready()
    for j in range(1, last):
        for c in others:
            over_chips(c, p.chip, turn(p, j)).start()
    for c in gox:
        c.start()
    for g in range(GROUPS):
        weight_x(g).start()

    first_query = p.b * rows
    low = low_half((rows, 128))
    for c in first_in:
        c.wait()
    o_in.wait()
    y_in.wait()
    chip_sum(0)
    for z in range(GROUPS):
        at = pl.ds(z * rows, rows)
        both = dog[z, 0:rows, :]
        zero = jnp.zeros_like(both)
        do3[0, at, :] = jnp.where(low, both, zero)
        do3[1, at, :] = jnp.where(low, zero, both)
        top, bottom = unpack_tail(dog[z, rows:, :])
        do3[2, pl.ds(z * rows, rows // 2), :] = top
        do3[2, pl.ds(z * rows + rows // 2, rows // 2), :] = bottom
        for h in range(GH):
            delta = jnp.sum(dq3[h, at, :] * do3[h, at, :].astype(F32), axis=1, keepdims=True)
            gqb[h * rows : (h + 1) * rows, z * 128 : (z + 1) * 128] = jnp.broadcast_to(delta, (rows, 128))
    dq3[...] = jnp.zeros_like(dq3)
    gone = jnp.where(lens[0] > keys, 0.0, -MASKED).astype(F32)

    def chunk(i, carry):
        c = chunk_of(i)
        fetch(i).wait()

        if slots > 1:

            @pl.when(i < last)
            def _():
                fetch(i + 1).start()

        dead = jnp.where(c > 0, gone, 0.0)

        def head(h, carry):
            kt = pl.multiple_of(128 * (h // 2), 128)
            vt = pl.multiple_of(jnp.where(h == 2, 128, 256), 128)

            def step(z, masked):
                at_q = pl.ds(pl.multiple_of(z * rows, rows), rows)
                q = q3[h, at_q, :]
                do = do3[h, at_q, :]
                lse = l3[h, at_q, 0:1] + dead
                delta = gqb[
                    pl.ds(pl.multiple_of(h * rows, rows), rows),
                    pl.ds(pl.multiple_of(z * 128, 128), 128),
                ][:, 0:1]
                def keys_of(sub, carry):
                    at = pl.ds(pl.multiple_of(sub * size, size), size)
                    k = kvc[i % slots, at, pl.ds(kt, 128)]
                    v = kvc[i % slots, at, pl.ds(vt, 128)]
                    scores = dg(q, k, NT) * (SCALE * LOG2E)
                    if masked:
                        scores = jnp.where(
                            causal(scores.shape, sub, size, first_query), scores, MASKED
                        )
                    weights = jnp.exp2(scores - lse)
                    gp = dg(do, v, NT)
                    gs = (weights * (gp - delta)).astype(BF16)
                    dq3[h, at_q, :] += dot(gs, k)
                    gv = dg(weights.astype(BF16), do, TN)
                    gk_ = dg(gs, q, TN) * SCALE
                    if masked:
                        dkv[at, pl.ds(kt, 128)] = jnp.where(h == 1, dkv[at, pl.ds(kt, 128)], 0.0) + gk_
                        dkv[at, pl.ds(vt, 128)] = jnp.where(h == 0, 0.0, dkv[at, pl.ds(vt, 128)]) + gv
                    else:
                        dkv[at, pl.ds(kt, 128)] += gk_
                        dkv[at, pl.ds(vt, 128)] += gv
                    return carry

                if subs > 1:
                    lax.fori_loop(0, subs, keys_of, 0)
                else:
                    keys_of(0, 0)

            step(c, True)

            def rest(z, carry):
                step(z, False)
                return carry

            lax.fori_loop(c + 1, GROUPS, rest, 0)

            @pl.when(h == 0)
            def _():
                @pl.when(i >= 1)
                def _():
                    kv_2(i - 1)

                @pl.when(i == 1)
                def _():
                    for c in others:
                        over_chips(c, p.chip, turn(p, last)).start()
                    chip_sum(1)
                    reduce_step(1)

                @pl.when(i == 2)
                def _():
                    reduce_step(2)

                @pl.when(i == 3)
                def _():
                    chip_sum(3)
                    reduce_step(3)
                    gather_first()

            @pl.when((h == 1) & (i >= 2))
            def _():
                kv_3(i - 2, True)

            @pl.when(h == 2)
            def _():
                @pl.when(i == 1)
                def _():
                    chip_sum(2)

                @pl.when(i == 2)
                def _():
                    out_0()

                @pl.when(i == last)
                def _():
                    for g in range(GROUPS):
                        weight_x(g).wait_recv()
                        weight_core(g, p.k).start()

            return carry

        lax.fori_loop(0, GH, head, 0)
        if slots == 1:

            @pl.when(i < last)
            def _():
                fetch(i + 1).start()

        kv_1(i)
        return carry

    lax.fori_loop(0, GROUPS, chunk, 0)
    kv_2(3)
    spread(p.a)
    out_1()
    for d in range(1, GROUPS + 1):
        z = (p.a + d) % GROUPS
        at = pl.ds(pl.multiple_of(z * rows, rows), rows)
        gps[z, :, 0:128] = (jnp.where(low, dq3[0, at, :], dq3[1, at, :]) * SCALE).astype(BF16)
        third = (jnp.where(low, dq3[2, at, :], 0.0) * SCALE).astype(BF16)
        gps[z, :, 128:256] = third
        if d < GROUPS:
            qz_[z, 0:rows, :] = gps[z, :, 0:128]
            bottom = pltpu.roll(third[rows // 2 :], HD, 1)
            qz_[z, rows:, :] = jnp.where(low[: rows // 2], third[: rows // 2], bottom)
            zq(p.a, z).start()
    kv_3(2, True)

    def rows_of(i, core):
        return pl.ds(pl.multiple_of(i * half + core * quarter, quarter), quarter)

    for c in late:
        c.wait()
    for t in range(width // 256):
        at = pl.ds(t * 256, 256)
        gqb[at, 0:256] = dg(h1[p.a, :, at], gps[p.a, :, 0:256], TN)
        gqb[at, 256:640] = jnp.zeros((256, 384), F32)

    def rowdot(d, carry):
        z = (p.a + d) % GROUPS
        for t in range(width // 256):
            at = pl.ds(t * 256, 256)
            gqb[at, :] += dg(h1[z, :, at], gps[z], TN)
        return carry

    lax.fori_loop(1, GROUPS, rowdot, 0)
    kv_3(3, False)
    gpr[p.a] = gps[p.a]
    for t in range(width // 256):
        at = pl.ds(t * 256, 256)
        gqb[at, 256:640] += dg(h1[p.a, :, at], gps[p.a, :, 256:640], TN)
    for i in range(2):
        qk[0, i] = gqb[rows_of(i, 1 - p.k), :].astype(BF16)
    q_k = rcopy(qk.at[0], qk.at[1], qs.at[0], qr.at[0], p.sibling())
    q_k.start()
    gather_step(1)
    for c in local:
        c.wait()
    q_k.wait()
    for i in range(2):
        gqb[rows_of(i, p.k), :] += qk[1, i].astype(F32)
    qk[0, 0] = gqb[rows_of(1 - p.x, p.k), :].astype(BF16)
    q_x = rcopy(qk.at[0, 0], qx, qs.at[1], qr.at[1], p.xpeer())
    q_x.start()
    out_2()
    q_x.wait()
    gqb[rows_of(p.x, p.k), :] += qx[...].astype(F32)
    share = quarter // p.chips

    def own_rows(chip):
        start = p.x * half + p.k * quarter + chip * share
        return pl.ds(pl.multiple_of(start, share), share)

    def qc(chip, slot):
        return rcopy(qs_.at[chip], qy.at[slot], ns.at[chip], nr.at[slot], p.on_chip(chip))

    for c in others:
        qs_[c] = gqb[own_rows(c), :].astype(BF16)
        qc(c, p.chip).start()

    @pl.when((p.a > 0) & (p.a < last))
    def _():
        spread(p.a - 1)

    gather_step(2)
    total = gqb[own_rows(p.chip), :]
    for c in others:
        qc(c, c).wait_recv()
        total = total + qy[c].astype(F32)
    gq[p.a, p.k, p.chip] = total.astype(BF16)

    def bc(slot, to, sem):
        r = gq.at[slot, p.k, p.chip]
        return rcopy(r, r, bs.at[sem], br.at[slot], p.on_line(to))

    def qshare(slot, chip, to):
        r = gq.at[slot, p.k, chip]
        return rcopy(r, r, vs2.at[slot, to], vr2.at[slot, chip], p.on_chip(to))

    def sc(slot, core, chip):
        r = gq.at[slot, core, chip]
        return rcopy(r, r, cs.at[slot, chip], cr.at[slot, chip], p.sibling())

    def qspread(slot):
        for c in others:
            qshare(slot, p.chip, c).start()
        sc(slot, p.k, p.chip).start()

    @pl.when(p.a < last)
    def _():
        bc(p.a, p.a + 1, 0).start()

    @pl.when(p.a > 0)
    def _():
        bc(p.a, p.a - 1, 1).start()

    qspread(p.a)
    for g in range(GROUPS):
        weight_core(g, 1 - p.k).wait_recv()
        weight_core(g, p.k).wait_send()
        weight_x(g).wait_send()
    h = dg(gpr[p.a], wfull[p.a], NT)
    for g in line:
        zkv(g, g).wait_recv()
        zq(g, g).wait_recv()
        gpr[g, :, 0:128] = qr_[g, 0:rows, :]
        t = qr_[g, rows:, :]
        zero = jnp.zeros_like(t)
        at_low = low_half(t.shape)
        gpr[g, 0 : rows // 2, 128:256] = jnp.where(at_low, t, zero)
        gpr[g, rows // 2 :, 128:256] = jnp.where(at_low, pltpu.roll(t, HD, 1), zero)
        h = h + dg(gpr[g], wfull[g], NT)
    out_3()
    u = ext_of(rp[...].astype(F32))
    inv = inv_rms(u)
    gain = jnp.concatenate([gfull[0, 0:1, :], gfull[1, 0:1, :]], axis=1)
    result = gmid[...] + crms_back(u, inv, gain, h)
    gin[...] = result.T
    first = jnp.sum(h * (u * inv), axis=0, keepdims=True)
    which = lax.broadcasted_iota(jnp.int32, (8, width), 0)
    g0[...] = jnp.where(which == 0, first, dg2[...])
    g_k = rcopy(g0, gk, qs.at[2], qr.at[2], p.sibling())
    g_k.start()
    gather_step(3)
    g_k.wait()
    g0[...] += gk[...]
    g_x = rcopy(g0, gx, qs.at[3], qr.at[3], p.xpeer())
    g_x.start()
    for s in range(1, GROUPS):

        @pl.when(p.a - s >= 0)
        def _():
            bc(p.a - s, p.a, 0).wait_recv()

            @pl.when(p.a < last)
            def _():
                bc(p.a - s, p.a + 1, 2 * s).start()

            qspread(p.a - s)

        @pl.when(p.a + s <= last)
        def _():
            bc(p.a + s, p.a, 0).wait_recv()

            @pl.when(p.a > 0)
            def _():
                bc(p.a + s, p.a - 1, 2 * s + 1).start()

            qspread(p.a + s)

        if s == 1:
            out_4()
            g_x.wait()
            gy[p.chip] = g0[...] + gx[...]

            def gc(chip, slot):
                return rcopy(
                    gy.at[p.chip], gy.at[slot], ys.at[GROUPS, chip], yr.at[GROUPS, slot],
                    p.on_chip(chip),
                )

            for c in others:
                gc(c, p.chip).start()
        if s == 2:
            for z in range(GROUPS):
                pass_on(z)
            for c in others:
                gc(c, c).wait_recv()
            total = gy[0]
            for c in range(1, p.chips):
                total = total + gy[c]
            ga[p.a] = total

            def lc(slot, to):
                return rcopy(
                    ga.at[p.a], ga.at[slot], zs.at[GROUPS + to], zr.at[GROUPS + slot], p.on_line(to)
                )

            for g in line:
                lc(p.a, g).start()
    for g in range(GROUPS):
        for c in range(p.chips):
            core_share(1 - p.k, c, g).wait_recv()
    res_out = pltpu.make_async_copy(res, res_, ls.at[0])
    res_out.start()
    for g in line:
        lc(g, g).wait_recv()
    total = ga[0]
    for g in range(1, GROUPS):
        total = total + ga[g]
    gains[...] = total
    for c in others:
        if oc > 1:
            for g in range(GROUPS):
                out_spread(c, g, c).wait_recv()
                out_share(p.k, c, g).start()
    for g in [p.a] + line:
        for c in others:
            qshare(g, c, c).wait_recv()
            sc(g, p.k, c).start()
    for g in range(GROUPS):
        for c in range(p.chips):
            sc(g, 1 - p.k, c).wait_recv()
            sc(g, p.k, c).wait_send()
        for c in others:
            qshare(g, p.chip, c).wait_send()
            if oc > 1:
                out_spread(p.chip, g, c).wait_send()
        for c in range(oc):
            out_share(1 - p.k, c, g).wait_recv()
            out_share(p.k, c, g).wait_send()
        for c in range(p.chips):
            core_share(p.k, c, g).wait_send()
        for c in others:
            chip_share(p.chip, g, c).wait_send()
            yc(g, c, p.chip).wait_send()
    for c in others:
        for j in range(1, GROUPS):
            over_chips(c, p.chip, turn(p, j)).wait_send()
        qc(c, p.chip).wait_send()
        gc(c, p.chip).wait_send()
        out_chip(c, p.chip).wait_send()
    for g in line:
        zkv(p.a, g).wait_send()
        zq(p.a, g).wait_send()
        lc(p.a, g).wait_send()
        out_line(p.a, g).wait_send()
        out_back(p.a, g).wait_send()
    for s in range(GROUPS):

        @pl.when((p.a - s >= 0) & (p.a < last))
        def _():
            bc(p.a - s, p.a + 1, 2 * s).wait_send()
            line_share(p.a - s, p.a + 1, 2 * s).wait_send()

        @pl.when((p.a + s <= last) & (p.a > 0))
        def _():
            bc(p.a + s, p.a - 1, 2 * s + 1).wait_send()
            line_share(p.a + s, p.a - 1, 2 * s + 1).wait_send()

        if s > 0:

            @pl.when(p.a + s <= last)
            def _():
                rightward(p.a + s, red.at[0]).wait_send()

            @pl.when(p.a - s >= 0)
            def _():
                leftward(p.a - s, red.at[0]).wait_send()

    res_out.wait()


def back(n, lens, q3, kv, o3, l3, dog, wg, h1, rp, gmid, gfull, dg2, ysum, y0, gb, att):
    rows, width = rp.shape
    quarter = width // 4
    lanes = wg.shape[2]
    chips = n // GROUPS // 2
    keys = kv.shape[0] // GROUPS
    piece = ysum.shape[2]
    half = width // 2
    orow = half // 2
    oc = chips if orow % (chips * GROUPS * 8) == 0 else 1
    oyrow = orow // oc
    sds = jax.ShapeDtypeStruct
    v = pltpu.VMEM
    sem = lambda *shape: [DMA(shape), DMA(shape)]
    return pl.pallas_call(
        functools.partial(back_kernel, n),
        name="back",
        out_shape=(
            sds((width, rows), F32),
            sds((GROUPS, 2, chips, quarter // chips, lanes), BF16),
            sds((8, width), F32),
            sds((2, chips, GROUPS, piece, width), BF16),
            sds((2, oc, GROUPS, oyrow // GROUPS, width), BF16),
        ),
        in_specs=[SM, ANY, ANY, ANY, ANY, ANY, ANY, ANY, ANY, ANY, VM, VM, ANY, VM, ANY, ANY],
        out_specs=[VM, VM, VM, ANY, VM],
        scratch_shapes=[
            v(q3.shape, BF16),
            v(l3.shape, F32),
            v(dog.shape, BF16),
            v((2, chips, GROUPS, piece, width), BF16),
            v(h1.shape, BF16),
            v(rp.shape, BF16),
            v(gmid.shape, F32),
            v((half, width), BF16),
            v((2, rows, width), BF16),
            v((2, 2) + att.shape[1:], BF16),
            v((GROUPS, piece, width), BF16),
            v((GROUPS, piece, width), BF16),
            v(ysum.shape, BF16),
            v(q3.shape, BF16),
            v(q3.shape, F32),
            v((2 if keys <= SUB else 1, keys, 384), BF16),
            v((keys, 384), F32),
            v((keys, 384), BF16),
            v((GROUPS, chips, rows, 384), BF16),
            v((GROUPS, chips, rows, 384), BF16),
            v((GROUPS, width, lanes), BF16),
            v((GROUPS, rows, lanes), BF16),
            v((GROUPS, rows, lanes), BF16),
            v((width, lanes), F32),
            v((2, 2, quarter, lanes), BF16),
            v((quarter, lanes), BF16),
            v((chips, quarter // chips, lanes), BF16),
            v((chips, quarter // chips, lanes), BF16),
            v((GROUPS, rows * 3 // 2, 128), BF16),
            v((GROUPS, rows * 3 // 2, 128), BF16),
            v((8, width), F32),
            v((8, width), F32),
            v((8, width), F32),
            v((chips, 8, width), F32),
            v((GROUPS, 8, width), F32),
            v((GROUPS, piece, width), BF16),
            v((GROUPS, piece, width), BF16),
            v((GROUPS, piece, width), BF16),
            v((GROUPS, piece, width), BF16),
            v((orow, width), BF16),
            v((oc, oyrow, width), BF16),
            v((chips, oyrow, width), BF16),
            v((GROUPS, oyrow // GROUPS, width), BF16),
            v((GROUPS, oyrow // GROUPS, width), BF16),
            *sem(GROUPS),
            DMA((GROUPS + 10,)),
            DMA((2,)),
            *sem(GROUPS, chips),
            *sem(GROUPS + 1, chips),
            *sem(2 * GROUPS),
            *sem(GROUPS),
            *sem(4),
            *sem(chips),
            DMA((2 * GROUPS,)),
            DMA((GROUPS,)),
            *sem(GROUPS, chips),
            *sem(GROUPS),
            *sem(GROUPS),
            DMA((2 * GROUPS,)),
            DMA((GROUPS,)),
            *sem(chips, GROUPS),
            *sem(chips, GROUPS),
            *sem(chips),
            *sem(2 * GROUPS),
            *sem(1 + chips * GROUPS),
            *sem(chips, GROUPS),
            *sem(GROUPS),
            *sem(2),
            *sem(GROUPS, chips),
            *sem(GROUPS, chips),
        ],
        compiler_params=pltpu.CompilerParams(
            collective_id=2, has_side_effects=True, vmem_limit_bytes=67043328
        ),
    )(lens, q3, kv, o3, l3, dog, wg, h1, rp, gmid, gfull, dg2, ysum, y0, gb, att)


def deliver_kernel(gq, ra, rb, rd, goo, gsum, gin, out, out_, gin_, g1_, qkv_, go_, g2_, up_, down_):
    narrow = gin_.shape[0]
    half = g1_.shape[0]
    width = 2 * half
    out_[0] = out[:, :narrow]

    @pl.when(pl.program_id(0) == 0)
    def _():
        gin_[:, 0, :] = gin[:narrow, :]

    go_[...] = goo[:, :narrow].astype(F32)
    down_[...] = rd[0, :, :narrow].astype(F32)
    up_[:, :width] = ra[0].astype(F32)
    up_[:, width:] = rb[0].astype(F32)
    first = lax.axis_index("fsdp") == 0
    g1_[...] = jnp.where(first, gsum[0, :half], gsum[0, half:])
    g2_[...] = jnp.where(first, gsum[1, :half], gsum[1, half:])
    low = low_half((gq.shape[1], 128))

    def tile(g, t):
        return gq[g, :, t * 128 : (t + 1) * 128].astype(F32)

    def swap(t):
        return pltpu.roll(t, HD, 1)

    for j in range(GROUPS // 2):
        a, b = 2 * j, 2 * j + 1
        parts = []
        for t in (0, 2):
            pair = swap(tile(b, t))
            parts.append(
                (tile(a, t), jnp.where(low, tile(a, t + 1), pair), jnp.where(low, pair, swap(tile(b, t + 1))))
            )
        pair = swap(tile(b, 4))
        parts.append(
            (tile(a, 4), jnp.where(low, swap(tile(a, 3)), pair), jnp.where(low, pair, tile(b, 3)))
        )
        for i, three in enumerate(parts):
            for t, value in enumerate(three):
                at = i * width + j * 384 + t * 128
                qkv_[:, at : at + 128] = value


def deliver(gq, res, goo, gsum, gin, out):
    width, rows = gin.shape
    half = width // 2
    ff = res.shape[1]
    steps = 2
    sds = jax.ShapeDtypeStruct
    spec = pl.BlockSpec
    return pl.pallas_call(
        deliver_kernel,
        name="deliver",
        grid=(steps,),
        out_shape=(
            sds((1, rows, width - 1), BF16),
            sds((width - 1, 1, rows), F32),
            sds((half,), F32),
            sds((half, 3 * width), F32),
            sds((half, width - 1), F32),
            sds((half,), F32),
            sds((width, ff), F32),
            sds((ff, width - 1), F32),
        ),
        in_specs=[
            spec((GROUPS, half // steps, gq.shape[2]), lambda i: (0, i, 0)),
            spec((1, width // steps, width), lambda i: (0, i, 0)),
            spec((1, width // steps, width), lambda i: (0, steps + i, 0)),
            spec((1, ff // steps, width), lambda i: (1, i, 0)),
            spec((half // steps, width), lambda i: (i, 0)),
            spec(gsum.shape, lambda i: (0, 0)),
            spec((width, rows), lambda i: (0, 0)),
            spec((rows // steps, width), lambda i: (i, 0)),
        ],
        out_specs=[
            spec((1, rows // steps, width - 1), lambda i: (0, i, 0)),
            spec((width - 1, 1, rows), lambda i: (0, 0, 0)),
            spec((half,), lambda i: (0,)),
            spec((half // steps, 3 * width), lambda i: (i, 0)),
            spec((half // steps, width - 1), lambda i: (i, 0)),
            spec((half,), lambda i: (0,)),
            spec((width // steps, ff), lambda i: (i, 0)),
            spec((ff // steps, width - 1), lambda i: (i, 0)),
        ],
        compiler_params=pltpu.CompilerParams(vmem_limit_bytes=VLIM),
    )(gq, res, res, res, goo, gsum, gin, out)


def shards(n, resid, lengths, gain_one, w_qkv, w_out, gain_two, w_up, w_down, cotangent):
    width = resid.shape[2] + 1
    ff = w_up.shape[1]
    out, gmid, ysum, y0, gb, attg, dog, dg2, rp, wg, h1, q3, kv, o3, l3, gfull = front(
        n, lengths, resid[0], cotangent[0], gain_one, gain_two, w_qkv, w_out, w_up, w_down
    )
    gin, gq, gsum, res, goo = back(
        n, lengths, q3, kv, o3, l3, dog, wg, h1, rp, gmid, gfull, dg2, ysum, y0, gb, attg
    )

    half = width // 2
    delivered = deliver(
        gq.reshape(GROUPS, half, -1), res.reshape(2, ff, width), goo.reshape(half, width), gsum, gin, out
    )
    return delivered[0], jnp.transpose(delivered[1], (1, 2, 0)), *delivered[2:]


def solution(mesh):
    n = mesh.shape["ctx"]
    return jax.shard_map(
        functools.partial(shards, n),
        mesh=mesh,
        in_specs=(
            P("fsdp", "ctx", None),
            P("fsdp"),
            P("fsdp"),
            P("fsdp", None),
            P("fsdp", None),
            P("fsdp"),
            P(None, "fsdp"),
            P("fsdp", None),
            P("fsdp", "ctx", None),
        ),
        out_specs=(
            P("fsdp", "ctx", None),
            P("fsdp", "ctx", None),
            P("fsdp"),
            P("fsdp", None),
            P("fsdp", None),
            P("fsdp"),
            P(None, "fsdp"),
            P("fsdp", None),
        ),
        check_vma=False,
    )
```
